32 devices in a mesh: seq: 8 (over z, x), fsdp: 4 (over y, core).
Axes of the slice: x: 2, y: 2, z: 4, core: 2. Of those that a mesh axis runs over, the one named last changes fastest.
Arguments:
- inputs: bfloat16 [4, 8192, 768], P('fsdp', 'seq'), may hold values from -10 to 10
- cotangent: bfloat16 [4, 8192, 768], P('fsdp', 'seq'), may hold values from -6 to 6
- query_weight: bfloat16 [768, 768], P('fsdp'), may hold values from -0.21875 to 0.21875
- key_weight: bfloat16 [768, 768], P('fsdp'), may hold values from -0.21875 to 0.21875
- value_weight: bfloat16 [768, 768], P('fsdp'), may hold values from -0.21875 to 0.21875
- output_weight: bfloat16 [768, 768], P('fsdp'), may hold values from -0.21875 to 0.21875
- up_weight: bfloat16 [768, 3072], P('fsdp'), may hold values from -0.21875 to 0.21875
- down_weight: bfloat16 [3072, 768], P('fsdp'), may hold values from -0.109375 to 0.109375
- norm_gain: bfloat16 [768], P('fsdp'), may hold values from 0.5 to 1.5
- norm_shift: bfloat16 [768], P('fsdp'), may hold values from -2 to 2
- final_gain: bfloat16 [768], P('fsdp'), may hold values from 0.5 to 1.5
- final_shift: bfloat16 [768], P('fsdp'), may hold values from -2 to 2
- conv_kernel: float32 [65, 12], replicated, may hold values from -1 to 1
Outputs:
- output: bfloat16 [4, 8192, 768], P('fsdp', 'seq')
- grad_inputs: bfloat16 [4, 8192, 768], P('fsdp', 'seq')
- grad_query_weight: float32 [768, 768], P('fsdp')
- grad_key_weight: float32 [768, 768], P('fsdp')
- grad_value_weight: float32 [768, 768], P('fsdp')
- grad_output_weight: float32 [768, 768], P('fsdp')
- grad_up_weight: float32 [768, 3072], P('fsdp')
- grad_down_weight: float32 [3072, 768], P('fsdp')
- grad_norm_gain: float32 [768], P('fsdp')
- grad_norm_shift: float32 [768], P('fsdp')
- grad_final_gain: float32 [768], P('fsdp')
- grad_final_shift: float32 [768], P('fsdp')
- grad_conv_kernel: float32 [65, 12], replicated
The draws below stay inside these ranges and needn't reach their ends.
All inputs are finite; a program needn't handle non-finite values.
Results may differ from the reference program's by a relative error of at most 0.03.
Values may be sent and summed in bfloat16 or wider, within the bound.
No kernel may reach another device: no remote copies, remote signals or barrier semaphores. Data moves between devices by JAX's collectives and lax.ppermute only.
A program may use at most 256 MiB of HBM per device.

```python
import jax
import jax.numpy as jnp
from jax import lax

D = 768
FF = 3072
HEADS = 12
HDIM = 64
LANDMARKS = 64
KERNEL = 65
PINV_ITERS = 6
LEN = 8192
SEG = 128
SEQS = 4


def draw_inputs(key, part):
    jitter_key = jax.random.fold_in(key, 11)
    region_key = jax.random.fold_in(key, 23)
    jitter = jax.random.normal(jitter_key, (SEQS, LEN, D), jnp.float32)
    region = jax.random.normal(region_key, (SEQS, LANDMARKS, 1, D), jnp.float32)
    region = jnp.broadcast_to(region, (SEQS, LANDMARKS, SEG, D)).reshape(SEQS, LEN, D)
    return jnp.clip(jitter + region, -10.0, 10.0).astype(jnp.bfloat16)


def block_levels(key, extent, pieces, low, high):
    factor_of, own = 1.0, jax.random.fold_in(key, 6)
    for dim, parts in pieces:
        draws = jnp.exp(jax.random.uniform(jax.random.fold_in(own, dim), (parts,), jnp.float32, low / len(pieces), high / len(pieces)))
        factor_of = factor_of * jnp.repeat(draws, extent[dim] // parts).reshape([-1 if axis == dim else 1 for axis in range(len(extent))])
    return factor_of


def normal_values(key, dims, deviation, most, cuts=(), kind=jnp.bfloat16):
    drawn = deviation * jax.random.normal(key, dims, jnp.float32)
    if cuts:
        drawn = drawn * block_levels(key, dims, cuts, -0.22, 0.18)
    return jnp.clip(drawn, -most, most).astype(kind)


def setup_inputs(seed: int = 0) -> dict:
    streams_of = jax.random.split(jax.random.key(seed), 14)
    return {
        "inputs": draw_inputs(jax.random.fold_in(streams_of[13], 71), 0),
        "cotangent": normal_values(streams_of[1], (SEQS, LEN, D), 1.0, 6.0, ((0, 4), (1, 8))),
        "query_weight": normal_values(streams_of[2], (D, D), D ** -0.5, 0.21875, ((0, 4),)),
        "key_weight": normal_values(streams_of[3], (D, D), D ** -0.5, 0.21875, ((0, 4),)),
        "value_weight": normal_values(streams_of[4], (D, D), D ** -0.5, 0.21875, ((0, 4),)),
        "output_weight": normal_values(streams_of[5], (D, D), D ** -0.5, 0.21875, ((0, 4),)),
        "up_weight": normal_values(streams_of[6], (D, FF), D ** -0.5, 0.21875, ((0, 4),)),
        "down_weight": normal_values(streams_of[7], (FF, D), FF ** -0.5, 0.109375, ((0, 4),)),
        "norm_gain": jnp.clip(1.0 + 0.1 * jax.random.normal(streams_of[8], (D,), jnp.float32), 0.5, 1.5).astype(jnp.bfloat16),
        "norm_shift": normal_values(streams_of[9], (D,), 0.3, 2.0, ((0, 4),)),
        "final_gain": jnp.clip(1.0 + 0.1 * jax.random.normal(streams_of[10], (D,), jnp.float32), 0.5, 1.5).astype(jnp.bfloat16),
        "final_shift": normal_values(streams_of[11], (D,), 0.3, 2.0, ((0, 4),)),
        "conv_kernel": normal_values(streams_of[12], (KERNEL, HEADS), 0.2, 1.0, (), jnp.float32),
    }


PRECISE = lax.Precision.HIGHEST

@jax.custom_vjp
def low(v):
    return lax.optimization_barrier(v.astype(jnp.bfloat16)).astype(jnp.float32)

@jax.custom_vjp
def lowrank_rear(v):
    return v

def low_keep(v):
    return (low(v), None)

def low_pass(kept, grad):
    return (grad,)

def back_keep(v):
    return (v, None)

def back_low(kept, grad):
    return (low(grad),)
low.defvjp(low_keep, low_pass)
lowrank_rear.defvjp(back_keep, back_low)

def matrix_product(formula, former, latter):
    return jnp.einsum(formula, former, latter, precision=PRECISE)

def approximate_inverse(matrix):
    order_size = matrix.shape[-1]
    column_sums = lax.optimization_barrier(jnp.sum(matrix, axis=1))
    row_sums = lax.optimization_barrier(jnp.sum(matrix, axis=2))
    factor = 1.0 / (lax.optimization_barrier(jnp.max(column_sums, axis=1)) * lax.optimization_barrier(jnp.max(row_sums, axis=1)))
    approx = jnp.swapaxes(matrix, 1, 2) * factor[:, None, None]
    identity = jnp.eye(order_size, dtype=jnp.float32)
    for repeat in range(PINV_ITERS):
        applied = matrix_product('hij,hjk->hik', matrix, approx)
        nested = 7.0 * identity - applied
        nested = 15.0 * identity - matrix_product('hij,hjk->hik', applied, nested)
        nested = 13.0 * identity - matrix_product('hij,hjk->hik', applied, nested)
        approx = 0.25 * matrix_product('hij,hjk->hik', approx, nested)
    return approx

def landmark_core(landmark_queries, landmark_keys, blended_values):
    score_matrix = matrix_product('ytk,wtk->tyw', landmark_queries, landmark_keys)
    return matrix_product('ptr,prb->ptb', approximate_inverse(jax.nn.softmax(score_matrix, axis=2)), blended_values)

def normalize(residual, gain, shift):
    center = residual - lax.optimization_barrier(jnp.mean(residual, axis=-1, keepdims=True))
    variance = lax.optimization_barrier(jnp.mean(center * center, axis=-1, keepdims=True))
    return center * lax.rsqrt(variance + 1e-05) * gain + shift

def exact_gelu(values):
    return jax.nn.gelu(values, approximate=False)

def depth_conv(value_per_head, kernel):
    length = value_per_head.shape[0]
    reach = kernel.shape[0] // 2
    padded = jnp.pad(value_per_head, ((reach, reach), (0, 0), (0, 0)))
    summed = jnp.zeros(value_per_head.shape, jnp.float32)
    for offset in range(kernel.shape[0]):
        summed = summed + kernel[offset][None, :, None] * padded[offset:offset + length]
    return summed

def layer_forward(token_rows, params):
    query_weight, key_weight, value_weight, output_weight, up_weight, down_weight, norm_gain, norm_shift, final_gain, final_shift, conv_kernel = params
    factor = HDIM ** (-0.25)
    queries = low(lowrank_rear(factor * jnp.dot(token_rows, query_weight, precision=PRECISE)))
    keys = low(lowrank_rear(factor * jnp.dot(token_rows, key_weight, precision=PRECISE)))
    values = low(lowrank_rear(jnp.dot(token_rows, value_weight, precision=PRECISE)))
    query_landmark_rows = low(lax.optimization_barrier(jnp.mean(queries.reshape(LANDMARKS, SEG, D), axis=1))).reshape(LANDMARKS, HEADS, HDIM)
    key_landmark_rows = low(lax.optimization_barrier(jnp.mean(keys.reshape(LANDMARKS, SEG, D), axis=1))).reshape(LANDMARKS, HEADS, HDIM)
    query_per_head = queries.reshape(LEN, HEADS, HDIM)
    key_per_head = keys.reshape(LEN, HEADS, HDIM)
    value_per_head = values.reshape(LEN, HEADS, HDIM)
    score_lead = lowrank_rear(matrix_product('xfk,rfk->fxr', key_landmark_rows, query_per_head))
    probability_lead = low(jax.nn.softmax(score_lead, axis=1))
    score_rear = lowrank_rear(matrix_product('xfk,rfk->fxr', query_landmark_rows, key_per_head))
    probability_rear = jax.nn.softmax(score_rear, axis=2)
    blended_values = matrix_product('pal,lpx->pax', probability_rear, value_per_head)
    combined_output = low(landmark_core(query_landmark_rows, key_landmark_rows, blended_values))
    attended_rows = matrix_product('qas,qau->squ', probability_lead, combined_output)
    context = low(lowrank_rear((attended_rows + depth_conv(value_per_head, conv_kernel)).reshape(LEN, D)))
    branch = lowrank_rear(jnp.dot(context, output_weight, precision=PRECISE))
    hidden = normalize(token_rows + branch, norm_gain, norm_shift)
    expanded = lowrank_rear(jnp.dot(low(hidden), up_weight, precision=PRECISE))
    activated = low(exact_gelu(expanded))
    reduced = lowrank_rear(jnp.dot(activated, down_weight, precision=PRECISE))
    return normalize(hidden + reduced, final_gain, final_shift)

def reference(inputs, cotangent, query_weight, key_weight, value_weight, output_weight, up_weight, down_weight, norm_gain, norm_shift, final_gain, final_shift, conv_kernel):
    params = tuple((matrix.astype(jnp.float32) for matrix in (query_weight, key_weight, value_weight, output_weight, up_weight, down_weight, norm_gain, norm_shift, final_gain, final_shift, conv_kernel)))

    def one_sequence(totals, sequence_pair):
        token_rows, grad_rows = sequence_pair
        result, pullback = jax.vjp(layer_forward, token_rows.astype(jnp.float32), params)
        grad_tokens, grad_params = pullback(grad_rows.astype(jnp.float32))
        totals = jax.tree.map(jnp.add, totals, grad_params)
        return (totals, (result.astype(jnp.bfloat16), grad_tokens.astype(jnp.bfloat16)))
    zero_totals = jax.tree.map(jnp.zeros_like, params)
    totals, (outputs, grad_inputs) = lax.scan(one_sequence, zero_totals, (inputs, cotangent))
    return (outputs, grad_inputs, totals[0], totals[1], totals[2], totals[3], totals[4], totals[5], totals[6], totals[7], totals[8], totals[9], totals[10])
```

```python
import functools

import jax
import jax.numpy as jnp
from jax import lax
from jax.experimental import pallas as pl
from jax.experimental.pallas import tpu as pltpu
from jax.sharding import PartitionSpec as P

HEADS = 12
HDIM = 64
LANDMARKS = 64
KERNEL = 65
PINV_ITERS = 6
REACH = KERNEL // 2
EDGE = 128
SCALE = HDIM ** (-0.25)
F32 = jnp.float32
BF16 = jnp.bfloat16
VM = 56 * 1024 * 1024


def nn(a, b):
    return jnp.dot(a, b, preferred_element_type=F32)


def nt(a, b):
    return lax.dot_general(a, b, (((1,), (1,)), ((), ())), preferred_element_type=F32)


def tn(a, b):
    return lax.dot_general(a, b, (((0,), (0,)), ((), ())), preferred_element_type=F32)


def split(a):
    high = a.astype(BF16)
    return high, (a - high.astype(F32)).astype(BF16)


def nn3(a, b):
    ah, al = split(a)
    bh, bl = split(b)
    return nn(jnp.concatenate([ah, ah, al], 1), jnp.concatenate([bh, bl, bh], 0))


def nt3(a, b):
    ah, al = split(a)
    bh, bl = split(b)
    return nt(jnp.concatenate([ah, ah, al], 1), jnp.concatenate([bh, bl, bh], 1))


def tn3(a, b):
    ah, al = split(a)
    bh, bl = split(b)
    return tn(jnp.concatenate([ah, ah, al], 0), jnp.concatenate([bh, bl, bh], 0))


def lanes(shape):
    return lax.broadcasted_iota(jnp.int32, shape, len(shape) - 1)


def hs(h):
    return slice(h * HDIM, (h + 1) * HDIM)


def vspec():
    return pl.BlockSpec(memory_space=pltpu.VMEM)


def sspec():
    return pl.BlockSpec(memory_space=pltpu.SMEM)


def aspec():
    return pl.BlockSpec(memory_space=pl.ANY)


def shape(dims, kind):
    return jax.ShapeDtypeStruct(tuple(dims), kind)


def params():
    return pltpu.CompilerParams(vmem_limit_bytes=VM)


def cost(flops, traffic, trans=0):
    return pl.CostEstimate(flops=int(flops), bytes_accessed=int(traffic), transcendentals=int(trans))


def placed(pieces, whole, sems, me, start):
    rows = pieces[0].shape[0]
    for k, piece in enumerate(pieces):
        at = pl.multiple_of((me ^ k) * rows, 16)
        copy = pltpu.make_async_copy(piece, whole.at[pl.ds(at, rows)], sems.at[k])
        if start:
            copy.start()
        else:
            copy.wait()


def front_kernel(count, me_ref, x_ref, xm_ref, *refs):
    pieces = refs[:count]
    (xt_ref, qt_ref, kt_ref, vt_ref, fw_ref, eb_ref, mix_ref, st_ref, msg_ref, qm_ref, km_ref,
     top_ref, end_ref, w_ref, sems) = refs[count:]
    me = me_ref[0]
    placed(pieces, w_ref, sems, me, True)
    tokens, width = x_ref.shape
    step = 256
    for b in range(tokens // step):
        rows = slice(b * step, (b + 1) * step)
        xt_ref[:, rows] = x_ref[rows, :].T
    placed(pieces, w_ref, sems, me, False)
    high, low = split(xm_ref[...])
    both = w_ref[:, : 2 * width]
    marks = SCALE * (nn(high, both) + nn(low, both))
    qm = marks[:, :width].astype(BF16)
    km = marks[:, width:].astype(BF16)
    qm_ref[...] = qm
    km_ref[...] = km
    for b in range(tokens // step):
        rows = slice(b * step, (b + 1) * step)
        part = x_ref[rows, :]
        for i, (out, scale) in enumerate(((qt_ref, SCALE), (kt_ref, SCALE), (vt_ref, None))):
            y = nn(part, w_ref[:, i * width : (i + 1) * width])
            if scale is not None:
                y = y * scale
            y = y.astype(BF16)
            if i == 2 and b == 0:
                top_ref[...] = y[:REACH]
            if i == 2 and b == tokens // step - 1:
                end_ref[...] = y[step - REACH :]
            out[:, rows] = y.T
    lane = lanes((LANDMARKS, 128))
    stats = jnp.zeros((LANDMARKS, 128), F32)
    pair = []
    for h in range(HEADS):
        s = nn(km[:, hs(h)], qt_ref[hs(h), :])
        s = jnp.exp(s - jnp.max(s, axis=0, keepdims=True))
        fw_ref[hs(h), :] = (s * (1.0 / jnp.sum(s, axis=0, keepdims=True))).astype(BF16)
        s = nn(qm[:, hs(h)], kt_ref[hs(h), :])
        top = jnp.max(s, axis=1, keepdims=True).astype(BF16).astype(F32)
        e = jnp.exp(s - top).astype(BF16)
        eb_ref[hs(h), :] = e
        total = jnp.sum(e.astype(F32), axis=1, keepdims=True)
        stats = jnp.where(lane == h, top, stats)
        stats = jnp.where(lane == 16 + h, total, stats)
        pair.append(nt(e, vt_ref[hs(h), :]))
        if h % 2:
            both = jnp.concatenate(pair, 1)
            mix_ref[h // 2] = both
            msg_ref[h // 2] = both.astype(BF16)
            pair = []
    st_ref[...] = stats
    msg_ref[HEADS // 2] = stat_message(stats)


def stat_message(stats):
    lane = lanes(stats.shape)
    high = stats.astype(BF16).astype(F32)
    low = pltpu.roll(stats - high, 16, 1)
    return jnp.where((lane >= 32) & (lane < 48), low, high).astype(BF16)


def front(me, x, xm, pieces):
    tokens, width = x.shape
    pairs = HEADS // 2
    flat = shape((width, tokens), BF16)
    return pl.pallas_call(
        functools.partial(front_kernel, len(pieces)),
        out_shape=[flat] * 6
        + [
            shape((pairs, LANDMARKS, 128), F32),
            shape((LANDMARKS, 128), F32),
            shape((pairs + 1, LANDMARKS, 128), BF16),
            shape((LANDMARKS, width), BF16),
            shape((LANDMARKS, width), BF16),
            shape((REACH, width), BF16),
            shape((REACH, width), BF16),
        ],
        in_specs=[sspec(), vspec(), vspec()] + [aspec()] * len(pieces),
        out_specs=[vspec()] * 13,
        scratch_shapes=[
            pltpu.VMEM((width, 3 * width), BF16),
            pltpu.SemaphoreType.DMA((len(pieces),)),
        ],
        compiler_params=params(),
        cost_estimate=cost(4.5e9, 16e6, 2e6),
        name="front",
    )(me, x, xm, *pieces)


def merge_kernel(mix_ref, st_ref, got_ref, mix_out, st_out, msg_ref):
    lane = lanes((LANDMARKS, 128))
    got = got_ref[HEADS // 2].astype(F32)
    stats = st_ref[...]
    got = got + jnp.where((lane >= 16) & (lane < 32), pltpu.roll(got, 112, 1), 0.0)
    largest = jnp.maximum(stats, got)
    mine = jnp.exp(jnp.minimum(stats - largest, 0.0))
    theirs = jnp.exp(jnp.minimum(got - largest, 0.0))
    totals = stats * pltpu.roll(mine, 16, 1) + got * pltpu.roll(theirs, 16, 1)
    new = jnp.where(lane < 16, largest, jnp.where(lane < 32, totals, 0.0))
    st_out[...] = new
    for i in range(HEADS // 2):
        a = jnp.where(lane < 64, mine[:, 2 * i : 2 * i + 1], mine[:, 2 * i + 1 : 2 * i + 2])
        b = jnp.where(lane < 64, theirs[:, 2 * i : 2 * i + 1], theirs[:, 2 * i + 1 : 2 * i + 2])
        y = mix_ref[i] * a + got_ref[i].astype(F32) * b
        mix_out[i] = y
        msg_ref[i] = y.astype(BF16)
    msg_ref[HEADS // 2] = stat_message(new)


def merge(mix, stats, got):
    return pl.pallas_call(
        merge_kernel,
        out_shape=[shape(mix.shape, F32), shape(stats.shape, F32), shape(got.shape, BF16)],
        in_specs=[vspec()] * 3,
        out_specs=[vspec()] * 3,
        compiler_params=params(),
        cost_estimate=cost(1e6, 1e6),
        name="merge",
    )(mix, stats, got)


def eye(scale):
    n = LANDMARKS
    return jnp.where(
        lax.broadcasted_iota(jnp.int32, (n, n), 0) == lax.broadcasted_iota(jnp.int32, (n, n), 1),
        jnp.float32(scale),
        0.0,
    )


def landmark_softmax(qm, km, h):
    s = nt(qm[:, hs(h)], km[:, hs(h)])
    s = jnp.exp(s - jnp.max(s, axis=1, keepdims=True))
    return s / jnp.sum(s, axis=1, keepdims=True)


def first_inverse(a):
    columns = jnp.max(jnp.sum(a, axis=0, keepdims=True), axis=1, keepdims=True)
    rows = jnp.max(jnp.sum(a, axis=1, keepdims=True), axis=0, keepdims=True)
    return a.T * (1.0 / (columns * rows))


def inverse_kernel(qm_ref, km_ref, a_ref, z_ref):
    qm, km = qm_ref[...], km_ref[...]
    for h in range(HEADS):
        a = landmark_softmax(qm, km, h)
        a_ref[h] = a
        z_ref[h] = first_inverse(a)

    def step(_, carry):
        ps = [nn3(a_ref[h], z_ref[h]) for h in range(HEADS)]
        ns = [eye(7.0) - p for p in ps]
        ns = [eye(15.0) - nn3(p, n) for p, n in zip(ps, ns)]
        ns = [eye(13.0) - nn3(p, n) for p, n in zip(ps, ns)]
        for h in range(HEADS):
            z_ref[h] = 0.25 * nn3(z_ref[h], ns[h])
        return carry

    lax.fori_loop(0, PINV_ITERS, step, 0)


def inverse(qm, km):
    square = shape((HEADS, LANDMARKS, LANDMARKS), F32)
    return pl.pallas_call(
        inverse_kernel,
        out_shape=[square] * 2,
        in_specs=[vspec()] * 2,
        out_specs=[vspec()] * 2,
        compiler_params=params(),
        cost_estimate=cost(1e9, 1e6),
        name="inverse",
    )(qm, km)


def inverse_back_kernel(qm_ref, km_ref, a_ref, mix_ref, gc_ref, gq_ref, gk_ref, zs, ps, ms, ns, gz, ga):
    qm, km = qm_ref[...], km_ref[...]
    every = range(HEADS)
    for h in every:
        zs[0, h] = first_inverse(a_ref[h])

    def ahead(i, carry):
        p = [nn3(a_ref[h], zs[i, h]) for h in every]
        m = [eye(15.0) - nn3(x, eye(7.0) - x) for x in p]
        n = [eye(13.0) - nn3(x, y) for x, y in zip(p, m)]
        for h in every:
            ps[i, h] = p[h]
            ms[i, h] = m[h]
            ns[i, h] = n[h]
            zs[i + 1, h] = 0.25 * nn3(zs[i, h], n[h])
        return carry

    lax.fori_loop(0, PINV_ITERS - 1, ahead, 0)
    last = PINV_ITERS - 1
    for h in every:
        p = nn3(a_ref[h], zs[last, h])
        m = eye(15.0) - nn3(p, eye(7.0) - p)
        ps[last, h] = p
        ms[last, h] = m
        ns[last, h] = eye(13.0) - nn3(p, m)
        half = slice((h % 2) * HDIM, (h % 2) * HDIM + HDIM)
        gz[h] = nt3(gc_ref[h // 2][:, half], mix_ref[h // 2][:, half])
        ga[h] = jnp.zeros((LANDMARKS, LANDMARKS), F32)

    def back(i, carry):
        i = last - i
        g = [0.25 * gz[h] for h in every]
        g3 = [-tn3(zs[i, h], g[h]) for h in every]
        gz1 = [nt3(g[h], ns[i, h]) for h in every]
        gp = [nt3(g3[h], ms[i, h]) for h in every]
        g2 = [-tn3(ps[i, h], g3[h]) for h in every]
        gp = [gp[h] + nt3(g2[h], eye(7.0) - ps[i, h]) for h in every]
        gp = [gp[h] - tn3(ps[i, h], g2[h]) for h in every]
        for h in every:
            ga[h] = ga[h] + nt3(gp[h], zs[i, h])
            gz[h] = gz1[h] + tn3(a_ref[h], gp[h])
        return carry

    lax.fori_loop(0, PINV_ITERS, back, 0)
    n = LANDMARKS
    for pair in range(HEADS // 2):
        gqs, gks = [], []
        for h in (2 * pair, 2 * pair + 1):
            a = a_ref[h]
            csum = jnp.sum(a, axis=0, keepdims=True)
            rsum = jnp.sum(a, axis=1, keepdims=True)
            cmax = jnp.max(csum, axis=1, keepdims=True)
            rmax = jnp.max(rsum, axis=0, keepdims=True)
            scale = 1.0 / (cmax * rmax)
            gfirst = gz[h]
            gs = jnp.sum(jnp.sum(gfirst * a.T, axis=1, keepdims=True), axis=0, keepdims=True)
            ctop = (csum == cmax).astype(F32)
            rtop = (rsum == rmax).astype(F32)
            gcol = -gs * scale / cmax * ctop / jnp.sum(ctop, axis=1, keepdims=True)
            grow = -gs * scale / rmax * rtop / jnp.sum(rtop, axis=0, keepdims=True)
            g = ga[h] + gfirst.T * scale + gcol + grow
            g = a * (g - jnp.sum(g * a, axis=1, keepdims=True))
            high, low = split(g)
            gqs.append(nn(jnp.concatenate([high, low], 1), jnp.concatenate([km[:, hs(h)]] * 2, 0)))
            gks.append(tn(jnp.concatenate([high, low], 0), jnp.concatenate([qm[:, hs(h)]] * 2, 0)))
        both = slice(pair * 128, pair * 128 + 128)
        gq_ref[:, both] = jnp.concatenate(gqs, 1)
        gk_ref[:, both] = jnp.concatenate(gks, 1)


def inverse_back(qm, km, a, mix, gc):
    square = (HEADS, LANDMARKS, LANDMARKS)
    out = shape(qm.shape, F32)
    return pl.pallas_call(
        inverse_back_kernel,
        out_shape=[out] * 2,
        in_specs=[vspec()] * 5,
        out_specs=[vspec()] * 2,
        scratch_shapes=[pltpu.VMEM((PINV_ITERS,) + square, F32) for _ in range(4)]
        + [pltpu.VMEM(square, F32)] * 2,
        compiler_params=params(),
        cost_estimate=cost(3e9, 2e6),
        name="inverse_back",
    )(qm, km, a, mix, gc)


def widen(out_ref, flat_ref, before_ref, after_ref):
    width, tokens = flat_ref.shape
    zero = jnp.zeros((EDGE - REACH, width), BF16)
    out_ref[:, :EDGE] = jnp.concatenate([zero, before_ref[...]], 0).T
    out_ref[:, EDGE : EDGE + tokens] = flat_ref[...]
    out_ref[:, EDGE + tokens :] = jnp.concatenate([after_ref[...], zero], 0).T


def band(row, step):
    wide = jnp.broadcast_to(row, (step, step + 2 * EDGE))
    return pltpu.roll(wide, 0, 1, stride=1, stride_axis=0).astype(BF16)


def stacked(ref, h, step, margin):
    blocks = (ref.shape[1] - 2 * margin) // step if margin else ref.shape[1] // step
    return jnp.concatenate(
        [ref[hs(h), b * step : (b + 1) * step + 2 * margin] for b in range(blocks)], 0
    )


def conv_kernel_body(vt_ref, before_ref, after_ref, taps_ref, out_ref, wide_ref):
    widen(wide_ref, vt_ref, before_ref, after_ref)
    step = 256
    for h in range(HEADS):
        y = nt(stacked(wide_ref, h, step, EDGE), band(taps_ref[h : h + 1, :], step))
        for b in range(vt_ref.shape[1] // step):
            out_ref[hs(h), b * step : (b + 1) * step] = y[b * HDIM : (b + 1) * HDIM, :]


def conv(vt, before, after, taps):
    width, tokens = vt.shape
    return pl.pallas_call(
        conv_kernel_body,
        out_shape=shape(vt.shape, F32),
        in_specs=[vspec()] * 4,
        out_specs=vspec(),
        scratch_shapes=[pltpu.VMEM((width, tokens + 2 * EDGE), BF16)],
        compiler_params=params(),
        cost_estimate=cost(2e9, 6e6),
        name="conv",
    )(vt, before, after, taps)


def conv_back_kernel(vt_ref, vb_ref, va_ref, gt_ref, gb_ref, ga_ref, taps_ref, out_ref, tap_ref, vwide, gwide):
    widen(vwide, vt_ref, vb_ref, va_ref)
    widen(gwide, gt_ref, gb_ref, ga_ref)
    step = 256
    tokens = vt_ref.shape[1]
    flip = (
        lax.broadcasted_iota(jnp.int32, (step, step), 0)
        + lax.broadcasted_iota(jnp.int32, (step, step), 1)
        == step - 1
    ).astype(BF16)
    rows = []
    for h in range(HEADS):
        y = nt(stacked(gwide, h, step, EDGE), band(taps_ref[h : h + 1, :], step))
        for b in range(tokens // step):
            out_ref[hs(h), b * step : (b + 1) * step] = y[b * HDIM : (b + 1) * HDIM, :]
        turned = nn(stacked(gt_ref, h, step, 0), flip).astype(BF16)
        d = tn(turned, stacked(vwide, h, step, EDGE))
        d = pltpu.roll(d, 0, 1, stride=1, stride_axis=0)
        rows.append(jnp.sum(d, axis=0, keepdims=True))
    rows = jnp.concatenate(rows + [jnp.zeros((4, step + 2 * EDGE), F32)], 0)
    first = step - 1 + EDGE - REACH
    tap_ref[...] = pltpu.roll(rows, step + 2 * EDGE - first, 1)[:, :128]


def conv_back(vt, vb, va, gt, gb, ga, taps):
    width, tokens = vt.shape
    wide = pltpu.VMEM((width, tokens + 2 * EDGE), BF16)
    return pl.pallas_call(
        conv_back_kernel,
        out_shape=[shape(vt.shape, F32), shape((16, 128), F32)],
        in_specs=[vspec()] * 7,
        out_specs=[vspec()] * 2,
        scratch_shapes=[wide, wide],
        compiler_params=params(),
        cost_estimate=cost(4e9, 10e6),
        name="conv_back",
    )(vt, vb, va, gt, gb, ga, taps)


def gelu_pair(x):
    phi = 0.5 * (1.0 + lax.erf(x * (0.5**0.5)))
    return x * phi, phi + x * ((0.5 / jnp.pi) ** 0.5 * jnp.exp(-0.5 * x * x))


def norm_stats(r):
    center = r - jnp.mean(r, axis=-1, keepdims=True)
    rstd = lax.rsqrt(jnp.mean(center * center, axis=-1, keepdims=True) + 1e-05)
    return center * rstd, rstd


def norm_back(gy, xhat, rstd):
    return rstd * (
        gy - jnp.mean(gy, axis=-1, keepdims=True) - xhat * jnp.mean(gy * xhat, axis=-1, keepdims=True)
    )


def mid1_kernel(count, me_ref, z_ref, mix_ref, st_ref, fw_ref, conv_ref, x_ref, gains_ref, *refs):
    wo, up = refs[:count], refs[count : 2 * count]
    (ctx_ref, hidt_ref, xhat_ref, rstd_ref, act_ref, slope_ref, comb_ref, mixn_ref,
     wo_ref, up_ref, sems) = refs[2 * count :]
    me = me_ref[0]

    @pl.when(pl.program_id(0) == 0)
    def _():
        placed(wo, wo_ref, sems.at[0], me, True)
        placed(up, up_ref, sems.at[1], me, True)
        lane = lanes((LANDMARKS, 128))
        stats = st_ref[...]
        for i in range(HEADS // 2):
            low, high = 16 + 2 * i, 17 + 2 * i
            total = jnp.where(lane < 64, stats[:, low : low + 1], stats[:, high : high + 1])
            mixed = mix_ref[i] / total
            mixn_ref[i] = mixed
            comb_ref[i] = jnp.concatenate(
                [nn3(z_ref[2 * i], mixed[:, :HDIM]), nn3(z_ref[2 * i + 1], mixed[:, HDIM:])], 1
            ).astype(BF16)
        placed(wo, wo_ref, sems.at[0], me, False)
        placed(up, up_ref, sems.at[1], me, False)

    for h in range(HEADS):
        half = slice((h % 2) * HDIM, (h % 2) * HDIM + HDIM)
        att = tn(comb_ref[h // 2][:, half], fw_ref[hs(h), :])
        ctx_ref[hs(h), :] = (att + conv_ref[hs(h), :]).astype(BF16)
    context = ctx_ref[...].T
    branch = nn(context, wo_ref[...])
    xhat, rstd = norm_stats(x_ref[...].astype(F32) + branch)
    xhat_ref[...] = xhat
    rstd_ref[...] = jnp.broadcast_to(rstd, rstd_ref.shape)
    hidden = (xhat * gains_ref[0:1, :] + gains_ref[1:2, :]).astype(BF16)
    hidt_ref[...] = hidden.T
    step = 512
    for c in range(up_ref.shape[1] // step):
        cols = slice(c * step, (c + 1) * step)
        act, slope = gelu_pair(nn(hidden, up_ref[:, cols]))
        act_ref[:, cols] = act.astype(BF16)
        slope_ref[:, cols] = slope.astype(BF16)


def mid1(me, z, mix, stats, fw, convt, x, gains, wo, up):
    tokens, width = x.shape
    ff = up[0].shape[1]
    step = 256
    pairs = HEADS // 2

    def whole(a):
        return pl.BlockSpec(a.shape, lambda i, n=a.ndim: (0,) * n)

    tall = pl.BlockSpec((width, step), lambda i: (0, i))
    row = pl.BlockSpec((step, width), lambda i: (i, 0))
    big = pl.BlockSpec((step, ff), lambda i: (i, 0))
    small = pl.BlockSpec((pairs, LANDMARKS, 128), lambda i: (0, 0, 0))
    return pl.pallas_call(
        functools.partial(mid1_kernel, len(wo)),
        grid=(tokens // step,),
        out_shape=[
            shape((width, tokens), BF16),
            shape((width, tokens), BF16),
            shape((tokens, width), F32),
            shape((tokens, 128), F32),
            shape((tokens, ff), BF16),
            shape((tokens, ff), BF16),
            shape((pairs, LANDMARKS, 128), BF16),
            shape((pairs, LANDMARKS, 128), F32),
        ],
        in_specs=[sspec(), whole(z), whole(mix), whole(stats), tall, tall, row, whole(gains)]
        + [aspec()] * (len(wo) + len(up)),
        out_specs=[tall, tall, row, pl.BlockSpec((step, 128), lambda i: (i, 0)), big, big, small, small],
        scratch_shapes=[
            pltpu.VMEM((width, width), BF16),
            pltpu.VMEM((width, ff), BF16),
            pltpu.SemaphoreType.DMA((2, len(wo))),
        ],
        compiler_params=params(),
        cost_estimate=cost(20e9, 30e6, 6e6),
        name="mid_one",
    )(me, z, mix, stats, fw, convt, x, gains, *wo, *up)


def mid2_kernel(count, me_ref, act_ref, xhat_ref, ct_ref, gains_ref, *refs):
    down = refs[:count]
    out_ref, second_ref, redt_ref, sums_ref, down_ref, sems = refs[count:]
    me = me_ref[0]

    @pl.when(pl.program_id(0) == 0)
    def _():
        placed(down, down_ref, sems, me, True)
        sums_ref[...] = jnp.zeros_like(sums_ref)
        placed(down, down_ref, sems, me, False)

    reduced = nn(act_ref[...], down_ref[...])
    hidden = xhat_ref[...] * gains_ref[0:1, :] + gains_ref[1:2, :]
    xhat, rstd = norm_stats(hidden + reduced)
    out_ref[...] = (xhat * gains_ref[2:3, :] + gains_ref[3:4, :]).astype(BF16)
    ct = ct_ref[...].astype(F32)
    sums_ref[0:1, :] = sums_ref[0:1, :] + jnp.sum(ct * xhat, axis=0, keepdims=True)
    sums_ref[1:2, :] = sums_ref[1:2, :] + jnp.sum(ct, axis=0, keepdims=True)
    second = norm_back(ct * gains_ref[2:3, :], xhat, rstd)
    second_ref[...] = second
    redt_ref[...] = second.astype(BF16).T


def mid2(me, act, xhat, ct, gains, down):
    tokens, width = ct.shape
    ff = act.shape[1]
    step = 256
    row = pl.BlockSpec((step, width), lambda i: (i, 0))
    return pl.pallas_call(
        functools.partial(mid2_kernel, len(down)),
        grid=(tokens // step,),
        out_shape=[
            shape((tokens, width), BF16),
            shape((tokens, width), F32),
            shape((width, tokens), BF16),
            shape((8, width), F32),
        ],
        in_specs=[
            sspec(),
            pl.BlockSpec((step, ff), lambda i: (i, 0)),
            row,
            row,
            pl.BlockSpec(gains.shape, lambda i: (0, 0)),
        ]
        + [aspec()] * len(down),
        out_specs=[
            row,
            row,
            pl.BlockSpec((width, step), lambda i: (0, i)),
            pl.BlockSpec((8, width), lambda i: (0, 0)),
        ],
        scratch_shapes=[pltpu.VMEM((ff, width), BF16), pltpu.SemaphoreType.DMA((len(down),))],
        compiler_params=params(),
        cost_estimate=cost(7e9, 20e6),
        name="mid_two",
    )(me, act, xhat, ct, gains, *down)


def mid3_kernel(count, me_ref, second_ref, slope_ref, xhat_ref, rstd_ref, fw_ref, gains_ref, *refs):
    wo, up, down = refs[:count], refs[count : 2 * count], refs[2 * count : 3 * count]
    (ge_ref, first_ref, branch_ref, gct_ref, top_ref, end_ref, sums_ref, gc_ref,
     wo_ref, up_ref, down_ref, sems) = refs[3 * count :]
    me = me_ref[0]
    at = pl.program_id(0)

    @pl.when(at == 0)
    def _():
        placed(down, down_ref, sems.at[0], me, True)
        placed(up, up_ref, sems.at[1], me, True)
        placed(wo, wo_ref, sems.at[2], me, True)
        sums_ref[...] = jnp.zeros_like(sums_ref)
        gc_ref[...] = jnp.zeros_like(gc_ref)
        placed(down, down_ref, sems.at[0], me, False)
        placed(up, up_ref, sems.at[1], me, False)
        placed(wo, wo_ref, sems.at[2], me, False)

    second = second_ref[...]
    red = second.astype(BF16)
    step = 512
    g = second
    for c in range(up_ref.shape[1] // step):
        cols = slice(c * step, (c + 1) * step)
        ge = (nt(red, down_ref[cols, :]) * slope_ref[:, cols].astype(F32)).astype(BF16)
        ge_ref[:, cols] = ge
        g = g + nt(ge, up_ref[:, cols])
    xhat = xhat_ref[...]
    sums_ref[0:1, :] = sums_ref[0:1, :] + jnp.sum(g * xhat, axis=0, keepdims=True)
    sums_ref[1:2, :] = sums_ref[1:2, :] + jnp.sum(g, axis=0, keepdims=True)
    first = norm_back(g * gains_ref[0:1, :], xhat, rstd_ref[:, 0:1])
    first_ref[...] = first
    branch = first.astype(BF16)
    branch_ref[...] = branch
    gctx = nt(branch, wo_ref[...]).astype(BF16)

    @pl.when(at == 0)
    def _():
        top_ref[...] = gctx[:REACH]

    @pl.when(at == pl.num_programs(0) - 1)
    def _():
        end_ref[...] = gctx[gctx.shape[0] - REACH :]

    gct_ref[...] = gctx.T
    for i in range(HEADS // 2):
        gc_ref[i] = gc_ref[i] + jnp.concatenate(
            [nt(fw_ref[hs(h), :], gct_ref[hs(h), :]) for h in (2 * i, 2 * i + 1)], 1
        )


def mid3(me, second, slope, xhat, rstd, fw, gains, wo, up, down):
    tokens, width = second.shape
    ff = slope.shape[1]
    step = 256
    pairs = HEADS // 2
    row = pl.BlockSpec((step, width), lambda i: (i, 0))
    tall = pl.BlockSpec((width, step), lambda i: (0, i))
    big = pl.BlockSpec((step, ff), lambda i: (i, 0))
    edge = pl.BlockSpec((REACH, width), lambda i: (0, 0))
    return pl.pallas_call(
        functools.partial(mid3_kernel, len(wo)),
        grid=(tokens // step,),
        out_shape=[
            shape((tokens, ff), BF16),
            shape((tokens, width), F32),
            shape((tokens, width), BF16),
            shape((width, tokens), BF16),
            shape((REACH, width), BF16),
            shape((REACH, width), BF16),
            shape((8, width), F32),
            shape((pairs, LANDMARKS, 128), F32),
        ],
        in_specs=[
            sspec(),
            row,
            big,
            row,
            pl.BlockSpec((step, 128), lambda i: (i, 0)),
            tall,
            pl.BlockSpec(gains.shape, lambda i: (0, 0)),
        ]
        + [aspec()] * (3 * len(wo)),
        out_specs=[
            big,
            row,
            row,
            tall,
            edge,
            edge,
            pl.BlockSpec((8, width), lambda i: (0, 0)),
            pl.BlockSpec((pairs, LANDMARKS, 128), lambda i: (0, 0, 0)),
        ],
        scratch_shapes=[
            pltpu.VMEM((width, width), BF16),
            pltpu.VMEM((width, ff), BF16),
            pltpu.VMEM((ff, width), BF16),
            pltpu.SemaphoreType.DMA((3, len(wo))),
        ],
        compiler_params=params(),
        cost_estimate=cost(20e9, 40e6),
        name="mid_three",
    )(me, second, slope, xhat, rstd, fw, gains, *wo, *up, *down)


def lead_back_kernel(gct_ref, fw_ref, qt_ref, comb_ref, km_ref, gq_ref, gkm_ref):
    km = km_ref[...]
    pair = []
    for h in range(HEADS):
        half = slice((h % 2) * HDIM, (h % 2) * HDIM + HDIM)
        pf = fw_ref[hs(h), :].astype(F32)
        g = nn(comb_ref[h // 2][:, half], gct_ref[hs(h), :])
        gs = (pf * (g - jnp.sum(pf * g, axis=0, keepdims=True))).astype(BF16)
        gq_ref[hs(h), :] = tn(km[:, hs(h)], gs).astype(BF16)
        pair.append(nt(gs, qt_ref[hs(h), :]))
        if h % 2:
            gkm_ref[:, (h - 1) * HDIM : (h + 1) * HDIM] = jnp.concatenate(pair, 1)
            pair = []


def lead_back(gct, fw, qt, comb, km):
    return pl.pallas_call(
        lead_back_kernel,
        out_shape=[shape(gct.shape, BF16), shape(km.shape, F32)],
        in_specs=[vspec()] * 5,
        out_specs=[vspec()] * 2,
        compiler_params=params(),
        cost_estimate=cost(3e9, 6e6),
        name="lead_back",
    )(gct, fw, qt, comb, km)


def rear_back_kernel(z_ref, gc_ref, mixn_ref, st_ref, own_ref, eb_ref, vt_ref, kt_ref, qm_ref, gvc_ref,
                     gk_ref, gv_ref, gqm_ref):
    qm = qm_ref[...]
    scale = jnp.exp(own_ref[...] - st_ref[...])
    pair = []
    for h in range(HEADS):
        half = slice((h % 2) * HDIM, (h % 2) * HDIM + HDIM)
        gmix = tn3(z_ref[h], gc_ref[h // 2][:, half]).astype(BF16)
        dot = jnp.sum(gmix.astype(F32) * mixn_ref[h // 2][:, half], axis=1, keepdims=True)
        factor = scale[:, h : h + 1] / st_ref[:, 16 + h : 17 + h]
        pb = eb_ref[hs(h), :].astype(F32) * factor
        gs = (pb * (nn(gmix, vt_ref[hs(h), :]) - dot)).astype(BF16)
        gk_ref[hs(h), :] = tn(qm[:, hs(h)], gs).astype(BF16)
        gv_ref[hs(h), :] = (tn(gmix, pb.astype(BF16)) + gvc_ref[hs(h), :]).astype(BF16)
        pair.append(nt(gs, kt_ref[hs(h), :]))
        if h % 2:
            gqm_ref[:, (h - 1) * HDIM : (h + 1) * HDIM] = jnp.concatenate(pair, 1)
            pair = []


def rear_back(z, gc, mixn, stats, own, eb, vt, kt, qm, gvc):
    return pl.pallas_call(
        rear_back_kernel,
        out_shape=[shape(vt.shape, BF16), shape(vt.shape, BF16), shape(qm.shape, F32)],
        in_specs=[vspec()] * 10,
        out_specs=[vspec()] * 3,
        compiler_params=params(),
        cost_estimate=cost(3e9, 10e6),
        name="rear_back",
    )(z, gc, mixn, stats, own, eb, vt, kt, qm, gvc)


def last_kernel(count, segment, me_ref, gq_ref, gk_ref, gv_ref, first_ref, own_ref, *refs):
    pieces = refs[:count]
    out_ref, w_ref, sems = refs[count:]
    me = me_ref[0]
    width = gq_ref.shape[0]

    @pl.when(pl.program_id(0) == 0)
    def _():
        placed(pieces, w_ref, sems, me, True)
        placed(pieces, w_ref, sems, me, False)

    wq, wk, wv = (w_ref[:, i * width : (i + 1) * width] for i in range(3))
    g = SCALE * (nn(wq, gq_ref[...]) + nn(wk, gk_ref[...])) + nn(wv, gv_ref[...])
    own = own_ref[...]
    marks = (SCALE / segment) * (
        nt(own[:, :width].astype(BF16), wq) + nt(own[:, width:].astype(BF16), wk)
    )
    step = out_ref.shape[0]
    token = pl.program_id(0) * step + lax.broadcasted_iota(jnp.int32, (step, own.shape[0]), 0)
    mark = lax.broadcasted_iota(jnp.int32, (step, own.shape[0]), 1) * segment
    pick = ((token >= mark) & (token < mark + segment)).astype(BF16)
    high, low = split(marks)
    spread = nn(pick, high) + nn(pick, low)
    out_ref[...] = (first_ref[...] + g.T + spread).astype(BF16)


def last(me, gq, gk, gv, first, own, pieces, segment):
    width, tokens = gq.shape
    step = 256
    tall = pl.BlockSpec((width, step), lambda i: (0, i))
    row = pl.BlockSpec((step, width), lambda i: (i, 0))
    return pl.pallas_call(
        functools.partial(last_kernel, len(pieces), segment),
        grid=(tokens // step,),
        out_shape=shape((tokens, width), BF16),
        in_specs=[sspec(), tall, tall, tall, row, pl.BlockSpec(own.shape, lambda i: (0, 0))]
        + [aspec()] * len(pieces),
        out_specs=row,
        scratch_shapes=[
            pltpu.VMEM((width, 3 * width), BF16),
            pltpu.SemaphoreType.DMA((len(pieces),)),
        ],
        compiler_params=params(),
        cost_estimate=cost(4e9, 12e6),
        name="last",
    )(me, gq, gk, gv, first, own, *pieces)


def bits(axis):
    size = lax.axis_size(axis)
    assert size & (size - 1) == 0
    return [1 << i for i in range(size.bit_length() - 1)]


def swap(array, axis, bit):
    return lax.ppermute(array, axis, [(i, i ^ bit) for i in range(lax.axis_size(axis))])


def shift(array, axis, by):
    size = lax.axis_size(axis)
    return lax.ppermute(array, axis, [(i, i + by) for i in range(size) if 0 <= i + by < size])


def gathered(array, axis):
    pieces = {0: array}
    order = bits(axis)
    for bit in order[1:] + order[:1]:
        pieces.update({k | bit: swap(piece, axis, bit) for k, piece in list(pieces.items())})
    return [pieces[k] for k in range(lax.axis_size(axis))]


def scattered(pieces, axis):
    pieces = dict(enumerate(pieces))
    for bit in bits(axis):
        pieces = {
            k: (piece.astype(F32) + swap(pieces[k | bit], axis, bit).astype(F32)).astype(BF16)
            for k, piece in pieces.items()
            if not k & bit
        }
    return pieces[0]


def joined(array, axis, dim):
    index = lax.axis_index(axis)
    for bit in bits(axis):
        other = swap(array, axis, bit)
        upper = (index & bit) != 0
        array = jnp.where(
            upper,
            jnp.concatenate([other, array], dim),
            jnp.concatenate([array, other], dim),
        )
    return array


def halved(array, axis, dim):
    index = lax.axis_index(axis)
    for bit in reversed(bits(axis)):
        half = array.shape[dim] // 2
        upper = ((index & bit) != 0).astype(jnp.int32)
        keep = lax.dynamic_slice_in_dim(array, upper * half, half, dim)
        send = lax.dynamic_slice_in_dim(array, (1 - upper) * half, half, dim)
        array = (keep.astype(F32) + swap(send, axis, bit).astype(F32)).astype(BF16)
    return array


def halved_near(array, axis, dim):
    index = lax.axis_index(axis)
    for bit in bits(axis):
        half = array.shape[dim] // 2
        upper = ((index & bit) != 0).astype(jnp.int32)
        keep = lax.dynamic_slice_in_dim(array, upper * half, half, dim)
        send = lax.dynamic_slice_in_dim(array, (1 - upper) * half, half, dim)
        array = (keep.astype(F32) + swap(send, axis, bit).astype(F32)).astype(BF16)
    return array


def joined_near(array, axis, dim):
    index = lax.axis_index(axis)
    for bit in reversed(bits(axis)):
        other = swap(array, axis, bit)
        array = jnp.where(
            (index & bit) != 0,
            jnp.concatenate([other, array], dim),
            jnp.concatenate([array, other], dim),
        )
    return array


def summed(pieces, dim=0):
    mine = scattered(pieces, "fsdp")
    return joined_near(halved_near(mine, "seq", dim), "seq", dim)


def shards(
    inputs,
    cotangent,
    query_weight,
    key_weight,
    value_weight,
    output_weight,
    up_weight,
    down_weight,
    norm_gain,
    norm_shift,
    final_gain,
    final_shift,
    conv_kernel,
):
    x = inputs[0]
    ct = cotangent[0]
    tokens, width = x.shape
    marks = LANDMARKS // lax.axis_size("seq")
    segment = tokens // marks
    count = lax.axis_size("fsdp")
    rows = width // count
    ff = up_weight.shape[1]
    here = lax.axis_index("fsdp")
    me = here.astype(jnp.int32).reshape(1)
    place = lax.axis_index("seq")

    wqkv = gathered(jnp.concatenate([query_weight, key_weight, value_weight], 1), "fsdp")
    xm = jnp.mean(x.reshape(marks, segment, width), axis=1, dtype=F32)
    xm = joined(xm, "seq", 0)
    gains = jnp.stack([norm_gain, norm_shift, final_gain, final_shift])
    gains = lax.all_gather(gains, "fsdp", axis=1, tiled=True).astype(F32)
    gains = jnp.pad(gains, ((0, 4), (0, 0)))
    wo = gathered(output_weight, "fsdp")
    up = gathered(up_weight, "fsdp")
    down = gathered(down_weight, "fsdp")
    space = 256 + 2 * EDGE
    taps = jnp.pad(conv_kernel.T, ((0, 4), (EDGE - REACH, space - KERNEL - EDGE + REACH)))
    spat = jnp.pad(conv_kernel[::-1].T, ((0, 4), (EDGE - REACH, space - KERNEL - EDGE + REACH)))

    (xt, qt, kt, vt, fw, eb, mix, stats, msg, qm, km, v_top, v_end) = front(me, x, xm, wqkv)
    own = stats
    v_before = shift(v_end, "seq", 1)
    v_after = shift(v_top, "seq", -1)
    a, z = inverse(qm, km)
    for bit in bits("seq"):
        mix, stats, msg = merge(mix, stats, swap(msg, "seq", bit))
    convt = conv(vt, v_before, v_after, taps)

    ctxt, hidt, xhat, rstd, act, slope, comb, mixn = mid1(
        me, z, mix, stats, fw, convt, x, gains, wo, up
    )
    out, second, redt, sums2 = mid2(me, act, xhat, ct, gains, down)

    def cut(array, k, size, dim):
        return lax.dynamic_slice_in_dim(array, (here ^ k) * size, size, dim)

    part = ff // count
    g_down = summed([nn(redt, cut(act, k, part, 1)).astype(BF16) for k in range(count)])
    ge, first, branch, gct, g_top, g_end, sums1, gc = mid3(
        me, second, slope, xhat, rstd, fw, gains, wo, up, down
    )
    g_before = shift(g_end, "seq", 1)
    g_after = shift(g_top, "seq", -1)
    for bit in bits("seq"):
        gc = gc + swap(gc.astype(BF16), "seq", bit).astype(F32)
    g_up = summed([nn(cut(hidt, k, rows, 0), ge).astype(BF16) for k in range(count)])
    g_wo = summed([nn(cut(ctxt, k, rows, 0), branch).astype(BF16) for k in range(count)])
    gq, gkm = lead_back(gct, fw, qt, comb, km)
    gvc, g_taps = conv_back(vt, v_before, v_after, gct, g_before, g_after, spat)
    little = jnp.concatenate([sums1[:2], sums2[:2], g_taps[:HEADS].reshape(-1, width)], 0)
    little = jnp.pad(little, ((0, -little.shape[0] % 8), (0, 0)))
    for axis in ("fsdp", "seq"):
        for bit in bits(axis):
            little = little + swap(little, axis, bit)

    gqm_core, gkm_core = inverse_back(qm, km, a, mixn, gc)
    gk, gv, gqm = rear_back(z, gc, mixn, stats, own, eb, vt, kt, qm, gvc)
    mark = lax.broadcasted_iota(jnp.int32, (LANDMARKS, 1), 0)
    owned = (mark >= place * marks) & (mark < (place + 1) * marks)
    gqm = gqm + jnp.where(owned, gqm_core, 0.0)
    gkm = gkm + jnp.where(owned, gkm_core, 0.0)
    landed = halved(jnp.concatenate([gqm, gkm], 1).astype(BF16), "seq", 0).astype(F32)
    xmt = xm.T.astype(BF16)
    xe = jnp.concatenate([xt, xmt], 1)
    gqe = jnp.concatenate([gq, gqm.T.astype(BF16)], 1)
    gke = jnp.concatenate([gk, gkm.T.astype(BF16)], 1)

    def qkv(k):
        lhs = cut(xe, k, rows, 0)
        return jnp.concatenate(
            [
                (SCALE * nt(lhs, gqe)).astype(BF16),
                (SCALE * nt(lhs, gke)).astype(BF16),
                nt(lhs[:, :tokens], gv).astype(BF16),
            ],
            1,
        )

    g_qkv = summed([qkv(k) for k in range(count)])
    grad_x = last(me, gq, gk, gv, first, landed, wqkv, segment)

    def mine(row):
        return lax.dynamic_slice_in_dim(row, here * rows, rows, 0)

    g_kernel = little[4:].reshape(-1)[: HEADS * 128].reshape(HEADS, 128)[:, :KERNEL].T
    return (
        out[None],
        grad_x[None],
        g_qkv[:, :width].astype(F32),
        g_qkv[:, width : 2 * width].astype(F32),
        g_qkv[:, 2 * width :].astype(F32),
        g_wo.astype(F32),
        g_up.astype(F32),
        g_down.T.astype(F32),
        mine(little[0]),
        mine(little[1]),
        mine(little[2]),
        mine(little[3]),
        g_kernel,
    )


def solution(mesh):
    tokens = P("fsdp", "seq", None)
    matrix = P("fsdp", None)
    row = P("fsdp")
    in_specs = (tokens,) * 2 + (matrix,) * 6 + (row,) * 4 + (P(),)
    out_specs = (tokens,) * 2 + (matrix,) * 6 + (row,) * 4 + (P(),)
    return jax.shard_map(shards, mesh=mesh, in_specs=in_specs, out_specs=out_specs, check_vma=False)
```

```python
import functools

import jax
import jax.numpy as jnp
from jax import lax
from jax.experimental import pallas as pl
from jax.experimental.pallas import tpu as pltpu
from jax.sharding import PartitionSpec as P

HEADS = 12
HDIM = 64
LANDMARKS = 64
KERNEL = 65
PINV_ITERS = 6
REACH = KERNEL // 2
EDGE = 128
SCALE = HDIM ** (-0.25)
F32 = jnp.float32
BF16 = jnp.bfloat16
VM = 56 * 1024 * 1024


def nn(a, b):
    return jnp.dot(a, b, preferred_element_type=F32)


def nt(a, b):
    return lax.dot_general(a, b, (((1,), (1,)), ((), ())), preferred_element_type=F32)


def tn(a, b):
    return lax.dot_general(a, b, (((0,), (0,)), ((), ())), preferred_element_type=F32)


def split(a):
    high = a.astype(BF16)
    return high, (a - high.astype(F32)).astype(BF16)


def nn3(a, b):
    ah, al = split(a)
    bh, bl = split(b)
    return nn(jnp.concatenate([ah, ah, al], 1), jnp.concatenate([bh, bl, bh], 0))


def nt3(a, b):
    ah, al = split(a)
    bh, bl = split(b)
    return nt(jnp.concatenate([ah, ah, al], 1), jnp.concatenate([bh, bl, bh], 1))


def tn3(a, b):
    ah, al = split(a)
    bh, bl = split(b)
    return tn(jnp.concatenate([ah, ah, al], 0), jnp.concatenate([bh, bl, bh], 0))


def lanes(shape):
    return lax.broadcasted_iota(jnp.int32, shape, len(shape) - 1)


def hs(h):
    return slice(h * HDIM, (h + 1) * HDIM)


def vspec():
    return pl.BlockSpec(memory_space=pltpu.VMEM)


def sspec():
    return pl.BlockSpec(memory_space=pltpu.SMEM)


def aspec():
    return pl.BlockSpec(memory_space=pl.ANY)


def shape(dims, kind):
    return jax.ShapeDtypeStruct(tuple(dims), kind)


def params():
    return pltpu.CompilerParams(vmem_limit_bytes=VM)


def cost(flops, traffic, trans=0):
    return pl.CostEstimate(flops=int(flops), bytes_accessed=int(traffic), transcendentals=int(trans))


def call(kernel, args, in_specs, out_shape, out_specs, name, work, grid=(), scratch=(), after=()):
    count, extra = len(args), len(after)

    def body(*refs):
        kernel(*refs[:count], *refs[count + extra :])

    return pl.pallas_call(
        body,
        grid=grid,
        out_shape=out_shape,
        in_specs=list(in_specs) + [aspec()] * extra,
        out_specs=out_specs,
        scratch_shapes=list(scratch),
        compiler_params=params(),
        cost_estimate=work,
        name=name,
    )(*args, *after)


def placed(pieces, whole, sems, me, start):
    rows = pieces[0].shape[0]
    for k, piece in enumerate(pieces):
        at = pl.multiple_of((me ^ k) * rows, 16)
        copy = pltpu.make_async_copy(piece, whole.at[pl.ds(at, rows)], sems.at[k])
        if start:
            copy.start()
        else:
            copy.wait()


def xor_rows(out_ref, value, me, count):
    rows = value.shape[0] // count
    for r in range(count):
        at = pl.multiple_of((me ^ r) * rows, 16)
        out_ref[pl.ds(at, rows), :] = value[r * rows : (r + 1) * rows]


def pack_kernel(x_ref, *refs):
    weights, (all_ref, xm_ref, sems) = refs[:-3], refs[-3:]
    copies = []
    for i, w in enumerate(weights):
        to = all_ref.at[:, pl.ds(i * w.shape[1], w.shape[1])]
        copies.append(pltpu.make_async_copy(w, to, sems.at[i]))
        copies[-1].start()
    size, marks, width = xm_ref.shape
    tokens = x_ref.shape[0]
    segment = tokens // marks
    means = [
        jnp.mean(x_ref[m * segment : (m + 1) * segment, :].astype(F32), axis=0, keepdims=True)
        for m in range(marks)
    ]
    means = jnp.concatenate(means, 0)
    for i in range(size):
        xm_ref[i] = means
    for copy in copies:
        copy.wait()


def pack(x, weights, size, marks):
    rows, width = weights[0].shape
    return call(
        pack_kernel,
        (x, *weights),
        [vspec()] * 4,
        [shape((rows, 3 * width), BF16), shape((size, marks, width), F32)],
        [vspec()] * 2,
        "pack",
        cost(1e6, 1e5),
        scratch=[pltpu.SemaphoreType.DMA((3,))],
    )


def front_kernel(count, me_ref, x_ref, xm_ref, *refs):
    pieces = refs[:count]
    (xt_ref, xmt_ref, qt_ref, kt_ref, vt_ref, fw_ref, eb_ref, st_ref, msg_ref, qm_ref, km_ref,
     top_ref, end_ref, w_ref, sems) = refs[count:]
    me = me_ref[0]
    placed(pieces, w_ref, sems, me, True)
    tokens, width = x_ref.shape
    step = 256
    for b in range(tokens // step):
        rows = slice(b * step, (b + 1) * step)
        xor_rows(xt_ref.at[:, rows], x_ref[rows, :].T, me, count)
    placed(pieces, w_ref, sems, me, False)
    high, low = split(xm_ref[...])
    wide = jnp.concatenate([xm_ref[...], jnp.zeros_like(xm_ref)], 0)
    xor_rows(xmt_ref, wide.T.astype(BF16)[:, :LANDMARKS], me, count)
    both = w_ref[:, : 2 * width]
    marks = SCALE * (nn(high, both) + nn(low, both))
    qm = marks[:, :width].astype(BF16)
    km = marks[:, width:].astype(BF16)
    qm_ref[...] = qm
    km_ref[...] = km
    for b in range(tokens // step):
        rows = slice(b * step, (b + 1) * step)
        part = x_ref[rows, :]
        for i, (out, scale) in enumerate(((qt_ref, SCALE), (kt_ref, SCALE), (vt_ref, None))):
            y = nn(part, w_ref[:, i * width : (i + 1) * width])
            if scale is not None:
                y = y * scale
            y = y.astype(BF16)
            if i == 2 and b == 0:
                top_ref[...] = y[:REACH]
            if i == 2 and b == tokens // step - 1:
                end_ref[...] = y[step - REACH :]
            out[:, rows] = y.T
    lane = lanes((LANDMARKS, 128))
    stats = jnp.zeros((LANDMARKS, 128), F32)
    pair = []
    for h in range(HEADS):
        s = nn(km[:, hs(h)], qt_ref[hs(h), :])
        s = jnp.exp(s - jnp.max(s, axis=0, keepdims=True))
        fw_ref[hs(h), :] = (s * (1.0 / jnp.sum(s, axis=0, keepdims=True))).astype(BF16)
        s = nn(qm[:, hs(h)], kt_ref[hs(h), :])
        top = jnp.max(s, axis=1, keepdims=True).astype(BF16).astype(F32)
        e = jnp.exp(s - top).astype(BF16)
        eb_ref[hs(h), :] = e
        total = jnp.sum(e.astype(F32), axis=1, keepdims=True)
        stats = jnp.where(lane == h, top, stats)
        stats = jnp.where(lane == 16 + h, total, stats)
        pair.append(nt(e, vt_ref[hs(h), :]))
        if h % 2:
            both = jnp.concatenate(pair, 1).astype(BF16)
            for d in range(msg_ref.shape[0]):
                msg_ref[d, h // 2] = both
            pair = []
    st_ref[...] = stats
    for d in range(msg_ref.shape[0]):
        msg_ref[d, HEADS // 2] = stat_message(stats)


def stat_message(stats):
    lane = lanes(stats.shape)
    high = stats.astype(BF16).astype(F32)
    low = pltpu.roll(stats - high, 16, 1)
    return jnp.where((lane >= 32) & (lane < 48), low, high).astype(BF16)


def front(me, x, xm, pieces, size):
    tokens, width = x.shape
    pairs = HEADS // 2
    flat = shape((width, tokens), BF16)
    return pl.pallas_call(
        functools.partial(front_kernel, len(pieces)),
        out_shape=[flat, shape((width, LANDMARKS), BF16)]
        + [flat] * 5
        + [
            shape((LANDMARKS, 128), F32),
            shape((size, pairs + 1, LANDMARKS, 128), BF16),
            shape((LANDMARKS, width), BF16),
            shape((LANDMARKS, width), BF16),
            shape((REACH, width), BF16),
            shape((REACH, width), BF16),
        ],
        in_specs=[sspec(), vspec(), vspec()] + [aspec()] * len(pieces),
        out_specs=[vspec()] * 13,
        scratch_shapes=[
            pltpu.VMEM((width, 3 * width), BF16),
            pltpu.SemaphoreType.DMA((len(pieces),)),
        ],
        compiler_params=params(),
        cost_estimate=cost(4.5e+08, 1.6e+06),
        name="front",
    )(me, x, xm, *pieces)


def merged(msg_ref, mixn_ref, st_ref):
    lane = lanes((LANDMARKS, 128))
    size = msg_ref.shape[0]
    stats = []
    for d in range(size):
        got = msg_ref[d, HEADS // 2].astype(F32)
        stats.append(got + jnp.where((lane >= 16) & (lane < 32), pltpu.roll(got, 112, 1), 0.0))
    largest = functools.reduce(jnp.maximum, stats)
    weights = [jnp.exp(jnp.minimum(st - largest, 0.0)) for st in stats]
    total = sum(st * pltpu.roll(w, 16, 1) for st, w in zip(stats, weights))
    st_ref[...] = jnp.where(lane < 16, largest, total)
    for i in range(HEADS // 2):

        def both(a, at):
            return jnp.where(lane < HDIM, a[:, at : at + 1], a[:, at + 1 : at + 2])

        y = sum(msg_ref[d, i].astype(F32) * both(weights[d], 2 * i) for d in range(size))
        mixn_ref[i] = y / both(total, 16 + 2 * i)


def eye(scale):
    n = LANDMARKS
    return jnp.where(
        lax.broadcasted_iota(jnp.int32, (n, n), 0) == lax.broadcasted_iota(jnp.int32, (n, n), 1),
        jnp.float32(scale),
        0.0,
    )


def landmark_softmax(qm, km, h):
    s = nt(qm[:, hs(h)], km[:, hs(h)])
    s = jnp.exp(s - jnp.max(s, axis=1, keepdims=True))
    return s / jnp.sum(s, axis=1, keepdims=True)


def first_inverse(a):
    columns = jnp.max(jnp.sum(a, axis=0, keepdims=True), axis=1, keepdims=True)
    rows = jnp.max(jnp.sum(a, axis=1, keepdims=True), axis=0, keepdims=True)
    return a.T * (1.0 / (columns * rows))


def inverse_kernel(qm_ref, km_ref, a_ref, z_ref, zs, ps, ms, ns):
    qm, km = qm_ref[...], km_ref[...]
    every = range(HEADS)
    for h in every:
        a = landmark_softmax(qm, km, h)
        a_ref[h] = a
        z_ref[h] = first_inverse(a)

    def step(i, carry):
        p = [nn3(a_ref[h], z_ref[h]) for h in every]
        m = [eye(15.0) - nn3(x, eye(7.0) - x) for x in p]
        n = [eye(13.0) - nn3(x, y) for x, y in zip(p, m)]
        for h in every:
            ps[i, h] = p[h]
            ms[i, h] = m[h]
            ns[i, h] = n[h]
            zs[i, h] = z_ref[h]
            z_ref[h] = 0.25 * nn3(z_ref[h], n[h])
        return carry

    lax.fori_loop(0, PINV_ITERS, step, 0)


def inverse(qm, km):
    square = shape((HEADS, LANDMARKS, LANDMARKS), F32)
    steps = shape((PINV_ITERS, HEADS, LANDMARKS, LANDMARKS), F32)
    return call(
        inverse_kernel,
        (qm, km),
        [vspec()] * 2,
        [square] * 2 + [steps] * 4,
        [vspec()] * 6,
        "inverse",
        cost(1e8, 1e6),
    )


def inverse_back_kernel(size, me_ref, qm_ref, km_ref, a_ref, mix_ref, gc_ref, zs, ps, ms, ns, gqp_ref, gkp_ref,
                        gq_ref, gk_ref, gz, ga):
    place = me_ref[1]
    slots = range(-(-HEADS // size))
    heads = [place + size * j for j in slots]
    safe = [jnp.minimum(h, HEADS - 1) for h in heads]
    lane = lanes((LANDMARKS, 128))
    last = PINV_ITERS - 1
    gq_ref[...] = gqp_ref[...]
    gk_ref[...] = gkp_ref[...]

    def half(pair, h):
        return jnp.where(h % 2 == 0, pair[:, :HDIM], pair[:, HDIM:])

    for j in slots:
        h = safe[j]
        gz[j] = nt3(half(gc_ref[h // 2], h), half(mix_ref[h // 2], h))
        ga[j] = jnp.zeros((LANDMARKS, LANDMARKS), F32)

    def back(i, carry):
        i = last - i
        for j in slots:
            h = safe[j]
            z, p, m, n, a = zs[i, h], ps[i, h], ms[i, h], ns[i, h], a_ref[h]
            g = 0.25 * gz[j]
            g3 = -tn3(z, g)
            g2 = -tn3(p, g3)
            gp = nt3(g3, m) + nt3(g2, eye(7.0) - p) - tn3(p, g2)
            ga[j] = ga[j] + nt3(gp, z)
            gz[j] = nt3(g, n) + tn3(a, gp)
        return carry

    lax.fori_loop(0, PINV_ITERS, back, 0)
    for j in slots:
        h = safe[j]
        a = a_ref[h]
        csum = jnp.sum(a, axis=0, keepdims=True)
        rsum = jnp.sum(a, axis=1, keepdims=True)
        cmax = jnp.max(csum, axis=1, keepdims=True)
        rmax = jnp.max(rsum, axis=0, keepdims=True)
        scale = 1.0 / (cmax * rmax)
        gfirst = gz[j]
        gs = jnp.sum(jnp.sum(gfirst * a.T, axis=1, keepdims=True), axis=0, keepdims=True)
        ctop = (csum == cmax).astype(F32)
        rtop = (rsum == rmax).astype(F32)
        gcol = -gs * scale / cmax * ctop / jnp.sum(ctop, axis=1, keepdims=True)
        grow = -gs * scale / rmax * rtop / jnp.sum(rtop, axis=0, keepdims=True)
        g = ga[j] + gfirst.T * scale + gcol + grow
        g = a * (g - jnp.sum(g * a, axis=1, keepdims=True))
        high, low = split(g)
        at = pl.ds(pl.multiple_of(h // 2 * 128, 128), 128)
        qm, km = half(qm_ref[:, at].astype(F32), h), half(km_ref[:, at].astype(F32), h)
        qm, km = qm.astype(BF16), km.astype(BF16)
        gq = nn(jnp.concatenate([high, low], 1), jnp.concatenate([km] * 2, 0))
        gk = tn(jnp.concatenate([high, low], 0), jnp.concatenate([qm] * 2, 0))
        mine = ((lane >= HDIM) == (h % 2 == 1)) & (heads[j] < HEADS)
        gq_ref[:, at] = gq_ref[:, at] + jnp.where(mine, jnp.concatenate([gq, gq], 1), 0.0)
        gk_ref[:, at] = gk_ref[:, at] + jnp.where(mine, jnp.concatenate([gk, gk], 1), 0.0)


def inverse_back(me, qm, km, a, mix, gc, saved, gqm, gkm, size, after=()):
    square = (-(-HEADS // size), LANDMARKS, LANDMARKS)
    out = shape(qm.shape, F32)
    return call(
        functools.partial(inverse_back_kernel, size),
        (me, qm, km, a, mix, gc, *saved, gqm, gkm),
        [sspec()] + [vspec()] * 11,
        [out] * 2,
        [vspec()] * 2,
        "inverse_back",
        cost(2e8, 2e6),
        scratch=[pltpu.VMEM(square, F32)] * 2,
        after=after,
    )


def widen(out_ref, flat_ref, before_ref, after_ref):
    width, tokens = flat_ref.shape
    zero = jnp.zeros((EDGE - REACH, width), BF16)
    out_ref[:, :EDGE] = jnp.concatenate([zero, before_ref[...]], 0).T
    out_ref[:, EDGE : EDGE + tokens] = flat_ref[...]
    out_ref[:, EDGE + tokens :] = jnp.concatenate([after_ref[...], zero], 0).T


def band(row, step):
    wide = jnp.broadcast_to(row, (step, step + 2 * EDGE))
    return pltpu.roll(wide, 0, 1, stride=1, stride_axis=0).astype(BF16)


def stacked(ref, h, step, margin):
    blocks = (ref.shape[1] - 2 * margin) // step if margin else ref.shape[1] // step
    return jnp.concatenate(
        [ref[hs(h), b * step : (b + 1) * step + 2 * margin] for b in range(blocks)], 0
    )


def conv_kernel_body(vt_ref, before_ref, after_ref, taps_ref, out_ref, wide_ref):
    widen(wide_ref, vt_ref, before_ref, after_ref)
    step = 256
    for h in range(HEADS):
        y = nt(stacked(wide_ref, h, step, EDGE), band(taps_ref[h : h + 1, :], step))
        for b in range(vt_ref.shape[1] // step):
            out_ref[hs(h), b * step : (b + 1) * step] = y[b * HDIM : (b + 1) * HDIM, :]


def conv(vt, before, after, taps):
    width, tokens = vt.shape
    return pl.pallas_call(
        conv_kernel_body,
        out_shape=shape(vt.shape, F32),
        in_specs=[vspec()] * 4,
        out_specs=vspec(),
        scratch_shapes=[pltpu.VMEM((width, tokens + 2 * EDGE), BF16)],
        compiler_params=params(),
        cost_estimate=cost(2e+08, 600000),
        name="conv",
    )(vt, before, after, taps)


def conv_back_kernel(vt_ref, vb_ref, va_ref, gt_ref, gb_ref, ga_ref, taps_ref, out_ref, tap_ref, vwide, gwide):
    widen(vwide, vt_ref, vb_ref, va_ref)
    widen(gwide, gt_ref, gb_ref, ga_ref)
    step = 256
    tokens = vt_ref.shape[1]
    flip = (
        lax.broadcasted_iota(jnp.int32, (step, step), 0)
        + lax.broadcasted_iota(jnp.int32, (step, step), 1)
        == step - 1
    ).astype(BF16)
    rows = []
    for h in range(HEADS):
        y = nt(stacked(gwide, h, step, EDGE), band(taps_ref[h : h + 1, :], step))
        for b in range(tokens // step):
            out_ref[hs(h), b * step : (b + 1) * step] = y[b * HDIM : (b + 1) * HDIM, :]
        turned = nn(stacked(gt_ref, h, step, 0), flip).astype(BF16)
        d = tn(turned, stacked(vwide, h, step, EDGE))
        d = pltpu.roll(d, 0, 1, stride=1, stride_axis=0)
        rows.append(jnp.sum(d, axis=0, keepdims=True))
    rows = jnp.concatenate(rows + [jnp.zeros((4, step + 2 * EDGE), F32)], 0)
    first = step - 1 + EDGE - REACH
    tap_ref[...] = pltpu.roll(rows, step + 2 * EDGE - first, 1)[:, :128]


def conv_back(vt, vb, va, gt, gb, ga, taps, after=()):
    width, tokens = vt.shape
    wide = pltpu.VMEM((width, tokens + 2 * EDGE), BF16)
    return call(
        conv_back_kernel,
        (vt, vb, va, gt, gb, ga, taps),
        [vspec()] * 7,
        [shape(vt.shape, F32), shape((16, 128), F32)],
        [vspec()] * 2,
        "conv_back",
        cost(4e8, 1e6),
        scratch=[wide, wide],
        after=after,
    )


def gelu_pair(x):
    phi = 0.5 * (1.0 + lax.erf(x * (0.5**0.5)))
    return x * phi, phi + x * ((0.5 / jnp.pi) ** 0.5 * jnp.exp(-0.5 * x * x))


def norm_stats(r):
    center = r - jnp.mean(r, axis=-1, keepdims=True)
    rstd = lax.rsqrt(jnp.mean(center * center, axis=-1, keepdims=True) + 1e-05)
    return center * rstd, rstd


def norm_back(gy, xhat, rstd):
    return rstd * (
        gy - jnp.mean(gy, axis=-1, keepdims=True) - xhat * jnp.mean(gy * xhat, axis=-1, keepdims=True)
    )


STEP = 256


def whole(a):
    return pl.BlockSpec(a.shape, lambda i, n=a.ndim: (0,) * n)


def fixed(*dims):
    return pl.BlockSpec(dims, lambda i, n=len(dims): (0,) * n)


def tall(rows):
    return pl.BlockSpec((rows, STEP), lambda i: (0, i))


def row(width):
    return pl.BlockSpec((STEP, width), lambda i: (i, 0))


def mid1_kernel(count, me_ref, z_ref, msg_ref, fw_ref, conv_ref, x_ref, gains_ref, *refs):
    wo, up = refs[:count], refs[count : 2 * count]
    (ctx_ref, hidt_ref, xhat_ref, rstd_ref, act_ref, slope_ref, comb_ref, mixn_ref, st_ref,
     wo_ref, up_ref, sems) = refs[2 * count :]
    me = me_ref[0]

    @pl.when(pl.program_id(0) == 0)
    def _():
        placed(wo, wo_ref, sems.at[0], me, True)
        placed(up, up_ref, sems.at[1], me, True)
        merged(msg_ref, mixn_ref, st_ref)
        for i in range(HEADS // 2):
            mixed = mixn_ref[i]
            comb_ref[i] = jnp.concatenate(
                [nn3(z_ref[2 * i], mixed[:, :HDIM]), nn3(z_ref[2 * i + 1], mixed[:, HDIM:])], 1
            ).astype(BF16)
        placed(wo, wo_ref, sems.at[0], me, False)
        placed(up, up_ref, sems.at[1], me, False)

    for h in range(HEADS):
        half = slice((h % 2) * HDIM, (h % 2) * HDIM + HDIM)
        att = tn(comb_ref[h // 2][:, half], fw_ref[hs(h), :])
        ctx_ref[hs(h), :] = (att + conv_ref[hs(h), :]).astype(BF16)
    branch = nn(ctx_ref[...].T, wo_ref[...])
    xhat, rstd = norm_stats(x_ref[...].astype(F32) + branch)
    xhat_ref[...] = xhat
    rstd_ref[...] = jnp.broadcast_to(rstd, rstd_ref.shape)
    hidden = (xhat * gains_ref[0:1, :] + gains_ref[1:2, :]).astype(BF16)
    xor_rows(hidt_ref, hidden.T, me, count)
    part = up_ref.shape[1] // count
    for c in range(count):
        at = slice(c * part, (c + 1) * part)
        act, slope = gelu_pair(nn(hidden, up_ref[:, at]))
        act_ref[:, at] = act.astype(BF16)
        slope_ref[:, at] = slope.astype(BF16)


def mid1(me, z, msgs, fw, convt, x, gains, wo, up, after=()):
    tokens, width = x.shape
    ff = up[0].shape[1]
    pairs = HEADS // 2
    return call(
        functools.partial(mid1_kernel, len(wo)),
        (me, z, msgs, fw, convt, x, gains, *wo, *up),
        [sspec(), whole(z), whole(msgs), tall(width), tall(width), row(width), whole(gains)]
        + [aspec()] * (len(wo) + len(up)),
        [
            shape((width, tokens), BF16),
            shape((width, tokens), BF16),
            shape((tokens, width), F32),
            shape((tokens, 128), F32),
            shape((tokens, ff), BF16),
            shape((tokens, ff), BF16),
            shape((pairs, LANDMARKS, 128), BF16),
            shape((pairs, LANDMARKS, 128), F32),
            shape((LANDMARKS, 128), F32),
        ],
        [tall(width), tall(width), row(width), row(128), row(ff), row(ff)]
        + [fixed(pairs, LANDMARKS, 128)] * 2
        + [fixed(LANDMARKS, 128)],
        "mid_one",
        cost(2e9, 3e6),
        grid=(tokens // STEP,),
        scratch=[
            pltpu.VMEM((width, width), BF16),
            pltpu.VMEM((width, ff), BF16),
            pltpu.SemaphoreType.DMA((2, len(wo))),
        ],
        after=after,
    )


def mid2_kernel(count, me_ref, act_ref, slope_ref, xhat_ref, ct_ref, gains_ref, *refs):
    down = refs[:count]
    out_ref, second_ref, redt_ref, ge_ref, sums_ref, down_ref, sems = refs[count:]
    me = me_ref[0]

    @pl.when(pl.program_id(0) == 0)
    def _():
        placed(down, down_ref, sems, me, True)
        sums_ref[...] = jnp.zeros_like(sums_ref)
        placed(down, down_ref, sems, me, False)

    reduced = nn(act_ref[...], down_ref[...])
    hidden = xhat_ref[...] * gains_ref[0:1, :] + gains_ref[1:2, :]
    xhat, rstd = norm_stats(hidden + reduced)
    out_ref[...] = (xhat * gains_ref[2:3, :] + gains_ref[3:4, :]).astype(BF16)
    ct = ct_ref[...].astype(F32)
    sums_ref[0:1, :] = sums_ref[0:1, :] + jnp.sum(ct * xhat, axis=0, keepdims=True)
    sums_ref[1:2, :] = sums_ref[1:2, :] + jnp.sum(ct, axis=0, keepdims=True)
    second = norm_back(ct * gains_ref[2:3, :], xhat, rstd)
    second_ref[...] = second
    red = second.astype(BF16)
    redt_ref[...] = red.T
    part = down_ref.shape[0] // count
    for k in range(count):
        cols = slice(k * part, (k + 1) * part)
        ge = nt(red, down_ref[cols, :]) * slope_ref[:, cols].astype(F32)
        ge_ref[:, cols] = ge.astype(BF16)


def mid2(me, act, slope, xhat, ct, gains, down, after=()):
    tokens, width = ct.shape
    ff = act.shape[1]
    return call(
        functools.partial(mid2_kernel, len(down)),
        (me, act, slope, xhat, ct, gains, *down),
        [sspec(), row(ff), row(ff), row(width), row(width), whole(gains)] + [aspec()] * len(down),
        [
            shape((tokens, width), BF16),
            shape((tokens, width), F32),
            shape((width, tokens), BF16),
            shape((tokens, ff), BF16),
            shape((8, width), F32),
        ],
        [row(width), row(width), tall(width), row(ff), fixed(8, width)],
        "mid_two",
        cost(2e9, 3e6),
        grid=(tokens // STEP,),
        scratch=[pltpu.VMEM((ff, width), BF16), pltpu.SemaphoreType.DMA((len(down),))],
        after=after,
    )


def mid3_kernel(count, me_ref, second_ref, ge_ref, xhat_ref, rstd_ref, fw_ref, gains_ref, *refs):
    wo, up = refs[:count], refs[count : 2 * count]
    (first_ref, branch_ref, gct_ref, top_ref, end_ref, sums_ref, parts_ref,
     wo_ref, up_ref, gc_ref, sems) = refs[2 * count :]
    me = me_ref[0]
    at = pl.program_id(0)

    @pl.when(at == 0)
    def _():
        placed(up, up_ref, sems.at[0], me, True)
        placed(wo, wo_ref, sems.at[1], me, True)
        sums_ref[...] = jnp.zeros_like(sums_ref)
        gc_ref[...] = jnp.zeros_like(gc_ref)
        placed(up, up_ref, sems.at[0], me, False)
        placed(wo, wo_ref, sems.at[1], me, False)

    g = second_ref[...] + nt(ge_ref[...], up_ref[...])
    xhat = xhat_ref[...]
    sums_ref[0:1, :] = sums_ref[0:1, :] + jnp.sum(g * xhat, axis=0, keepdims=True)
    sums_ref[1:2, :] = sums_ref[1:2, :] + jnp.sum(g, axis=0, keepdims=True)
    first = norm_back(g * gains_ref[0:1, :], xhat, rstd_ref[:, 0:1])
    first_ref[...] = first
    branch = first.astype(BF16)
    branch_ref[...] = branch
    gctx = nt(branch, wo_ref[...]).astype(BF16)

    @pl.when(at == 0)
    def _():
        top_ref[...] = gctx[:REACH]

    @pl.when(at == pl.num_programs(0) - 1)
    def _():
        end_ref[...] = gctx[gctx.shape[0] - REACH :]

    gct_ref[...] = gctx.T
    for i in range(HEADS // 2):
        gc_ref[i] = gc_ref[i] + jnp.concatenate(
            [nt(fw_ref[hs(h), :], gct_ref[hs(h), :]) for h in (2 * i, 2 * i + 1)], 1
        )

    @pl.when(at == pl.num_programs(0) - 1)
    def _():
        for d in range(parts_ref.shape[0]):
            parts_ref[d] = gc_ref[...].astype(BF16)


def mid3(me, second, ge, xhat, rstd, fw, gains, wo, up, size, after=()):
    tokens, width = second.shape
    ff = ge.shape[1]
    pairs = HEADS // 2
    return call(
        functools.partial(mid3_kernel, len(wo)),
        (me, second, ge, xhat, rstd, fw, gains, *wo, *up),
        [sspec(), row(width), row(ff), row(width), row(128), tall(width), whole(gains)]
        + [aspec()] * (2 * len(wo)),
        [
            shape((tokens, width), F32),
            shape((tokens, width), BF16),
            shape((width, tokens), BF16),
            shape((REACH, width), BF16),
            shape((REACH, width), BF16),
            shape((8, width), F32),
            shape((size, pairs, LANDMARKS, 128), BF16),
        ],
        [row(width), row(width), tall(width), fixed(REACH, width), fixed(REACH, width),
         fixed(8, width), fixed(size, pairs, LANDMARKS, 128)],
        "mid_three",
        cost(2e9, 3e6),
        grid=(tokens // STEP,),
        scratch=[
            pltpu.VMEM((width, width), BF16),
            pltpu.VMEM((width, ff), BF16),
            pltpu.VMEM((pairs, LANDMARKS, 128), F32),
            pltpu.SemaphoreType.DMA((2, len(wo))),
        ],
        after=after,
    )


def grad_down_kernel(count, me_ref, red_ref, act_ref, *outs):
    part = act_ref.shape[1] // count
    for k in range(count):
        at = pl.ds(pl.multiple_of((me_ref[0] ^ k) * part, 128), part)
        outs[k][...] = nn(red_ref[...], act_ref[:, at]).astype(BF16)


def grad_down(count, me, redt, act, after=()):
    width = redt.shape[0]
    return call(
        functools.partial(grad_down_kernel, count),
        (me, redt, act),
        [sspec(), vspec(), vspec()],
        [shape((width, act.shape[1] // count), BF16)] * count,
        [vspec()] * count,
        "grad_down",
        cost(5e8, 1e6),
        after=after,
    )


def grad_up_kernel(count, hid_ref, ge_ref, *outs):
    y = nn(hid_ref[...], ge_ref[...]).astype(BF16)
    rows = y.shape[0] // count
    for k in range(count):
        outs[k][...] = y[k * rows : (k + 1) * rows]


def grad_up(count, hidt, ge, after=()):
    width, tokens = hidt.shape
    ff = ge.shape[1]
    step = 768
    return call(
        functools.partial(grad_up_kernel, count),
        (hidt, ge),
        [whole(hidt), pl.BlockSpec((tokens, step), lambda i: (0, i))],
        [shape((width // count, ff), BF16)] * count,
        [pl.BlockSpec((width // count, step), lambda i: (0, i))] * count,
        "grad_up",
        cost(5e8, 1e6),
        grid=(ff // step,),
        after=after,
    )


def grad_o_kernel(count, me_ref, ctx_ref, branch_ref, sums1_ref, sums2_ref, taps_ref, *refs):
    outs, y_ref = refs[:count], refs[count]
    width = ctx_ref.shape[0]
    rows = width // count
    taps = jnp.concatenate([taps_ref[:HEADS], jnp.zeros((HEADS, width - 128), F32)], 1)
    little = jnp.concatenate(
        [sums1_ref[0:2, :], sums2_ref[0:2, :], taps, jnp.zeros((128 - 4 - HEADS, width), F32)], 0
    )
    y_ref[:, width:] = little.T.astype(BF16)
    y_ref[:, :width] = nn(ctx_ref[...], branch_ref[...]).astype(BF16)
    for k in range(count):
        outs[k][...] = y_ref[pl.ds(pl.multiple_of((me_ref[0] ^ k) * rows, 16), rows), :]


def grad_o(count, me, ctxt, branch, sums1, sums2, taps, after=()):
    width = ctxt.shape[0]
    return call(
        functools.partial(grad_o_kernel, count),
        (me, ctxt, branch, sums1, sums2, taps),
        [sspec()] + [vspec()] * 5,
        [shape((width // count, width + 128), BF16)] * count,
        [vspec()] * count,
        "grad_o",
        cost(2e8, 1e6),
        scratch=[pltpu.VMEM((width, width + 128), BF16)],
        after=after,
    )


def grad_qkv_kernel(count, xt_ref, xmt_ref, gq_ref, gk_ref, gv_ref, gqm_ref, gkm_ref, *outs):
    width = xt_ref.shape[0]
    rows = width // count
    for i, (g_ref, m_ref) in enumerate(((gq_ref, gqm_ref), (gk_ref, gkm_ref), (gv_ref, None))):
        y = nt(xt_ref[...], g_ref[...])
        if m_ref is not None:
            y = y + nn(xmt_ref[...], m_ref[...].astype(BF16))
        y = y.astype(BF16)
        for k in range(count):
            outs[k][:, i * width : (i + 1) * width] = y[k * rows : (k + 1) * rows]


def grad_qkv(count, xt, xmt, gq, gk, gv, gqm, gkm, after=()):
    width = xt.shape[0]
    return call(
        functools.partial(grad_qkv_kernel, count),
        (xt, xmt, gq, gk, gv, gqm, gkm),
        [vspec()] * 7,
        [shape((width // count, 3 * width), BF16)] * count,
        [vspec()] * count,
        "grad_qkv",
        cost(2e8, 1e6),
        after=after,
    )


def lead_back_kernel(gct_ref, fw_ref, qt_ref, comb_ref, km_ref, gq_ref, gkm_ref):
    km = km_ref[...]
    pair = []
    for h in range(HEADS):
        half = slice((h % 2) * HDIM, (h % 2) * HDIM + HDIM)
        pf = fw_ref[hs(h), :].astype(F32)
        g = nn(comb_ref[h // 2][:, half], gct_ref[hs(h), :])
        gs = (pf * (g - jnp.sum(pf * g, axis=0, keepdims=True))).astype(BF16)
        gq_ref[hs(h), :] = tn(km[:, hs(h)], gs).astype(BF16)
        pair.append(nt(gs, qt_ref[hs(h), :]))
        if h % 2:
            gkm_ref[:, (h - 1) * HDIM : (h + 1) * HDIM] = jnp.concatenate(pair, 1)
            pair = []


def lead_back(gct, fw, qt, comb, km):
    return pl.pallas_call(
        lead_back_kernel,
        out_shape=[shape(gct.shape, BF16), shape(km.shape, F32)],
        in_specs=[vspec()] * 5,
        out_specs=[vspec()] * 2,
        compiler_params=params(),
        cost_estimate=cost(3e+08, 600000),
        name="lead_back",
    )(gct, fw, qt, comb, km)


def rear_back_kernel(z_ref, parts_ref, mixn_ref, st_ref, own_ref, eb_ref, vt_ref, kt_ref, qm_ref, gvc_ref,
                     gk_ref, gv_ref, gqm_ref, gc_ref):
    qm = qm_ref[...]
    gc_ref[...] = sum(parts_ref[d].astype(F32) for d in range(parts_ref.shape[0]))
    scale = jnp.exp(own_ref[...] - st_ref[...])
    pair = []
    for h in range(HEADS):
        half = slice((h % 2) * HDIM, (h % 2) * HDIM + HDIM)
        gmix = tn3(z_ref[h], gc_ref[h // 2][:, half]).astype(BF16)
        dot = jnp.sum(gmix.astype(F32) * mixn_ref[h // 2][:, half], axis=1, keepdims=True)
        factor = scale[:, h : h + 1] / st_ref[:, 16 + h : 17 + h]
        pb = eb_ref[hs(h), :].astype(F32) * factor
        gs = (pb * (nn(gmix, vt_ref[hs(h), :]) - dot)).astype(BF16)
        gk_ref[hs(h), :] = tn(qm[:, hs(h)], gs).astype(BF16)
        gv_ref[hs(h), :] = (tn(gmix, pb.astype(BF16)) + gvc_ref[hs(h), :]).astype(BF16)
        pair.append(nt(gs, kt_ref[hs(h), :]))
        if h % 2:
            gqm_ref[:, (h - 1) * HDIM : (h + 1) * HDIM] = jnp.concatenate(pair, 1)
            pair = []


def rear_back(z, parts, mixn, stats, own, eb, vt, kt, qm, gvc, after=()):
    return call(
        rear_back_kernel,
        (z, parts, mixn, stats, own, eb, vt, kt, qm, gvc),
        [vspec()] * 10,
        [shape(vt.shape, BF16), shape(vt.shape, BF16), shape(qm.shape, F32), shape(mixn.shape, F32)],
        [vspec()] * 4,
        "rear_back",
        cost(3e8, 1e6),
        after=after,
    )


def last_kernel(count, segment, me_ref, gq_ref, gk_ref, gv_ref, first_ref, own_ref, *refs):
    pieces = refs[:count]
    out_ref, w_ref, sems = refs[count:]
    me = me_ref[0]
    width = gq_ref.shape[0]

    @pl.when(pl.program_id(0) == 0)
    def _():
        placed(pieces, w_ref, sems, me, True)
        placed(pieces, w_ref, sems, me, False)

    wq, wk, wv = (w_ref[:, i * width : (i + 1) * width] for i in range(3))
    g = SCALE * (nn(wq, gq_ref[...]) + nn(wk, gk_ref[...])) + nn(wv, gv_ref[...])
    own = own_ref[...]
    marks = (SCALE / segment) * (
        nt(own[:, :width].astype(BF16), wq) + nt(own[:, width:].astype(BF16), wk)
    )
    step = out_ref.shape[0]
    token = pl.program_id(0) * step + lax.broadcasted_iota(jnp.int32, (step, own.shape[0]), 0)
    mark = lax.broadcasted_iota(jnp.int32, (step, own.shape[0]), 1) * segment
    pick = ((token >= mark) & (token < mark + segment)).astype(BF16)
    high, low = split(marks)
    spread = nn(pick, high) + nn(pick, low)
    out_ref[...] = (first_ref[...] + g.T + spread).astype(BF16)


def last(me, gq, gk, gv, first, own, pieces, segment):
    width, tokens = gq.shape
    step = 256
    tall = pl.BlockSpec((width, step), lambda i: (0, i))
    row = pl.BlockSpec((step, width), lambda i: (i, 0))
    return pl.pallas_call(
        functools.partial(last_kernel, len(pieces), segment),
        grid=(tokens // step,),
        out_shape=shape((tokens, width), BF16),
        in_specs=[sspec(), tall, tall, tall, row, pl.BlockSpec(own.shape, lambda i: (0, 0))]
        + [aspec()] * len(pieces),
        out_specs=row,
        scratch_shapes=[
            pltpu.VMEM((width, 3 * width), BF16),
            pltpu.SemaphoreType.DMA((len(pieces),)),
        ],
        compiler_params=params(),
        cost_estimate=cost(4e+08, 1.2e+06),
        name="last",
    )(me, gq, gk, gv, first, own, *pieces)


def bits(axis):
    size = lax.axis_size(axis)
    assert size & (size - 1) == 0
    return [1 << i for i in range(size.bit_length() - 1)]


def swap(array, axis, bit):
    return lax.ppermute(array, axis, [(i, i ^ bit) for i in range(lax.axis_size(axis))])


def shift(array, axis, by):
    size = lax.axis_size(axis)
    return lax.ppermute(array, axis, [(i, i + by) for i in range(size) if 0 <= i + by < size])


def spread(pieces, axis, steps):
    for bit in steps:
        pieces = {**pieces, **{k | bit: swap(piece, axis, bit) for k, piece in pieces.items()}}
    return pieces


def far(array, axis):
    return spread({0: array}, axis, bits(axis)[1:])


def near(pieces, axis):
    pieces = spread(pieces, axis, bits(axis)[:1])
    return [pieces[k] for k in range(lax.axis_size(axis))]


def gathered(array, axis):
    return near(far(array, axis), axis)


def tie(*values):
    return lax.optimization_barrier(values)


def rows_out(array, groups=None):
    size = len(groups[0]) if groups else lax.axis_size("seq")
    blocks = array.reshape(size, -1, array.shape[1])
    return lax.all_to_all(blocks, "seq", 0, 0, axis_index_groups=groups)


def rows_in(blocks):
    return jnp.sum(blocks.astype(F32), axis=0)


def copies(array, axis, groups=None):
    size = len(groups[0]) if groups else lax.axis_size(axis)
    blocks = jnp.broadcast_to(array[None], (size, *array.shape))
    return lax.all_to_all(blocks, axis, 0, 0, axis_index_groups=groups)


class Total:
    def __init__(self, pieces, order):
        self.pieces = dict(enumerate(pieces))
        self.order = list(order)
        self.back = [step for step in reversed(order) if step[0] != "swap"]
        self.got = None

    def send(self):
        if self.order:
            kind, what = self.order[0]
            if kind == "swap":
                self.got = {k: swap(p, "fsdp", what) for k, p in self.pieces.items() if k & what}
                self.pieces = {k: p for k, p in self.pieces.items() if not k & what}
                return
            (piece,) = self.pieces.values()
            if kind == "rows":
                self.got = {0: rows_out(piece, what)}
                return
            upper = ((lax.axis_index("seq") & what) != 0).astype(jnp.int32)
            half = piece.shape[0] // 2
            self.pieces = {0: lax.dynamic_slice_in_dim(piece, upper * half, half, 0)}
            sent = lax.dynamic_slice_in_dim(piece, (1 - upper) * half, half, 0)
            self.got = {0: swap(sent, "seq", what)}
        else:
            kind, what = self.back[0]
            if kind == "rows":
                self.got = {0: copies(self.pieces[0], "seq", what)}
            else:
                self.got = {0: swap(self.pieces[0], "seq", what)}

    def take(self):
        if self.order:
            kind, what = self.order.pop(0)
            if kind == "rows":
                self.pieces = {0: rows_in(self.got[0]).astype(BF16)}
            else:
                extra = what if kind == "swap" else 0
                self.pieces = {
                    k: (p.astype(F32) + self.got[k | extra].astype(F32)).astype(BF16)
                    for k, p in self.pieces.items()
                }
        else:
            kind, what = self.back.pop(0)
            mine, other = self.pieces[0], self.got[0]
            if kind == "rows":
                self.pieces = {0: other.reshape(-1, other.shape[2])}
            else:
                upper = (lax.axis_index("seq") & what) != 0
                self.pieces = {
                    0: jnp.where(
                        upper, jnp.concatenate([other, mine], 0), jnp.concatenate([mine, other], 0)
                    )
                }
        self.got = None

    def step(self, *values):
        self.got, values = tie(self.got, values)
        self.take()
        if self.order or self.back:
            self.send()
        return values

    def ready(self, *values):
        self.pieces, values = tie(self.pieces, values)
        return values

    def finish(self):
        while self.got is not None:
            self.step()
        return self.pieces[0]


def orders():
    size = lax.axis_size("seq")
    over = [("swap", bit) for bit in bits("fsdp")]
    parts = size // 4
    groups = [[low + parts * high for high in range(4)] for low in range(parts)]
    near = [("half", bit) for bit in bits("seq") if bit < parts]
    tree = over + [("half", bit) for bit in bits("seq")]
    return over, over + near + [("rows", groups)], over + [("rows", None)], tree


def shards(
    inputs,
    cotangent,
    query_weight,
    key_weight,
    value_weight,
    output_weight,
    up_weight,
    down_weight,
    norm_gain,
    norm_shift,
    final_gain,
    final_shift,
    conv_kernel,
):
    x = inputs[0]
    ct = cotangent[0]
    tokens, width = x.shape
    marks = LANDMARKS // lax.axis_size("seq")
    segment = tokens // marks
    count = lax.axis_size("fsdp")
    rows = width // count
    here = lax.axis_index("fsdp")
    place = lax.axis_index("seq")
    size = lax.axis_size("seq")
    me = jnp.stack([here, place]).astype(jnp.int32)
    over, nested, flat, tree = orders()

    packed, xm = pack(x, (query_weight, key_weight, value_weight), size, marks)
    first_weights = far(packed, "fsdp")
    space = 256 + 2 * EDGE
    taps = jnp.pad(conv_kernel.T, ((0, 4), (EDGE - REACH, space - KERNEL - EDGE + REACH)))
    spat = jnp.pad(conv_kernel[::-1].T, ((0, 4), (EDGE - REACH, space - KERNEL - EDGE + REACH)))
    xm, taps, spat, me = tie(xm, taps, spat, me)
    xm = lax.all_to_all(xm, "seq", 0, 0).reshape(LANDMARKS, width)
    gains = jnp.stack([norm_gain, norm_shift, final_gain, final_shift] * 2)
    gains = gathered(gains, "fsdp")
    first_weights, gains, xm, output_weight = tie(first_weights, gains, xm, output_weight)
    wqkv = near(first_weights, "fsdp")
    wo = far(output_weight, "fsdp")
    wqkv, up_weight = tie(wqkv, up_weight)
    up = far(up_weight, "fsdp")
    source = lax.broadcasted_iota(jnp.int32, (8, width), 1) // rows ^ here
    gains = sum(
        jnp.where(source == k, jnp.concatenate([piece.astype(F32)] * count, 1), 0.0)
        for k, piece in enumerate(gains)
    )

    (xt, xmt, qt, kt, vt, fw, eb, own, msg, qm, km, v_top, v_end) = front(me, x, xm, wqkv, size)
    msg, down_weight = tie(msg, down_weight)
    msgs = lax.all_to_all(msg, "seq", 0, 0)
    down = far(down_weight, "fsdp")
    v_before = shift(v_end, "seq", 1)
    v_after = shift(v_top, "seq", -1)
    a, z, *saved = inverse(qm, km)
    v_before, v_after, z, up, wo = tie(v_before, v_after, z, up, wo)
    up = near(up, "fsdp")
    wo = near(wo, "fsdp")
    convt = conv(vt, v_before, v_after, taps)

    ctxt, hidt, xhat, rstd, act, slope, comb, mixn, stats = mid1(
        me, z, msgs, fw, convt, x, gains, wo, up
    )
    down, act = tie(down, act)
    down = near(down, "fsdp")
    out, second, redt, ge, sums2 = mid2(me, act, slope, xhat, ct, gains, down)
    d_up = grad_up(count, hidt, ge)
    t_up = Total(d_up, tree)
    t_up.send()
    d_down = grad_down(count, me, redt, act, after=d_up)
    second, d_down = t_up.step(second, d_down)
    t_down = Total(d_down, tree)
    t_down.send()
    (second,) = t_up.ready(second)
    first, branch, gct, g_top, g_end, sums1, gc = mid3(
        me, second, ge, xhat, rstd, fw, gains, wo, up, size, after=d_down
    )
    g_before = shift(g_end, "seq", 1)
    g_after = shift(g_top, "seq", -1)
    gc, g_before, g_after = tie(gc, g_before, g_after)
    parts = lax.all_to_all(gc, "seq", 0, 0)
    (gct,) = t_down.step(gct)
    gq, gkm = lead_back(gct, fw, qt, comb, km)
    gct, gq = t_up.step(gct, gq)
    gct, gq = t_up.ready(gct, gq)
    gvc, g_taps = conv_back(vt, v_before, v_after, gct, g_before, g_after, spat)
    d_o = grad_o(count, me, ctxt, branch, sums1, sums2, g_taps)
    t_o = Total(d_o, tree)
    t_o.send()
    gk, gv, gqm, gc = rear_back(z, parts, mixn, stats, own, eb, vt, kt, qm, gvc, after=d_o)
    for t in (t_up, t_o, t_down):
        (gqm,) = t.step(gqm)
        (gqm,) = t.ready(gqm)
    gqm, gkm = inverse_back(me, qm, km, a, mixn, gc, saved, gqm, gkm, size)
    for t in (t_up, t_down):
        (gqm,) = t.step(gqm)
        (gqm,) = t.ready(gqm)
    d_qkv = grad_qkv(count, xt, xmt, gq, gk, gv, gqm, gkm)
    t_qkv = Total(d_qkv, flat)
    t_qkv.send()
    for _ in over[:-1]:
        gqm, gkm = t_qkv.step(gqm, gkm)
    (gqm,) = t_qkv.ready(gqm)
    for t in (t_up, t_down, t_o):
        (gqm,) = t.step(gqm)
        (gqm,) = t.ready(gqm)
    landed = rows_out(jnp.concatenate([gqm, gkm], 1).astype(BF16))
    for t in (t_up, t_down, t_o):
        (landed,) = t.step(landed)
        (landed,) = t.ready(landed)
    landed = rows_in(landed)
    grad_x = last(me, gq, gk, gv, first, landed, wqkv, segment)
    (grad_x,) = t_qkv.step(grad_x)
    for t in (t_up, t_down, t_o) * 2:
        if t.got is not None:
            (grad_x,) = t.step(grad_x)
    g_up = t_up.finish().astype(F32)
    g_down = t_down.finish().T.astype(F32)
    (grad_x, g_up, g_down) = t_qkv.step(grad_x, g_up, g_down)
    g_o = t_o.finish().astype(F32)
    qkv = t_qkv.finish().astype(F32)

    tap = g_o[:KERNEL, width + 4 : width + 4 + HEADS]
    tap = jnp.where(here == 0, tap, 0.0)
    for _, bit in over:
        tap = tap + swap(tap, "fsdp", bit)
    return (
        out[None],
        grad_x[None],
        SCALE * qkv[:, :width],
        SCALE * qkv[:, width : 2 * width],
        qkv[:, 2 * width :],
        g_o[:, :width],
        g_up,
        g_down,
        g_o[:, width],
        g_o[:, width + 1],
        g_o[:, width + 2],
        g_o[:, width + 3],
        tap,
    )


def solution(mesh):
    tokens = P("fsdp", "seq", None)
    matrix = P("fsdp", None)
    row = P("fsdp")
    in_specs = (tokens,) * 2 + (matrix,) * 6 + (row,) * 4 + (P(),)
    out_specs = (tokens,) * 2 + (matrix,) * 6 + (row,) * 4 + (P(),)
    return jax.shard_map(shards, mesh=mesh, in_specs=in_specs, out_specs=out_specs, check_vma=False)
```

```python
import functools

import jax
import jax.numpy as jnp
from jax import lax
from jax.experimental import pallas as pl
from jax.experimental.pallas import tpu as pltpu
from jax.sharding import PartitionSpec as P

HEADS = 12
HDIM = 64
LANDMARKS = 64
KERNEL = 65
PINV_ITERS = 6
REACH = KERNEL // 2
EDGE = 128
SCALE = HDIM ** (-0.25)
F32 = jnp.float32
BF16 = jnp.bfloat16
VM = 56 * 1024 * 1024


def nn(a, b):
    return jnp.dot(a, b, preferred_element_type=F32)


def nt(a, b):
    return lax.dot_general(a, b, (((1,), (1,)), ((), ())), preferred_element_type=F32)


def tn(a, b):
    return lax.dot_general(a, b, (((0,), (0,)), ((), ())), preferred_element_type=F32)


def split(a):
    high = a.astype(BF16)
    return high, (a - high.astype(F32)).astype(BF16)


def nn3(a, b):
    ah, al = split(a)
    bh, bl = split(b)
    return nn(jnp.concatenate([ah, ah, al], 1), jnp.concatenate([bh, bl, bh], 0))


def nt3(a, b):
    ah, al = split(a)
    bh, bl = split(b)
    return nt(jnp.concatenate([ah, ah, al], 1), jnp.concatenate([bh, bl, bh], 1))


def tn3(a, b):
    ah, al = split(a)
    bh, bl = split(b)
    return tn(jnp.concatenate([ah, ah, al], 0), jnp.concatenate([bh, bl, bh], 0))


def lanes(shape):
    return lax.broadcasted_iota(jnp.int32, shape, len(shape) - 1)


def hs(h):
    return slice(h * HDIM, (h + 1) * HDIM)


def vspec():
    return pl.BlockSpec(memory_space=pltpu.VMEM)


def sspec():
    return pl.BlockSpec(memory_space=pltpu.SMEM)


def aspec():
    return pl.BlockSpec(memory_space=pl.ANY)


def shape(dims, kind):
    return jax.ShapeDtypeStruct(tuple(dims), kind)


def params():
    return pltpu.CompilerParams(vmem_limit_bytes=VM)


def cost(flops, traffic, trans=0):
    return pl.CostEstimate(flops=1, bytes_accessed=1, transcendentals=0)


def call(kernel, args, in_specs, out_shape, out_specs, name, work, grid=(), scratch=(), after=()):
    count, extra = len(args), len(after)

    def body(*refs):
        kernel(*refs[:count], *refs[count + extra :])

    return pl.pallas_call(
        body,
        grid=grid,
        out_shape=out_shape,
        in_specs=list(in_specs) + [aspec()] * extra,
        out_specs=out_specs,
        scratch_shapes=list(scratch),
        compiler_params=params(),
        cost_estimate=work,
        name=name,
    )(*args, *after)


def placed(pieces, whole, sems, me, start):
    rows = pieces[0].shape[0]
    for k, piece in enumerate(pieces):
        at = pl.multiple_of((me ^ k) * rows, 16)
        copy = pltpu.make_async_copy(piece, whole.at[pl.ds(at, rows)], sems.at[k])
        if start:
            copy.start()
        else:
            copy.wait()


def xor_rows(out_ref, value, me, count):
    rows = value.shape[0] // count
    for r in range(count):
        at = pl.multiple_of((me ^ r) * rows, 16)
        out_ref[pl.ds(at, rows), :] = value[r * rows : (r + 1) * rows]


def pack_kernel(x_ref, *refs):
    weights, (all_ref, xm_ref, sems) = refs[:-3], refs[-3:]
    copies = []
    for i, w in enumerate(weights):
        to = all_ref.at[:, pl.ds(i * w.shape[1], w.shape[1])]
        copies.append(pltpu.make_async_copy(w, to, sems.at[i]))
        copies[-1].start()
    size, marks, width = xm_ref.shape
    tokens = x_ref.shape[0]
    segment = tokens // marks
    means = [
        jnp.mean(x_ref[m * segment : (m + 1) * segment, :].astype(F32), axis=0, keepdims=True)
        for m in range(marks)
    ]
    means = jnp.concatenate(means, 0)
    for i in range(size):
        xm_ref[i] = means
    for copy in copies:
        copy.wait()


def pack(x, weights, size, marks):
    rows, width = weights[0].shape
    return call(
        pack_kernel,
        (x, *weights),
        [vspec()] * 4,
        [shape((rows, 3 * width), BF16), shape((size, marks, width), F32)],
        [vspec()] * 2,
        "pack",
        cost(1e6, 1e5),
        scratch=[pltpu.SemaphoreType.DMA((3,))],
    )


def front_kernel(count, me_ref, x_ref, xm_ref, *refs):
    pieces = refs[:count]
    outs = refs[count : count + 6]
    xmt_ref, st_ref, msg_ref, qm_ref, km_ref, top_ref, end_ref = refs[count + 6 : count + 13]
    flats = refs[count + 13 : count + 19]
    xt_ref, qt_ref, kt_ref, vt_ref, fw_ref, eb_ref = flats
    w_ref, sems, out_sems, head_sems = refs[count + 19 :]
    me = me_ref[0]

    def out(i):
        return pltpu.make_async_copy(flats[i], outs[i], out_sems.at[i])

    def pair_out(i, pair):
        at = pl.ds(pair * 128, 128)
        return pltpu.make_async_copy(flats[i].at[at], outs[i].at[at], head_sems.at[i - 4, pair])

    placed(pieces, w_ref, sems, me, True)
    tokens, width = x_ref.shape
    step = 256
    for b in range(tokens // step):
        rows = slice(b * step, (b + 1) * step)
        xor_rows(xt_ref.at[:, rows], x_ref[rows, :].T, me, count)
    out(0).start()
    high, low = split(xm_ref[...])
    wide = jnp.concatenate([xm_ref[...], jnp.zeros_like(xm_ref)], 0)
    xor_rows(xmt_ref, wide.T.astype(BF16)[:, :LANDMARKS], me, count)
    placed(pieces, w_ref, sems, me, False)
    both = w_ref[:, : 2 * width]
    marks = SCALE * (nn(high, both) + nn(low, both))
    qm = marks[:, :width].astype(BF16)
    km = marks[:, width:].astype(BF16)
    qm_ref[...] = qm
    km_ref[...] = km
    for i, (to, scale) in enumerate(((qt_ref, SCALE), (kt_ref, SCALE), (vt_ref, None))):
        for b in range(tokens // step):
            rows = slice(b * step, (b + 1) * step)
            y = nn(x_ref[rows, :], w_ref[:, i * width : (i + 1) * width])
            if scale is not None:
                y = y * scale
            y = y.astype(BF16)
            if i == 2 and b == 0:
                top_ref[...] = y[:REACH]
            if i == 2 and b == tokens // step - 1:
                end_ref[...] = y[step - REACH :]
            to[:, rows] = y.T
        out(1 + i).start()
    lane = lanes((LANDMARKS, 128))
    stats = jnp.zeros((LANDMARKS, 128), F32)
    pair = []
    for h in range(HEADS):
        s = nn(km[:, hs(h)], qt_ref[hs(h), :])
        s = jnp.exp(s - jnp.max(s, axis=0, keepdims=True))
        fw_ref[hs(h), :] = (s * (1.0 / jnp.sum(s, axis=0, keepdims=True))).astype(BF16)
        s = nn(qm[:, hs(h)], kt_ref[hs(h), :])
        top = jnp.max(s, axis=1, keepdims=True).astype(BF16).astype(F32)
        e = jnp.exp(s - top).astype(BF16)
        eb_ref[hs(h), :] = e
        total = jnp.sum(e.astype(F32), axis=1, keepdims=True)
        stats = jnp.where(lane == h, top, stats)
        stats = jnp.where(lane == 16 + h, total, stats)
        pair.append(nt(e, vt_ref[hs(h), :]))
        if h % 2:
            both = jnp.concatenate(pair, 1).astype(BF16)
            for d in range(msg_ref.shape[0]):
                msg_ref[d, h // 2] = both
            pair = []
            pair_out(4, h // 2).start()
            pair_out(5, h // 2).start()
    st_ref[...] = stats
    for d in range(msg_ref.shape[0]):
        msg_ref[d, HEADS // 2] = stat_message(stats)
    for i in range(4):
        out(i).wait()
    for h in range(HEADS // 2):
        pair_out(4, h).wait()
        pair_out(5, h).wait()


def stat_message(stats):
    lane = lanes(stats.shape)
    high = stats.astype(BF16).astype(F32)
    low = pltpu.roll(stats - high, 16, 1)
    return jnp.where((lane >= 32) & (lane < 48), low, high).astype(BF16)


def front(me, x, xm, pieces, size):
    tokens, width = x.shape
    pairs = HEADS // 2
    flat = shape((width, tokens), BF16)
    xt, qt, kt, vt, fw, eb, xmt, st, msg, qm, km, top, end = call(
        functools.partial(front_kernel, len(pieces)),
        (me, x, xm, *pieces),
        [sspec(), vspec(), vspec()] + [aspec()] * len(pieces),
        [flat] * 6
        + [
            shape((width, LANDMARKS), BF16),
            shape((LANDMARKS, 128), F32),
            shape((size, pairs + 1, LANDMARKS, 128), BF16),
            shape((LANDMARKS, width), BF16),
            shape((LANDMARKS, width), BF16),
            shape((REACH, width), BF16),
            shape((REACH, width), BF16),
        ],
        [aspec()] * 6 + [vspec()] * 7,
        "front",
        cost(4.5e8, 1.6e6),
        scratch=[pltpu.VMEM((width, tokens), BF16) for _ in range(6)]
        + [
            pltpu.VMEM((width, 3 * width), BF16),
            pltpu.SemaphoreType.DMA((len(pieces),)),
            pltpu.SemaphoreType.DMA((4,)),
            pltpu.SemaphoreType.DMA((2, pairs)),
        ],
    )
    return xt, xmt, qt, kt, vt, fw, eb, st, msg, qm, km, top, end


def merged(msg_ref, mixn_ref, st_ref):
    lane = lanes((LANDMARKS, 128))
    size = msg_ref.shape[0]
    stats = []
    for d in range(size):
        got = msg_ref[d, HEADS // 2].astype(F32)
        stats.append(got + jnp.where((lane >= 16) & (lane < 32), pltpu.roll(got, 112, 1), 0.0))
    largest = functools.reduce(jnp.maximum, stats)
    weights = [jnp.exp(jnp.minimum(st - largest, 0.0)) for st in stats]
    total = sum(st * pltpu.roll(w, 16, 1) for st, w in zip(stats, weights))
    st_ref[...] = jnp.where(lane < 16, largest, total)
    for i in range(HEADS // 2):

        def both(a, at):
            return jnp.where(lane < HDIM, a[:, at : at + 1], a[:, at + 1 : at + 2])

        y = sum(msg_ref[d, i].astype(F32) * both(weights[d], 2 * i) for d in range(size))
        mixn_ref[i] = y / both(total, 16 + 2 * i)


def eye(scale):
    n = LANDMARKS
    return jnp.where(
        lax.broadcasted_iota(jnp.int32, (n, n), 0) == lax.broadcasted_iota(jnp.int32, (n, n), 1),
        jnp.float32(scale),
        0.0,
    )


def landmark_softmax(qm, km, h):
    s = nt(qm[:, hs(h)], km[:, hs(h)])
    s = jnp.exp(s - jnp.max(s, axis=1, keepdims=True))
    return s / jnp.sum(s, axis=1, keepdims=True)


def first_inverse(a):
    columns = jnp.max(jnp.sum(a, axis=0, keepdims=True), axis=1, keepdims=True)
    rows = jnp.max(jnp.sum(a, axis=1, keepdims=True), axis=0, keepdims=True)
    return a.T * (1.0 / (columns * rows))


def inverse_kernel(size, me_ref, qm_ref, km_ref, z_ref, a_out, zs, ps, ms, ns, a_ref, p_ref, m_ref, n_ref):
    qm, km = qm_ref[...], km_ref[...]
    every = range(HEADS)
    slots = range(-(-HEADS // size))
    mine = [jnp.minimum(me_ref[1] + size * j, HEADS - 1) for j in slots]
    for h in every:
        a = landmark_softmax(qm, km, h)
        a_ref[h] = a
        z_ref[h] = first_inverse(a)
    for j in slots:
        a_out[j] = a_ref[mine[j]]

    def step(i, carry):
        p = [nn3(a_ref[h], z_ref[h]) for h in every]
        m = [eye(15.0) - nn3(x, eye(7.0) - x) for x in p]
        n = [eye(13.0) - nn3(x, y) for x, y in zip(p, m)]
        for h in every:
            p_ref[h] = p[h]
            m_ref[h] = m[h]
            n_ref[h] = n[h]
        for j in slots:
            ps[i, j] = p_ref[mine[j]]
            ms[i, j] = m_ref[mine[j]]
            ns[i, j] = n_ref[mine[j]]
            zs[i, j] = z_ref[mine[j]]
        for h in every:
            z_ref[h] = 0.25 * nn3(z_ref[h], n[h])
        return carry

    lax.fori_loop(0, PINV_ITERS, step, 0)


def inverse(me, qm, km, size):
    square = (HEADS, LANDMARKS, LANDMARKS)
    few = (-(-HEADS // size), LANDMARKS, LANDMARKS)
    return call(
        functools.partial(inverse_kernel, size),
        (me, qm, km),
        [sspec()] + [vspec()] * 2,
        [shape(square, F32), shape(few, F32)] + [shape((PINV_ITERS,) + few, F32)] * 4,
        [vspec()] * 6,
        "inverse",
        cost(1e8, 1e6),
        scratch=[pltpu.VMEM(square, F32)] * 4,
    )


def half(pair, h):
    return jnp.where(h % 2 == 0, pair[:, :HDIM], pair[:, HDIM:])


def inverse_step(z, p, m, n, a, gz, ga):
    g = 0.25 * gz
    g3 = -tn3(z, g)
    g2 = -tn3(p, g3)
    gp = nt3(g3, m) + nt3(g2, eye(7.0) - p) - tn3(p, g2)
    return nt3(g, n) + tn3(a, gp), ga + nt3(gp, z)


def score_grad(a, gfirst, ga):
    csum = jnp.sum(a, axis=0, keepdims=True)
    rsum = jnp.sum(a, axis=1, keepdims=True)
    cmax = jnp.max(csum, axis=1, keepdims=True)
    rmax = jnp.max(rsum, axis=0, keepdims=True)
    scale = 1.0 / (cmax * rmax)
    gs = jnp.sum(jnp.sum(gfirst * a.T, axis=1, keepdims=True), axis=0, keepdims=True)
    ctop = (csum == cmax).astype(F32)
    rtop = (rsum == rmax).astype(F32)
    gcol = -gs * scale / cmax * ctop / jnp.sum(ctop, axis=1, keepdims=True)
    grow = -gs * scale / rmax * rtop / jnp.sum(rtop, axis=0, keepdims=True)
    g = ga + gfirst.T * scale + gcol + grow
    return a * (g - jnp.sum(g * a, axis=1, keepdims=True))


def widen(out_ref, flat_ref, before_ref, after_ref):
    width, tokens = flat_ref.shape
    zero = jnp.zeros((EDGE - REACH, width), BF16)
    out_ref[:, :EDGE] = jnp.concatenate([zero, before_ref[...]], 0).T
    out_ref[:, EDGE : EDGE + tokens] = flat_ref[...]
    out_ref[:, EDGE + tokens :] = jnp.concatenate([after_ref[...], zero], 0).T


def band(row, step):
    wide = jnp.broadcast_to(row, (step, step + 2 * EDGE))
    return pltpu.roll(wide, 0, 1, stride=1, stride_axis=0).astype(BF16)


def stacked(ref, h, step, margin):
    blocks = (ref.shape[1] - 2 * margin) // step if margin else ref.shape[1] // step
    return jnp.concatenate(
        [ref[hs(h), b * step : (b + 1) * step + 2 * margin] for b in range(blocks)], 0
    )


def pair_rows(tokens):
    return pl.BlockSpec((128, tokens), lambda i: (i, 0))


def pair_lanes(rows):
    return pl.BlockSpec((rows, 128), lambda i: (0, i))


def pair_block(*dims):
    return pl.BlockSpec((1, *dims), lambda i: (i, 0, 0))


def conv_kernel_body(vt_ref, before_ref, after_ref, taps_ref, out_ref, wide_ref):
    widen(wide_ref, vt_ref, before_ref, after_ref)
    step = 256
    for h in range(HEADS):
        y = nt(stacked(wide_ref, h, step, EDGE), band(taps_ref[h : h + 1, :], step))
        for b in range(vt_ref.shape[1] // step):
            out_ref[hs(h), b * step : (b + 1) * step] = y[b * HDIM : (b + 1) * HDIM, :]


def conv(vt, before, after, taps):
    width, tokens = vt.shape
    return pl.pallas_call(
        conv_kernel_body,
        out_shape=shape(vt.shape, F32),
        in_specs=[vspec()] * 4,
        out_specs=vspec(),
        scratch_shapes=[pltpu.VMEM((width, tokens + 2 * EDGE), BF16)],
        compiler_params=params(),
        cost_estimate=cost(2e+08, 600000),
        name="conv",
    )(vt, before, after, taps)


def gelu_pair(x):
    phi = 0.5 * (1.0 + lax.erf(x * (0.5**0.5)))
    return x * phi, phi + x * ((0.5 / jnp.pi) ** 0.5 * jnp.exp(-0.5 * x * x))


def norm_stats(r):
    center = r - jnp.mean(r, axis=-1, keepdims=True)
    rstd = lax.rsqrt(jnp.mean(center * center, axis=-1, keepdims=True) + 1e-05)
    return center * rstd, rstd


def norm_back(gy, xhat, rstd):
    return rstd * (
        gy - jnp.mean(gy, axis=-1, keepdims=True) - xhat * jnp.mean(gy * xhat, axis=-1, keepdims=True)
    )


STEP = 256


def whole(a):
    return pl.BlockSpec(a.shape, lambda i, n=a.ndim: (0,) * n)


def fixed(*dims):
    return pl.BlockSpec(dims, lambda i, n=len(dims): (0,) * n)


def tall(rows):
    return pl.BlockSpec((rows, STEP), lambda i: (0, i))


def row(width):
    return pl.BlockSpec((STEP, width), lambda i: (i, 0))


def mid1_kernel(count, me_ref, z_ref, msg_ref, fw_ref, conv_ref, x_ref, gains_ref, *refs):
    wo, up = refs[:count], refs[count : 2 * count]
    (ctx_ref, hidt_ref, xhat_ref, rstd_ref, act_ref, slope_ref, comb_ref, mixn_ref, st_ref,
     wo_ref, up_ref, sems) = refs[2 * count :]
    me = me_ref[0]

    @pl.when(pl.program_id(0) == 0)
    def _():
        placed(wo, wo_ref, sems.at[0], me, True)
        placed(up, up_ref, sems.at[1], me, True)
        merged(msg_ref, mixn_ref, st_ref)
        for i in range(HEADS // 2):
            mixed = mixn_ref[i]
            comb_ref[i] = jnp.concatenate(
                [nn3(z_ref[2 * i], mixed[:, :HDIM]), nn3(z_ref[2 * i + 1], mixed[:, HDIM:])], 1
            ).astype(BF16)
        placed(wo, wo_ref, sems.at[0], me, False)

    for h in range(HEADS):
        half = slice((h % 2) * HDIM, (h % 2) * HDIM + HDIM)
        att = tn(comb_ref[h // 2][:, half], fw_ref[hs(h), :])
        ctx_ref[hs(h), :] = (att + conv_ref[hs(h), :]).astype(BF16)
    branch = nn(ctx_ref[...].T, wo_ref[...])
    xhat, rstd = norm_stats(x_ref[...].astype(F32) + branch)
    xhat_ref[...] = xhat
    rstd_ref[...] = jnp.broadcast_to(rstd, rstd_ref.shape)
    hidden = (xhat * gains_ref[0:1, :] + gains_ref[1:2, :]).astype(BF16)
    xor_rows(hidt_ref, hidden.T, me, count)
    @pl.when(pl.program_id(0) == 0)
    def _():
        placed(up, up_ref, sems.at[1], me, False)

    part = up_ref.shape[1] // count
    for c in range(count):
        at = slice(c * part, (c + 1) * part)
        act, slope = gelu_pair(nn(hidden, up_ref[:, at]))
        act_ref[:, at] = act.astype(BF16)
        slope_ref[:, at] = slope.astype(BF16)


def mid1(me, z, msgs, fw, convt, x, gains, wo, up, after=()):
    tokens, width = x.shape
    ff = up[0].shape[1]
    pairs = HEADS // 2
    return call(
        functools.partial(mid1_kernel, len(wo)),
        (me, z, msgs, fw, convt, x, gains, *wo, *up),
        [sspec(), whole(z), whole(msgs), tall(width), tall(width), row(width), whole(gains)]
        + [aspec()] * (len(wo) + len(up)),
        [
            shape((width, tokens), BF16),
            shape((width, tokens), BF16),
            shape((tokens, width), F32),
            shape((tokens, 128), F32),
            shape((tokens, ff), BF16),
            shape((tokens, ff), BF16),
            shape((pairs, LANDMARKS, 128), BF16),
            shape((pairs, LANDMARKS, 128), F32),
            shape((LANDMARKS, 128), F32),
        ],
        [tall(width), tall(width), row(width), row(128), row(ff), row(ff)]
        + [fixed(pairs, LANDMARKS, 128)] * 2
        + [fixed(LANDMARKS, 128)],
        "mid_one",
        cost(2e9, 3e6),
        grid=(tokens // STEP,),
        scratch=[
            pltpu.VMEM((width, width), BF16),
            pltpu.VMEM((width, ff), BF16),
            pltpu.SemaphoreType.DMA((2, len(wo))),
        ],
        after=after,
    )


def mid2_kernel(count, me_ref, act_ref, slope_ref, xhat_ref, ct_ref, gains_ref, *refs):
    down = refs[:count]
    out_ref, second_ref, redt_ref, ge_ref, sums_ref, down_ref, sems = refs[count:]
    me = me_ref[0]

    @pl.when(pl.program_id(0) == 0)
    def _():
        placed(down, down_ref, sems, me, True)
        sums_ref[...] = jnp.zeros_like(sums_ref)
        placed(down, down_ref, sems, me, False)

    reduced = nn(act_ref[...], down_ref[...])
    hidden = xhat_ref[...] * gains_ref[0:1, :] + gains_ref[1:2, :]
    xhat, rstd = norm_stats(hidden + reduced)
    out_ref[...] = (xhat * gains_ref[2:3, :] + gains_ref[3:4, :]).astype(BF16)
    ct = ct_ref[...].astype(F32)
    sums_ref[0:1, :] = sums_ref[0:1, :] + jnp.sum(ct * xhat, axis=0, keepdims=True)
    sums_ref[1:2, :] = sums_ref[1:2, :] + jnp.sum(ct, axis=0, keepdims=True)
    second = norm_back(ct * gains_ref[2:3, :], xhat, rstd)
    second_ref[...] = second
    red = second.astype(BF16)
    redt_ref[...] = red.T
    part = down_ref.shape[0] // count
    for k in range(count):
        cols = slice(k * part, (k + 1) * part)
        ge = nt(red, down_ref[cols, :]) * slope_ref[:, cols].astype(F32)
        ge_ref[:, cols] = ge.astype(BF16)


def mid2(me, act, slope, xhat, ct, gains, down, after=()):
    tokens, width = ct.shape
    ff = act.shape[1]
    return call(
        functools.partial(mid2_kernel, len(down)),
        (me, act, slope, xhat, ct, gains, *down),
        [sspec(), row(ff), row(ff), row(width), row(width), whole(gains)] + [aspec()] * len(down),
        [
            shape((tokens, width), BF16),
            shape((tokens, width), F32),
            shape((width, tokens), BF16),
            shape((tokens, ff), BF16),
            shape((8, width), F32),
        ],
        [row(width), row(width), tall(width), row(ff), fixed(8, width)],
        "mid_two",
        cost(2e9, 3e6),
        grid=(tokens // STEP,),
        scratch=[pltpu.VMEM((ff, width), BF16), pltpu.SemaphoreType.DMA((len(down),))],
        after=after,
    )


def mid3_kernel(count, me_ref, second_ref, ge_ref, xhat_ref, rstd_ref, fw_ref, gains_ref, *refs):
    wo, up = refs[:count], refs[count : 2 * count]
    (first_ref, branch_ref, gct_ref, top_ref, end_ref, sums_ref, parts_ref,
     wo_ref, up_ref, gc_ref, sems) = refs[2 * count :]
    me = me_ref[0]
    at = pl.program_id(0)

    @pl.when(at == 0)
    def _():
        placed(up, up_ref, sems.at[0], me, True)
        placed(wo, wo_ref, sems.at[1], me, True)
        sums_ref[...] = jnp.zeros_like(sums_ref)
        gc_ref[...] = jnp.zeros_like(gc_ref)
        placed(up, up_ref, sems.at[0], me, False)
        placed(wo, wo_ref, sems.at[1], me, False)

    g = second_ref[...] + nt(ge_ref[...], up_ref[...])
    xhat = xhat_ref[...]
    sums_ref[0:1, :] = sums_ref[0:1, :] + jnp.sum(g * xhat, axis=0, keepdims=True)
    sums_ref[1:2, :] = sums_ref[1:2, :] + jnp.sum(g, axis=0, keepdims=True)
    first = norm_back(g * gains_ref[0:1, :], xhat, rstd_ref[:, 0:1])
    first_ref[...] = first
    branch = first.astype(BF16)
    branch_ref[...] = branch
    gctx = nt(branch, wo_ref[...]).astype(BF16)

    @pl.when(at == 0)
    def _():
        top_ref[...] = gctx[:REACH]

    @pl.when(at == pl.num_programs(0) - 1)
    def _():
        end_ref[...] = gctx[gctx.shape[0] - REACH :]

    gct_ref[...] = gctx.T
    for i in range(HEADS // 2):
        gc_ref[i] = gc_ref[i] + jnp.concatenate(
            [nt(fw_ref[hs(h), :], gct_ref[hs(h), :]) for h in (2 * i, 2 * i + 1)], 1
        )

    @pl.when(at == pl.num_programs(0) - 1)
    def _():
        for d in range(parts_ref.shape[0]):
            parts_ref[d] = gc_ref[...].astype(BF16)


def mid3(me, second, ge, xhat, rstd, fw, gains, wo, up, size, after=()):
    tokens, width = second.shape
    ff = ge.shape[1]
    pairs = HEADS // 2
    return call(
        functools.partial(mid3_kernel, len(wo)),
        (me, second, ge, xhat, rstd, fw, gains, *wo, *up),
        [sspec(), row(width), row(ff), row(width), row(128), tall(width), whole(gains)]
        + [aspec()] * (2 * len(wo)),
        [
            shape((tokens, width), F32),
            shape((tokens, width), BF16),
            shape((width, tokens), BF16),
            shape((REACH, width), BF16),
            shape((REACH, width), BF16),
            shape((8, width), F32),
            shape((size, pairs, LANDMARKS, 128), BF16),
        ],
        [row(width), row(width), tall(width), fixed(REACH, width), fixed(REACH, width),
         fixed(8, width), fixed(size, pairs, LANDMARKS, 128)],
        "mid_three",
        cost(2e9, 3e6),
        grid=(tokens // STEP,),
        scratch=[
            pltpu.VMEM((width, width), BF16),
            pltpu.VMEM((width, ff), BF16),
            pltpu.VMEM((pairs, LANDMARKS, 128), F32),
            pltpu.SemaphoreType.DMA((2, len(wo))),
        ],
        after=after,
    )


def grad_down_kernel(count, me_ref, red_ref, act_ref, *outs):
    y = nn(red_ref[...], act_ref[...]).astype(BF16)
    for k in range(count):

        @pl.when(pl.program_id(0) ^ me_ref[0] == k)
        def _():
            outs[k][...] = y


def grad_down(count, me, redt, act, after=()):
    width, tokens = redt.shape
    part = act.shape[1] // count
    return call(
        functools.partial(grad_down_kernel, count),
        (me, redt, act),
        [sspec(), whole(redt), pl.BlockSpec((tokens, part), lambda i: (0, i))],
        [shape((width, part), BF16)] * count,
        [fixed(width, part)] * count,
        "grad_down",
        cost(5e8, 1e6),
        grid=(count,),
        after=after,
    )


def grad_up_kernel(count, hid_ref, ge_ref, *outs):
    y = nn(hid_ref[...], ge_ref[...]).astype(BF16)
    rows = y.shape[0] // count
    for k in range(count):
        outs[k][...] = y[k * rows : (k + 1) * rows]


def grad_up(count, hidt, ge, after=()):
    width, tokens = hidt.shape
    ff = ge.shape[1]
    step = 768
    return call(
        functools.partial(grad_up_kernel, count),
        (hidt, ge),
        [whole(hidt), pl.BlockSpec((tokens, step), lambda i: (0, i))],
        [shape((width // count, ff), BF16)] * count,
        [pl.BlockSpec((width // count, step), lambda i: (0, i))] * count,
        "grad_up",
        cost(5e8, 1e6),
        grid=(ff // step,),
        after=after,
    )


class Moves:
    def __init__(self, sems):
        self.sems, self.used, self.open = sems, 0, []

    def start(self, src, dst):
        copy = pltpu.make_async_copy(src, dst, self.sems.at[self.used])
        self.used += 1
        copy.start()
        self.open.append(copy)
        return copy

    def wait(self, *copies):
        for copy in copies or list(self.open):
            copy.wait()
            self.open.remove(copy)


def gap_kernel(count, me_ref, gct_hbm, fw_hbm, qt_hbm, vt_hbm, ctx_hbm, branch_hbm, comb_ref, km_ref,
               vb_ref, va_ref, gb_ref, ga_ref, taps_ref, sums1_ref, sums2_ref, *refs):
    outs = refs[:count]
    (gq_hbm, gvc_hbm, gkm_ref, gct_ref, fw_ref, qt_ref, vt_ref, ctx_ref, branch_ref, gq_ref, gvc_ref,
     vwide, gwide, y_ref, sems) = refs[count:]
    moves = Moves(sems)
    lead = [
        moves.start(a, b)
        for a, b in ((gct_hbm, gct_ref), (fw_hbm, fw_ref), (qt_hbm, qt_ref))
    ]
    values = moves.start(vt_hbm, vt_ref)
    rest = [moves.start(ctx_hbm, ctx_ref), moves.start(branch_hbm, branch_ref)]
    km = km_ref[...]
    moves.wait(*lead)
    pair = []
    for h in range(HEADS):
        comb = comb_ref[h // 2][:, hs(h % 2)]
        pf = fw_ref[hs(h), :].astype(F32)
        g = nn(comb, gct_ref[hs(h), :])
        gs = (pf * (g - jnp.sum(pf * g, axis=0, keepdims=True))).astype(BF16)
        gq_ref[hs(h), :] = tn(km[:, hs(h)], gs).astype(BF16)
        pair.append(nt(gs, qt_ref[hs(h), :]))
        if h % 2:
            gkm_ref[:, (h - 1) * HDIM : (h + 1) * HDIM] = jnp.concatenate(pair, 1)
            pair = []
    moves.start(gq_ref, gq_hbm)
    moves.wait(values)
    widen(vwide, vt_ref, vb_ref, va_ref)
    widen(gwide, gct_ref, gb_ref, ga_ref)
    step = 256
    tokens = vt_ref.shape[1]
    flip = (
        lax.broadcasted_iota(jnp.int32, (step, step), 0)
        + lax.broadcasted_iota(jnp.int32, (step, step), 1)
        == step - 1
    ).astype(BF16)
    rows = []
    for h in range(HEADS):
        y = nt(stacked(gwide, h, step, EDGE), band(taps_ref[h : h + 1, :], step))
        for b in range(tokens // step):
            gvc_ref[hs(h), b * step : (b + 1) * step] = y[b * HDIM : (b + 1) * HDIM, :]
        turned = nn(stacked(gct_ref, h, step, 0), flip).astype(BF16)
        d = tn(turned, stacked(vwide, h, step, EDGE))
        d = pltpu.roll(d, 0, 1, stride=1, stride_axis=0)
        rows.append(jnp.sum(d, axis=0, keepdims=True))
    moves.start(gvc_ref, gvc_hbm)
    rows = jnp.concatenate(rows + [jnp.zeros((4, step + 2 * EDGE), F32)], 0)
    first = step - 1 + EDGE - REACH
    taps = pltpu.roll(rows, step + 2 * EDGE - first, 1)[:HEADS, :128]
    width = ctx_ref.shape[0]
    taps = jnp.concatenate([taps, jnp.zeros((HEADS, width - 128), F32)], 1)
    little = jnp.concatenate(
        [sums1_ref[0:2, :], sums2_ref[0:2, :], taps, jnp.zeros((128 - 4 - HEADS, width), F32)], 0
    )
    y_ref[:, width:] = little.T.astype(BF16)
    moves.wait(*rest)
    y_ref[:, :width] = nn(ctx_ref[...], branch_ref[...]).astype(BF16)
    size = width // count
    for k in range(count):
        outs[k][...] = y_ref[pl.ds(pl.multiple_of((me_ref[0] ^ k) * size, 16), size), :]
    moves.wait()


def gap(count, me, gct, fw, qt, vt, ctxt, branch, comb, km, vb, va, gb, ga, taps, sums1, sums2, after=()):
    width, tokens = vt.shape
    flat = pltpu.VMEM((width, tokens), BF16)
    wide = pltpu.VMEM((width, tokens + 2 * EDGE), BF16)
    *pieces, gq, gvc, gkm = call(
        functools.partial(gap_kernel, count),
        (me, gct, fw, qt, vt, ctxt, branch, comb, km, vb, va, gb, ga, taps, sums1, sums2),
        [sspec()] + [aspec()] * 6 + [vspec()] * 9,
        [shape((width // count, width + 128), BF16)] * count
        + [shape(gct.shape, BF16), shape(gct.shape, F32), shape(km.shape, F32)],
        [vspec()] * count + [aspec()] * 2 + [vspec()],
        "gap",
        cost(1e9, 1e6),
        scratch=[flat] * 5
        + [
            pltpu.VMEM((tokens, width), BF16),
            flat,
            pltpu.VMEM((width, tokens), F32),
            wide,
            wide,
            pltpu.VMEM((width, width + 128), BF16),
            pltpu.SemaphoreType.DMA((8,)),
        ],
        after=after,
    )
    return pieces, gq, gvc, gkm


def rear_kernel(count, size, me_ref, eb_hbm, vt_hbm, kt_hbm, gvc_hbm, xt_hbm, gq_hbm, z_ref, parts_ref,
                mixn_ref, st_ref, own_ref, qm_ref, km_ref, gkmp_ref, xmt_ref, a_ref, zs, ps, ms, ns, *refs):
    outs = refs[:count]
    (gk_hbm, gv_hbm, gqm_ref, gkm_ref, eb_ref, vt_ref, kt_ref, gvc_ref, xt_ref, gq_ref, gk_ref, gv_ref,
     gc_ref, y_ref, sems) = refs[count:]
    moves = Moves(sems)
    early = [
        moves.start(a, b)
        for a, b in ((vt_hbm, vt_ref), (eb_hbm, eb_ref), (kt_hbm, kt_ref), (gvc_hbm, gvc_ref))
    ]
    late = [moves.start(xt_hbm, xt_ref), moves.start(gq_hbm, gq_ref)]
    qm, km = qm_ref[...], km_ref[...]
    lane = lanes((LANDMARKS, 128))
    gc_ref[...] = sum(parts_ref[d].astype(F32) for d in range(parts_ref.shape[0]))
    slots = range(-(-HEADS // size))
    heads = [me_ref[1] + size * j for j in slots]
    safe = [jnp.minimum(h, HEADS - 1) for h in heads]
    gz = [nt3(half(gc_ref[h // 2], h), half(mixn_ref[h // 2], h)) for h in safe]
    ga = [jnp.zeros((LANDMARKS, LANDMARKS), F32) for _ in slots]
    stats = st_ref[...]
    scale = jnp.exp(own_ref[...] - stats)
    moves.wait(*early)
    for p in range(HEADS // 2):
        if p < PINV_ITERS:
            i = PINV_ITERS - 1 - p
            for j in slots:
                gz[j], ga[j] = inverse_step(
                    zs[i, j], ps[i, j], ms[i, j], ns[i, j], a_ref[j], gz[j], ga[j]
                )
        pair = []
        for h in (2 * p, 2 * p + 1):
            gmix = tn3(z_ref[h], gc_ref[p][:, hs(h % 2)]).astype(BF16)
            dot = jnp.sum(gmix.astype(F32) * mixn_ref[p][:, hs(h % 2)], axis=1, keepdims=True)
            factor = scale[:, h : h + 1] / stats[:, 16 + h : 17 + h]
            pb = eb_ref[hs(h), :].astype(F32) * factor
            gs = (pb * (nn(gmix, vt_ref[hs(h), :]) - dot)).astype(BF16)
            gk_ref[hs(h), :] = tn(qm[:, hs(h)], gs).astype(BF16)
            gv_ref[hs(h), :] = (tn(gmix, pb.astype(BF16)) + gvc_ref[hs(h), :]).astype(BF16)
            pair.append(nt(gs, kt_ref[hs(h), :]))
        both = slice(p * 128, p * 128 + 128)
        gqm_ref[:, both] = jnp.concatenate(pair, 1)
        gkm_ref[:, both] = gkmp_ref[:, both]
    moves.start(gk_ref, gk_hbm)
    moves.start(gv_ref, gv_hbm)
    moves.wait(*late)
    width = xt_ref.shape[0]
    rows = width // count

    def weight(i, y):
        y_ref[i] = y.astype(BF16)
        for k in range(count):
            moves.start(y_ref.at[i, pl.ds(k * rows, rows)], outs[k].at[i])

    weight(2, nt(xt_ref[...], gv_ref[...]))
    for j in slots:
        h = safe[j]
        high, low = split(score_grad(a_ref[j], gz[j], ga[j]))
        at = pl.ds(pl.multiple_of(h // 2 * 128, 128), 128)
        qmh = half(qm_ref[:, at].astype(F32), h).astype(BF16)
        kmh = half(km_ref[:, at].astype(F32), h).astype(BF16)
        gq = nn(jnp.concatenate([high, low], 1), jnp.concatenate([kmh] * 2, 0))
        gk = tn(jnp.concatenate([high, low], 0), jnp.concatenate([qmh] * 2, 0))
        mine = ((lane >= HDIM) == (h % 2 == 1)) & (heads[j] < HEADS)
        gqm_ref[:, at] = gqm_ref[:, at] + jnp.where(mine, jnp.concatenate([gq, gq], 1), 0.0)
        gkm_ref[:, at] = gkm_ref[:, at] + jnp.where(mine, jnp.concatenate([gk, gk], 1), 0.0)
    weight(0, nt(xt_ref[...], gq_ref[...]) + nn(xmt_ref[...], gqm_ref[...].astype(BF16)))
    weight(1, nt(xt_ref[...], gk_ref[...]) + nn(xmt_ref[...], gkm_ref[...].astype(BF16)))
    moves.wait()


def rear(count, size, me, eb, vt, kt, gvc, xt, gq, z, parts, mixn, stats, own, qm, km, gkm, xmt, a, saved,
         after=()):
    width, tokens = vt.shape
    rows = width // count
    flat = pltpu.VMEM((width, tokens), BF16)
    mark = shape(qm.shape, F32)
    *pieces, gk, gv, gqm, gkm = call(
        functools.partial(rear_kernel, count, size),
        (me, eb, vt, kt, gvc, xt, gq, z, parts, mixn, stats, own, qm, km, gkm, xmt, a, *saved),
        [sspec()] + [aspec()] * 6 + [vspec()] * 14,
        [shape((3, rows, width), BF16)] * count + [shape(vt.shape, BF16)] * 2 + [mark] * 2,
        [aspec()] * (count + 2) + [vspec()] * 2,
        "rear",
        cost(2e9, 2e6),
        scratch=[flat] * 3
        + [pltpu.VMEM((width, tokens), F32)]
        + [flat] * 4
        + [
            pltpu.VMEM(mixn.shape, F32),
            pltpu.VMEM((3, width, width), BF16),
            pltpu.SemaphoreType.DMA((8 + 3 * count,)),
        ],
        after=after,
    )
    return [piece.reshape(3 * rows, width) for piece in pieces], gk, gv, gqm, gkm


def last_kernel(count, me_ref, gq_ref, gk_ref, gv_ref, first_ref, *refs):
    pieces = refs[:count]
    out_ref, w_ref, sems = refs[count:]
    me = me_ref[0]
    width = gq_ref.shape[0]

    @pl.when(pl.program_id(0) == 0)
    def _():
        placed(pieces, w_ref, sems, me, True)
        placed(pieces, w_ref, sems, me, False)

    wq, wk, wv = (w_ref[:, i * width : (i + 1) * width] for i in range(3))
    g = SCALE * (nn(wq, gq_ref[...]) + nn(wk, gk_ref[...])) + nn(wv, gv_ref[...])
    out_ref[...] = first_ref[...] + g.T


def last(me, gq, gk, gv, first, pieces, after=()):
    width, tokens = gq.shape
    return call(
        functools.partial(last_kernel, len(pieces)),
        (me, gq, gk, gv, first, *pieces),
        [sspec(), tall(width), tall(width), tall(width), row(width)] + [aspec()] * len(pieces),
        shape((tokens, width), F32),
        row(width),
        "last",
        cost(4e8, 1e6),
        grid=(tokens // STEP,),
        scratch=[
            pltpu.VMEM((width, 3 * width), BF16),
            pltpu.SemaphoreType.DMA((len(pieces),)),
        ],
        after=after,
    )


def share_kernel(segment, count, me_ref, own_ref, most_ref, *refs):
    pieces = refs[:count]
    out_ref, w_ref, sems = refs[count:]
    placed(pieces, w_ref, sems, me_ref[0], True)
    placed(pieces, w_ref, sems, me_ref[0], False)
    own = own_ref[...]
    width = own.shape[1] // 2
    marks = (SCALE / segment) * (
        nt(own[:, :width].astype(BF16), w_ref[:, :width])
        + nt(own[:, width:].astype(BF16), w_ref[:, width : 2 * width])
    )
    for m in range(own.shape[0]):
        rows = slice(m * segment, (m + 1) * segment)
        out_ref[rows, :] = (most_ref[rows, :] + marks[m : m + 1, :]).astype(BF16)


def share(me, own, most, pieces):
    tokens, width = most.shape
    return call(
        functools.partial(share_kernel, tokens // own.shape[0], len(pieces)),
        (me, own, most, *pieces),
        [sspec(), vspec(), vspec()] + [aspec()] * len(pieces),
        shape(most.shape, BF16),
        vspec(),
        "share",
        cost(4e8, 1e6),
        scratch=[
            pltpu.VMEM((width, 3 * width), BF16),
            pltpu.SemaphoreType.DMA((len(pieces),)),
        ],
    )


def bits(axis):
    size = lax.axis_size(axis)
    assert size & (size - 1) == 0
    return [1 << i for i in range(size.bit_length() - 1)]


def swap(array, axis, bit):
    return lax.ppermute(array, axis, [(i, i ^ bit) for i in range(lax.axis_size(axis))])


def shift(array, axis, by):
    size = lax.axis_size(axis)
    return lax.ppermute(array, axis, [(i, i + by) for i in range(size) if 0 <= i + by < size])


def spread(pieces, axis, steps):
    for bit in steps:
        pieces = {**pieces, **{k | bit: swap(piece, axis, bit) for k, piece in pieces.items()}}
    return pieces


def far(array, axis):
    return spread({0: array}, axis, bits(axis)[1:])


def near(pieces, axis):
    pieces = spread(pieces, axis, bits(axis)[:1])
    return [pieces[k] for k in range(lax.axis_size(axis))]


def gathered(array, axis):
    return near(far(array, axis), axis)


def tie(*values):
    return lax.optimization_barrier(values)


def rows_out(array, groups=None):
    size = len(groups[0]) if groups else lax.axis_size("seq")
    blocks = array.reshape(size, -1, array.shape[1])
    return lax.all_to_all(blocks, "seq", 0, 0, axis_index_groups=groups)


def rows_in(blocks):
    return jnp.sum(blocks.astype(F32), axis=0)


def copies(array, axis, groups=None):
    size = len(groups[0]) if groups else lax.axis_size(axis)
    blocks = jnp.broadcast_to(array[None], (size, *array.shape))
    return lax.all_to_all(blocks, axis, 0, 0, axis_index_groups=groups)


class Total:
    def __init__(self, pieces, order):
        self.pieces = dict(enumerate(pieces))
        self.order = list(order)
        self.back = [step for step in reversed(order) if step[0] != "swap"]
        self.got = None

    def send(self, *values):
        if not self.order and not self.back:
            return values
        back = not self.order
        kind, what = self.back[0] if back else self.order[0]
        axis = "seq"
        if kind == "swap":
            axis = "fsdp"
            sent = {k: p for k, p in self.pieces.items() if k & what}
            self.pieces = {k: p for k, p in self.pieces.items() if not k & what}
        elif kind == "half" and not back:
            piece = self.pieces[0]
            upper = ((lax.axis_index("seq") & what) != 0).astype(jnp.int32)
            half = piece.shape[0] // 2
            self.pieces = {0: lax.dynamic_slice_in_dim(piece, upper * half, half, 0)}
            sent = {0: lax.dynamic_slice_in_dim(piece, (1 - upper) * half, half, 0)}
        elif kind == "rows" and back:
            size = len(what[0]) if what else lax.axis_size("seq")
            sent = {0: jnp.broadcast_to(self.pieces[0][None], (size, *self.pieces[0].shape))}
        elif kind == "rows":
            size = len(what[0]) if what else lax.axis_size("seq")
            sent = {0: self.pieces[0].reshape(size, -1, self.pieces[0].shape[1])}
        else:
            sent = dict(self.pieces)
        if values:
            sent, values = tie(sent, values)
        if kind == "rows":
            self.got = {
                k: lax.all_to_all(p, "seq", 0, 0, axis_index_groups=what) for k, p in sent.items()
            }
        else:
            self.got = {k: swap(p, axis, what) for k, p in sent.items()}
        return values

    def take(self):
        if self.order:
            kind, what = self.order.pop(0)
            if kind == "rows":
                self.pieces = {0: rows_in(self.got[0]).astype(BF16)}
            else:
                extra = what if kind == "swap" else 0
                self.pieces = {
                    k: (p.astype(F32) + self.got[k | extra].astype(F32)).astype(BF16)
                    for k, p in self.pieces.items()
                }
        else:
            kind, what = self.back.pop(0)
            mine, other = self.pieces[0], self.got[0]
            if kind == "rows":
                self.pieces = {0: other.reshape(-1, other.shape[2])}
            else:
                upper = (lax.axis_index("seq") & what) != 0
                self.pieces = {
                    0: jnp.where(
                        upper, jnp.concatenate([other, mine], 0), jnp.concatenate([mine, other], 0)
                    )
                }
        self.got = None

    def step(self, *values):
        self.got, values = tie(self.got, values)
        self.take()
        return self.send(*values)

    def finish(self):
        while self.got is not None:
            self.step()
        return self.pieces[0]


def orders():
    size = lax.axis_size("seq")
    over = [("swap", bit) for bit in bits("fsdp")]
    parts = size // 4
    groups = [[low + parts * high for high in range(4)] for low in range(parts)]
    near = [("half", bit) for bit in bits("seq") if bit < parts]
    tree = over + [("half", bit) for bit in bits("seq")]
    return over, over + near + [("rows", groups)], over + [("rows", None)], tree


def shards(
    inputs,
    cotangent,
    query_weight,
    key_weight,
    value_weight,
    output_weight,
    up_weight,
    down_weight,
    norm_gain,
    norm_shift,
    final_gain,
    final_shift,
    conv_kernel,
):
    x = inputs[0]
    ct = cotangent[0]
    tokens, width = x.shape
    marks = LANDMARKS // lax.axis_size("seq")
    segment = tokens // marks
    count = lax.axis_size("fsdp")
    rows = width // count
    here = lax.axis_index("fsdp")
    place = lax.axis_index("seq")
    size = lax.axis_size("seq")
    me = jnp.stack([here, place]).astype(jnp.int32)
    over, nested, flat, tree = orders()

    packed, xm = pack(x, (query_weight, key_weight, value_weight), size, marks)
    first_weights = far(packed, "fsdp")
    space = 256 + 2 * EDGE
    taps = jnp.pad(conv_kernel.T, ((0, 4), (EDGE - REACH, space - KERNEL - EDGE + REACH)))
    spat = jnp.pad(conv_kernel[::-1].T, ((0, 4), (EDGE - REACH, space - KERNEL - EDGE + REACH)))
    xm, taps, spat, me = tie(xm, taps, spat, me)
    xm = lax.all_to_all(xm, "seq", 0, 0).reshape(LANDMARKS, width)
    gains = jnp.stack([norm_gain, norm_shift, final_gain, final_shift] * 2)
    gains = gathered(gains, "fsdp")
    first_weights, gains, xm, output_weight = tie(first_weights, gains, xm, output_weight)
    wqkv = near(first_weights, "fsdp")
    wo = far(output_weight, "fsdp")
    wqkv, up_weight = tie(wqkv, up_weight)
    up = far(up_weight, "fsdp")
    source = lax.broadcasted_iota(jnp.int32, (8, width), 1) // rows ^ here
    gains = sum(
        jnp.where(source == k, jnp.concatenate([piece.astype(F32)] * count, 1), 0.0)
        for k, piece in enumerate(gains)
    )

    (xt, xmt, qt, kt, vt, fw, eb, own, msg, qm, km, v_top, v_end) = front(me, x, xm, wqkv, size)
    msg, down_weight = tie(msg, down_weight)
    msgs = lax.all_to_all(msg, "seq", 0, 0)
    down = far(down_weight, "fsdp")
    v_before = shift(v_end, "seq", 1)
    v_after = shift(v_top, "seq", -1)
    z, a, *saved = inverse(me, qm, km, size)
    v_before, v_after, z, up, wo = tie(v_before, v_after, z, up, wo)
    up = near(up, "fsdp")
    wo = near(wo, "fsdp")
    convt = conv(vt, v_before, v_after, taps)

    ctxt, hidt, xhat, rstd, act, slope, comb, mixn, stats = mid1(
        me, z, msgs, fw, convt, x, gains, wo, up
    )
    down, act = tie(down, act)
    down = near(down, "fsdp")
    out, second, redt, ge, sums2 = mid2(me, act, slope, xhat, ct, gains, down)
    d_up = grad_up(count, hidt, ge)
    t_up = Total(d_up, tree)
    t_up.send()
    d_down = grad_down(count, me, redt, act, after=d_up)
    second, d_down = t_up.step(second, d_down)
    t_down = Total(d_down, over)
    t_down.send()
    (second,) = t_down.step(second)
    first, branch, gct, g_top, g_end, sums1, gc = mid3(
        me, second, ge, xhat, rstd, fw, gains, wo, up, size, after=d_down
    )
    g_before = shift(g_end, "seq", 1)
    g_after = shift(g_top, "seq", -1)
    gc, g_before, g_after = tie(gc, g_before, g_after)
    parts = lax.all_to_all(gc, "seq", 0, 0)
    (gct,) = t_up.step(gct)
    while t_down.got is not None:
        (gct,) = t_down.step(gct)
    g_down, gct = tie(t_down.pieces[0], gct)
    d_o, gq, gvc, gkm = gap(
        count, me, gct, fw, qt, vt, ctxt, branch, comb, km, v_before, v_after, g_before, g_after, spat, sums1, sums2
    )
    t_o = Total(d_o, over)
    t_o.send()
    (parts,) = t_up.step(parts)
    (parts,) = t_o.step(parts)
    d_qkv, gk, gv, gqm, gkm = rear(
        count, size, me, eb, vt, kt, gvc, xt, gq, z, parts, mixn, stats, own, qm, km, gkm, xmt, a, saved, after=d_o
    )
    t_qkv = Total(d_qkv, tree)
    t_qkv.send()
    landed = rows_out(jnp.concatenate([gqm, gkm], 1).astype(BF16))
    while t_o.got is not None:
        (gk,) = t_o.step(gk)
    g_o = t_o.pieces[0]
    part = g_down.shape[1]
    g_down = g_down.reshape(-1, width)
    sizes = [g_down.shape[0], rows, rows * 128 // width]
    both = jnp.concatenate([g_down, g_o[:, :width], g_o[:, width:].reshape(-1, width)], 0)
    t_both = Total([both], tree[len(over) :])
    (gk,) = t_both.send(gk)
    (gk,) = t_up.step(gk)
    for _ in over[:-1]:
        (gk,) = t_qkv.step(gk)
    most = last(me, gq, gk, gv, first, wqkv)
    for t in (t_up, t_both):
        (most,) = t.step(most)
    landed, most = tie(landed, most)
    grad_x = share(me, rows_in(landed), most, wqkv)
    totals = (t_qkv, t_up, t_both)
    while any(t.got is not None for t in totals):
        for t in totals:
            if t.got is not None:
                (grad_x,) = t.step(grad_x)
    g_up, both, qkv = (t.pieces[0].astype(F32) for t in (t_up, t_both, t_qkv))
    g_down = both[: sizes[0]].reshape(width, part).T
    g_o = both[sizes[0] : sizes[0] + sizes[1]]
    little = both[sizes[0] + sizes[1] :].reshape(rows, 128)

    tap = little[:KERNEL, 4 : 4 + HEADS]
    tap = jnp.where(here == 0, tap, 0.0)
    for _, bit in over:
        tap = tap + swap(tap, "fsdp", bit)
    return (
        out[None],
        grad_x[None],
        SCALE * qkv[:rows],
        SCALE * qkv[rows : 2 * rows],
        qkv[2 * rows :],
        g_o,
        g_up,
        g_down,
        little[:, 0],
        little[:, 1],
        little[:, 2],
        little[:, 3],
        tap,
    )


def solution(mesh):
    tokens = P("fsdp", "seq", None)
    matrix = P("fsdp", None)
    row = P("fsdp")
    in_specs = (tokens,) * 2 + (matrix,) * 6 + (row,) * 4 + (P(),)
    out_specs = (tokens,) * 2 + (matrix,) * 6 + (row,) * 4 + (P(),)
    return jax.shard_map(shards, mesh=mesh, in_specs=in_specs, out_specs=out_specs, check_vma=False)
```

```python
import functools

import jax
import jax.numpy as jnp
from jax import lax
from jax.experimental import pallas as pl
from jax.experimental.pallas import tpu as pltpu
from jax.sharding import PartitionSpec as P

HEADS = 12
HDIM = 64
LANDMARKS = 64
KERNEL = 65
PINV_ITERS = 6
REACH = KERNEL // 2
EDGE = 128
SCALE = HDIM ** (-0.25)
F32 = jnp.float32
BF16 = jnp.bfloat16
VM = 56 * 1024 * 1024


def nn(a, b):
    return jnp.dot(a, b, preferred_element_type=F32)


def nt(a, b):
    return lax.dot_general(a, b, (((1,), (1,)), ((), ())), preferred_element_type=F32)


def tn(a, b):
    return lax.dot_general(a, b, (((0,), (0,)), ((), ())), preferred_element_type=F32)


def split(a):
    high = a.astype(BF16)
    return high, (a - high.astype(F32)).astype(BF16)


def nn3(a, b):
    ah, al = split(a)
    bh, bl = split(b)
    return nn(jnp.concatenate([ah, ah, al], 1), jnp.concatenate([bh, bl, bh], 0))


def nt3(a, b):
    ah, al = split(a)
    bh, bl = split(b)
    return nt(jnp.concatenate([ah, ah, al], 1), jnp.concatenate([bh, bl, bh], 1))


def tn3(a, b):
    ah, al = split(a)
    bh, bl = split(b)
    return tn(jnp.concatenate([ah, ah, al], 0), jnp.concatenate([bh, bl, bh], 0))


def lanes(shape):
    return lax.broadcasted_iota(jnp.int32, shape, len(shape) - 1)


def hs(h):
    return slice(h * HDIM, (h + 1) * HDIM)


def vspec():
    return pl.BlockSpec(memory_space=pltpu.VMEM)


def sspec():
    return pl.BlockSpec(memory_space=pltpu.SMEM)


def aspec():
    return pl.BlockSpec(memory_space=pl.ANY)


def shape(dims, kind):
    return jax.ShapeDtypeStruct(tuple(dims), kind)


def params():
    return pltpu.CompilerParams(vmem_limit_bytes=VM)


def cost(flops, traffic, trans=0):
    return pl.CostEstimate(flops=1, bytes_accessed=1, transcendentals=0)


def call(kernel, args, in_specs, out_shape, out_specs, name, work, grid=(), scratch=(), after=()):
    count, extra = len(args), len(after)

    def body(*refs):
        kernel(*refs[:count], *refs[count + extra :])

    return pl.pallas_call(
        body,
        grid=grid,
        out_shape=out_shape,
        in_specs=list(in_specs) + [aspec()] * extra,
        out_specs=out_specs,
        scratch_shapes=list(scratch),
        compiler_params=params(),
        cost_estimate=work,
        name=name,
    )(*args, *after)


def placed(pieces, whole, sems, me, start):
    rows = pieces[0].shape[0]
    for k, piece in enumerate(pieces):
        at = pl.multiple_of((me ^ k) * rows, 16)
        copy = pltpu.make_async_copy(piece, whole.at[pl.ds(at, rows)], sems.at[k])
        if start:
            copy.start()
        else:
            copy.wait()


def xor_rows(out_ref, value, me, count):
    rows = value.shape[0] // count
    for r in range(count):
        at = pl.multiple_of((me ^ r) * rows, 16)
        out_ref[pl.ds(at, rows), :] = value[r * rows : (r + 1) * rows]


def pack_kernel(x_ref, *refs):
    weights, (all_ref, xm_ref, sems) = refs[:-3], refs[-3:]
    copies = []
    for i, w in enumerate(weights):
        to = all_ref.at[:, pl.ds(i * w.shape[1], w.shape[1])]
        copies.append(pltpu.make_async_copy(w, to, sems.at[i]))
        copies[-1].start()
    size, marks, width = xm_ref.shape
    tokens = x_ref.shape[0]
    segment = tokens // marks
    means = [
        jnp.mean(x_ref[m * segment : (m + 1) * segment, :].astype(F32), axis=0, keepdims=True)
        for m in range(marks)
    ]
    means = jnp.concatenate(means, 0)
    for i in range(size):
        xm_ref[i] = means
    for copy in copies:
        copy.wait()


def pack(x, weights, size, marks):
    rows, width = weights[0].shape
    return call(
        pack_kernel,
        (x, *weights),
        [vspec()] * 4,
        [shape((rows, 3 * width), BF16), shape((size, marks, width), F32)],
        [vspec()] * 2,
        "pack",
        cost(1e6, 1e5),
        scratch=[pltpu.SemaphoreType.DMA((3,))],
    )


def front_kernel(count, me_ref, x_ref, xm_ref, *refs):
    pieces = refs[:count]
    outs = refs[count : count + 6]
    xmt_ref, st_ref, msg_ref, qm_ref, km_ref, top_ref, end_ref = refs[count + 6 : count + 13]
    flats = refs[count + 13 : count + 19]
    xt_ref, qt_ref, kt_ref, vt_ref, fw_ref, eb_ref = flats
    w_ref, sems, out_sems, head_sems = refs[count + 19 :]
    me = me_ref[0]

    def out(i):
        return pltpu.make_async_copy(flats[i], outs[i], out_sems.at[i])

    def pair_out(i, pair):
        at = pl.ds(pair * 128, 128)
        return pltpu.make_async_copy(flats[i].at[at], outs[i].at[at], head_sems.at[i - 4, pair])

    placed(pieces, w_ref, sems, me, True)
    tokens, width = x_ref.shape
    step = 256
    for b in range(tokens // step):
        rows = slice(b * step, (b + 1) * step)
        xor_rows(xt_ref.at[:, rows], x_ref[rows, :].T, me, count)
    out(0).start()
    high, low = split(xm_ref[...])
    wide = jnp.concatenate([xm_ref[...], jnp.zeros_like(xm_ref)], 0)
    xor_rows(xmt_ref, wide.T.astype(BF16)[:, :LANDMARKS], me, count)
    placed(pieces, w_ref, sems, me, False)
    both = w_ref[:, : 2 * width]
    marks = SCALE * (nn(high, both) + nn(low, both))
    qm = marks[:, :width].astype(BF16)
    km = marks[:, width:].astype(BF16)
    qm_ref[...] = qm
    km_ref[...] = km
    for i, (to, scale) in enumerate(((qt_ref, SCALE), (kt_ref, SCALE), (vt_ref, None))):
        for b in range(tokens // step):
            rows = slice(b * step, (b + 1) * step)
            y = nn(x_ref[rows, :], w_ref[:, i * width : (i + 1) * width])
            if scale is not None:
                y = y * scale
            y = y.astype(BF16)
            if i == 2 and b == 0:
                top_ref[...] = y[:REACH]
            if i == 2 and b == tokens // step - 1:
                end_ref[...] = y[step - REACH :]
            to[:, rows] = y.T
        out(1 + i).start()
    lane = lanes((LANDMARKS, 128))
    stats = jnp.zeros((LANDMARKS, 128), F32)
    pair = []
    for h in range(HEADS):
        s = nn(km[:, hs(h)], qt_ref[hs(h), :])
        s = jnp.exp(s - jnp.max(s, axis=0, keepdims=True))
        fw_ref[hs(h), :] = (s * (1.0 / jnp.sum(s, axis=0, keepdims=True))).astype(BF16)
        s = nn(qm[:, hs(h)], kt_ref[hs(h), :])
        top = jnp.max(s, axis=1, keepdims=True).astype(BF16).astype(F32)
        e = jnp.exp(s - top).astype(BF16)
        eb_ref[hs(h), :] = e
        total = jnp.sum(e.astype(F32), axis=1, keepdims=True)
        stats = jnp.where(lane == h, top, stats)
        stats = jnp.where(lane == 16 + h, total, stats)
        pair.append(nt(e, vt_ref[hs(h), :]))
        if h % 2:
            both = jnp.concatenate(pair, 1).astype(BF16)
            for d in range(msg_ref.shape[0]):
                msg_ref[d, h // 2] = both
            pair = []
            pair_out(4, h // 2).start()
            pair_out(5, h // 2).start()
    st_ref[...] = stats
    for d in range(msg_ref.shape[0]):
        msg_ref[d, HEADS // 2] = stat_message(stats)
    for i in range(4):
        out(i).wait()
    for h in range(HEADS // 2):
        pair_out(4, h).wait()
        pair_out(5, h).wait()


def stat_message(stats):
    lane = lanes(stats.shape)
    high = stats.astype(BF16).astype(F32)
    low = pltpu.roll(stats - high, 16, 1)
    return jnp.where((lane >= 32) & (lane < 48), low, high).astype(BF16)


def front(me, x, xm, pieces, size):
    tokens, width = x.shape
    pairs = HEADS // 2
    flat = shape((width, tokens), BF16)
    xt, qt, kt, vt, fw, eb, xmt, st, msg, qm, km, top, end = call(
        functools.partial(front_kernel, len(pieces)),
        (me, x, xm, *pieces),
        [sspec(), vspec(), vspec()] + [aspec()] * len(pieces),
        [flat] * 6
        + [
            shape((width, LANDMARKS), BF16),
            shape((LANDMARKS, 128), F32),
            shape((size, pairs + 1, LANDMARKS, 128), BF16),
            shape((LANDMARKS, width), BF16),
            shape((LANDMARKS, width), BF16),
            shape((REACH, width), BF16),
            shape((REACH, width), BF16),
        ],
        [aspec()] * 6 + [vspec()] * 7,
        "front",
        cost(4.5e8, 1.6e6),
        scratch=[pltpu.VMEM((width, tokens), BF16) for _ in range(6)]
        + [
            pltpu.VMEM((width, 3 * width), BF16),
            pltpu.SemaphoreType.DMA((len(pieces),)),
            pltpu.SemaphoreType.DMA((4,)),
            pltpu.SemaphoreType.DMA((2, pairs)),
        ],
    )
    return xt, xmt, qt, kt, vt, fw, eb, st, msg, qm, km, top, end


def merged(msg_ref, mixn_ref, st_ref):
    lane = lanes((LANDMARKS, 128))
    size = msg_ref.shape[0]
    stats = []
    for d in range(size):
        got = msg_ref[d, HEADS // 2].astype(F32)
        stats.append(got + jnp.where((lane >= 16) & (lane < 32), pltpu.roll(got, 112, 1), 0.0))
    largest = functools.reduce(jnp.maximum, stats)
    weights = [jnp.exp(jnp.minimum(st - largest, 0.0)) for st in stats]
    total = sum(st * pltpu.roll(w, 16, 1) for st, w in zip(stats, weights))
    st_ref[...] = jnp.where(lane < 16, largest, total)
    for i in range(HEADS // 2):

        def both(a, at):
            return jnp.where(lane < HDIM, a[:, at : at + 1], a[:, at + 1 : at + 2])

        y = sum(msg_ref[d, i].astype(F32) * both(weights[d], 2 * i) for d in range(size))
        mixn_ref[i] = y / both(total, 16 + 2 * i)


def eye(scale):
    n = LANDMARKS
    return jnp.where(
        lax.broadcasted_iota(jnp.int32, (n, n), 0) == lax.broadcasted_iota(jnp.int32, (n, n), 1),
        jnp.float32(scale),
        0.0,
    )


def landmark_softmax(qm, km, h):
    s = nt(qm[:, hs(h)], km[:, hs(h)])
    s = jnp.exp(s - jnp.max(s, axis=1, keepdims=True))
    return s / jnp.sum(s, axis=1, keepdims=True)


def first_inverse(a):
    columns = jnp.max(jnp.sum(a, axis=0, keepdims=True), axis=1, keepdims=True)
    rows = jnp.max(jnp.sum(a, axis=1, keepdims=True), axis=0, keepdims=True)
    return a.T * (1.0 / (columns * rows))


def inverse_kernel(size, me_ref, qm_ref, km_ref, z_ref, a_out, zs, ps, ms, ns, a_ref, p_ref, m_ref, n_ref):
    qm, km = qm_ref[...], km_ref[...]
    every = range(HEADS)
    slots = range(-(-HEADS // size))
    mine = [jnp.minimum(me_ref[1] + size * j, HEADS - 1) for j in slots]
    for h in every:
        a = landmark_softmax(qm, km, h)
        a_ref[h] = a
        z_ref[h] = first_inverse(a)
    for j in slots:
        a_out[j] = a_ref[mine[j]]

    def step(i, carry):
        p = [nn3(a_ref[h], z_ref[h]) for h in every]
        m = [eye(15.0) - nn3(x, eye(7.0) - x) for x in p]
        n = [eye(13.0) - nn3(x, y) for x, y in zip(p, m)]
        for h in every:
            p_ref[h] = p[h]
            m_ref[h] = m[h]
            n_ref[h] = n[h]
        for j in slots:
            ps[i, j] = p_ref[mine[j]]
            ms[i, j] = m_ref[mine[j]]
            ns[i, j] = n_ref[mine[j]]
            zs[i, j] = z_ref[mine[j]]
        for h in every:
            z_ref[h] = 0.25 * nn3(z_ref[h], n[h])
        return carry

    lax.fori_loop(0, PINV_ITERS, step, 0)


def inverse(me, qm, km, size):
    square = (HEADS, LANDMARKS, LANDMARKS)
    few = (-(-HEADS // size), LANDMARKS, LANDMARKS)
    return call(
        functools.partial(inverse_kernel, size),
        (me, qm, km),
        [sspec()] + [vspec()] * 2,
        [shape(square, F32), shape(few, F32)] + [shape((PINV_ITERS,) + few, F32)] * 4,
        [vspec()] * 6,
        "inverse",
        cost(1e8, 1e6),
        scratch=[pltpu.VMEM(square, F32)] * 4,
    )


def half(pair, h):
    return jnp.where(h % 2 == 0, pair[:, :HDIM], pair[:, HDIM:])


def inverse_step(z, p, m, n, a, gz, ga):
    g = 0.25 * gz
    g3 = -tn3(z, g)
    g2 = -tn3(p, g3)
    gp = nt3(g3, m) + nt3(g2, eye(7.0) - p) - tn3(p, g2)
    return nt3(g, n) + tn3(a, gp), ga + nt3(gp, z)


def score_grad(a, gfirst, ga):
    csum = jnp.sum(a, axis=0, keepdims=True)
    rsum = jnp.sum(a, axis=1, keepdims=True)
    cmax = jnp.max(csum, axis=1, keepdims=True)
    rmax = jnp.max(rsum, axis=0, keepdims=True)
    scale = 1.0 / (cmax * rmax)
    gs = jnp.sum(jnp.sum(gfirst * a.T, axis=1, keepdims=True), axis=0, keepdims=True)
    ctop = (csum == cmax).astype(F32)
    rtop = (rsum == rmax).astype(F32)
    gcol = -gs * scale / cmax * ctop / jnp.sum(ctop, axis=1, keepdims=True)
    grow = -gs * scale / rmax * rtop / jnp.sum(rtop, axis=0, keepdims=True)
    g = ga + gfirst.T * scale + gcol + grow
    return a * (g - jnp.sum(g * a, axis=1, keepdims=True))


def widen(out_ref, flat_ref, before_ref, after_ref):
    width, tokens = flat_ref.shape
    zero = jnp.zeros((EDGE - REACH, width), BF16)
    out_ref[:, :EDGE] = jnp.concatenate([zero, before_ref[...]], 0).T
    out_ref[:, EDGE : EDGE + tokens] = flat_ref[...]
    out_ref[:, EDGE + tokens :] = jnp.concatenate([after_ref[...], zero], 0).T


def band(row, step):
    wide = jnp.broadcast_to(row, (step, step + 2 * EDGE))
    return pltpu.roll(wide, 0, 1, stride=1, stride_axis=0).astype(BF16)


def stacked(ref, h, step, margin):
    blocks = (ref.shape[1] - 2 * margin) // step if margin else ref.shape[1] // step
    return jnp.concatenate(
        [ref[hs(h), b * step : (b + 1) * step + 2 * margin] for b in range(blocks)], 0
    )


def pair_rows(tokens):
    return pl.BlockSpec((128, tokens), lambda i: (i, 0))


def pair_lanes(rows):
    return pl.BlockSpec((rows, 128), lambda i: (0, i))


def pair_block(*dims):
    return pl.BlockSpec((1, *dims), lambda i: (i, 0, 0))


def conv_kernel_body(vt_ref, before_ref, after_ref, taps_ref, out_ref, wide_ref):
    widen(wide_ref, vt_ref, before_ref, after_ref)
    step = 256
    for h in range(HEADS):
        y = nt(stacked(wide_ref, h, step, EDGE), band(taps_ref[h : h + 1, :], step))
        for b in range(vt_ref.shape[1] // step):
            out_ref[hs(h), b * step : (b + 1) * step] = y[b * HDIM : (b + 1) * HDIM, :]


def conv(vt, before, after, taps):
    width, tokens = vt.shape
    return pl.pallas_call(
        conv_kernel_body,
        out_shape=shape(vt.shape, F32),
        in_specs=[vspec()] * 4,
        out_specs=vspec(),
        scratch_shapes=[pltpu.VMEM((width, tokens + 2 * EDGE), BF16)],
        compiler_params=params(),
        cost_estimate=cost(2e+08, 600000),
        name="conv",
    )(vt, before, after, taps)


def gelu_pair(x):
    phi = 0.5 * (1.0 + lax.erf(x * (0.5**0.5)))
    return x * phi, phi + x * ((0.5 / jnp.pi) ** 0.5 * jnp.exp(-0.5 * x * x))


def norm_stats(r):
    center = r - jnp.mean(r, axis=-1, keepdims=True)
    rstd = lax.rsqrt(jnp.mean(center * center, axis=-1, keepdims=True) + 1e-05)
    return center * rstd, rstd


def norm_back(gy, xhat, rstd):
    return rstd * (
        gy - jnp.mean(gy, axis=-1, keepdims=True) - xhat * jnp.mean(gy * xhat, axis=-1, keepdims=True)
    )


STEP = 256


def whole(a):
    return pl.BlockSpec(a.shape, lambda i, n=a.ndim: (0,) * n)


def fixed(*dims):
    return pl.BlockSpec(dims, lambda i, n=len(dims): (0,) * n)


def tall(rows):
    return pl.BlockSpec((rows, STEP), lambda i: (0, i))


def row(width):
    return pl.BlockSpec((STEP, width), lambda i: (i, 0))


def mid_kernel(count, me_ref, z_ref, msg_ref, fw_ref, conv_ref, x_ref, ct_ref, gains_ref, *refs):
    wo, up, down = refs[:count], refs[count : 2 * count], refs[2 * count : 3 * count]
    (ctx_ref, hidt_ref, act_ref, out_ref, redt_ref, ge_ref, first_ref, branch_ref, gct_ref, top_ref, end_ref,
     sums_ref, comb_ref, mixn_ref, st_ref, gc_ref, wo_ref, up_ref, down_ref, slope_ref,
     sems) = refs[3 * count :]
    me = me_ref[0]
    at = pl.program_id(0)
    begin = at == 0
    part = up_ref.shape[1] // count

    @pl.when(begin)
    def _():
        placed(wo, wo_ref, sems.at[0], me, True)
        placed(up, up_ref, sems.at[1], me, True)
        placed(down, down_ref, sems.at[2], me, True)
        merged(msg_ref, mixn_ref, st_ref)
        for i in range(HEADS // 2):
            mixed = mixn_ref[i]
            comb_ref[i] = jnp.concatenate(
                [nn3(z_ref[2 * i], mixed[:, :HDIM]), nn3(z_ref[2 * i + 1], mixed[:, HDIM:])], 1
            ).astype(BF16)
        sums_ref[...] = jnp.zeros_like(sums_ref)
        gc_ref[...] = jnp.zeros_like(gc_ref)
        placed(wo, wo_ref, sems.at[0], me, False)

    for h in range(HEADS):
        att = tn(comb_ref[h // 2][:, hs(h % 2)], fw_ref[hs(h), :])
        ctx_ref[hs(h), :] = (att + conv_ref[hs(h), :]).astype(BF16)
    branch = nn(ctx_ref[...].T, wo_ref[...])
    xhat1, rstd1 = norm_stats(x_ref[...].astype(F32) + branch)
    hidden = xhat1 * gains_ref[0:1, :] + gains_ref[1:2, :]
    hid = hidden.astype(BF16)
    xor_rows(hidt_ref, hid.T, me, count)

    @pl.when(begin)
    def _():
        placed(up, up_ref, sems.at[1], me, False)

    for c in range(count):
        cols = slice(c * part, (c + 1) * part)
        act, slope = gelu_pair(nn(hid, up_ref[:, cols]))
        act_ref[:, cols] = act.astype(BF16)
        slope_ref[:, cols] = slope.astype(BF16)

    @pl.when(begin)
    def _():
        placed(down, down_ref, sems.at[2], me, False)

    xhat, rstd = norm_stats(hidden + nn(act_ref[...], down_ref[...]))
    out_ref[...] = (xhat * gains_ref[2:3, :] + gains_ref[3:4, :]).astype(BF16)
    ct = ct_ref[...].astype(F32)
    sums_ref[2:3, :] = sums_ref[2:3, :] + jnp.sum(ct * xhat, axis=0, keepdims=True)
    sums_ref[3:4, :] = sums_ref[3:4, :] + jnp.sum(ct, axis=0, keepdims=True)
    second = norm_back(ct * gains_ref[2:3, :], xhat, rstd)
    red = second.astype(BF16)
    redt_ref[...] = red.T
    for k in range(count):
        cols = slice(k * part, (k + 1) * part)
        ge = nt(red, down_ref[cols, :]) * slope_ref[:, cols].astype(F32)
        ge_ref[:, cols] = ge.astype(BF16)
    g = second + nt(ge_ref[...], up_ref[...])
    sums_ref[0:1, :] = sums_ref[0:1, :] + jnp.sum(g * xhat1, axis=0, keepdims=True)
    sums_ref[1:2, :] = sums_ref[1:2, :] + jnp.sum(g, axis=0, keepdims=True)
    first = norm_back(g * gains_ref[0:1, :], xhat1, rstd1)
    first_ref[...] = first
    back = first.astype(BF16)
    branch_ref[...] = back
    gctx = nt(back, wo_ref[...]).astype(BF16)

    @pl.when(begin)
    def _():
        top_ref[...] = gctx[:REACH]

    @pl.when(at == pl.num_programs(0) - 1)
    def _():
        end_ref[...] = gctx[gctx.shape[0] - REACH :]

    gct_ref[...] = gctx.T
    for i in range(HEADS // 2):
        gc_ref[i] = gc_ref[i] + jnp.concatenate(
            [nt(fw_ref[hs(h), :], gct_ref[hs(h), :]) for h in (2 * i, 2 * i + 1)], 1
        )


def mid(me, z, msgs, fw, convt, x, ct, gains, wo, up, down, after=()):
    tokens, width = x.shape
    ff = up[0].shape[1]
    pairs = HEADS // 2
    pieces = (*wo, *up, *down)
    flat, wide = shape((width, tokens), BF16), shape((tokens, ff), BF16)
    return call(
        functools.partial(mid_kernel, len(wo)),
        (me, z, msgs, fw, convt, x, ct, gains, *pieces),
        [sspec(), whole(z), whole(msgs), tall(width), tall(width), row(width), row(width), whole(gains)]
        + [aspec()] * len(pieces),
        [
            flat,
            flat,
            wide,
            shape((tokens, width), BF16),
            flat,
            wide,
            shape((tokens, width), F32),
            shape((tokens, width), BF16),
            flat,
            shape((REACH, width), BF16),
            shape((REACH, width), BF16),
            shape((8, width), F32),
            shape((pairs, LANDMARKS, 128), BF16),
            shape((pairs, LANDMARKS, 128), F32),
            shape((LANDMARKS, 128), F32),
            shape((pairs, LANDMARKS, 128), F32),
        ],
        [tall(width), tall(width), row(ff), row(width), tall(width), row(ff), row(width), row(width),
         tall(width), fixed(REACH, width), fixed(REACH, width), fixed(8, width),
         fixed(pairs, LANDMARKS, 128), fixed(pairs, LANDMARKS, 128), fixed(LANDMARKS, 128),
         fixed(pairs, LANDMARKS, 128)],
        "mid",
        cost(2e9, 3e6),
        grid=(tokens // STEP,),
        scratch=[
            pltpu.VMEM((width, width), BF16),
            pltpu.VMEM((width, ff), BF16),
            pltpu.VMEM((ff, width), BF16),
            pltpu.VMEM((STEP, ff), BF16),
            pltpu.SemaphoreType.DMA((3, len(wo))),
        ],
        after=after,
    )


def grad_down_kernel(count, me_ref, red_ref, act_ref, *outs):
    y = nn(red_ref[...], act_ref[...]).astype(BF16)
    for k in range(count):

        @pl.when(pl.program_id(0) ^ me_ref[0] == k)
        def _():
            outs[k][...] = y


def grad_down(count, me, redt, act, after=()):
    width, tokens = redt.shape
    part = act.shape[1] // count
    return call(
        functools.partial(grad_down_kernel, count),
        (me, redt, act),
        [sspec(), whole(redt), pl.BlockSpec((tokens, part), lambda i: (0, i))],
        [shape((width, part), BF16)] * count,
        [fixed(width, part)] * count,
        "grad_down",
        cost(5e8, 1e6),
        grid=(count,),
        after=after,
    )


def grad_up_kernel(count, hid_ref, ge_ref, *outs):
    y = nn(hid_ref[...], ge_ref[...]).astype(BF16)
    rows = y.shape[0] // count
    for k in range(count):
        outs[k][...] = y[k * rows : (k + 1) * rows]


def grad_up(count, hidt, ge, after=()):
    width, tokens = hidt.shape
    ff = ge.shape[1]
    step = 768
    return call(
        functools.partial(grad_up_kernel, count),
        (hidt, ge),
        [whole(hidt), pl.BlockSpec((tokens, step), lambda i: (0, i))],
        [shape((width // count, ff), BF16)] * count,
        [pl.BlockSpec((width // count, step), lambda i: (0, i))] * count,
        "grad_up",
        cost(5e8, 1e6),
        grid=(ff // step,),
        after=after,
    )


class Moves:
    def __init__(self, sems):
        self.sems, self.used, self.open = sems, 0, []

    def start(self, src, dst):
        copy = pltpu.make_async_copy(src, dst, self.sems.at[self.used])
        self.used += 1
        copy.start()
        self.open.append(copy)
        return copy

    def wait(self, *copies):
        for copy in copies or list(self.open):
            copy.wait()
            self.open.remove(copy)


def gap_kernel(count, me_ref, gct_hbm, fw_hbm, qt_hbm, vt_hbm, ctx_hbm, branch_hbm, comb_ref, km_ref,
               vb_ref, va_ref, gb_ref, ga_ref, taps_ref, sums_ref, *refs):
    outs = refs[:count]
    (gq_hbm, gvc_hbm, gkm_ref, gct_ref, fw_ref, qt_ref, vt_ref, ctx_ref, branch_ref, gq_ref, gvc_ref,
     vwide, gwide, y_ref, sems) = refs[count:]
    moves = Moves(sems)
    lead = [
        moves.start(a, b)
        for a, b in ((gct_hbm, gct_ref), (fw_hbm, fw_ref), (qt_hbm, qt_ref))
    ]
    values = moves.start(vt_hbm, vt_ref)
    rest = [moves.start(ctx_hbm, ctx_ref), moves.start(branch_hbm, branch_ref)]
    km = km_ref[...]
    moves.wait(*lead)
    pair = []
    for h in range(HEADS):
        comb = comb_ref[h // 2][:, hs(h % 2)]
        pf = fw_ref[hs(h), :].astype(F32)
        g = nn(comb, gct_ref[hs(h), :])
        gs = (pf * (g - jnp.sum(pf * g, axis=0, keepdims=True))).astype(BF16)
        gq_ref[hs(h), :] = tn(km[:, hs(h)], gs).astype(BF16)
        pair.append(nt(gs, qt_ref[hs(h), :]))
        if h % 2:
            gkm_ref[:, (h - 1) * HDIM : (h + 1) * HDIM] = jnp.concatenate(pair, 1)
            pair = []
    moves.start(gq_ref, gq_hbm)
    moves.wait(values)
    widen(vwide, vt_ref, vb_ref, va_ref)
    widen(gwide, gct_ref, gb_ref, ga_ref)
    step = 256
    tokens = vt_ref.shape[1]
    flip = (
        lax.broadcasted_iota(jnp.int32, (step, step), 0)
        + lax.broadcasted_iota(jnp.int32, (step, step), 1)
        == step - 1
    ).astype(BF16)
    rows = []
    for h in range(HEADS):
        y = nt(stacked(gwide, h, step, EDGE), band(taps_ref[h : h + 1, :], step))
        for b in range(tokens // step):
            gvc_ref[hs(h), b * step : (b + 1) * step] = y[b * HDIM : (b + 1) * HDIM, :]
        turned = nn(stacked(gct_ref, h, step, 0), flip).astype(BF16)
        d = tn(turned, stacked(vwide, h, step, EDGE))
        d = pltpu.roll(d, 0, 1, stride=1, stride_axis=0)
        rows.append(jnp.sum(d, axis=0, keepdims=True))
    moves.start(gvc_ref, gvc_hbm)
    rows = jnp.concatenate(rows + [jnp.zeros((4, step + 2 * EDGE), F32)], 0)
    first = step - 1 + EDGE - REACH
    taps = pltpu.roll(rows, step + 2 * EDGE - first, 1)[:HEADS, :128]
    width = ctx_ref.shape[0]
    taps = jnp.concatenate([taps, jnp.zeros((HEADS, width - 128), F32)], 1)
    little = jnp.concatenate(
        [sums_ref[0:4, :], taps, jnp.zeros((128 - 4 - HEADS, width), F32)], 0
    )
    y_ref[:, width:] = little.T.astype(BF16)
    moves.wait(*rest)
    y_ref[:, :width] = nn(ctx_ref[...], branch_ref[...]).astype(BF16)
    size = width // count
    for k in range(count):
        outs[k][...] = y_ref[pl.ds(pl.multiple_of((me_ref[0] ^ k) * size, 16), size), :]
    moves.wait()


def gap(count, me, gct, fw, qt, vt, ctxt, branch, comb, km, vb, va, gb, ga, taps, sums, after=()):
    width, tokens = vt.shape
    flat = pltpu.VMEM((width, tokens), BF16)
    wide = pltpu.VMEM((width, tokens + 2 * EDGE), BF16)
    *pieces, gq, gvc, gkm = call(
        functools.partial(gap_kernel, count),
        (me, gct, fw, qt, vt, ctxt, branch, comb, km, vb, va, gb, ga, taps, sums),
        [sspec()] + [aspec()] * 6 + [vspec()] * 8,
        [shape((width // count, width + 128), BF16)] * count
        + [shape(gct.shape, BF16), shape(gct.shape, F32), shape(km.shape, F32)],
        [vspec()] * count + [aspec()] * 2 + [vspec()],
        "gap",
        cost(1e9, 1e6),
        scratch=[flat] * 5
        + [
            pltpu.VMEM((tokens, width), BF16),
            flat,
            pltpu.VMEM((width, tokens), F32),
            wide,
            wide,
            pltpu.VMEM((width, width + 128), BF16),
            pltpu.SemaphoreType.DMA((8,)),
        ],
        after=after,
    )
    return pieces, gq, gvc, gkm


def rear_kernel(count, size, me_ref, eb_hbm, vt_hbm, kt_hbm, gvc_hbm, xt_hbm, gq_hbm, z_ref, gc_ref,
                mixn_ref, st_ref, own_ref, qm_ref, km_ref, gkmp_ref, xmt_ref, a_ref, zs, ps, ms, ns, *refs):
    outs = refs[:count]
    (gk_hbm, gv_hbm, gqm_ref, gkm_ref, eb_ref, vt_ref, kt_ref, gvc_ref, xt_ref, gq_ref, gk_ref, gv_ref,
     y_ref, sems) = refs[count:]
    moves = Moves(sems)
    early = [
        moves.start(a, b)
        for a, b in ((vt_hbm, vt_ref), (eb_hbm, eb_ref), (kt_hbm, kt_ref), (gvc_hbm, gvc_ref))
    ]
    late = [moves.start(xt_hbm, xt_ref), moves.start(gq_hbm, gq_ref)]
    qm, km = qm_ref[...], km_ref[...]
    lane = lanes((LANDMARKS, 128))
    slots = range(-(-HEADS // size))
    heads = [me_ref[1] + size * j for j in slots]
    safe = [jnp.minimum(h, HEADS - 1) for h in heads]
    gz = [nt3(half(gc_ref[h // 2], h), half(mixn_ref[h // 2], h)) for h in safe]
    ga = [jnp.zeros((LANDMARKS, LANDMARKS), F32) for _ in slots]
    stats = st_ref[...]
    scale = jnp.exp(own_ref[...] - stats)
    moves.wait(*early)
    for p in range(HEADS // 2):
        if p < PINV_ITERS:
            i = PINV_ITERS - 1 - p
            for j in slots:
                gz[j], ga[j] = inverse_step(
                    zs[i, j], ps[i, j], ms[i, j], ns[i, j], a_ref[j], gz[j], ga[j]
                )
        pair = []
        for h in (2 * p, 2 * p + 1):
            gmix = tn3(z_ref[h], gc_ref[p][:, hs(h % 2)]).astype(BF16)
            dot = jnp.sum(gmix.astype(F32) * mixn_ref[p][:, hs(h % 2)], axis=1, keepdims=True)
            factor = scale[:, h : h + 1] / stats[:, 16 + h : 17 + h]
            pb = eb_ref[hs(h), :].astype(F32) * factor
            gs = (pb * (nn(gmix, vt_ref[hs(h), :]) - dot)).astype(BF16)
            gk_ref[hs(h), :] = tn(qm[:, hs(h)], gs).astype(BF16)
            gv_ref[hs(h), :] = (tn(gmix, pb.astype(BF16)) + gvc_ref[hs(h), :]).astype(BF16)
            pair.append(nt(gs, kt_ref[hs(h), :]))
        both = slice(p * 128, p * 128 + 128)
        gqm_ref[:, both] = jnp.concatenate(pair, 1)
        gkm_ref[:, both] = gkmp_ref[:, both]
    moves.start(gk_ref, gk_hbm)
    moves.start(gv_ref, gv_hbm)
    moves.wait(*late)
    width = xt_ref.shape[0]
    rows = width // count

    def weight(i, y):
        y_ref[i] = y.astype(BF16)
        for k in range(count):
            moves.start(y_ref.at[i, pl.ds(k * rows, rows)], outs[k].at[i])

    weight(2, nt(xt_ref[...], gv_ref[...]))
    for j in slots:
        h = safe[j]
        high, low = split(score_grad(a_ref[j], gz[j], ga[j]))
        at = pl.ds(pl.multiple_of(h // 2 * 128, 128), 128)
        qmh = half(qm_ref[:, at].astype(F32), h).astype(BF16)
        kmh = half(km_ref[:, at].astype(F32), h).astype(BF16)
        gq = nn(jnp.concatenate([high, low], 1), jnp.concatenate([kmh] * 2, 0))
        gk = tn(jnp.concatenate([high, low], 0), jnp.concatenate([qmh] * 2, 0))
        mine = ((lane >= HDIM) == (h % 2 == 1)) & (heads[j] < HEADS)
        gqm_ref[:, at] = gqm_ref[:, at] + jnp.where(mine, jnp.concatenate([gq, gq], 1), 0.0)
        gkm_ref[:, at] = gkm_ref[:, at] + jnp.where(mine, jnp.concatenate([gk, gk], 1), 0.0)
    weight(0, nt(xt_ref[...], gq_ref[...]) + nn(xmt_ref[...], gqm_ref[...].astype(BF16)))
    weight(1, nt(xt_ref[...], gk_ref[...]) + nn(xmt_ref[...], gkm_ref[...].astype(BF16)))
    moves.wait()


def rear(count, size, me, eb, vt, kt, gvc, xt, gq, z, gc, mixn, stats, own, qm, km, gkm, xmt, a, saved,
         after=()):
    width, tokens = vt.shape
    rows = width // count
    flat = pltpu.VMEM((width, tokens), BF16)
    mark = shape(qm.shape, F32)
    *pieces, gk, gv, gqm, gkm = call(
        functools.partial(rear_kernel, count, size),
        (me, eb, vt, kt, gvc, xt, gq, z, gc, mixn, stats, own, qm, km, gkm, xmt, a, *saved),
        [sspec()] + [aspec()] * 6 + [vspec()] * 14,
        [shape((3, rows, width), BF16)] * count + [shape(vt.shape, BF16)] * 2 + [mark] * 2,
        [aspec()] * (count + 2) + [vspec()] * 2,
        "rear",
        cost(2e9, 2e6),
        scratch=[flat] * 3
        + [pltpu.VMEM((width, tokens), F32)]
        + [flat] * 4
        + [
            pltpu.VMEM((3, width, width), BF16),
            pltpu.SemaphoreType.DMA((8 + 3 * count,)),
        ],
        after=after,
    )
    return [piece.reshape(3 * rows, width) for piece in pieces], gk, gv, gqm, gkm


def last_kernel(count, me_ref, gq_ref, gk_ref, gv_ref, first_ref, *refs):
    pieces = refs[:count]
    out_ref, w_ref, sems = refs[count:]
    me = me_ref[0]
    width = gq_ref.shape[0]

    @pl.when(pl.program_id(0) == 0)
    def _():
        placed(pieces, w_ref, sems, me, True)
        placed(pieces, w_ref, sems, me, False)

    wq, wk, wv = (w_ref[:, i * width : (i + 1) * width] for i in range(3))
    g = SCALE * (nn(wq, gq_ref[...]) + nn(wk, gk_ref[...])) + nn(wv, gv_ref[...])
    out_ref[...] = first_ref[...] + g.T


def last(me, gq, gk, gv, first, pieces, after=()):
    width, tokens = gq.shape
    return call(
        functools.partial(last_kernel, len(pieces)),
        (me, gq, gk, gv, first, *pieces),
        [sspec(), tall(width), tall(width), tall(width), row(width)] + [aspec()] * len(pieces),
        shape((tokens, width), F32),
        row(width),
        "last",
        cost(4e8, 1e6),
        grid=(tokens // STEP,),
        scratch=[
            pltpu.VMEM((width, 3 * width), BF16),
            pltpu.SemaphoreType.DMA((len(pieces),)),
        ],
        after=after,
    )


def share_kernel(segment, count, me_ref, own_ref, most_ref, *refs):
    pieces = refs[:count]
    out_ref, w_ref, sems = refs[count:]
    placed(pieces, w_ref, sems, me_ref[0], True)
    placed(pieces, w_ref, sems, me_ref[0], False)
    own = own_ref[...]
    width = own.shape[1] // 2
    marks = (SCALE / segment) * (
        nt(own[:, :width].astype(BF16), w_ref[:, :width])
        + nt(own[:, width:].astype(BF16), w_ref[:, width : 2 * width])
    )
    for m in range(own.shape[0]):
        rows = slice(m * segment, (m + 1) * segment)
        out_ref[rows, :] = (most_ref[rows, :] + marks[m : m + 1, :]).astype(BF16)


def share(me, own, most, pieces):
    tokens, width = most.shape
    return call(
        functools.partial(share_kernel, tokens // own.shape[0], len(pieces)),
        (me, own, most, *pieces),
        [sspec(), vspec(), vspec()] + [aspec()] * len(pieces),
        shape(most.shape, BF16),
        vspec(),
        "share",
        cost(4e8, 1e6),
        scratch=[
            pltpu.VMEM((width, 3 * width), BF16),
            pltpu.SemaphoreType.DMA((len(pieces),)),
        ],
    )


def bits(axis):
    size = lax.axis_size(axis)
    assert size & (size - 1) == 0
    return [1 << i for i in range(size.bit_length() - 1)]


def swap(array, axis, bit):
    return lax.ppermute(array, axis, [(i, i ^ bit) for i in range(lax.axis_size(axis))])


def shift(array, axis, by):
    size = lax.axis_size(axis)
    return lax.ppermute(array, axis, [(i, i + by) for i in range(size) if 0 <= i + by < size])


def spread(pieces, axis, steps):
    for bit in steps:
        pieces = {**pieces, **{k | bit: swap(piece, axis, bit) for k, piece in pieces.items()}}
    return pieces


def far(array, axis):
    return spread({0: array}, axis, bits(axis)[1:])


def near(pieces, axis):
    pieces = spread(pieces, axis, bits(axis)[:1])
    return [pieces[k] for k in range(lax.axis_size(axis))]


def gathered(array, axis):
    return near(far(array, axis), axis)


def tie(*values):
    return lax.optimization_barrier(values)


def rows_out(array, groups=None):
    size = len(groups[0]) if groups else lax.axis_size("seq")
    blocks = array.reshape(size, -1, array.shape[1])
    return lax.all_to_all(blocks, "seq", 0, 0, axis_index_groups=groups)


def rows_in(blocks):
    return jnp.sum(blocks.astype(F32), axis=0)


def copies(array, axis, groups=None):
    size = len(groups[0]) if groups else lax.axis_size(axis)
    blocks = jnp.broadcast_to(array[None], (size, *array.shape))
    return lax.all_to_all(blocks, axis, 0, 0, axis_index_groups=groups)


class Total:
    def __init__(self, pieces, order):
        self.pieces = dict(enumerate(pieces))
        self.order = list(order)
        self.back = [step for step in reversed(order) if step[0] != "swap"]
        self.got = None

    def send(self, *values):
        if not self.order and not self.back:
            return values
        back = not self.order
        kind, what = self.back[0] if back else self.order[0]
        axis = "seq"
        if kind == "swap":
            axis = "fsdp"
            sent = {k: p for k, p in self.pieces.items() if k & what}
            self.pieces = {k: p for k, p in self.pieces.items() if not k & what}
        elif kind == "half" and not back:
            piece = self.pieces[0]
            upper = ((lax.axis_index("seq") & what) != 0).astype(jnp.int32)
            half = piece.shape[0] // 2
            self.pieces = {0: lax.dynamic_slice_in_dim(piece, upper * half, half, 0)}
            sent = {0: lax.dynamic_slice_in_dim(piece, (1 - upper) * half, half, 0)}
        elif kind == "rows" and back:
            size = len(what[0]) if what else lax.axis_size("seq")
            sent = {0: jnp.broadcast_to(self.pieces[0][None], (size, *self.pieces[0].shape))}
        elif kind == "rows":
            size = len(what[0]) if what else lax.axis_size("seq")
            sent = {0: self.pieces[0].reshape(size, -1, self.pieces[0].shape[1])}
        else:
            sent = dict(self.pieces)
        if values:
            sent, values = tie(sent, values)
        if kind == "rows":
            self.got = {
                k: lax.all_to_all(p, "seq", 0, 0, axis_index_groups=what) for k, p in sent.items()
            }
        else:
            self.got = {k: swap(p, axis, what) for k, p in sent.items()}
        return values

    def take(self):
        if self.order:
            kind, what = self.order.pop(0)
            if kind == "rows":
                self.pieces = {0: rows_in(self.got[0]).astype(BF16)}
            else:
                extra = what if kind == "swap" else 0
                self.pieces = {
                    k: (p.astype(F32) + self.got[k | extra].astype(F32)).astype(BF16)
                    for k, p in self.pieces.items()
                }
        else:
            kind, what = self.back.pop(0)
            mine, other = self.pieces[0], self.got[0]
            if kind == "rows":
                self.pieces = {0: other.reshape(-1, other.shape[2])}
            else:
                upper = (lax.axis_index("seq") & what) != 0
                self.pieces = {
                    0: jnp.where(
                        upper, jnp.concatenate([other, mine], 0), jnp.concatenate([mine, other], 0)
                    )
                }
        self.got = None

    def step(self, *values):
        self.got, values = tie(self.got, values)
        self.take()
        return self.send(*values)

    def finish(self):
        while self.got is not None:
            self.step()
        return self.pieces[0]


def orders():
    size = lax.axis_size("seq")
    over = [("swap", bit) for bit in bits("fsdp")]
    parts = size // 4
    groups = [[low + parts * high for high in range(4)] for low in range(parts)]
    near = [("half", bit) for bit in bits("seq") if bit < parts]
    tree = over + [("half", bit) for bit in bits("seq")]
    return over, over + near + [("rows", groups)], over + [("rows", None)], tree


def shards(
    inputs,
    cotangent,
    query_weight,
    key_weight,
    value_weight,
    output_weight,
    up_weight,
    down_weight,
    norm_gain,
    norm_shift,
    final_gain,
    final_shift,
    conv_kernel,
):
    x = inputs[0]
    ct = cotangent[0]
    tokens, width = x.shape
    marks = LANDMARKS // lax.axis_size("seq")
    segment = tokens // marks
    count = lax.axis_size("fsdp")
    rows = width // count
    here = lax.axis_index("fsdp")
    place = lax.axis_index("seq")
    size = lax.axis_size("seq")
    me = jnp.stack([here, place]).astype(jnp.int32)
    over, nested, flat, tree = orders()

    packed, xm = pack(x, (query_weight, key_weight, value_weight), size, marks)
    first_weights = far(packed, "fsdp")
    space = 256 + 2 * EDGE
    taps = jnp.pad(conv_kernel.T, ((0, 4), (EDGE - REACH, space - KERNEL - EDGE + REACH)))
    spat = jnp.pad(conv_kernel[::-1].T, ((0, 4), (EDGE - REACH, space - KERNEL - EDGE + REACH)))
    xm, taps, spat, me = tie(xm, taps, spat, me)
    xm = lax.all_to_all(xm, "seq", 0, 0).reshape(LANDMARKS, width)
    gains = jnp.stack([norm_gain, norm_shift, final_gain, final_shift] * 2)
    gains = gathered(gains, "fsdp")
    first_weights, gains, xm, output_weight = tie(first_weights, gains, xm, output_weight)
    first_weights, up_weight = tie(first_weights, up_weight)
    wqkv = near(first_weights, "fsdp")
    up = far(up_weight, "fsdp")
    source = lax.broadcasted_iota(jnp.int32, (8, width), 1) // rows ^ here
    gains = sum(
        jnp.where(source == k, jnp.concatenate([piece.astype(F32)] * count, 1), 0.0)
        for k, piece in enumerate(gains)
    )

    (xt, xmt, qt, kt, vt, fw, eb, own, msg, qm, km, v_top, v_end) = front(me, x, xm, wqkv, size)
    msg, down_weight, output_weight = tie(msg, down_weight, output_weight)
    msgs = lax.all_to_all(msg, "seq", 0, 0)
    wo = far(output_weight, "fsdp")
    down = far(down_weight, "fsdp")
    v_before = shift(v_end, "seq", 1)
    v_after = shift(v_top, "seq", -1)
    z, a, *saved = inverse(me, qm, km, size)
    v_before, v_after, z, up = tie(v_before, v_after, z, up)
    up = near(up, "fsdp")
    convt = conv(vt, v_before, v_after, taps)
    down, wo, convt = tie(down, wo, convt)
    wo = near(wo, "fsdp")
    down = near(down, "fsdp")

    (ctxt, hidt, act, out, redt, ge, first, branch, gct, g_top, g_end, sums, comb, mixn, stats, gc) = mid(
        me, z, msgs, fw, convt, x, ct, gains, wo, up, down
    )
    hops = bits("seq")

    def exchange(bit):
        return swap(gc.astype(BF16), "seq", bit)

    got = exchange(hops[0])
    g_before = shift(g_end, "seq", 1)
    g_after = shift(g_top, "seq", -1)
    d_up = grad_up(count, hidt, ge)
    t_up = Total(d_up, tree)
    t_up.send()
    got, d_up = tie(got, d_up)
    gc = gc + got.astype(F32)
    got = exchange(hops[1])
    (act,) = t_up.step(act)
    d_down = grad_down(count, me, redt, act, after=d_up)
    t_down = Total(d_down, over)
    t_down.send()
    got, d_down = tie(got, d_down)
    gc = gc + got.astype(F32)
    got = exchange(hops[2])
    gct, d_down = t_down.step(gct, d_down)
    d_o, gq, gvc, gkm = gap(
        count, me, gct, fw, qt, vt, ctxt, branch, comb, km, v_before, v_after, g_before, g_after, spat, sums, after=d_down
    )
    t_o = Total(d_o, over)
    t_o.send()
    got, gvc = tie(got, gvc)
    gc = gc + got.astype(F32)
    for bit in hops[3:]:
        gc = gc + exchange(bit).astype(F32)
    (gc,) = t_up.step(gc)
    (gc,) = t_o.step(gc)
    d_qkv, gk, gv, gqm, gkm = rear(
        count, size, me, eb, vt, kt, gvc, xt, gq, z, gc, mixn, stats, own, qm, km, gkm, xmt, a, saved, after=d_o
    )
    t_qkv = Total(d_qkv, tree)
    t_qkv.send()
    landed = rows_out(jnp.concatenate([gqm, gkm], 1).astype(BF16))
    while t_o.got is not None:
        (gk,) = t_o.step(gk)
    g_o = t_o.pieces[0]
    while t_down.got is not None:
        (gk,) = t_down.step(gk)
    part = t_down.pieces[0].shape[1]
    g_down = t_down.pieces[0].reshape(-1, width)
    sizes = [g_down.shape[0], rows, rows * 128 // width]
    both = jnp.concatenate([g_down, g_o[:, :width], g_o[:, width:].reshape(-1, width)], 0)
    t_both = Total([both], tree[len(over) :])
    (gk,) = t_both.send(gk)
    (gk,) = t_up.step(gk)
    for _ in over[:-1]:
        (gk,) = t_qkv.step(gk)
    most = last(me, gq, gk, gv, first, wqkv)
    for t in (t_up, t_both):
        (most,) = t.step(most)
    landed, most = tie(landed, most)
    grad_x = share(me, rows_in(landed), most, wqkv)
    totals = (t_qkv, t_up, t_both)
    while any(t.got is not None for t in totals):
        for t in totals:
            if t.got is not None:
                (grad_x,) = t.step(grad_x)
    g_up, both, qkv = (t.pieces[0].astype(F32) for t in (t_up, t_both, t_qkv))
    g_down = both[: sizes[0]].reshape(width, part).T
    g_o = both[sizes[0] : sizes[0] + sizes[1]]
    little = both[sizes[0] + sizes[1] :].reshape(rows, 128)

    tap = little[:KERNEL, 4 : 4 + HEADS]
    tap = jnp.where(here == 0, tap, 0.0)
    for _, bit in over:
        tap = tap + swap(tap, "fsdp", bit)
    return (
        out[None],
        grad_x[None],
        SCALE * qkv[:rows],
        SCALE * qkv[rows : 2 * rows],
        qkv[2 * rows :],
        g_o,
        g_up,
        g_down,
        little[:, 0],
        little[:, 1],
        little[:, 2],
        little[:, 3],
        tap,
    )


def solution(mesh):
    tokens = P("fsdp", "seq", None)
    matrix = P("fsdp", None)
    row = P("fsdp")
    in_specs = (tokens,) * 2 + (matrix,) * 6 + (row,) * 4 + (P(),)
    out_specs = (tokens,) * 2 + (matrix,) * 6 + (row,) * 4 + (P(),)
    return jax.shard_map(shards, mesh=mesh, in_specs=in_specs, out_specs=out_specs, check_vma=False)
```

```python
import functools

import jax
import jax.numpy as jnp
from jax import lax
from jax.experimental import pallas as pl
from jax.experimental.pallas import tpu as pltpu
from jax.sharding import PartitionSpec as P

HEADS = 12
HDIM = 64
LANDMARKS = 64
KERNEL = 65
PINV_ITERS = 6
REACH = KERNEL // 2
EDGE = 128
SCALE = HDIM ** (-0.25)
F32 = jnp.float32
BF16 = jnp.bfloat16
VM = 56 * 1024 * 1024


def nn(a, b):
    return jnp.dot(a, b, preferred_element_type=F32)


def nt(a, b):
    return lax.dot_general(a, b, (((1,), (1,)), ((), ())), preferred_element_type=F32)


def tn(a, b):
    return lax.dot_general(a, b, (((0,), (0,)), ((), ())), preferred_element_type=F32)


def split(a):
    high = a.astype(BF16)
    return high, (a - high.astype(F32)).astype(BF16)


def nn3(a, b):
    ah, al = split(a)
    bh, bl = split(b)
    return nn(jnp.concatenate([ah, ah, al], 1), jnp.concatenate([bh, bl, bh], 0))


def nt3(a, b):
    ah, al = split(a)
    bh, bl = split(b)
    return nt(jnp.concatenate([ah, ah, al], 1), jnp.concatenate([bh, bl, bh], 1))


def tn3(a, b):
    ah, al = split(a)
    bh, bl = split(b)
    return tn(jnp.concatenate([ah, ah, al], 0), jnp.concatenate([bh, bl, bh], 0))


def lanes(shape):
    return lax.broadcasted_iota(jnp.int32, shape, len(shape) - 1)


def hs(h):
    return slice(h * HDIM, (h + 1) * HDIM)


def vspec():
    return pl.BlockSpec(memory_space=pltpu.VMEM)


def sspec():
    return pl.BlockSpec(memory_space=pltpu.SMEM)


def aspec():
    return pl.BlockSpec(memory_space=pl.ANY)


def shape(dims, kind):
    return jax.ShapeDtypeStruct(tuple(dims), kind)


def params():
    return pltpu.CompilerParams(vmem_limit_bytes=VM)


def cost(flops, traffic, trans=0):
    return pl.CostEstimate(flops=1, bytes_accessed=1, transcendentals=0)


def call(kernel, args, in_specs, out_shape, out_specs, name, work, grid=(), scratch=(), after=()):
    count, extra = len(args), len(after)

    def body(*refs):
        kernel(*refs[:count], *refs[count + extra :])

    return pl.pallas_call(
        body,
        grid=grid,
        out_shape=out_shape,
        in_specs=list(in_specs) + [aspec()] * extra,
        out_specs=out_specs,
        scratch_shapes=list(scratch),
        compiler_params=params(),
        cost_estimate=work,
        name=name,
    )(*args, *after)


def placed(pieces, whole, sems, me, start):
    rows = pieces[0].shape[0]
    for k, piece in enumerate(pieces):
        at = pl.multiple_of((me ^ k) * rows, 16)
        copy = pltpu.make_async_copy(piece, whole.at[pl.ds(at, rows)], sems.at[k])
        if start:
            copy.start()
        else:
            copy.wait()


def placed_halves(pieces, whole, sems, me, side, start):
    rows = pieces[0].shape[0]
    for i, piece in enumerate(pieces):
        if i < 2:
            at = (me ^ i) * rows
        else:
            at = (me ^ (i // 2 + 1)) * rows + (side ^ (i % 2)) * (rows // 2)
        to = whole.at[pl.ds(pl.multiple_of(at, 16), piece.shape[0])]
        copy = pltpu.make_async_copy(piece, to, sems.at[i])
        if start:
            copy.start()
        else:
            copy.wait()


def xor_rows(out_ref, value, me, count):
    rows = value.shape[0] // count
    for r in range(count):
        at = pl.multiple_of((me ^ r) * rows, 16)
        out_ref[pl.ds(at, rows), :] = value[r * rows : (r + 1) * rows]


def pack_kernel(x_ref, *refs):
    weights, (all_ref, xm_ref, sems) = refs[:-3], refs[-3:]
    copies = []
    for i, w in enumerate(weights):
        to = all_ref.at[:, pl.ds(i * w.shape[1], w.shape[1])]
        copies.append(pltpu.make_async_copy(w, to, sems.at[i]))
        copies[-1].start()
    size, marks, width = xm_ref.shape
    tokens = x_ref.shape[0]
    segment = tokens // marks
    means = [
        jnp.mean(x_ref[m * segment : (m + 1) * segment, :].astype(F32), axis=0, keepdims=True)
        for m in range(marks)
    ]
    means = jnp.concatenate(means, 0)
    for i in range(size):
        xm_ref[i] = means
    for copy in copies:
        copy.wait()


def pack(x, weights, size, marks):
    rows, width = weights[0].shape
    return call(
        pack_kernel,
        (x, *weights),
        [vspec()] * 4,
        [shape((rows, 3 * width), BF16), shape((size, marks, width), F32)],
        [vspec()] * 2,
        "pack",
        cost(1e6, 1e5),
        scratch=[pltpu.SemaphoreType.DMA((3,))],
    )


def front_kernel(count, me_ref, x_ref, xm_ref, *refs):
    pieces = refs[:count]
    outs = refs[count : count + 6]
    xmt_ref, st_ref, msg_ref, qm_ref, km_ref, edge_ref = refs[count + 6 : count + 12]
    flats = refs[count + 12 : count + 18]
    xt_ref, qt_ref, kt_ref, vt_ref, fw_ref, eb_ref = flats
    w_ref, sems, out_sems, head_sems = refs[count + 18 :]
    me = me_ref[0]

    def out(i):
        return pltpu.make_async_copy(flats[i], outs[i], out_sems.at[i])

    def pair_out(i, pair):
        at = pl.ds(pair * 128, 128)
        return pltpu.make_async_copy(flats[i].at[at], outs[i].at[at], head_sems.at[i - 4, pair])

    placed(pieces, w_ref, sems, me, True)
    tokens, width = x_ref.shape
    step = 256
    for b in range(tokens // step):
        rows = slice(b * step, (b + 1) * step)
        xor_rows(xt_ref.at[:, rows], x_ref[rows, :].T, me, count)
    out(0).start()
    high, low = split(xm_ref[...])
    wide = jnp.concatenate([xm_ref[...], jnp.zeros_like(xm_ref)], 0)
    xor_rows(xmt_ref, wide.T.astype(BF16)[:, :LANDMARKS], me, count)
    placed(pieces, w_ref, sems, me, False)
    both = w_ref[:, : 2 * width]
    marks = SCALE * (nn(high, both) + nn(low, both))
    qm = marks[:, :width].astype(BF16)
    km = marks[:, width:].astype(BF16)
    qm_ref[...] = qm
    km_ref[...] = km
    for i, (to, scale) in enumerate(((qt_ref, SCALE), (kt_ref, SCALE), (vt_ref, None))):
        for b in range(tokens // step):
            rows = slice(b * step, (b + 1) * step)
            y = nn(x_ref[rows, :], w_ref[:, i * width : (i + 1) * width])
            if scale is not None:
                y = y * scale
            y = y.astype(BF16)
            if i == 2 and b == 0:
                edge_ref[:REACH] = y[:REACH]
            if i == 2 and b == tokens // step - 1:
                edge_ref[REACH:] = y[step - REACH :]
            to[:, rows] = y.T
        out(1 + i).start()
    lane = lanes((LANDMARKS, 128))
    stats = jnp.zeros((LANDMARKS, 128), F32)
    pair = []
    for h in range(HEADS):
        s = nn(km[:, hs(h)], qt_ref[hs(h), :])
        s = jnp.exp(s - jnp.max(s, axis=0, keepdims=True))
        fw_ref[hs(h), :] = (s * (1.0 / jnp.sum(s, axis=0, keepdims=True))).astype(BF16)
        s = nn(qm[:, hs(h)], kt_ref[hs(h), :])
        top = jnp.max(s, axis=1, keepdims=True).astype(BF16).astype(F32)
        e = jnp.exp(s - top).astype(BF16)
        eb_ref[hs(h), :] = e
        total = jnp.sum(e.astype(F32), axis=1, keepdims=True)
        stats = jnp.where(lane == h, top, stats)
        stats = jnp.where(lane == 16 + h, total, stats)
        pair.append(nt(e, vt_ref[hs(h), :]))
        if h % 2:
            both = jnp.concatenate(pair, 1).astype(BF16)
            for d in range(msg_ref.shape[0]):
                msg_ref[d, h // 2] = both
            pair = []
            pair_out(4, h // 2).start()
            pair_out(5, h // 2).start()
    st_ref[...] = stats
    for d in range(msg_ref.shape[0]):
        msg_ref[d, HEADS // 2] = stat_message(stats)
    for i in range(4):
        out(i).wait()
    for h in range(HEADS // 2):
        pair_out(4, h).wait()
        pair_out(5, h).wait()


def stat_message(stats):
    lane = lanes(stats.shape)
    high = stats.astype(BF16).astype(F32)
    low = pltpu.roll(stats - high, 16, 1)
    return jnp.where((lane >= 32) & (lane < 48), low, high).astype(BF16)


def front(me, x, xm, pieces, size):
    tokens, width = x.shape
    pairs = HEADS // 2
    flat = shape((width, tokens), BF16)
    xt, qt, kt, vt, fw, eb, xmt, st, msg, qm, km, edge = call(
        functools.partial(front_kernel, len(pieces)),
        (me, x, xm, *pieces),
        [sspec(), vspec(), vspec()] + [aspec()] * len(pieces),
        [flat] * 6
        + [
            shape((width, LANDMARKS), BF16),
            shape((LANDMARKS, 128), F32),
            shape((size, pairs + 1, LANDMARKS, 128), BF16),
            shape((LANDMARKS, width), BF16),
            shape((LANDMARKS, width), BF16),
            shape((2 * REACH, width), BF16),
        ],
        [aspec()] * 6 + [vspec()] * 6,
        "front",
        cost(4.5e8, 1.6e6),
        scratch=[pltpu.VMEM((width, tokens), BF16) for _ in range(6)]
        + [
            pltpu.VMEM((width, 3 * width), BF16),
            pltpu.SemaphoreType.DMA((len(pieces),)),
            pltpu.SemaphoreType.DMA((4,)),
            pltpu.SemaphoreType.DMA((2, pairs)),
        ],
    )
    return xt, xmt, qt, kt, vt, fw, eb, st, msg, qm, km, edge


def merged(msg_ref, mixn_ref, st_ref):
    lane = lanes((LANDMARKS, 128))
    size = msg_ref.shape[0]
    stats = []
    for d in range(size):
        got = msg_ref[d, HEADS // 2].astype(F32)
        stats.append(got + jnp.where((lane >= 16) & (lane < 32), pltpu.roll(got, 112, 1), 0.0))
    largest = functools.reduce(jnp.maximum, stats)
    weights = [jnp.exp(jnp.minimum(st - largest, 0.0)) for st in stats]
    total = sum(st * pltpu.roll(w, 16, 1) for st, w in zip(stats, weights))
    st_ref[...] = jnp.where(lane < 16, largest, total)
    for i in range(HEADS // 2):

        def both(a, at):
            return jnp.where(lane < HDIM, a[:, at : at + 1], a[:, at + 1 : at + 2])

        y = sum(msg_ref[d, i].astype(F32) * both(weights[d], 2 * i) for d in range(size))
        mixn_ref[i] = y / both(total, 16 + 2 * i)


def eye(scale):
    n = LANDMARKS
    return jnp.where(
        lax.broadcasted_iota(jnp.int32, (n, n), 0) == lax.broadcasted_iota(jnp.int32, (n, n), 1),
        jnp.float32(scale),
        0.0,
    )


def landmark_softmax(qm, km, h):
    s = nt(qm[:, hs(h)], km[:, hs(h)])
    s = jnp.exp(s - jnp.max(s, axis=1, keepdims=True))
    return s / jnp.sum(s, axis=1, keepdims=True)


def first_inverse(a):
    columns = jnp.max(jnp.sum(a, axis=0, keepdims=True), axis=1, keepdims=True)
    rows = jnp.max(jnp.sum(a, axis=1, keepdims=True), axis=0, keepdims=True)
    return a.T * (1.0 / (columns * rows))


def inverse_kernel(size, me_ref, qm_ref, km_ref, z_ref, a_out, zs, ps, ms, ns, a_ref, p_ref, m_ref, n_ref):
    qm, km = qm_ref[...], km_ref[...]
    every = range(HEADS)
    slots = range(-(-HEADS // size))
    mine = [jnp.minimum(me_ref[1] + size * j, HEADS - 1) for j in slots]
    for h in every:
        a = landmark_softmax(qm, km, h)
        a_ref[h] = a
        z_ref[h] = first_inverse(a)
    for j in slots:
        a_out[j] = a_ref[mine[j]]

    def step(i, carry):
        p = [nn3(a_ref[h], z_ref[h]) for h in every]
        m = [eye(15.0) - nn3(x, eye(7.0) - x) for x in p]
        n = [eye(13.0) - nn3(x, y) for x, y in zip(p, m)]
        for h in every:
            p_ref[h] = p[h]
            m_ref[h] = m[h]
            n_ref[h] = n[h]
        for j in slots:
            ps[i, j] = p_ref[mine[j]]
            ms[i, j] = m_ref[mine[j]]
            ns[i, j] = n_ref[mine[j]]
            zs[i, j] = z_ref[mine[j]]
        for h in every:
            z_ref[h] = 0.25 * nn3(z_ref[h], n[h])
        return carry

    lax.fori_loop(0, PINV_ITERS, step, 0)


def inverse(me, qm, km, size):
    square = (HEADS, LANDMARKS, LANDMARKS)
    few = (-(-HEADS // size), LANDMARKS, LANDMARKS)
    return call(
        functools.partial(inverse_kernel, size),
        (me, qm, km),
        [sspec()] + [vspec()] * 2,
        [shape(square, F32), shape(few, F32)] + [shape((PINV_ITERS,) + few, F32)] * 4,
        [vspec()] * 6,
        "inverse",
        cost(1e8, 1e6),
        scratch=[pltpu.VMEM(square, F32)] * 4,
    )


def half(pair, h):
    return jnp.where(h % 2 == 0, pair[:, :HDIM], pair[:, HDIM:])


def inverse_step(z, p, m, n, a, gz, ga):
    g = 0.25 * gz
    g3 = -tn3(z, g)
    g2 = -tn3(p, g3)
    gp = nt3(g3, m) + nt3(g2, eye(7.0) - p) - tn3(p, g2)
    return nt3(g, n) + tn3(a, gp), ga + nt3(gp, z)


def score_grad(a, gfirst, ga):
    csum = jnp.sum(a, axis=0, keepdims=True)
    rsum = jnp.sum(a, axis=1, keepdims=True)
    cmax = jnp.max(csum, axis=1, keepdims=True)
    rmax = jnp.max(rsum, axis=0, keepdims=True)
    scale = 1.0 / (cmax * rmax)
    gs = jnp.sum(jnp.sum(gfirst * a.T, axis=1, keepdims=True), axis=0, keepdims=True)
    ctop = (csum == cmax).astype(F32)
    rtop = (rsum == rmax).astype(F32)
    gcol = -gs * scale / cmax * ctop / jnp.sum(ctop, axis=1, keepdims=True)
    grow = -gs * scale / rmax * rtop / jnp.sum(rtop, axis=0, keepdims=True)
    g = ga + gfirst.T * scale + gcol + grow
    return a * (g - jnp.sum(g * a, axis=1, keepdims=True))


def widen(out_ref, flat_ref, pair_ref, next_ref, odd):
    width, tokens = flat_ref.shape
    zero = jnp.zeros((EDGE - REACH, width), BF16)
    pair, other = pair_ref[...].astype(F32), next_ref[...].astype(F32)
    before = jnp.where(odd, pair[REACH:], other[REACH:]).astype(BF16)
    after = jnp.where(odd, other[:REACH], pair[:REACH]).astype(BF16)
    out_ref[:, :EDGE] = jnp.concatenate([zero, before], 0).T
    out_ref[:, EDGE : EDGE + tokens] = flat_ref[...]
    out_ref[:, EDGE + tokens :] = jnp.concatenate([after, zero], 0).T


def band(row, step):
    wide = jnp.broadcast_to(row, (step, step + 2 * EDGE))
    return pltpu.roll(wide, 0, 1, stride=1, stride_axis=0).astype(BF16)


def stacked(ref, h, step, margin):
    blocks = (ref.shape[1] - 2 * margin) // step if margin else ref.shape[1] // step
    return jnp.concatenate(
        [ref[hs(h), b * step : (b + 1) * step + 2 * margin] for b in range(blocks)], 0
    )


def pair_rows(tokens):
    return pl.BlockSpec((128, tokens), lambda i: (i, 0))


def pair_lanes(rows):
    return pl.BlockSpec((rows, 128), lambda i: (0, i))


def pair_block(*dims):
    return pl.BlockSpec((1, *dims), lambda i: (i, 0, 0))


def conv_kernel_body(me_ref, vt_ref, pair_ref, next_ref, taps_ref, out_ref, wide_ref):
    widen(wide_ref, vt_ref, pair_ref, next_ref, me_ref[1] % 2 == 1)
    step = 256
    for h in range(HEADS):
        y = nt(stacked(wide_ref, h, step, EDGE), band(taps_ref[h : h + 1, :], step))
        for b in range(vt_ref.shape[1] // step):
            out_ref[hs(h), b * step : (b + 1) * step] = y[b * HDIM : (b + 1) * HDIM, :]


def conv(me, vt, edges, taps):
    width, tokens = vt.shape
    return call(
        conv_kernel_body,
        (me, vt, *edges, taps),
        [sspec()] + [vspec()] * 4,
        shape(vt.shape, F32),
        vspec(),
        "conv",
        cost(2e9, 6e6),
        scratch=[pltpu.VMEM((width, tokens + 2 * EDGE), BF16)],
    )


def gelu_pair(x):
    phi = 0.5 * (1.0 + lax.erf(x * (0.5**0.5)))
    return x * phi, phi + x * ((0.5 / jnp.pi) ** 0.5 * jnp.exp(-0.5 * x * x))


def norm_stats(r):
    center = r - jnp.mean(r, axis=-1, keepdims=True)
    rstd = lax.rsqrt(jnp.mean(center * center, axis=-1, keepdims=True) + 1e-05)
    return center * rstd, rstd


def norm_back(gy, xhat, rstd):
    return rstd * (
        gy - jnp.mean(gy, axis=-1, keepdims=True) - xhat * jnp.mean(gy * xhat, axis=-1, keepdims=True)
    )


STEP = 256


def whole(a):
    return pl.BlockSpec(a.shape, lambda i, n=a.ndim: (0,) * n)


def fixed(*dims):
    return pl.BlockSpec(dims, lambda i, n=len(dims): (0,) * n)


def tall(rows):
    return pl.BlockSpec((rows, STEP), lambda i: (0, i))


def row(width):
    return pl.BlockSpec((STEP, width), lambda i: (i, 0))


def mid_kernel(count, me_ref, z_ref, msg_ref, fw_ref, conv_ref, x_ref, ct_ref, gains_ref, *refs):
    halves = 2 * count - 2
    wo, down, up = refs[:count], refs[count : 2 * count], refs[2 * count : 2 * count + halves]
    (ctx_ref, hidt_ref, act_ref, out_ref, redt_ref, ge_ref, first_ref, branch_ref, gct_ref, edge_ref,
     sums_ref, comb_ref, mixn_ref, st_ref, gc_ref, wo_ref, up_ref, down_ref, slope_ref,
     sems, up_sems) = refs[2 * count + halves :]
    me, side = me_ref[0], me_ref[1] % 2
    at = pl.program_id(0)
    begin = at == 0
    part = up_ref.shape[1] // count

    @pl.when(begin)
    def _():
        placed(wo, wo_ref, sems.at[0], me, True)
        placed_halves(up, up_ref, up_sems, me, side, True)
        placed(down, down_ref, sems.at[1], me, True)
        merged(msg_ref, mixn_ref, st_ref)
        for i in range(HEADS // 2):
            mixed = mixn_ref[i]
            comb_ref[i] = jnp.concatenate(
                [nn3(z_ref[2 * i], mixed[:, :HDIM]), nn3(z_ref[2 * i + 1], mixed[:, HDIM:])], 1
            ).astype(BF16)
        sums_ref[...] = jnp.zeros_like(sums_ref)
        gc_ref[...] = jnp.zeros_like(gc_ref)
        placed(wo, wo_ref, sems.at[0], me, False)

    for h in range(HEADS):
        att = tn(comb_ref[h // 2][:, hs(h % 2)], fw_ref[hs(h), :])
        ctx_ref[hs(h), :] = (att + conv_ref[hs(h), :]).astype(BF16)
    branch = nn(ctx_ref[...].T, wo_ref[...])
    xhat1, rstd1 = norm_stats(x_ref[...].astype(F32) + branch)
    hidden = xhat1 * gains_ref[0:1, :] + gains_ref[1:2, :]
    hid = hidden.astype(BF16)
    xor_rows(hidt_ref, hid.T, me, count)

    @pl.when(begin)
    def _():
        placed_halves(up, up_ref, up_sems, me, side, False)

    for c in range(count):
        cols = slice(c * part, (c + 1) * part)
        act, slope = gelu_pair(nn(hid, up_ref[:, cols]))
        act_ref[:, cols] = act.astype(BF16)
        slope_ref[:, cols] = slope.astype(BF16)

    @pl.when(begin)
    def _():
        placed(down, down_ref, sems.at[1], me, False)

    xhat, rstd = norm_stats(hidden + nn(act_ref[...], down_ref[...]))
    out_ref[...] = (xhat * gains_ref[2:3, :] + gains_ref[3:4, :]).astype(BF16)
    ct = ct_ref[...].astype(F32)
    sums_ref[2:3, :] = sums_ref[2:3, :] + jnp.sum(ct * xhat, axis=0, keepdims=True)
    sums_ref[3:4, :] = sums_ref[3:4, :] + jnp.sum(ct, axis=0, keepdims=True)
    second = norm_back(ct * gains_ref[2:3, :], xhat, rstd)
    red = second.astype(BF16)
    redt_ref[...] = red.T
    for k in range(count):
        cols = slice(k * part, (k + 1) * part)
        ge = nt(red, down_ref[cols, :]) * slope_ref[:, cols].astype(F32)
        ge_ref[:, cols] = ge.astype(BF16)
    g = second + nt(ge_ref[...], up_ref[...])
    sums_ref[0:1, :] = sums_ref[0:1, :] + jnp.sum(g * xhat1, axis=0, keepdims=True)
    sums_ref[1:2, :] = sums_ref[1:2, :] + jnp.sum(g, axis=0, keepdims=True)
    first = norm_back(g * gains_ref[0:1, :], xhat1, rstd1)
    first_ref[...] = first
    back = first.astype(BF16)
    branch_ref[...] = back
    gctx = nt(back, wo_ref[...]).astype(BF16)

    @pl.when(begin)
    def _():
        edge_ref[:REACH] = gctx[:REACH]

    @pl.when(at == pl.num_programs(0) - 1)
    def _():
        edge_ref[REACH:] = gctx[gctx.shape[0] - REACH :]

    gct_ref[...] = gctx.T
    for i in range(HEADS // 2):
        gc_ref[i] = gc_ref[i] + jnp.concatenate(
            [nt(fw_ref[hs(h), :], gct_ref[hs(h), :]) for h in (2 * i, 2 * i + 1)], 1
        )


def mid(me, z, msgs, fw, convt, x, ct, gains, wo, up, down, after=()):
    tokens, width = x.shape
    ff = up[0].shape[1]
    pairs = HEADS // 2
    pieces = (*wo, *down, *up)
    flat, wide = shape((width, tokens), BF16), shape((tokens, ff), BF16)
    return call(
        functools.partial(mid_kernel, len(wo)),
        (me, z, msgs, fw, convt, x, ct, gains, *pieces),
        [sspec(), whole(z), whole(msgs), tall(width), tall(width), row(width), row(width), whole(gains)]
        + [aspec()] * len(pieces),
        [
            flat,
            flat,
            wide,
            shape((tokens, width), BF16),
            flat,
            wide,
            shape((tokens, width), F32),
            shape((tokens, width), BF16),
            flat,
            shape((2 * REACH, width), BF16),
            shape((8, width), F32),
            shape((pairs, LANDMARKS, 128), BF16),
            shape((pairs, LANDMARKS, 128), F32),
            shape((LANDMARKS, 128), F32),
            shape((pairs, LANDMARKS, 128), F32),
        ],
        [tall(width), tall(width), row(ff), row(width), tall(width), row(ff), row(width), row(width),
         tall(width), fixed(2 * REACH, width), fixed(8, width),
         fixed(pairs, LANDMARKS, 128), fixed(pairs, LANDMARKS, 128), fixed(LANDMARKS, 128),
         fixed(pairs, LANDMARKS, 128)],
        "mid",
        cost(2e9, 3e6),
        grid=(tokens // STEP,),
        scratch=[
            pltpu.VMEM((width, width), BF16),
            pltpu.VMEM((width, ff), BF16),
            pltpu.VMEM((ff, width), BF16),
            pltpu.VMEM((STEP, ff), BF16),
            pltpu.SemaphoreType.DMA((2, len(wo))),
            pltpu.SemaphoreType.DMA((len(up),)),
        ],
        after=after,
    )


def grad_down_kernel(count, me_ref, red_ref, act_ref, *outs):
    part = act_ref.shape[1] // count
    for k in range(count):
        at = pl.ds(pl.multiple_of((me_ref[0] ^ k) * part, 128), part)
        outs[k][...] = nn(red_ref[...], act_ref[:, at]).astype(BF16)


def grad_down(count, me, redt, act, after=()):
    width = redt.shape[0]
    return call(
        functools.partial(grad_down_kernel, count),
        (me, redt, act),
        [sspec(), vspec(), vspec()],
        [shape((width, act.shape[1] // count), BF16)] * count,
        [vspec()] * count,
        "grad_down",
        cost(5e8, 1e6),
        after=after,
    )


def grad_up_kernel(count, hid_ref, ge_ref, *outs):
    y = nn(hid_ref[...], ge_ref[...]).astype(BF16)
    rows = y.shape[0] // count
    for k in range(count):
        outs[k][...] = y[k * rows : (k + 1) * rows]


def grad_up(count, hidt, ge, after=()):
    width, tokens = hidt.shape
    ff = ge.shape[1]
    step = 768
    return call(
        functools.partial(grad_up_kernel, count),
        (hidt, ge),
        [whole(hidt), pl.BlockSpec((tokens, step), lambda i: (0, i))],
        [shape((width // count, ff), BF16)] * count,
        [pl.BlockSpec((width // count, step), lambda i: (0, i))] * count,
        "grad_up",
        cost(5e8, 1e6),
        grid=(ff // step,),
        after=after,
    )


class Moves:
    def __init__(self, sems):
        self.sems, self.used, self.open = sems, 0, []

    def start(self, src, dst):
        copy = pltpu.make_async_copy(src, dst, self.sems.at[self.used])
        self.used += 1
        copy.start()
        self.open.append(copy)
        return copy

    def wait(self, *copies):
        for copy in copies or list(self.open):
            copy.wait()
            self.open.remove(copy)


def gap_kernel(count, me_ref, gct_hbm, fw_hbm, qt_hbm, vt_hbm, ctx_hbm, branch_hbm, comb_ref, km_ref,
               vb_ref, va_ref, gb_ref, ga_ref, taps_ref, sums_ref, *refs):
    outs = refs[:count]
    (gq_hbm, gvc_hbm, gkm_ref, gct_ref, fw_ref, qt_ref, vt_ref, ctx_ref, branch_ref, gq_ref, gvc_ref,
     vwide, gwide, y_ref, sems) = refs[count:]
    moves = Moves(sems)
    lead = [
        moves.start(a, b)
        for a, b in ((gct_hbm, gct_ref), (fw_hbm, fw_ref), (qt_hbm, qt_ref))
    ]
    values = moves.start(vt_hbm, vt_ref)
    rest = [moves.start(ctx_hbm, ctx_ref), moves.start(branch_hbm, branch_ref)]
    km = km_ref[...]
    moves.wait(*lead)
    pair = []
    for h in range(HEADS):
        comb = comb_ref[h // 2][:, hs(h % 2)]
        pf = fw_ref[hs(h), :].astype(F32)
        g = nn(comb, gct_ref[hs(h), :])
        gs = (pf * (g - jnp.sum(pf * g, axis=0, keepdims=True))).astype(BF16)
        gq_ref[hs(h), :] = tn(km[:, hs(h)], gs).astype(BF16)
        pair.append(nt(gs, qt_ref[hs(h), :]))
        if h % 2:
            gkm_ref[:, (h - 1) * HDIM : (h + 1) * HDIM] = jnp.concatenate(pair, 1)
            pair = []
    moves.start(gq_ref, gq_hbm)
    moves.wait(values)
    odd = me_ref[1] % 2 == 1
    widen(vwide, vt_ref, vb_ref, va_ref, odd)
    widen(gwide, gct_ref, gb_ref, ga_ref, odd)
    step = 256
    tokens = vt_ref.shape[1]
    flip = (
        lax.broadcasted_iota(jnp.int32, (step, step), 0)
        + lax.broadcasted_iota(jnp.int32, (step, step), 1)
        == step - 1
    ).astype(BF16)
    rows = []
    for h in range(HEADS):
        y = nt(stacked(gwide, h, step, EDGE), band(taps_ref[h : h + 1, :], step))
        for b in range(tokens // step):
            gvc_ref[hs(h), b * step : (b + 1) * step] = y[b * HDIM : (b + 1) * HDIM, :]
        turned = nn(stacked(gct_ref, h, step, 0), flip).astype(BF16)
        d = tn(turned, stacked(vwide, h, step, EDGE))
        d = pltpu.roll(d, 0, 1, stride=1, stride_axis=0)
        rows.append(jnp.sum(d, axis=0, keepdims=True))
    moves.start(gvc_ref, gvc_hbm)
    rows = jnp.concatenate(rows + [jnp.zeros((4, step + 2 * EDGE), F32)], 0)
    first = step - 1 + EDGE - REACH
    taps = pltpu.roll(rows, step + 2 * EDGE - first, 1)[:HEADS, :128]
    width = ctx_ref.shape[0]
    taps = jnp.concatenate([taps, jnp.zeros((HEADS, width - 128), F32)], 1)
    little = jnp.concatenate(
        [sums_ref[0:4, :], taps, jnp.zeros((128 - 4 - HEADS, width), F32)], 0
    )
    y_ref[:, width:] = little.T.astype(BF16)
    moves.wait(*rest)
    y_ref[:, :width] = nn(ctx_ref[...], branch_ref[...]).astype(BF16)
    size = width // count
    for k in range(count):
        outs[k][...] = y_ref[pl.ds(pl.multiple_of((me_ref[0] ^ k) * size, 16), size), :]
    moves.wait()


def gap(count, me, gct, fw, qt, vt, ctxt, branch, comb, km, vb, va, gb, ga, taps, sums, after=()):
    width, tokens = vt.shape
    flat = pltpu.VMEM((width, tokens), BF16)
    wide = pltpu.VMEM((width, tokens + 2 * EDGE), BF16)
    *pieces, gq, gvc, gkm = call(
        functools.partial(gap_kernel, count),
        (me, gct, fw, qt, vt, ctxt, branch, comb, km, vb, va, gb, ga, taps, sums),
        [sspec()] + [aspec()] * 6 + [vspec()] * 8,
        [shape((width // count, width + 128), BF16)] * count
        + [shape(gct.shape, BF16), shape(gct.shape, F32), shape(km.shape, F32)],
        [vspec()] * count + [aspec()] * 2 + [vspec()],
        "gap",
        cost(1e9, 1e6),
        scratch=[flat] * 5
        + [
            pltpu.VMEM((tokens, width), BF16),
            flat,
            pltpu.VMEM((width, tokens), F32),
            wide,
            wide,
            pltpu.VMEM((width, width + 128), BF16),
            pltpu.SemaphoreType.DMA((8,)),
        ],
        after=after,
    )
    return pieces, gq, gvc, gkm


def rear_kernel(count, size, me_ref, eb_hbm, vt_hbm, kt_hbm, gvc_hbm, xt_hbm, gq_hbm, z_ref, gc_ref,
                mixn_ref, st_ref, own_ref, qm_ref, km_ref, gkmp_ref, xmt_ref, a_ref, zs, ps, ms, ns, *refs):
    outs = refs[:count]
    (gk_hbm, gv_hbm, gqm_ref, gkm_ref, eb_ref, vt_ref, kt_ref, gvc_ref, xt_ref, gq_ref, gk_ref, gv_ref,
     y_ref, sems) = refs[count:]
    moves = Moves(sems)
    early = [
        moves.start(a, b)
        for a, b in ((vt_hbm, vt_ref), (eb_hbm, eb_ref), (kt_hbm, kt_ref), (gvc_hbm, gvc_ref))
    ]
    late = [moves.start(xt_hbm, xt_ref), moves.start(gq_hbm, gq_ref)]
    qm, km = qm_ref[...], km_ref[...]
    lane = lanes((LANDMARKS, 128))
    slots = range(-(-HEADS // size))
    heads = [me_ref[1] + size * j for j in slots]
    safe = [jnp.minimum(h, HEADS - 1) for h in heads]
    gz = [nt3(half(gc_ref[h // 2], h), half(mixn_ref[h // 2], h)) for h in safe]
    ga = [jnp.zeros((LANDMARKS, LANDMARKS), F32) for _ in slots]
    stats = st_ref[...]
    scale = jnp.exp(own_ref[...] - stats)
    moves.wait(*early)
    for p in range(HEADS // 2):
        if p < PINV_ITERS:
            i = PINV_ITERS - 1 - p
            for j in slots:
                gz[j], ga[j] = inverse_step(
                    zs[i, j], ps[i, j], ms[i, j], ns[i, j], a_ref[j], gz[j], ga[j]
                )
        pair = []
        for h in (2 * p, 2 * p + 1):
            gmix = tn3(z_ref[h], gc_ref[p][:, hs(h % 2)]).astype(BF16)
            dot = jnp.sum(gmix.astype(F32) * mixn_ref[p][:, hs(h % 2)], axis=1, keepdims=True)
            factor = scale[:, h : h + 1] / stats[:, 16 + h : 17 + h]
            pb = eb_ref[hs(h), :].astype(F32) * factor
            gs = (pb * (nn(gmix, vt_ref[hs(h), :]) - dot)).astype(BF16)
            gk_ref[hs(h), :] = tn(qm[:, hs(h)], gs).astype(BF16)
            gv_ref[hs(h), :] = (tn(gmix, pb.astype(BF16)) + gvc_ref[hs(h), :]).astype(BF16)
            pair.append(nt(gs, kt_ref[hs(h), :]))
        both = slice(p * 128, p * 128 + 128)
        gqm_ref[:, both] = jnp.concatenate(pair, 1)
        gkm_ref[:, both] = gkmp_ref[:, both]
    moves.start(gk_ref, gk_hbm)
    moves.start(gv_ref, gv_hbm)
    moves.wait(*late)
    width = xt_ref.shape[0]
    rows = width // count

    def weight(i, y):
        y_ref[i] = y.astype(BF16)
        for k in range(count):
            moves.start(y_ref.at[i, pl.ds(k * rows, rows)], outs[k].at[i])

    weight(2, nt(xt_ref[...], gv_ref[...]))
    for j in slots:
        h = safe[j]
        high, low = split(score_grad(a_ref[j], gz[j], ga[j]))
        at = pl.ds(pl.multiple_of(h // 2 * 128, 128), 128)
        qmh = half(qm_ref[:, at].astype(F32), h).astype(BF16)
        kmh = half(km_ref[:, at].astype(F32), h).astype(BF16)
        gq = nn(jnp.concatenate([high, low], 1), jnp.concatenate([kmh] * 2, 0))
        gk = tn(jnp.concatenate([high, low], 0), jnp.concatenate([qmh] * 2, 0))
        mine = ((lane >= HDIM) == (h % 2 == 1)) & (heads[j] < HEADS)
        gqm_ref[:, at] = gqm_ref[:, at] + jnp.where(mine, jnp.concatenate([gq, gq], 1), 0.0)
        gkm_ref[:, at] = gkm_ref[:, at] + jnp.where(mine, jnp.concatenate([gk, gk], 1), 0.0)
    weight(0, nt(xt_ref[...], gq_ref[...]) + nn(xmt_ref[...], gqm_ref[...].astype(BF16)))
    weight(1, nt(xt_ref[...], gk_ref[...]) + nn(xmt_ref[...], gkm_ref[...].astype(BF16)))
    moves.wait()


def rear(count, size, me, eb, vt, kt, gvc, xt, gq, z, gc, mixn, stats, own, qm, km, gkm, xmt, a, saved,
         after=()):
    width, tokens = vt.shape
    rows = width // count
    flat = pltpu.VMEM((width, tokens), BF16)
    mark = shape(qm.shape, F32)
    *pieces, gk, gv, gqm, gkm = call(
        functools.partial(rear_kernel, count, size),
        (me, eb, vt, kt, gvc, xt, gq, z, gc, mixn, stats, own, qm, km, gkm, xmt, a, *saved),
        [sspec()] + [aspec()] * 6 + [vspec()] * 14,
        [shape((3, rows, width), BF16)] * count + [shape(vt.shape, BF16)] * 2 + [mark] * 2,
        [aspec()] * (count + 2) + [vspec()] * 2,
        "rear",
        cost(2e9, 2e6),
        scratch=[flat] * 3
        + [pltpu.VMEM((width, tokens), F32)]
        + [flat] * 4
        + [
            pltpu.VMEM((3, width, width), BF16),
            pltpu.SemaphoreType.DMA((8 + 3 * count,)),
        ],
        after=after,
    )
    return [piece.reshape(3 * rows, width) for piece in pieces], gk, gv, gqm, gkm


def last_kernel(count, me_ref, gq_ref, gk_ref, gv_ref, first_ref, *refs):
    pieces = refs[:count]
    out_ref, w_ref, sems = refs[count:]
    me = me_ref[0]
    width = gq_ref.shape[0]

    @pl.when(pl.program_id(0) == 0)
    def _():
        placed(pieces, w_ref, sems, me, True)
        placed(pieces, w_ref, sems, me, False)

    wq, wk, wv = (w_ref[:, i * width : (i + 1) * width] for i in range(3))
    g = SCALE * (nn(wq, gq_ref[...]) + nn(wk, gk_ref[...])) + nn(wv, gv_ref[...])
    out_ref[...] = first_ref[...] + g.T


def last(me, gq, gk, gv, first, pieces, after=()):
    width, tokens = gq.shape
    return call(
        functools.partial(last_kernel, len(pieces)),
        (me, gq, gk, gv, first, *pieces),
        [sspec(), tall(width), tall(width), tall(width), row(width)] + [aspec()] * len(pieces),
        shape((tokens, width), F32),
        row(width),
        "last",
        cost(4e8, 1e6),
        grid=(tokens // STEP,),
        scratch=[
            pltpu.VMEM((width, 3 * width), BF16),
            pltpu.SemaphoreType.DMA((len(pieces),)),
        ],
        after=after,
    )


def share_kernel(segment, count, me_ref, own_ref, most_ref, *refs):
    pieces = refs[:count]
    out_ref, w_ref, sems = refs[count:]
    own = own_ref[...]
    width = own.shape[1] // 2
    pieces = [piece.at[:, pl.ds(0, 2 * width)] for piece in pieces]
    placed(pieces, w_ref, sems, me_ref[0], True)
    placed(pieces, w_ref, sems, me_ref[0], False)
    marks = (SCALE / segment) * (
        nt(own[:, :width].astype(BF16), w_ref[:, :width])
        + nt(own[:, width:].astype(BF16), w_ref[:, width : 2 * width])
    )
    for m in range(own.shape[0]):
        rows = slice(m * segment, (m + 1) * segment)
        out_ref[rows, :] = (most_ref[rows, :] + marks[m : m + 1, :]).astype(BF16)


def share(me, own, most, pieces):
    tokens, width = most.shape
    return call(
        functools.partial(share_kernel, tokens // own.shape[0], len(pieces)),
        (me, own, most, *pieces),
        [sspec(), vspec(), vspec()] + [aspec()] * len(pieces),
        shape(most.shape, BF16),
        vspec(),
        "share",
        cost(4e8, 1e6),
        scratch=[
            pltpu.VMEM((width, 2 * width), BF16),
            pltpu.SemaphoreType.DMA((len(pieces),)),
        ],
    )


def bits(axis):
    size = lax.axis_size(axis)
    assert size & (size - 1) == 0
    return [1 << i for i in range(size.bit_length() - 1)]


def swap(array, axis, bit):
    return lax.ppermute(array, axis, [(i, i ^ bit) for i in range(lax.axis_size(axis))])


def neighbours(array):
    size = lax.axis_size("seq")
    odd = [(i, i + 1) for i in range(1, size - 1, 2)]
    return swap(array, "seq", 1), lax.ppermute(array, "seq", odd + [(j, i) for i, j in odd])


def spread(pieces, axis, steps):
    for bit in steps:
        pieces = {**pieces, **{k | bit: swap(piece, axis, bit) for k, piece in pieces.items()}}
    return pieces


def far(array, axis):
    return spread({0: array}, axis, bits(axis)[1:])


def near(pieces, axis):
    pieces = spread(pieces, axis, bits(axis)[:1])
    return [pieces[k] for k in range(lax.axis_size(axis))]


def gathered(array, axis):
    return near(far(array, axis), axis)


def tie(*values):
    return lax.optimization_barrier(values)


def rows_out(array, groups=None):
    size = len(groups[0]) if groups else lax.axis_size("seq")
    blocks = array.reshape(size, -1, array.shape[1])
    return lax.all_to_all(blocks, "seq", 0, 0, axis_index_groups=groups)


def rows_in(blocks):
    return jnp.sum(blocks.astype(F32), axis=0)


def copies(array, axis, groups=None):
    size = len(groups[0]) if groups else lax.axis_size(axis)
    blocks = jnp.broadcast_to(array[None], (size, *array.shape))
    return lax.all_to_all(blocks, axis, 0, 0, axis_index_groups=groups)


class Total:
    def __init__(self, pieces, order):
        self.pieces = dict(enumerate(pieces))
        self.order = list(order)
        self.back = [step for step in reversed(order) if step[0] != "swap"]
        self.got = None

    def send(self, *values):
        if not self.order and not self.back:
            return values
        back = not self.order
        kind, what = self.back[0] if back else self.order[0]
        axis = "seq"
        if kind == "swap":
            axis = "fsdp"
            sent = {k: p for k, p in self.pieces.items() if k & what}
            self.pieces = {k: p for k, p in self.pieces.items() if not k & what}
        elif kind == "half" and not back:
            piece = self.pieces[0]
            upper = ((lax.axis_index("seq") & what) != 0).astype(jnp.int32)
            half = piece.shape[0] // 2
            self.pieces = {0: lax.dynamic_slice_in_dim(piece, upper * half, half, 0)}
            sent = {0: lax.dynamic_slice_in_dim(piece, (1 - upper) * half, half, 0)}
        elif kind == "rows" and back:
            size = len(what[0]) if what else lax.axis_size("seq")
            sent = {0: jnp.broadcast_to(self.pieces[0][None], (size, *self.pieces[0].shape))}
        elif kind == "rows":
            size = len(what[0]) if what else lax.axis_size("seq")
            sent = {0: self.pieces[0].reshape(size, -1, self.pieces[0].shape[1])}
        else:
            sent = dict(self.pieces)
        if values:
            sent, values = tie(sent, values)
        if kind == "rows":
            self.got = {
                k: lax.all_to_all(p, "seq", 0, 0, axis_index_groups=what) for k, p in sent.items()
            }
        else:
            self.got = {k: swap(p, axis, what) for k, p in sent.items()}
        return values

    def take(self):
        if self.order:
            kind, what = self.order.pop(0)
            if kind == "rows":
                self.pieces = {0: rows_in(self.got[0]).astype(BF16)}
            else:
                extra = what if kind == "swap" else 0
                self.pieces = {
                    k: (p.astype(F32) + self.got[k | extra].astype(F32)).astype(BF16)
                    for k, p in self.pieces.items()
                }
        else:
            kind, what = self.back.pop(0)
            mine, other = self.pieces[0], self.got[0]
            if kind == "rows":
                self.pieces = {0: other.reshape(-1, other.shape[2])}
            else:
                upper = (lax.axis_index("seq") & what) != 0
                self.pieces = {
                    0: jnp.where(
                        upper, jnp.concatenate([other, mine], 0), jnp.concatenate([mine, other], 0)
                    )
                }
        self.got = None

    def step(self, *values):
        self.got, values = tie(self.got, values)
        self.take()
        return self.send(*values)

    def finish(self):
        while self.got is not None:
            self.step()
        return self.pieces[0]


def orders():
    size = lax.axis_size("seq")
    over = [("swap", bit) for bit in bits("fsdp")]
    parts = size // 4
    groups = [[low + parts * high for high in range(4)] for low in range(parts)]
    near = [("half", bit) for bit in bits("seq") if bit < parts]
    tree = over + [("half", bit) for bit in bits("seq")]
    return over, over + near + [("rows", groups)], over + [("rows", None)], tree


def shards(
    inputs,
    cotangent,
    query_weight,
    key_weight,
    value_weight,
    output_weight,
    up_weight,
    down_weight,
    norm_gain,
    norm_shift,
    final_gain,
    final_shift,
    conv_kernel,
):
    x = inputs[0]
    ct = cotangent[0]
    tokens, width = x.shape
    marks = LANDMARKS // lax.axis_size("seq")
    segment = tokens // marks
    count = lax.axis_size("fsdp")
    rows = width // count
    here = lax.axis_index("fsdp")
    place = lax.axis_index("seq")
    size = lax.axis_size("seq")
    me = jnp.stack([here, place]).astype(jnp.int32)
    over, nested, flat, tree = orders()

    packed, xm = pack(x, (query_weight, key_weight, value_weight), size, marks)
    first_weights = far(packed, "fsdp")
    space = 256 + 2 * EDGE
    taps = jnp.pad(conv_kernel.T, ((0, 4), (EDGE - REACH, space - KERNEL - EDGE + REACH)))
    spat = jnp.pad(conv_kernel[::-1].T, ((0, 4), (EDGE - REACH, space - KERNEL - EDGE + REACH)))
    xm, taps, spat, me = tie(xm, taps, spat, me)
    xm = lax.all_to_all(xm, "seq", 0, 0).reshape(LANDMARKS, width)
    gains = jnp.stack([norm_gain, norm_shift, final_gain, final_shift] * 2)
    gains = gathered(gains, "fsdp")
    first_weights, gains, xm, output_weight = tie(first_weights, gains, xm, output_weight)
    first_weights, up_weight, output_weight, down_weight = tie(
        first_weights, up_weight, output_weight, down_weight
    )
    wqkv = near(first_weights, "fsdp")
    side = (place & 1).astype(jnp.int32)
    up_far = spread({0: lax.dynamic_slice_in_dim(up_weight, side * (rows // 2), rows // 2, 0)}, "fsdp", bits("fsdp")[1:])
    up_far = [up_far[k] for k in range(2, count, 2)]
    wo = far(output_weight, "fsdp")
    down = far(down_weight, "fsdp")
    source = lax.broadcasted_iota(jnp.int32, (8, width), 1) // rows ^ here
    gains = sum(
        jnp.where(source == k, jnp.concatenate([piece.astype(F32)] * count, 1), 0.0)
        for k, piece in enumerate(gains)
    )

    (xt, xmt, qt, kt, vt, fw, eb, own, msg, qm, km, v_edge) = front(me, x, xm, wqkv, size)
    v_edges = neighbours(v_edge)
    msg, up_far, v_edges = tie(msg, up_far, v_edges)
    msgs = lax.all_to_all(msg, "seq", 0, 0)
    up_other = [swap(piece, "seq", 1) for piece in up_far]
    z, a, *saved = inverse(me, qm, km, size)
    v_edges, z = tie(v_edges, z)
    convt = conv(me, vt, v_edges, taps)
    down, wo, convt, up_far, up_other = tie(down, wo, convt, up_far, up_other)
    up = [up_weight, swap(up_weight, "fsdp", 1)]
    for mine, other in zip(up_far, up_other):
        up += [mine, other, swap(mine, "fsdp", 1), swap(other, "fsdp", 1)]
    wo = near(wo, "fsdp")
    down = near(down, "fsdp")

    (ctxt, hidt, act, out, redt, ge, first, branch, gct, g_edge, sums, comb, mixn, stats, gc) = mid(
        me, z, msgs, fw, convt, x, ct, gains, wo, up, down
    )
    hops = bits("seq")

    def exchange(bit):
        return swap(gc.astype(BF16), "seq", bit)

    got = exchange(hops[0])
    g_edges = neighbours(g_edge)
    d_up = grad_up(count, hidt, ge)
    t_up = Total(d_up, tree)
    t_up.send()
    got, d_up, g_edges = tie(got, d_up, g_edges)
    gc = gc + got.astype(F32)
    got = exchange(hops[1])
    (act,) = t_up.step(act)
    d_down = grad_down(count, me, redt, act, after=d_up)
    t_down = Total(d_down, over)
    t_down.send()
    got, d_down = tie(got, d_down)
    gc = gc + got.astype(F32)
    got = exchange(hops[2])
    gct, d_down = t_down.step(gct, d_down)
    d_o, gq, gvc, gkm = gap(
        count, me, gct, fw, qt, vt, ctxt, branch, comb, km, *v_edges, *g_edges, spat, sums, after=d_down
    )
    t_o = Total(d_o, over)
    t_o.send()
    got, gvc = tie(got, gvc)
    gc = gc + got.astype(F32)
    for bit in hops[3:]:
        gc = gc + exchange(bit).astype(F32)
    (gc,) = t_up.step(gc)
    (gc,) = t_o.step(gc)
    d_qkv, gk, gv, gqm, gkm = rear(
        count, size, me, eb, vt, kt, gvc, xt, gq, z, gc, mixn, stats, own, qm, km, gkm, xmt, a, saved, after=d_o
    )
    t_qkv = Total(d_qkv, tree)
    t_qkv.send()
    landed = rows_out(jnp.concatenate([gqm, gkm], 1).astype(BF16))
    while t_o.got is not None:
        (gk,) = t_o.step(gk)
    g_o = t_o.pieces[0]
    while t_down.got is not None:
        (gk,) = t_down.step(gk)
    part = t_down.pieces[0].shape[1]
    g_down = t_down.pieces[0].reshape(-1, width)
    sizes = [g_down.shape[0], rows, rows * 128 // width]
    both = jnp.concatenate([g_down, g_o[:, :width], g_o[:, width:].reshape(-1, width)], 0)
    t_both = Total([both], tree[len(over) :])
    (gk,) = t_both.send(gk)
    (gk,) = t_up.step(gk)
    for _ in over[:-1]:
        (gk,) = t_qkv.step(gk)
    most = last(me, gq, gk, gv, first, wqkv)
    for t in (t_up, t_both):
        (most,) = t.step(most)
    landed, most = tie(landed, most)
    grad_x = share(me, rows_in(landed), most, wqkv)
    totals = (t_qkv, t_up, t_both)
    while any(t.got is not None for t in totals):
        for t in totals:
            if t.got is not None:
                (grad_x,) = t.step(grad_x)
    g_up, both, qkv = (t.pieces[0].astype(F32) for t in (t_up, t_both, t_qkv))
    g_down = both[: sizes[0]].reshape(width, part).T
    g_o = both[sizes[0] : sizes[0] + sizes[1]]
    little = both[sizes[0] + sizes[1] :].reshape(rows, 128)

    tap = little[:KERNEL, 4 : 4 + HEADS]
    tap = jnp.where(here == 0, tap, 0.0)
    for _, bit in over:
        tap = tap + swap(tap, "fsdp", bit)
    return (
        out[None],
        grad_x[None],
        SCALE * qkv[:rows],
        SCALE * qkv[rows : 2 * rows],
        qkv[2 * rows :],
        g_o,
        g_up,
        g_down,
        little[:, 0],
        little[:, 1],
        little[:, 2],
        little[:, 3],
        tap,
    )


def solution(mesh):
    tokens = P("fsdp", "seq", None)
    matrix = P("fsdp", None)
    row = P("fsdp")
    in_specs = (tokens,) * 2 + (matrix,) * 6 + (row,) * 4 + (P(),)
    out_specs = (tokens,) * 2 + (matrix,) * 6 + (row,) * 4 + (P(),)
    return jax.shard_map(shards, mesh=mesh, in_specs=in_specs, out_specs=out_specs, check_vma=False)
```

```python
import functools

import jax
import jax.numpy as jnp
from jax import lax
from jax.experimental import pallas as pl
from jax.experimental.pallas import tpu as pltpu
from jax.sharding import PartitionSpec as P

HEADS = 12
HDIM = 64
LANDMARKS = 64
KERNEL = 65
PINV_ITERS = 6
REACH = KERNEL // 2
EDGE = 128
SCALE = HDIM ** (-0.25)
F32 = jnp.float32
BF16 = jnp.bfloat16
VM = 56 * 1024 * 1024


def nn(a, b):
    return jnp.dot(a, b, preferred_element_type=F32)


def nt(a, b):
    return lax.dot_general(a, b, (((1,), (1,)), ((), ())), preferred_element_type=F32)


def tn(a, b):
    return lax.dot_general(a, b, (((0,), (0,)), ((), ())), preferred_element_type=F32)


def split(a):
    high = a.astype(BF16)
    return high, (a - high.astype(F32)).astype(BF16)


def nn3(a, b):
    ah, al = split(a)
    bh, bl = split(b)
    return nn(jnp.concatenate([ah, ah, al], 1), jnp.concatenate([bh, bl, bh], 0))


def nt3(a, b):
    ah, al = split(a)
    bh, bl = split(b)
    return nt(jnp.concatenate([ah, ah, al], 1), jnp.concatenate([bh, bl, bh], 1))


def tn3(a, b):
    ah, al = split(a)
    bh, bl = split(b)
    return tn(jnp.concatenate([ah, ah, al], 0), jnp.concatenate([bh, bl, bh], 0))


def lanes(shape):
    return lax.broadcasted_iota(jnp.int32, shape, len(shape) - 1)


def hs(h):
    return slice(h * HDIM, (h + 1) * HDIM)


def vspec():
    return pl.BlockSpec(memory_space=pltpu.VMEM)


def sspec():
    return pl.BlockSpec(memory_space=pltpu.SMEM)


def aspec():
    return pl.BlockSpec(memory_space=pl.ANY)


def shape(dims, kind):
    return jax.ShapeDtypeStruct(tuple(dims), kind)


def params():
    return pltpu.CompilerParams(vmem_limit_bytes=VM)


def cost(flops, traffic, trans=0):
    return pl.CostEstimate(flops=1, bytes_accessed=1, transcendentals=0)


def call(kernel, args, in_specs, out_shape, out_specs, name, work, grid=(), scratch=(), after=()):
    count, extra = len(args), len(after)

    def body(*refs):
        kernel(*refs[:count], *refs[count + extra :])

    return pl.pallas_call(
        body,
        grid=grid,
        out_shape=out_shape,
        in_specs=list(in_specs) + [aspec()] * extra,
        out_specs=out_specs,
        scratch_shapes=list(scratch),
        compiler_params=params(),
        cost_estimate=work,
        name=name,
    )(*args, *after)


def placed(pieces, whole, sems, me, start):
    rows = pieces[0].shape[0]
    for k, piece in enumerate(pieces):
        at = pl.multiple_of((me ^ k) * rows, 16)
        copy = pltpu.make_async_copy(piece, whole.at[pl.ds(at, rows)], sems.at[k])
        if start:
            copy.start()
        else:
            copy.wait()


def placed_halves(pieces, whole, sems, me, side, start):
    rows = pieces[0].shape[0]
    for i, piece in enumerate(pieces):
        if i < 2:
            at = (me ^ i) * rows
        else:
            at = (me ^ (i // 2 + 1)) * rows + (side ^ (i % 2)) * (rows // 2)
        to = whole.at[pl.ds(pl.multiple_of(at, 16), piece.shape[0])]
        copy = pltpu.make_async_copy(piece, to, sems.at[i])
        if start:
            copy.start()
        else:
            copy.wait()


def xor_rows(out_ref, value, me, count):
    rows = value.shape[0] // count
    for r in range(count):
        at = pl.multiple_of((me ^ r) * rows, 16)
        out_ref[pl.ds(at, rows), :] = value[r * rows : (r + 1) * rows]


def pack_kernel(x_ref, *refs):
    weights, (all_ref, xm_ref, sems) = refs[:-3], refs[-3:]
    copies = []
    for i, w in enumerate(weights):
        to = all_ref.at[:, pl.ds(i * w.shape[1], w.shape[1])]
        copies.append(pltpu.make_async_copy(w, to, sems.at[i]))
        copies[-1].start()
    size, marks, width = xm_ref.shape
    tokens = x_ref.shape[0]
    segment = tokens // marks
    means = [
        jnp.mean(x_ref[m * segment : (m + 1) * segment, :].astype(F32), axis=0, keepdims=True)
        for m in range(marks)
    ]
    means = jnp.concatenate(means, 0)
    for i in range(size):
        xm_ref[i] = means
    for copy in copies:
        copy.wait()


def pack(x, weights, size, marks):
    rows, width = weights[0].shape
    return call(
        pack_kernel,
        (x, *weights),
        [vspec()] * 4,
        [shape((rows, 3 * width), BF16), shape((size, marks, width), F32)],
        [vspec()] * 2,
        "pack",
        cost(1e6, 1e5),
        scratch=[pltpu.SemaphoreType.DMA((3,))],
    )


def front_kernel(count, me_ref, x_ref, xm_ref, *refs):
    pieces = refs[:count]
    outs = refs[count : count + 6]
    xmt_ref, st_ref, msg_ref, qm_ref, km_ref, edge_ref = refs[count + 6 : count + 12]
    flats = refs[count + 12 : count + 18]
    xt_ref, qt_ref, kt_ref, vt_ref, fw_ref, eb_ref = flats
    w_ref, sems, out_sems, head_sems = refs[count + 18 :]
    me = me_ref[0]

    def out(i):
        return pltpu.make_async_copy(flats[i], outs[i], out_sems.at[i])

    def pair_out(i, pair):
        at = pl.ds(pair * 128, 128)
        return pltpu.make_async_copy(flats[i].at[at], outs[i].at[at], head_sems.at[i - 4, pair])

    placed(pieces, w_ref, sems, me, True)
    tokens, width = x_ref.shape
    step = 256
    for b in range(tokens // step):
        rows = slice(b * step, (b + 1) * step)
        xor_rows(xt_ref.at[:, rows], x_ref[rows, :].T, me, count)
    out(0).start()
    high, low = split(xm_ref[...])
    wide = jnp.concatenate([xm_ref[...], jnp.zeros_like(xm_ref)], 0)
    xor_rows(xmt_ref, wide.T.astype(BF16)[:, :LANDMARKS], me, count)
    placed(pieces, w_ref, sems, me, False)
    both = w_ref[:, : 2 * width]
    marks = SCALE * (nn(high, both) + nn(low, both))
    qm = marks[:, :width].astype(BF16)
    km = marks[:, width:].astype(BF16)
    qm_ref[...] = qm
    km_ref[...] = km
    for i, (to, scale) in enumerate(((qt_ref, SCALE), (kt_ref, SCALE), (vt_ref, None))):
        for b in range(tokens // step):
            rows = slice(b * step, (b + 1) * step)
            y = nn(x_ref[rows, :], w_ref[:, i * width : (i + 1) * width])
            if scale is not None:
                y = y * scale
            y = y.astype(BF16)
            if i == 2 and b == 0:
                edge_ref[:REACH] = y[:REACH]
            if i == 2 and b == tokens // step - 1:
                edge_ref[REACH:] = y[step - REACH :]
            to[:, rows] = y.T
        out(1 + i).start()
    lane = lanes((LANDMARKS, 128))
    stats = jnp.zeros((LANDMARKS, 128), F32)
    pair = []
    for h in range(HEADS):
        s = nn(km[:, hs(h)], qt_ref[hs(h), :])
        s = jnp.exp(s - jnp.max(s, axis=0, keepdims=True))
        fw_ref[hs(h), :] = (s * (1.0 / jnp.sum(s, axis=0, keepdims=True))).astype(BF16)
        s = nn(qm[:, hs(h)], kt_ref[hs(h), :])
        top = jnp.max(s, axis=1, keepdims=True).astype(BF16).astype(F32)
        e = jnp.exp(s - top).astype(BF16)
        eb_ref[hs(h), :] = e
        total = jnp.sum(e.astype(F32), axis=1, keepdims=True)
        stats = jnp.where(lane == h, top, stats)
        stats = jnp.where(lane == 16 + h, total, stats)
        pair.append(nt(e, vt_ref[hs(h), :]))
        if h % 2:
            both = jnp.concatenate(pair, 1).astype(BF16)
            for d in range(msg_ref.shape[0]):
                msg_ref[d, h // 2] = both
            pair = []
            pair_out(4, h // 2).start()
            pair_out(5, h // 2).start()
    st_ref[...] = stats
    for d in range(msg_ref.shape[0]):
        msg_ref[d, HEADS // 2] = stat_message(stats)
    for i in range(4):
        out(i).wait()
    for h in range(HEADS // 2):
        pair_out(4, h).wait()
        pair_out(5, h).wait()


def stat_message(stats):
    lane = lanes(stats.shape)
    high = stats.astype(BF16).astype(F32)
    low = pltpu.roll(stats - high, 16, 1)
    return jnp.where((lane >= 32) & (lane < 48), low, high).astype(BF16)


def front(me, x, xm, pieces, size):
    tokens, width = x.shape
    pairs = HEADS // 2
    flat = shape((width, tokens), BF16)
    xt, qt, kt, vt, fw, eb, xmt, st, msg, qm, km, edge = call(
        functools.partial(front_kernel, len(pieces)),
        (me, x, xm, *pieces),
        [sspec(), vspec(), vspec()] + [aspec()] * len(pieces),
        [flat] * 6
        + [
            shape((width, LANDMARKS), BF16),
            shape((LANDMARKS, 128), F32),
            shape((size, pairs + 1, LANDMARKS, 128), BF16),
            shape((LANDMARKS, width), BF16),
            shape((LANDMARKS, width), BF16),
            shape((2 * REACH, width), BF16),
        ],
        [aspec()] * 6 + [vspec()] * 6,
        "front",
        cost(4.5e8, 1.6e6),
        scratch=[pltpu.VMEM((width, tokens), BF16) for _ in range(6)]
        + [
            pltpu.VMEM((width, 3 * width), BF16),
            pltpu.SemaphoreType.DMA((len(pieces),)),
            pltpu.SemaphoreType.DMA((4,)),
            pltpu.SemaphoreType.DMA((2, pairs)),
        ],
    )
    return xt, xmt, qt, kt, vt, fw, eb, st, msg, qm, km, edge


def merged(msg_ref, mixn_ref, st_ref):
    lane = lanes((LANDMARKS, 128))
    size = msg_ref.shape[0]
    stats = []
    for d in range(size):
        got = msg_ref[d, HEADS // 2].astype(F32)
        stats.append(got + jnp.where((lane >= 16) & (lane < 32), pltpu.roll(got, 112, 1), 0.0))
    largest = functools.reduce(jnp.maximum, stats)
    weights = [jnp.exp(jnp.minimum(st - largest, 0.0)) for st in stats]
    total = sum(st * pltpu.roll(w, 16, 1) for st, w in zip(stats, weights))
    st_ref[...] = jnp.where(lane < 16, largest, total)
    for i in range(HEADS // 2):

        def both(a, at):
            return jnp.where(lane < HDIM, a[:, at : at + 1], a[:, at + 1 : at + 2])

        y = sum(msg_ref[d, i].astype(F32) * both(weights[d], 2 * i) for d in range(size))
        mixn_ref[i] = y / both(total, 16 + 2 * i)


def eye(scale):
    n = LANDMARKS
    return jnp.where(
        lax.broadcasted_iota(jnp.int32, (n, n), 0) == lax.broadcasted_iota(jnp.int32, (n, n), 1),
        jnp.float32(scale),
        0.0,
    )


def landmark_softmax(qm, km, h):
    s = nt(qm[:, hs(h)], km[:, hs(h)])
    s = jnp.exp(s - jnp.max(s, axis=1, keepdims=True))
    return s / jnp.sum(s, axis=1, keepdims=True)


def first_inverse(a):
    columns = jnp.max(jnp.sum(a, axis=0, keepdims=True), axis=1, keepdims=True)
    rows = jnp.max(jnp.sum(a, axis=1, keepdims=True), axis=0, keepdims=True)
    return a.T * (1.0 / (columns * rows))


def inverse_kernel(size, me_ref, qm_ref, km_ref, z_ref, a_out, zs, ps, ms, ns, a_ref, p_ref, m_ref, n_ref):
    qm, km = qm_ref[...], km_ref[...]
    every = range(HEADS)
    slots = range(-(-HEADS // size))
    mine = [jnp.minimum(me_ref[1] + size * j, HEADS - 1) for j in slots]
    for h in every:
        a = landmark_softmax(qm, km, h)
        a_ref[h] = a
        z_ref[h] = first_inverse(a)
    for j in slots:
        a_out[j] = a_ref[mine[j]]

    def step(i, carry):
        p = [nn3(a_ref[h], z_ref[h]) for h in every]
        m = [eye(15.0) - nn3(x, eye(7.0) - x) for x in p]
        n = [eye(13.0) - nn3(x, y) for x, y in zip(p, m)]
        for h in every:
            p_ref[h] = p[h]
            m_ref[h] = m[h]
            n_ref[h] = n[h]
        for j in slots:
            ps[i, j] = p_ref[mine[j]]
            ms[i, j] = m_ref[mine[j]]
            ns[i, j] = n_ref[mine[j]]
            zs[i, j] = z_ref[mine[j]]
        for h in every:
            z_ref[h] = 0.25 * nn3(z_ref[h], n[h])
        return carry

    lax.fori_loop(0, PINV_ITERS, step, 0)


def inverse(me, qm, km, size):
    square = (HEADS, LANDMARKS, LANDMARKS)
    few = (-(-HEADS // size), LANDMARKS, LANDMARKS)
    return call(
        functools.partial(inverse_kernel, size),
        (me, qm, km),
        [sspec()] + [vspec()] * 2,
        [shape(square, F32), shape(few, F32)] + [shape((PINV_ITERS,) + few, F32)] * 4,
        [vspec()] * 6,
        "inverse",
        cost(1e8, 1e6),
        scratch=[pltpu.VMEM(square, F32)] * 4,
    )


def half(pair, h):
    return jnp.where(h % 2 == 0, pair[:, :HDIM], pair[:, HDIM:])


def inverse_step(z, p, m, n, a, gz, ga):
    g = 0.25 * gz
    g3 = -tn3(z, g)
    g2 = -tn3(p, g3)
    gp = nt3(g3, m) + nt3(g2, eye(7.0) - p) - tn3(p, g2)
    return nt3(g, n) + tn3(a, gp), ga + nt3(gp, z)


def score_grad(a, gfirst, ga):
    csum = jnp.sum(a, axis=0, keepdims=True)
    rsum = jnp.sum(a, axis=1, keepdims=True)
    cmax = jnp.max(csum, axis=1, keepdims=True)
    rmax = jnp.max(rsum, axis=0, keepdims=True)
    scale = 1.0 / (cmax * rmax)
    gs = jnp.sum(jnp.sum(gfirst * a.T, axis=1, keepdims=True), axis=0, keepdims=True)
    ctop = (csum == cmax).astype(F32)
    rtop = (rsum == rmax).astype(F32)
    gcol = -gs * scale / cmax * ctop / jnp.sum(ctop, axis=1, keepdims=True)
    grow = -gs * scale / rmax * rtop / jnp.sum(rtop, axis=0, keepdims=True)
    g = ga + gfirst.T * scale + gcol + grow
    return a * (g - jnp.sum(g * a, axis=1, keepdims=True))


def widen(out_ref, flat_ref, pair_ref, next_ref, odd):
    width, tokens = flat_ref.shape
    zero = jnp.zeros((EDGE - REACH, width), BF16)
    pair, other = pair_ref[...].astype(F32), next_ref[...].astype(F32)
    before = jnp.where(odd, pair[REACH:], other[REACH:]).astype(BF16)
    after = jnp.where(odd, other[:REACH], pair[:REACH]).astype(BF16)
    out_ref[:, :EDGE] = jnp.concatenate([zero, before], 0).T
    out_ref[:, EDGE : EDGE + tokens] = flat_ref[...]
    out_ref[:, EDGE + tokens :] = jnp.concatenate([after, zero], 0).T


def band(row, step):
    wide = jnp.broadcast_to(row, (step, step + 2 * EDGE))
    return pltpu.roll(wide, 0, 1, stride=1, stride_axis=0).astype(BF16)


def stacked(ref, h, step, margin):
    blocks = (ref.shape[1] - 2 * margin) // step if margin else ref.shape[1] // step
    return jnp.concatenate(
        [ref[hs(h), b * step : (b + 1) * step + 2 * margin] for b in range(blocks)], 0
    )


def pair_rows(tokens):
    return pl.BlockSpec((128, tokens), lambda i: (i, 0))


def pair_lanes(rows):
    return pl.BlockSpec((rows, 128), lambda i: (0, i))


def pair_block(*dims):
    return pl.BlockSpec((1, *dims), lambda i: (i, 0, 0))


def conv_kernel_body(me_ref, vt_ref, pair_ref, next_ref, taps_ref, out_ref, wide_ref):
    widen(wide_ref, vt_ref, pair_ref, next_ref, me_ref[1] % 2 == 1)
    step = 256
    for h in range(HEADS):
        y = nt(stacked(wide_ref, h, step, EDGE), band(taps_ref[h : h + 1, :], step))
        for b in range(vt_ref.shape[1] // step):
            out_ref[hs(h), b * step : (b + 1) * step] = y[b * HDIM : (b + 1) * HDIM, :]


def conv(me, vt, edges, taps):
    width, tokens = vt.shape
    return call(
        conv_kernel_body,
        (me, vt, *edges, taps),
        [sspec()] + [vspec()] * 4,
        shape(vt.shape, F32),
        vspec(),
        "conv",
        cost(2e9, 6e6),
        scratch=[pltpu.VMEM((width, tokens + 2 * EDGE), BF16)],
    )


def gelu_pair(x):
    phi = 0.5 * (1.0 + lax.erf(x * (0.5**0.5)))
    return x * phi, phi + x * ((0.5 / jnp.pi) ** 0.5 * jnp.exp(-0.5 * x * x))


def norm_stats(r):
    center = r - jnp.mean(r, axis=-1, keepdims=True)
    rstd = lax.rsqrt(jnp.mean(center * center, axis=-1, keepdims=True) + 1e-05)
    return center * rstd, rstd


def norm_back(gy, xhat, rstd):
    return rstd * (
        gy - jnp.mean(gy, axis=-1, keepdims=True) - xhat * jnp.mean(gy * xhat, axis=-1, keepdims=True)
    )


STEP = 256


def whole(a):
    return pl.BlockSpec(a.shape, lambda i, n=a.ndim: (0,) * n)


def fixed(*dims):
    return pl.BlockSpec(dims, lambda i, n=len(dims): (0,) * n)


def tall(rows):
    return pl.BlockSpec((rows, STEP), lambda i: (0, i))


def row(width):
    return pl.BlockSpec((STEP, width), lambda i: (i, 0))


def mid_kernel(count, me_ref, z_ref, msg_ref, fw_ref, conv_ref, x_ref, ct_ref, gains_ref, *refs):
    halves = 2 * count - 2
    wo, down, up = refs[:count], refs[count : 2 * count], refs[2 * count : 2 * count + halves]
    (ctx_ref, hidt_ref, act_ref, out_ref, redt_ref, ge_ref, first_ref, branch_ref, gct_ref, edge_ref,
     sums_ref, comb_ref, mixn_ref, st_ref, gc_ref, wo_ref, up_ref, down_ref, slope_ref,
     sems, up_sems) = refs[2 * count + halves :]
    me, side = me_ref[0], me_ref[1] % 2
    at = pl.program_id(0)
    begin = at == 0
    part = up_ref.shape[1] // count

    @pl.when(begin)
    def _():
        placed(wo, wo_ref, sems.at[0], me, True)
        placed_halves(up, up_ref, up_sems, me, side, True)
        placed(down, down_ref, sems.at[1], me, True)
        merged(msg_ref, mixn_ref, st_ref)
        for i in range(HEADS // 2):
            mixed = mixn_ref[i]
            comb_ref[i] = jnp.concatenate(
                [nn3(z_ref[2 * i], mixed[:, :HDIM]), nn3(z_ref[2 * i + 1], mixed[:, HDIM:])], 1
            ).astype(BF16)
        sums_ref[...] = jnp.zeros_like(sums_ref)
        gc_ref[...] = jnp.zeros_like(gc_ref)
        placed(wo, wo_ref, sems.at[0], me, False)

    for h in range(HEADS):
        att = tn(comb_ref[h // 2][:, hs(h % 2)], fw_ref[hs(h), :])
        ctx_ref[hs(h), :] = (att + conv_ref[hs(h), :]).astype(BF16)
    branch = nn(ctx_ref[...].T, wo_ref[...])
    xhat1, rstd1 = norm_stats(x_ref[...].astype(F32) + branch)
    hidden = xhat1 * gains_ref[0:1, :] + gains_ref[1:2, :]
    hid = hidden.astype(BF16)
    xor_rows(hidt_ref, hid.T, me, count)

    @pl.when(begin)
    def _():
        placed_halves(up, up_ref, up_sems, me, side, False)

    for c in range(count):
        cols = slice(c * part, (c + 1) * part)
        act, slope = gelu_pair(nn(hid, up_ref[:, cols]))
        act_ref[:, cols] = act.astype(BF16)
        slope_ref[:, cols] = slope.astype(BF16)

    @pl.when(begin)
    def _():
        placed(down, down_ref, sems.at[1], me, False)

    xhat, rstd = norm_stats(hidden + nn(act_ref[...], down_ref[...]))
    out_ref[...] = (xhat * gains_ref[2:3, :] + gains_ref[3:4, :]).astype(BF16)
    ct = ct_ref[...].astype(F32)
    sums_ref[2:3, :] = sums_ref[2:3, :] + jnp.sum(ct * xhat, axis=0, keepdims=True)
    sums_ref[3:4, :] = sums_ref[3:4, :] + jnp.sum(ct, axis=0, keepdims=True)
    second = norm_back(ct * gains_ref[2:3, :], xhat, rstd)
    red = second.astype(BF16)
    redt_ref[...] = red.T
    for k in range(count):
        cols = slice(k * part, (k + 1) * part)
        ge = nt(red, down_ref[cols, :]) * slope_ref[:, cols].astype(F32)
        ge_ref[:, cols] = ge.astype(BF16)
    g = second + nt(ge_ref[...], up_ref[...])
    sums_ref[0:1, :] = sums_ref[0:1, :] + jnp.sum(g * xhat1, axis=0, keepdims=True)
    sums_ref[1:2, :] = sums_ref[1:2, :] + jnp.sum(g, axis=0, keepdims=True)
    first = norm_back(g * gains_ref[0:1, :], xhat1, rstd1)
    first_ref[...] = first
    back = first.astype(BF16)
    branch_ref[...] = back
    gctx = nt(back, wo_ref[...]).astype(BF16)

    @pl.when(begin)
    def _():
        edge_ref[:REACH] = gctx[:REACH]

    @pl.when(at == pl.num_programs(0) - 1)
    def _():
        edge_ref[REACH:] = gctx[gctx.shape[0] - REACH :]

    gct_ref[...] = gctx.T
    for i in range(HEADS // 2):
        gc_ref[i] = gc_ref[i] + jnp.concatenate(
            [nt(fw_ref[hs(h), :], gct_ref[hs(h), :]) for h in (2 * i, 2 * i + 1)], 1
        )


def mid(me, z, msgs, fw, convt, x, ct, gains, wo, up, down, after=()):
    tokens, width = x.shape
    ff = up[0].shape[1]
    pairs = HEADS // 2
    pieces = (*wo, *down, *up)
    flat, wide = shape((width, tokens), BF16), shape((tokens, ff), BF16)
    return call(
        functools.partial(mid_kernel, len(wo)),
        (me, z, msgs, fw, convt, x, ct, gains, *pieces),
        [sspec(), whole(z), whole(msgs), tall(width), tall(width), row(width), row(width), whole(gains)]
        + [aspec()] * len(pieces),
        [
            flat,
            flat,
            wide,
            shape((tokens, width), BF16),
            flat,
            wide,
            shape((tokens, width), F32),
            shape((tokens, width), BF16),
            flat,
            shape((2 * REACH, width), BF16),
            shape((8, width), F32),
            shape((pairs, LANDMARKS, 128), BF16),
            shape((pairs, LANDMARKS, 128), F32),
            shape((LANDMARKS, 128), F32),
            shape((pairs, LANDMARKS, 128), F32),
        ],
        [tall(width), tall(width), row(ff), row(width), tall(width), row(ff), row(width), row(width),
         tall(width), fixed(2 * REACH, width), fixed(8, width),
         fixed(pairs, LANDMARKS, 128), fixed(pairs, LANDMARKS, 128), fixed(LANDMARKS, 128),
         fixed(pairs, LANDMARKS, 128)],
        "mid",
        cost(2e9, 3e6),
        grid=(tokens // STEP,),
        scratch=[
            pltpu.VMEM((width, width), BF16),
            pltpu.VMEM((width, ff), BF16),
            pltpu.VMEM((ff, width), BF16),
            pltpu.VMEM((STEP, ff), BF16),
            pltpu.SemaphoreType.DMA((2, len(wo))),
            pltpu.SemaphoreType.DMA((len(up),)),
        ],
        after=after,
    )


def grad_down_kernel(count, me_ref, red_ref, act_ref, *outs):
    part = act_ref.shape[1] // count
    for k in range(count):
        at = pl.ds(pl.multiple_of((me_ref[0] ^ k) * part, 128), part)
        outs[k][...] = nn(red_ref[...], act_ref[:, at]).astype(BF16)


def grad_down(count, me, redt, act, after=()):
    width = redt.shape[0]
    return call(
        functools.partial(grad_down_kernel, count),
        (me, redt, act),
        [sspec(), vspec(), vspec()],
        [shape((width, act.shape[1] // count), BF16)] * count,
        [vspec()] * count,
        "grad_down",
        cost(5e8, 1e6),
        after=after,
    )


def grad_up_kernel(count, hid_ref, ge_ref, *outs):
    y = nn(hid_ref[...], ge_ref[...]).astype(BF16)
    rows = y.shape[0] // count
    for k in range(count):
        outs[k][...] = y[k * rows : (k + 1) * rows]


def grad_up(count, hidt, ge, after=()):
    width, tokens = hidt.shape
    ff = ge.shape[1]
    step = 768
    return call(
        functools.partial(grad_up_kernel, count),
        (hidt, ge),
        [whole(hidt), pl.BlockSpec((tokens, step), lambda i: (0, i))],
        [shape((width // count, ff), BF16)] * count,
        [pl.BlockSpec((width // count, step), lambda i: (0, i))] * count,
        "grad_up",
        cost(5e8, 1e6),
        grid=(ff // step,),
        after=after,
    )


class Moves:
    def __init__(self, sems):
        self.sems, self.used, self.open = sems, 0, []

    def start(self, src, dst):
        copy = pltpu.make_async_copy(src, dst, self.sems.at[self.used])
        self.used += 1
        copy.start()
        self.open.append(copy)
        return copy

    def wait(self, *copies):
        for copy in copies or list(self.open):
            copy.wait()
            self.open.remove(copy)


def gap_kernel(count, me_ref, gct_hbm, fw_hbm, qt_hbm, vt_hbm, ctx_hbm, branch_hbm, comb_ref, km_ref,
               vb_ref, va_ref, gb_ref, ga_ref, taps_ref, sums_ref, *refs):
    outs = refs[:count]
    (gq_hbm, gvc_hbm, gkm_ref, gct_ref, fw_ref, qt_ref, vt_ref, ctx_ref, branch_ref, gq_ref, gvc_ref,
     vwide, gwide, y_ref, sems) = refs[count:]
    moves = Moves(sems)
    lead = [
        moves.start(a, b)
        for a, b in ((gct_hbm, gct_ref), (fw_hbm, fw_ref), (qt_hbm, qt_ref))
    ]
    values = moves.start(vt_hbm, vt_ref)
    rest = [moves.start(ctx_hbm, ctx_ref), moves.start(branch_hbm, branch_ref)]
    km = km_ref[...]
    moves.wait(*lead)
    pair = []
    for h in range(HEADS):
        comb = comb_ref[h // 2][:, hs(h % 2)]
        pf = fw_ref[hs(h), :].astype(F32)
        g = nn(comb, gct_ref[hs(h), :])
        gs = (pf * (g - jnp.sum(pf * g, axis=0, keepdims=True))).astype(BF16)
        gq_ref[hs(h), :] = tn(km[:, hs(h)], gs).astype(BF16)
        pair.append(nt(gs, qt_ref[hs(h), :]))
        if h % 2:
            gkm_ref[:, (h - 1) * HDIM : (h + 1) * HDIM] = jnp.concatenate(pair, 1)
            pair = []
    moves.start(gq_ref, gq_hbm)
    moves.wait(values)
    odd = me_ref[1] % 2 == 1
    widen(vwide, vt_ref, vb_ref, va_ref, odd)
    widen(gwide, gct_ref, gb_ref, ga_ref, odd)
    step = 256
    tokens = vt_ref.shape[1]
    flip = (
        lax.broadcasted_iota(jnp.int32, (step, step), 0)
        + lax.broadcasted_iota(jnp.int32, (step, step), 1)
        == step - 1
    ).astype(BF16)
    rows = []
    for h in range(HEADS):
        y = nt(stacked(gwide, h, step, EDGE), band(taps_ref[h : h + 1, :], step))
        for b in range(tokens // step):
            gvc_ref[hs(h), b * step : (b + 1) * step] = y[b * HDIM : (b + 1) * HDIM, :]
        turned = nn(stacked(gct_ref, h, step, 0), flip).astype(BF16)
        d = tn(turned, stacked(vwide, h, step, EDGE))
        d = pltpu.roll(d, 0, 1, stride=1, stride_axis=0)
        rows.append(jnp.sum(d, axis=0, keepdims=True))
    moves.start(gvc_ref, gvc_hbm)
    rows = jnp.concatenate(rows + [jnp.zeros((4, step + 2 * EDGE), F32)], 0)
    first = step - 1 + EDGE - REACH
    taps = pltpu.roll(rows, step + 2 * EDGE - first, 1)[:HEADS, :128]
    width = ctx_ref.shape[0]
    taps = jnp.concatenate([taps, jnp.zeros((HEADS, width - 128), F32)], 1)
    little = jnp.concatenate(
        [sums_ref[0:4, :], taps, jnp.zeros((128 - 4 - HEADS, width), F32)], 0
    )
    y_ref[:, width:] = little.T.astype(BF16)
    moves.wait(*rest)
    y_ref[:, :width] = nn(ctx_ref[...], branch_ref[...]).astype(BF16)
    size = width // count
    for k in range(count):
        outs[k][...] = y_ref[pl.ds(pl.multiple_of((me_ref[0] ^ k) * size, 16), size), :]
    moves.wait()


def gap(count, me, gct, fw, qt, vt, ctxt, branch, comb, km, vb, va, gb, ga, taps, sums, after=()):
    width, tokens = vt.shape
    flat = pltpu.VMEM((width, tokens), BF16)
    wide = pltpu.VMEM((width, tokens + 2 * EDGE), BF16)
    *pieces, gq, gvc, gkm = call(
        functools.partial(gap_kernel, count),
        (me, gct, fw, qt, vt, ctxt, branch, comb, km, vb, va, gb, ga, taps, sums),
        [sspec()] + [aspec()] * 6 + [vspec()] * 8,
        [shape((width // count, width + 128), BF16)] * count
        + [shape(gct.shape, BF16), shape(gct.shape, F32), shape(km.shape, F32)],
        [vspec()] * count + [aspec()] * 2 + [vspec()],
        "gap",
        cost(1e9, 1e6),
        scratch=[flat] * 5
        + [
            pltpu.VMEM((tokens, width), BF16),
            flat,
            pltpu.VMEM((width, tokens), F32),
            wide,
            wide,
            pltpu.VMEM((width, width + 128), BF16),
            pltpu.SemaphoreType.DMA((8,)),
        ],
        after=after,
    )
    return pieces, gq, gvc, gkm


def rear_kernel(count, size, me_ref, eb_hbm, vt_hbm, kt_hbm, gvc_hbm, xt_hbm, gq_hbm, z_ref, gc_ref,
                mixn_ref, st_ref, own_ref, qm_ref, km_ref, gkmp_ref, xmt_ref, a_ref, zs, ps, ms, ns, *refs):
    outs = refs[:count]
    (gk_hbm, gv_hbm, gqm_ref, gkm_ref, eb_ref, vt_ref, kt_ref, gvc_ref, xt_ref, gq_ref, gk_ref, gv_ref,
     y_ref, sems) = refs[count:]
    moves = Moves(sems)
    early = [
        moves.start(a, b)
        for a, b in ((vt_hbm, vt_ref), (eb_hbm, eb_ref), (kt_hbm, kt_ref), (gvc_hbm, gvc_ref))
    ]
    late = [moves.start(xt_hbm, xt_ref), moves.start(gq_hbm, gq_ref)]
    qm, km = qm_ref[...], km_ref[...]
    lane = lanes((LANDMARKS, 128))
    slots = range(-(-HEADS // size))
    heads = [me_ref[1] + size * j for j in slots]
    safe = [jnp.minimum(h, HEADS - 1) for h in heads]
    gz = [nt3(half(gc_ref[h // 2], h), half(mixn_ref[h // 2], h)) for h in safe]
    ga = [jnp.zeros((LANDMARKS, LANDMARKS), F32) for _ in slots]
    stats = st_ref[...]
    scale = jnp.exp(own_ref[...] - stats)
    moves.wait(*early)
    for p in range(HEADS // 2):
        if p < PINV_ITERS:
            i = PINV_ITERS - 1 - p
            for j in slots:
                gz[j], ga[j] = inverse_step(
                    zs[i, j], ps[i, j], ms[i, j], ns[i, j], a_ref[j], gz[j], ga[j]
                )
        pair = []
        for h in (2 * p, 2 * p + 1):
            gmix = tn3(z_ref[h], gc_ref[p][:, hs(h % 2)]).astype(BF16)
            dot = jnp.sum(gmix.astype(F32) * mixn_ref[p][:, hs(h % 2)], axis=1, keepdims=True)
            factor = scale[:, h : h + 1] / stats[:, 16 + h : 17 + h]
            pb = eb_ref[hs(h), :].astype(F32) * factor
            gs = (pb * (nn(gmix, vt_ref[hs(h), :]) - dot)).astype(BF16)
            gk_ref[hs(h), :] = tn(qm[:, hs(h)], gs).astype(BF16)
            gv_ref[hs(h), :] = (tn(gmix, pb.astype(BF16)) + gvc_ref[hs(h), :]).astype(BF16)
            pair.append(nt(gs, kt_ref[hs(h), :]))
        both = slice(p * 128, p * 128 + 128)
        gqm_ref[:, both] = jnp.concatenate(pair, 1)
        gkm_ref[:, both] = gkmp_ref[:, both]
    moves.start(gk_ref, gk_hbm)
    moves.start(gv_ref, gv_hbm)
    moves.wait(*late)
    width = xt_ref.shape[0]
    rows = width // count

    def weight(i, y):
        y_ref[i] = y.astype(BF16)
        for k in range(count):
            moves.start(y_ref.at[i, pl.ds(k * rows, rows)], outs[k].at[i])

    weight(2, nt(xt_ref[...], gv_ref[...]))
    for j in slots:
        h = safe[j]
        high, low = split(score_grad(a_ref[j], gz[j], ga[j]))
        at = pl.ds(pl.multiple_of(h // 2 * 128, 128), 128)
        qmh = half(qm_ref[:, at].astype(F32), h).astype(BF16)
        kmh = half(km_ref[:, at].astype(F32), h).astype(BF16)
        gq = nn(jnp.concatenate([high, low], 1), jnp.concatenate([kmh] * 2, 0))
        gk = tn(jnp.concatenate([high, low], 0), jnp.concatenate([qmh] * 2, 0))
        mine = ((lane >= HDIM) == (h % 2 == 1)) & (heads[j] < HEADS)
        gqm_ref[:, at] = gqm_ref[:, at] + jnp.where(mine, jnp.concatenate([gq, gq], 1), 0.0)
        gkm_ref[:, at] = gkm_ref[:, at] + jnp.where(mine, jnp.concatenate([gk, gk], 1), 0.0)
    weight(0, nt(xt_ref[...], gq_ref[...]) + nn(xmt_ref[...], gqm_ref[...].astype(BF16)))
    weight(1, nt(xt_ref[...], gk_ref[...]) + nn(xmt_ref[...], gkm_ref[...].astype(BF16)))
    moves.wait()


def rear(count, size, me, eb, vt, kt, gvc, xt, gq, z, gc, mixn, stats, own, qm, km, gkm, xmt, a, saved,
         after=()):
    width, tokens = vt.shape
    rows = width // count
    flat = pltpu.VMEM((width, tokens), BF16)
    mark = shape(qm.shape, F32)
    *pieces, gk, gv, gqm, gkm = call(
        functools.partial(rear_kernel, count, size),
        (me, eb, vt, kt, gvc, xt, gq, z, gc, mixn, stats, own, qm, km, gkm, xmt, a, *saved),
        [sspec()] + [aspec()] * 6 + [vspec()] * 14,
        [shape((3, rows, width), BF16)] * count + [shape(vt.shape, BF16)] * 2 + [mark] * 2,
        [aspec()] * (count + 2) + [vspec()] * 2,
        "rear",
        cost(2e9, 2e6),
        scratch=[flat] * 3
        + [pltpu.VMEM((width, tokens), F32)]
        + [flat] * 4
        + [
            pltpu.VMEM((3, width, width), BF16),
            pltpu.SemaphoreType.DMA((8 + 3 * count,)),
        ],
        after=after,
    )
    return [piece.reshape(3 * rows, width) for piece in pieces], gk, gv, gqm, gkm


def last_kernel(count, me_ref, gq_ref, gk_ref, gv_ref, first_ref, *refs):
    pieces = refs[:count]
    out_ref, w_ref, sems = refs[count:]
    me = me_ref[0]
    width = gq_ref.shape[0]

    @pl.when(pl.program_id(0) == 0)
    def _():
        placed(pieces, w_ref, sems, me, True)
        placed(pieces, w_ref, sems, me, False)

    wq, wk, wv = (w_ref[:, i * width : (i + 1) * width] for i in range(3))
    g = SCALE * (nn(wq, gq_ref[...]) + nn(wk, gk_ref[...])) + nn(wv, gv_ref[...])
    out_ref[...] = first_ref[...] + g.T


def last(me, gq, gk, gv, first, pieces, after=()):
    width, tokens = gq.shape
    return call(
        functools.partial(last_kernel, len(pieces)),
        (me, gq, gk, gv, first, *pieces),
        [sspec(), tall(width), tall(width), tall(width), row(width)] + [aspec()] * len(pieces),
        shape((tokens, width), F32),
        row(width),
        "last",
        cost(4e8, 1e6),
        grid=(tokens // STEP,),
        scratch=[
            pltpu.VMEM((width, 3 * width), BF16),
            pltpu.SemaphoreType.DMA((len(pieces),)),
        ],
        after=after,
    )


def share_kernel(segment, count, me_ref, own_ref, most_ref, *refs):
    pieces = refs[:count]
    out_ref, w_ref, sems = refs[count:]
    own = own_ref[...]
    width = own.shape[1] // 2
    pieces = [piece.at[:, pl.ds(0, 2 * width)] for piece in pieces]
    placed(pieces, w_ref, sems, me_ref[0], True)
    placed(pieces, w_ref, sems, me_ref[0], False)
    marks = (SCALE / segment) * (
        nt(own[:, :width].astype(BF16), w_ref[:, :width])
        + nt(own[:, width:].astype(BF16), w_ref[:, width : 2 * width])
    )
    for m in range(own.shape[0]):
        rows = slice(m * segment, (m + 1) * segment)
        out_ref[rows, :] = (most_ref[rows, :] + marks[m : m + 1, :]).astype(BF16)


def share(me, own, most, pieces):
    tokens, width = most.shape
    return call(
        functools.partial(share_kernel, tokens // own.shape[0], len(pieces)),
        (me, own, most, *pieces),
        [sspec(), vspec(), vspec()] + [aspec()] * len(pieces),
        shape(most.shape, BF16),
        vspec(),
        "share",
        cost(4e8, 1e6),
        scratch=[
            pltpu.VMEM((width, 2 * width), BF16),
            pltpu.SemaphoreType.DMA((len(pieces),)),
        ],
    )


def bits(axis):
    size = lax.axis_size(axis)
    assert size & (size - 1) == 0
    return [1 << i for i in range(size.bit_length() - 1)]


def swap(array, axis, bit):
    return lax.ppermute(array, axis, [(i, i ^ bit) for i in range(lax.axis_size(axis))])


def neighbours(array):
    size = lax.axis_size("seq")
    odd = [(i, i + 1) for i in range(1, size - 1, 2)]
    return swap(array, "seq", 1), lax.ppermute(array, "seq", odd + [(j, i) for i, j in odd])


def spread(pieces, axis, steps):
    for bit in steps:
        pieces = {**pieces, **{k | bit: swap(piece, axis, bit) for k, piece in pieces.items()}}
    return pieces


def far(array, axis):
    return spread({0: array}, axis, bits(axis)[1:])


def near(pieces, axis):
    pieces = spread(pieces, axis, bits(axis)[:1])
    return [pieces[k] for k in range(lax.axis_size(axis))]


def gathered(array, axis):
    return near(far(array, axis), axis)


def tie(*values):
    return lax.optimization_barrier(values)


def rows_out(array, groups=None):
    size = len(groups[0]) if groups else lax.axis_size("seq")
    blocks = array.reshape(size, -1, array.shape[1])
    return lax.all_to_all(blocks, "seq", 0, 0, axis_index_groups=groups)


def rows_in(blocks):
    return jnp.sum(blocks.astype(F32), axis=0)


def copies(array, axis, groups=None):
    size = len(groups[0]) if groups else lax.axis_size(axis)
    blocks = jnp.broadcast_to(array[None], (size, *array.shape))
    return lax.all_to_all(blocks, axis, 0, 0, axis_index_groups=groups)


class Total:
    def __init__(self, pieces, order):
        self.pieces = dict(enumerate(pieces))
        self.order = list(order)
        self.back = [step for step in reversed(order) if step[0] != "swap"]
        self.got = None

    def send(self, *values):
        if not self.order and not self.back:
            return values
        back = not self.order
        kind, what = self.back[0] if back else self.order[0]
        axis = "seq"
        if kind == "swap":
            axis = "fsdp"
            sent = {k: p for k, p in self.pieces.items() if k & what}
            self.pieces = {k: p for k, p in self.pieces.items() if not k & what}
        elif kind == "half" and not back:
            piece = self.pieces[0]
            upper = ((lax.axis_index("seq") & what) != 0).astype(jnp.int32)
            half = piece.shape[0] // 2
            self.pieces = {0: lax.dynamic_slice_in_dim(piece, upper * half, half, 0)}
            sent = {0: lax.dynamic_slice_in_dim(piece, (1 - upper) * half, half, 0)}
        elif kind == "rows" and back:
            size = len(what[0]) if what else lax.axis_size("seq")
            sent = {0: jnp.broadcast_to(self.pieces[0][None], (size, *self.pieces[0].shape))}
        elif kind == "rows":
            size = len(what[0]) if what else lax.axis_size("seq")
            sent = {0: self.pieces[0].reshape(size, -1, self.pieces[0].shape[1])}
        else:
            sent = dict(self.pieces)
        if values:
            sent, values = tie(sent, values)
        if kind == "rows":
            self.got = {
                k: lax.all_to_all(p, "seq", 0, 0, axis_index_groups=what) for k, p in sent.items()
            }
        else:
            self.got = {k: swap(p, axis, what) for k, p in sent.items()}
        return values

    def take(self):
        if self.order:
            kind, what = self.order.pop(0)
            if kind == "rows":
                self.pieces = {0: rows_in(self.got[0]).astype(BF16)}
            else:
                extra = what if kind == "swap" else 0
                self.pieces = {
                    k: (p.astype(F32) + self.got[k | extra].astype(F32)).astype(BF16)
                    for k, p in self.pieces.items()
                }
        else:
            kind, what = self.back.pop(0)
            mine, other = self.pieces[0], self.got[0]
            if kind == "rows":
                self.pieces = {0: other.reshape(-1, other.shape[2])}
            else:
                upper = (lax.axis_index("seq") & what) != 0
                self.pieces = {
                    0: jnp.where(
                        upper, jnp.concatenate([other, mine], 0), jnp.concatenate([mine, other], 0)
                    )
                }
        self.got = None

    def step(self, *values):
        self.got, values = tie(self.got, values)
        self.take()
        return self.send(*values)

    def finish(self):
        while self.got is not None:
            self.step()
        return self.pieces[0]


def orders():
    size = lax.axis_size("seq")
    over = [("swap", bit) for bit in bits("fsdp")]
    parts = size // 4
    groups = [[low + parts * high for high in range(4)] for low in range(parts)]
    near = [("half", bit) for bit in bits("seq") if bit < parts]
    tree = over + [("half", bit) for bit in bits("seq")]
    return over, over + near + [("rows", groups)], over + [("rows", None)], tree


def shards(
    inputs,
    cotangent,
    query_weight,
    key_weight,
    value_weight,
    output_weight,
    up_weight,
    down_weight,
    norm_gain,
    norm_shift,
    final_gain,
    final_shift,
    conv_kernel,
):
    x = inputs[0]
    ct = cotangent[0]
    tokens, width = x.shape
    marks = LANDMARKS // lax.axis_size("seq")
    segment = tokens // marks
    count = lax.axis_size("fsdp")
    rows = width // count
    here = lax.axis_index("fsdp")
    place = lax.axis_index("seq")
    size = lax.axis_size("seq")
    me = jnp.stack([here, place]).astype(jnp.int32)
    over, nested, flat, tree = orders()

    packed, xm = pack(x, (query_weight, key_weight, value_weight), size, marks)
    first_weights = far(packed, "fsdp")
    space = 256 + 2 * EDGE
    taps = jnp.pad(conv_kernel.T, ((0, 4), (EDGE - REACH, space - KERNEL - EDGE + REACH)))
    spat = jnp.pad(conv_kernel[::-1].T, ((0, 4), (EDGE - REACH, space - KERNEL - EDGE + REACH)))
    xm, taps, spat, me = tie(xm, taps, spat, me)
    xm = lax.all_to_all(xm, "seq", 0, 0).reshape(LANDMARKS, width)
    gains = jnp.stack([norm_gain, norm_shift, final_gain, final_shift] * 2)
    gains = gathered(gains, "fsdp")
    first_weights, gains, xm, output_weight = tie(first_weights, gains, xm, output_weight)
    first_weights, up_weight, output_weight, down_weight = tie(
        first_weights, up_weight, output_weight, down_weight
    )
    wqkv = near(first_weights, "fsdp")
    side = (place & 1).astype(jnp.int32)
    up_far = spread({0: lax.dynamic_slice_in_dim(up_weight, side * (rows // 2), rows // 2, 0)}, "fsdp", bits("fsdp")[1:])
    up_far = [up_far[k] for k in range(2, count, 2)]
    wo = far(output_weight, "fsdp")
    down = far(down_weight, "fsdp")
    source = lax.broadcasted_iota(jnp.int32, (8, width), 1) // rows ^ here
    gains = sum(
        jnp.where(source == k, jnp.concatenate([piece.astype(F32)] * count, 1), 0.0)
        for k, piece in enumerate(gains)
    )

    (xt, xmt, qt, kt, vt, fw, eb, own, msg, qm, km, v_edge) = front(me, x, xm, wqkv, size)
    v_edges = neighbours(v_edge)
    msg, up_far, v_edges = tie(msg, up_far, v_edges)
    msgs = lax.all_to_all(msg, "seq", 0, 0)
    up_other = [swap(piece, "seq", 1) for piece in up_far]
    z, a, *saved = inverse(me, qm, km, size)
    v_edges, z = tie(v_edges, z)
    convt = conv(me, vt, v_edges, taps)
    down, wo, convt, up_far, up_other = tie(down, wo, convt, up_far, up_other)
    up = [up_weight, swap(up_weight, "fsdp", 1)]
    for mine, other in zip(up_far, up_other):
        up += [mine, other, swap(mine, "fsdp", 1), swap(other, "fsdp", 1)]
    wo = near(wo, "fsdp")
    down = near(down, "fsdp")

    (ctxt, hidt, act, out, redt, ge, first, branch, gct, g_edge, sums, comb, mixn, stats, gc) = mid(
        me, z, msgs, fw, convt, x, ct, gains, wo, up, down
    )
    hops = bits("seq")

    def exchange(bit):
        return swap(gc.astype(BF16), "seq", bit)

    got = exchange(hops[0])
    g_edges = neighbours(g_edge)
    d_up = grad_up(count, hidt, ge)
    t_up = Total(d_up, tree)
    t_up.send()
    got, d_up, g_edges = tie(got, d_up, g_edges)
    gc = gc + got.astype(F32)
    got = exchange(hops[1])
    (act,) = t_up.step(act)
    d_down = grad_down(count, me, redt, act, after=d_up)
    t_down = Total(d_down, over)
    t_down.send()
    got, d_down = tie(got, d_down)
    gc = gc + got.astype(F32)
    got = exchange(hops[2])
    gct, d_down = t_down.step(gct, d_down)
    d_o, gq, gvc, gkm = gap(
        count, me, gct, fw, qt, vt, ctxt, branch, comb, km, *v_edges, *g_edges, spat, sums, after=d_down
    )
    t_o = Total(d_o, over)
    t_o.send()
    got, gvc = tie(got, gvc)
    gc = gc + got.astype(F32)
    for bit in hops[3:]:
        gc = gc + exchange(bit).astype(F32)
    (gc,) = t_up.step(gc)
    (gc,) = t_o.step(gc)
    d_qkv, gk, gv, gqm, gkm = rear(
        count, size, me, eb, vt, kt, gvc, xt, gq, z, gc, mixn, stats, own, qm, km, gkm, xmt, a, saved, after=d_o
    )
    t_qkv = Total(d_qkv, tree)
    t_qkv.send()
    landed = rows_out(jnp.concatenate([gqm, gkm], 1).astype(BF16))
    while t_o.got is not None:
        (gk,) = t_o.step(gk)
    g_o = t_o.pieces[0]
    while t_down.got is not None:
        (gk,) = t_down.step(gk)
    part = t_down.pieces[0].shape[1]
    g_down = t_down.pieces[0].reshape(-1, width)
    sizes = [g_down.shape[0], rows, rows * 128 // width]
    both = jnp.concatenate([g_down, g_o[:, :width], g_o[:, width:].reshape(-1, width)], 0)
    t_both = Total([both], tree[len(over) :])
    (gk,) = t_both.send(gk)
    (gk,) = t_up.step(gk)
    for _ in over[:-1]:
        (gk,) = t_qkv.step(gk)
    most = last(me, gq, gk, gv, first, wqkv)
    for t in (t_up, t_both):
        (most,) = t.step(most)
    landed, most = tie(landed, most)
    grad_x = share(me, rows_in(landed), most, wqkv)
    g_up = g_both = None
    while any(t.got is not None for t in (t_qkv, t_up, t_both)):
        for t in (t_qkv, t_up, t_both):
            if t.got is not None:
                (grad_x,) = t.step(grad_x)
        if g_up is None and t_up.got is None:
            g_up, grad_x = tie(t_up.pieces[0].astype(F32), grad_x)
        if g_both is None and t_both.got is None:
            both = t_both.pieces[0].astype(F32)
            little = both[sizes[0] + sizes[1] :].reshape(rows, 128)
            tap = jnp.where(here == 0, little[:KERNEL, 4 : 4 + HEADS], 0.0)
            g_both = (
                both[: sizes[0]].reshape(width, part).T,
                both[sizes[0] : sizes[0] + sizes[1]],
                [little[:, i] for i in range(4)],
                tap,
            )
            g_both, grad_x = tie(g_both, grad_x)
            g_down, g_o, g_gains, tap = g_both
            for _, bit in over:
                tap = tap + swap(tap, "fsdp", bit)
    qkv = t_qkv.pieces[0].astype(F32)

    return (
        out[None],
        grad_x[None],
        SCALE * qkv[:rows],
        SCALE * qkv[rows : 2 * rows],
        qkv[2 * rows :],
        g_o,
        g_up,
        g_down,
        g_gains[0],
        g_gains[1],
        g_gains[2],
        g_gains[3],
        tap,
    )


def solution(mesh):
    tokens = P("fsdp", "seq", None)
    matrix = P("fsdp", None)
    row = P("fsdp")
    in_specs = (tokens,) * 2 + (matrix,) * 6 + (row,) * 4 + (P(),)
    out_specs = (tokens,) * 2 + (matrix,) * 6 + (row,) * 4 + (P(),)
    return jax.shard_map(shards, mesh=mesh, in_specs=in_specs, out_specs=out_specs, check_vma=False)
```

```python
import functools

import jax
import jax.numpy as jnp
from jax import lax
from jax.experimental import pallas as pl
from jax.experimental.pallas import tpu as pltpu
from jax.sharding import PartitionSpec as P

HEADS = 12
HDIM = 64
LANDMARKS = 64
KERNEL = 65
PINV_ITERS = 6
REACH = KERNEL // 2
EDGE = 128
SCALE = HDIM ** (-0.25)
F32 = jnp.float32
BF16 = jnp.bfloat16
VM = 56 * 1024 * 1024


def nn(a, b):
    return jnp.dot(a, b, preferred_element_type=F32)


def nt(a, b):
    return lax.dot_general(a, b, (((1,), (1,)), ((), ())), preferred_element_type=F32)


def tn(a, b):
    return lax.dot_general(a, b, (((0,), (0,)), ((), ())), preferred_element_type=F32)


def split(a):
    high = a.astype(BF16)
    return high, (a - high.astype(F32)).astype(BF16)


def nn3(a, b):
    ah, al = split(a)
    bh, bl = split(b)
    return nn(jnp.concatenate([ah, ah, al], 1), jnp.concatenate([bh, bl, bh], 0))


def nt3(a, b):
    ah, al = split(a)
    bh, bl = split(b)
    return nt(jnp.concatenate([ah, ah, al], 1), jnp.concatenate([bh, bl, bh], 1))


def tn3(a, b):
    ah, al = split(a)
    bh, bl = split(b)
    return tn(jnp.concatenate([ah, ah, al], 0), jnp.concatenate([bh, bl, bh], 0))


def lanes(shape):
    return lax.broadcasted_iota(jnp.int32, shape, len(shape) - 1)


def hs(h):
    return slice(h * HDIM, (h + 1) * HDIM)


def vspec():
    return pl.BlockSpec(memory_space=pltpu.VMEM)


def sspec():
    return pl.BlockSpec(memory_space=pltpu.SMEM)


def aspec():
    return pl.BlockSpec(memory_space=pl.ANY)


def shape(dims, kind):
    return jax.ShapeDtypeStruct(tuple(dims), kind)


def params():
    return pltpu.CompilerParams(vmem_limit_bytes=VM)


def cost(flops, traffic, trans=0):
    return pl.CostEstimate(flops=1, bytes_accessed=1, transcendentals=0)


def call(kernel, args, in_specs, out_shape, out_specs, name, work, grid=(), scratch=(), after=()):
    count, extra = len(args), len(after)

    def body(*refs):
        kernel(*refs[:count], *refs[count + extra :])

    return pl.pallas_call(
        body,
        grid=grid,
        out_shape=out_shape,
        in_specs=list(in_specs) + [aspec()] * extra,
        out_specs=out_specs,
        scratch_shapes=list(scratch),
        compiler_params=params(),
        cost_estimate=work,
        name=name,
    )(*args, *after)


def placed(pieces, whole, sems, me, start):
    rows = pieces[0].shape[0]
    for k, piece in enumerate(pieces):
        at = pl.multiple_of((me ^ k) * rows, 16)
        copy = pltpu.make_async_copy(piece, whole.at[pl.ds(at, rows)], sems.at[k])
        if start:
            copy.start()
        else:
            copy.wait()


def placed_halves(pieces, whole, sems, me, side, start):
    rows = pieces[0].shape[0]
    for i, piece in enumerate(pieces):
        if i < 2:
            at = (me ^ i) * rows
        else:
            at = (me ^ (i // 2 + 1)) * rows + (side ^ (i % 2)) * (rows // 2)
        to = whole.at[pl.ds(pl.multiple_of(at, 16), piece.shape[0])]
        copy = pltpu.make_async_copy(piece, to, sems.at[i])
        if start:
            copy.start()
        else:
            copy.wait()


def xor_rows(out_ref, value, me, count):
    rows = value.shape[0] // count
    for r in range(count):
        at = pl.multiple_of((me ^ r) * rows, 16)
        out_ref[pl.ds(at, rows), :] = value[r * rows : (r + 1) * rows]


def pack_kernel(x_ref, *refs):
    weights, (all_ref, xm_ref, sems) = refs[:-3], refs[-3:]
    copies = []
    for i, w in enumerate(weights):
        to = all_ref.at[:, pl.ds(i * w.shape[1], w.shape[1])]
        copies.append(pltpu.make_async_copy(w, to, sems.at[i]))
        copies[-1].start()
    size, marks, width = xm_ref.shape
    tokens = x_ref.shape[0]
    segment = tokens // marks
    means = [
        jnp.mean(x_ref[m * segment : (m + 1) * segment, :].astype(F32), axis=0, keepdims=True)
        for m in range(marks)
    ]
    means = jnp.concatenate(means, 0)
    for i in range(size):
        xm_ref[i] = means
    for copy in copies:
        copy.wait()


def pack(x, weights, size, marks):
    rows, width = weights[0].shape
    return call(
        pack_kernel,
        (x, *weights),
        [vspec()] * 4,
        [shape((rows, 3 * width), BF16), shape((size, marks, width), F32)],
        [vspec()] * 2,
        "pack",
        cost(1e6, 1e5),
        scratch=[pltpu.SemaphoreType.DMA((3,))],
    )


def front_kernel(count, me_ref, x_ref, xm_ref, *refs):
    pieces = refs[:count]
    outs = refs[count : count + 6]
    xmt_ref, st_ref, msg_ref, qm_ref, km_ref, edge_ref = refs[count + 6 : count + 12]
    flats = refs[count + 12 : count + 18]
    xt_ref, qt_ref, kt_ref, vt_ref, fw_ref, eb_ref = flats
    w_ref, sems, out_sems, head_sems = refs[count + 18 :]
    me = me_ref[0]

    def out(i):
        return pltpu.make_async_copy(flats[i], outs[i], out_sems.at[i])

    def pair_out(i, pair):
        at = pl.ds(pair * 128, 128)
        return pltpu.make_async_copy(flats[i].at[at], outs[i].at[at], head_sems.at[i - 4, pair])

    placed(pieces, w_ref, sems, me, True)
    tokens, width = x_ref.shape
    step = 256
    for b in range(tokens // step):
        rows = slice(b * step, (b + 1) * step)
        xor_rows(xt_ref.at[:, rows], x_ref[rows, :].T, me, count)
    out(0).start()
    high, low = split(xm_ref[...])
    wide = jnp.concatenate([xm_ref[...], jnp.zeros_like(xm_ref)], 0)
    xor_rows(xmt_ref, wide.T.astype(BF16)[:, :LANDMARKS], me, count)
    placed(pieces, w_ref, sems, me, False)
    both = w_ref[:, : 2 * width]
    marks = SCALE * (nn(high, both) + nn(low, both))
    qm = marks[:, :width].astype(BF16)
    km = marks[:, width:].astype(BF16)
    qm_ref[...] = qm
    km_ref[...] = km
    for i, (to, scale) in enumerate(((qt_ref, SCALE), (kt_ref, SCALE), (vt_ref, None))):
        for b in range(tokens // step):
            rows = slice(b * step, (b + 1) * step)
            y = nn(x_ref[rows, :], w_ref[:, i * width : (i + 1) * width])
            if scale is not None:
                y = y * scale
            y = y.astype(BF16)
            if i == 2 and b == 0:
                edge_ref[:REACH] = y[:REACH]
            if i == 2 and b == tokens // step - 1:
                edge_ref[REACH:] = y[step - REACH :]
            to[:, rows] = y.T
        out(1 + i).start()
    lane = lanes((LANDMARKS, 128))
    stats = jnp.zeros((LANDMARKS, 128), F32)
    pair = []
    for h in range(HEADS):
        s = nn(km[:, hs(h)], qt_ref[hs(h), :])
        s = jnp.exp(s - jnp.max(s, axis=0, keepdims=True))
        fw_ref[hs(h), :] = (s * (1.0 / jnp.sum(s, axis=0, keepdims=True))).astype(BF16)
        s = nn(qm[:, hs(h)], kt_ref[hs(h), :])
        top = jnp.max(s, axis=1, keepdims=True).astype(BF16).astype(F32)
        e = jnp.exp(s - top).astype(BF16)
        eb_ref[hs(h), :] = e
        total = jnp.sum(e.astype(F32), axis=1, keepdims=True)
        stats = jnp.where(lane == h, top, stats)
        stats = jnp.where(lane == 16 + h, total, stats)
        pair.append(nt(e, vt_ref[hs(h), :]))
        if h % 2:
            both = jnp.concatenate(pair, 1).astype(BF16)
            for d in range(msg_ref.shape[0]):
                msg_ref[d, h // 2] = both
            pair = []
            pair_out(4, h // 2).start()
            pair_out(5, h // 2).start()
    st_ref[...] = stats
    for d in range(msg_ref.shape[0]):
        msg_ref[d, HEADS // 2] = stat_message(stats)
    for i in range(4):
        out(i).wait()
    for h in range(HEADS // 2):
        pair_out(4, h).wait()
        pair_out(5, h).wait()


def stat_message(stats):
    lane = lanes(stats.shape)
    high = stats.astype(BF16).astype(F32)
    low = pltpu.roll(stats - high, 16, 1)
    return jnp.where((lane >= 32) & (lane < 48), low, high).astype(BF16)


def front(me, x, xm, pieces, size):
    tokens, width = x.shape
    pairs = HEADS // 2
    flat = shape((width, tokens), BF16)
    xt, qt, kt, vt, fw, eb, xmt, st, msg, qm, km, edge = call(
        functools.partial(front_kernel, len(pieces)),
        (me, x, xm, *pieces),
        [sspec(), vspec(), vspec()] + [aspec()] * len(pieces),
        [flat] * 6
        + [
            shape((width, LANDMARKS), BF16),
            shape((LANDMARKS, 128), F32),
            shape((size, pairs + 1, LANDMARKS, 128), BF16),
            shape((LANDMARKS, width), BF16),
            shape((LANDMARKS, width), BF16),
            shape((2 * REACH, width), BF16),
        ],
        [aspec()] * 6 + [vspec()] * 6,
        "front",
        cost(4.5e8, 1.6e6),
        scratch=[pltpu.VMEM((width, tokens), BF16) for _ in range(6)]
        + [
            pltpu.VMEM((width, 3 * width), BF16),
            pltpu.SemaphoreType.DMA((len(pieces),)),
            pltpu.SemaphoreType.DMA((4,)),
            pltpu.SemaphoreType.DMA((2, pairs)),
        ],
    )
    return xt, xmt, qt, kt, vt, fw, eb, st, msg, qm, km, edge


def merged(msg_ref, mixn_ref, st_ref):
    lane = lanes((LANDMARKS, 128))
    size = msg_ref.shape[0]
    stats = []
    for d in range(size):
        got = msg_ref[d, HEADS // 2].astype(F32)
        stats.append(got + jnp.where((lane >= 16) & (lane < 32), pltpu.roll(got, 112, 1), 0.0))
    largest = functools.reduce(jnp.maximum, stats)
    weights = [jnp.exp(jnp.minimum(st - largest, 0.0)) for st in stats]
    total = sum(st * pltpu.roll(w, 16, 1) for st, w in zip(stats, weights))
    st_ref[...] = jnp.where(lane < 16, largest, total)
    for i in range(HEADS // 2):

        def both(a, at):
            return jnp.where(lane < HDIM, a[:, at : at + 1], a[:, at + 1 : at + 2])

        y = sum(msg_ref[d, i].astype(F32) * both(weights[d], 2 * i) for d in range(size))
        mixn_ref[i] = y / both(total, 16 + 2 * i)


def eye(scale):
    n = LANDMARKS
    return jnp.where(
        lax.broadcasted_iota(jnp.int32, (n, n), 0) == lax.broadcasted_iota(jnp.int32, (n, n), 1),
        jnp.float32(scale),
        0.0,
    )


def landmark_softmax(qm, km, h):
    s = nt(qm[:, hs(h)], km[:, hs(h)])
    s = jnp.exp(s - jnp.max(s, axis=1, keepdims=True))
    return s / jnp.sum(s, axis=1, keepdims=True)


def first_inverse(a):
    columns = jnp.max(jnp.sum(a, axis=0, keepdims=True), axis=1, keepdims=True)
    rows = jnp.max(jnp.sum(a, axis=1, keepdims=True), axis=0, keepdims=True)
    return a.T * (1.0 / (columns * rows))


def inverse_kernel(size, me_ref, qm_ref, km_ref, z_ref, a_out, zs, ps, ms, ns, a_ref, p_ref, m_ref, n_ref):
    qm, km = qm_ref[...], km_ref[...]
    every = range(HEADS)
    slots = range(-(-HEADS // size))
    mine = [jnp.minimum(me_ref[1] + size * j, HEADS - 1) for j in slots]
    for h in every:
        a = landmark_softmax(qm, km, h)
        a_ref[h] = a
        z_ref[h] = first_inverse(a)
    for j in slots:
        a_out[j] = a_ref[mine[j]]

    def step(i, carry):
        p = [nn3(a_ref[h], z_ref[h]) for h in every]
        m = [eye(15.0) - nn3(x, eye(7.0) - x) for x in p]
        n = [eye(13.0) - nn3(x, y) for x, y in zip(p, m)]
        for h in every:
            p_ref[h] = p[h]
            m_ref[h] = m[h]
            n_ref[h] = n[h]
        for j in slots:
            ps[i, j] = p_ref[mine[j]]
            ms[i, j] = m_ref[mine[j]]
            ns[i, j] = n_ref[mine[j]]
            zs[i, j] = z_ref[mine[j]]
        for h in every:
            z_ref[h] = 0.25 * nn3(z_ref[h], n[h])
        return carry

    lax.fori_loop(0, PINV_ITERS, step, 0)


def inverse(me, qm, km, size):
    square = (HEADS, LANDMARKS, LANDMARKS)
    few = (-(-HEADS // size), LANDMARKS, LANDMARKS)
    return call(
        functools.partial(inverse_kernel, size),
        (me, qm, km),
        [sspec()] + [vspec()] * 2,
        [shape(square, F32), shape(few, F32)] + [shape((PINV_ITERS,) + few, F32)] * 4,
        [vspec()] * 6,
        "inverse",
        cost(1e8, 1e6),
        scratch=[pltpu.VMEM(square, F32)] * 4,
    )


def half(pair, h):
    return jnp.where(h % 2 == 0, pair[:, :HDIM], pair[:, HDIM:])


def inverse_step(z, p, m, n, a, gz, ga):
    g = 0.25 * gz
    g3 = -tn3(z, g)
    g2 = -tn3(p, g3)
    gp = nt3(g3, m) + nt3(g2, eye(7.0) - p) - tn3(p, g2)
    return nt3(g, n) + tn3(a, gp), ga + nt3(gp, z)


def score_grad(a, gfirst, ga):
    csum = jnp.sum(a, axis=0, keepdims=True)
    rsum = jnp.sum(a, axis=1, keepdims=True)
    cmax = jnp.max(csum, axis=1, keepdims=True)
    rmax = jnp.max(rsum, axis=0, keepdims=True)
    scale = 1.0 / (cmax * rmax)
    gs = jnp.sum(jnp.sum(gfirst * a.T, axis=1, keepdims=True), axis=0, keepdims=True)
    ctop = (csum == cmax).astype(F32)
    rtop = (rsum == rmax).astype(F32)
    gcol = -gs * scale / cmax * ctop / jnp.sum(ctop, axis=1, keepdims=True)
    grow = -gs * scale / rmax * rtop / jnp.sum(rtop, axis=0, keepdims=True)
    g = ga + gfirst.T * scale + gcol + grow
    return a * (g - jnp.sum(g * a, axis=1, keepdims=True))


def widen(out_ref, flat_ref, pair_ref, next_ref, odd):
    width, tokens = flat_ref.shape
    zero = jnp.zeros((EDGE - REACH, width), BF16)
    pair, other = pair_ref[...].astype(F32), next_ref[...].astype(F32)
    before = jnp.where(odd, pair[REACH:], other[REACH:]).astype(BF16)
    after = jnp.where(odd, other[:REACH], pair[:REACH]).astype(BF16)
    out_ref[:, :EDGE] = jnp.concatenate([zero, before], 0).T
    out_ref[:, EDGE : EDGE + tokens] = flat_ref[...]
    out_ref[:, EDGE + tokens :] = jnp.concatenate([after, zero], 0).T


def band(row, step):
    wide = jnp.broadcast_to(row, (step, step + 2 * EDGE))
    return pltpu.roll(wide, 0, 1, stride=1, stride_axis=0).astype(BF16)


def stacked(ref, h, step, margin):
    blocks = (ref.shape[1] - 2 * margin) // step if margin else ref.shape[1] // step
    return jnp.concatenate(
        [ref[hs(h), b * step : (b + 1) * step + 2 * margin] for b in range(blocks)], 0
    )


def pair_rows(tokens):
    return pl.BlockSpec((128, tokens), lambda i: (i, 0))


def pair_lanes(rows):
    return pl.BlockSpec((rows, 128), lambda i: (0, i))


def pair_block(*dims):
    return pl.BlockSpec((1, *dims), lambda i: (i, 0, 0))


def conv_kernel_body(me_ref, vt_ref, pair_ref, next_ref, taps_ref, out_ref, wide_ref):
    widen(wide_ref, vt_ref, pair_ref, next_ref, me_ref[1] % 2 == 1)
    step = 256
    for h in range(HEADS):
        y = nt(stacked(wide_ref, h, step, EDGE), band(taps_ref[h : h + 1, :], step))
        for b in range(vt_ref.shape[1] // step):
            out_ref[hs(h), b * step : (b + 1) * step] = y[b * HDIM : (b + 1) * HDIM, :]


def conv(me, vt, edges, taps):
    width, tokens = vt.shape
    return call(
        conv_kernel_body,
        (me, vt, *edges, taps),
        [sspec()] + [vspec()] * 4,
        shape(vt.shape, F32),
        vspec(),
        "conv",
        cost(2e9, 6e6),
        scratch=[pltpu.VMEM((width, tokens + 2 * EDGE), BF16)],
    )


def gelu_pair(x):
    phi = 0.5 * (1.0 + lax.erf(x * (0.5**0.5)))
    return x * phi, phi + x * ((0.5 / jnp.pi) ** 0.5 * jnp.exp(-0.5 * x * x))


def norm_stats(r):
    center = r - jnp.mean(r, axis=-1, keepdims=True)
    rstd = lax.rsqrt(jnp.mean(center * center, axis=-1, keepdims=True) + 1e-05)
    return center * rstd, rstd


def norm_back(gy, xhat, rstd):
    return rstd * (
        gy - jnp.mean(gy, axis=-1, keepdims=True) - xhat * jnp.mean(gy * xhat, axis=-1, keepdims=True)
    )


STEP = 256


def whole(a):
    return pl.BlockSpec(a.shape, lambda i, n=a.ndim: (0,) * n)


def fixed(*dims):
    return pl.BlockSpec(dims, lambda i, n=len(dims): (0,) * n)


def tall(rows):
    return pl.BlockSpec((rows, STEP), lambda i: (0, i))


def row(width):
    return pl.BlockSpec((STEP, width), lambda i: (i, 0))


def mid_kernel(count, me_ref, z_ref, msg_ref, fw_ref, conv_ref, x_ref, ct_ref, gains_ref, *refs):
    halves = 2 * count - 2
    wo, down, up = refs[:count], refs[count : 2 * count], refs[2 * count : 2 * count + halves]
    (ctx_ref, hidt_ref, act_ref, out_ref, redt_ref, ge_ref, first_ref, branch_ref, gct_ref, edge_ref,
     sums_ref, comb_ref, mixn_ref, st_ref, gc_ref, wo_ref, up_ref, down_ref, slope_ref,
     sems, up_sems) = refs[2 * count + halves :]
    me, side = me_ref[0], me_ref[1] % 2
    at = pl.program_id(0)
    begin = at == 0
    part = up_ref.shape[1] // count

    @pl.when(begin)
    def _():
        placed(wo, wo_ref, sems.at[0], me, True)
        placed_halves(up, up_ref, up_sems, me, side, True)
        placed(down, down_ref, sems.at[1], me, True)
        merged(msg_ref, mixn_ref, st_ref)
        for i in range(HEADS // 2):
            mixed = mixn_ref[i]
            comb_ref[i] = jnp.concatenate(
                [nn3(z_ref[2 * i], mixed[:, :HDIM]), nn3(z_ref[2 * i + 1], mixed[:, HDIM:])], 1
            ).astype(BF16)
        sums_ref[...] = jnp.zeros_like(sums_ref)
        gc_ref[...] = jnp.zeros_like(gc_ref)
        placed(wo, wo_ref, sems.at[0], me, False)

    for h in range(HEADS):
        att = tn(comb_ref[h // 2][:, hs(h % 2)], fw_ref[hs(h), :])
        ctx_ref[hs(h), :] = (att + conv_ref[hs(h), :]).astype(BF16)
    branch = nn(ctx_ref[...].T, wo_ref[...])
    xhat1, rstd1 = norm_stats(x_ref[...].astype(F32) + branch)
    hidden = xhat1 * gains_ref[0:1, :] + gains_ref[1:2, :]
    hid = hidden.astype(BF16)
    xor_rows(hidt_ref, hid.T, me, count)

    @pl.when(begin)
    def _():
        placed_halves(up, up_ref, up_sems, me, side, False)

    for c in range(count):
        cols = slice(c * part, (c + 1) * part)
        act, slope = gelu_pair(nn(hid, up_ref[:, cols]))
        act_ref[:, cols] = act.astype(BF16)
        slope_ref[:, cols] = slope.astype(BF16)

    @pl.when(begin)
    def _():
        placed(down, down_ref, sems.at[1], me, False)

    xhat, rstd = norm_stats(hidden + nn(act_ref[...], down_ref[...]))
    out_ref[...] = (xhat * gains_ref[2:3, :] + gains_ref[3:4, :]).astype(BF16)
    ct = ct_ref[...].astype(F32)
    sums_ref[2:3, :] = sums_ref[2:3, :] + jnp.sum(ct * xhat, axis=0, keepdims=True)
    sums_ref[3:4, :] = sums_ref[3:4, :] + jnp.sum(ct, axis=0, keepdims=True)
    second = norm_back(ct * gains_ref[2:3, :], xhat, rstd)
    red = second.astype(BF16)
    redt_ref[...] = red.T
    for k in range(count):
        cols = slice(k * part, (k + 1) * part)
        ge = nt(red, down_ref[cols, :]) * slope_ref[:, cols].astype(F32)
        ge_ref[:, cols] = ge.astype(BF16)
    g = second + nt(ge_ref[...], up_ref[...])
    sums_ref[0:1, :] = sums_ref[0:1, :] + jnp.sum(g * xhat1, axis=0, keepdims=True)
    sums_ref[1:2, :] = sums_ref[1:2, :] + jnp.sum(g, axis=0, keepdims=True)
    first = norm_back(g * gains_ref[0:1, :], xhat1, rstd1)
    first_ref[...] = first
    back = first.astype(BF16)
    branch_ref[...] = back
    gctx = nt(back, wo_ref[...]).astype(BF16)

    @pl.when(begin)
    def _():
        edge_ref[:REACH] = gctx[:REACH]

    @pl.when(at == pl.num_programs(0) - 1)
    def _():
        edge_ref[REACH:] = gctx[gctx.shape[0] - REACH :]

    gct_ref[...] = gctx.T
    for i in range(HEADS // 2):
        gc_ref[i] = gc_ref[i] + jnp.concatenate(
            [nt(fw_ref[hs(h), :], gct_ref[hs(h), :]) for h in (2 * i, 2 * i + 1)], 1
        )


def mid(me, z, msgs, fw, convt, x, ct, gains, wo, up, down, after=()):
    tokens, width = x.shape
    ff = up[0].shape[1]
    pairs = HEADS // 2
    pieces = (*wo, *down, *up)
    flat, wide = shape((width, tokens), BF16), shape((tokens, ff), BF16)
    return call(
        functools.partial(mid_kernel, len(wo)),
        (me, z, msgs, fw, convt, x, ct, gains, *pieces),
        [sspec(), whole(z), whole(msgs), tall(width), tall(width), row(width), row(width), whole(gains)]
        + [aspec()] * len(pieces),
        [
            flat,
            flat,
            wide,
            shape((tokens, width), BF16),
            flat,
            wide,
            shape((tokens, width), F32),
            shape((tokens, width), BF16),
            flat,
            shape((2 * REACH, width), BF16),
            shape((8, width), F32),
            shape((pairs, LANDMARKS, 128), BF16),
            shape((pairs, LANDMARKS, 128), F32),
            shape((LANDMARKS, 128), F32),
            shape((pairs, LANDMARKS, 128), F32),
        ],
        [tall(width), tall(width), row(ff), row(width), tall(width), row(ff), row(width), row(width),
         tall(width), fixed(2 * REACH, width), fixed(8, width),
         fixed(pairs, LANDMARKS, 128), fixed(pairs, LANDMARKS, 128), fixed(LANDMARKS, 128),
         fixed(pairs, LANDMARKS, 128)],
        "mid",
        cost(2e9, 3e6),
        grid=(tokens // STEP,),
        scratch=[
            pltpu.VMEM((width, width), BF16),
            pltpu.VMEM((width, ff), BF16),
            pltpu.VMEM((ff, width), BF16),
            pltpu.VMEM((STEP, ff), BF16),
            pltpu.SemaphoreType.DMA((2, len(wo))),
            pltpu.SemaphoreType.DMA((len(up),)),
        ],
        after=after,
    )


def grad_down_kernel(count, me_ref, red_ref, act_ref, *outs):
    part = act_ref.shape[1] // count
    for k in range(count):
        at = pl.ds(pl.multiple_of((me_ref[0] ^ k) * part, 128), part)
        outs[k][...] = nn(red_ref[...], act_ref[:, at]).astype(BF16)


def grad_down(count, me, redt, act, after=()):
    width = redt.shape[0]
    return call(
        functools.partial(grad_down_kernel, count),
        (me, redt, act),
        [sspec(), vspec(), vspec()],
        [shape((width, act.shape[1] // count), BF16)] * count,
        [vspec()] * count,
        "grad_down",
        cost(5e8, 1e6),
        after=after,
    )


def grad_up_kernel(count, hid_ref, ge_ref, *outs):
    y = nn(hid_ref[...], ge_ref[...]).astype(BF16)
    rows = y.shape[0] // count
    for k in range(count):
        outs[k][...] = y[k * rows : (k + 1) * rows]


def grad_up(count, hidt, ge, after=()):
    width, tokens = hidt.shape
    ff = ge.shape[1]
    step = 768
    return call(
        functools.partial(grad_up_kernel, count),
        (hidt, ge),
        [whole(hidt), pl.BlockSpec((tokens, step), lambda i: (0, i))],
        [shape((width // count, ff), BF16)] * count,
        [pl.BlockSpec((width // count, step), lambda i: (0, i))] * count,
        "grad_up",
        cost(5e8, 1e6),
        grid=(ff // step,),
        after=after,
    )


class Moves:
    def __init__(self, sems):
        self.sems, self.used, self.open = sems, 0, []

    def start(self, src, dst):
        copy = pltpu.make_async_copy(src, dst, self.sems.at[self.used])
        self.used += 1
        copy.start()
        self.open.append(copy)
        return copy

    def wait(self, *copies):
        for copy in copies or list(self.open):
            copy.wait()
            self.open.remove(copy)


def gap_kernel(count, me_ref, gct_hbm, fw_hbm, qt_hbm, vt_hbm, ctx_hbm, branch_hbm, comb_ref, km_ref,
               vb_ref, va_ref, gb_ref, ga_ref, taps_ref, sums_ref, *refs):
    outs = refs[:count]
    (gq_hbm, gvc_hbm, gkm_ref, gct_ref, fw_ref, qt_ref, vt_ref, ctx_ref, branch_ref, gq_ref, gvc_ref,
     vwide, gwide, y_ref, sems) = refs[count:]
    moves = Moves(sems)
    lead = [
        moves.start(a, b)
        for a, b in ((gct_hbm, gct_ref), (fw_hbm, fw_ref), (qt_hbm, qt_ref))
    ]
    values = moves.start(vt_hbm, vt_ref)
    rest = [moves.start(ctx_hbm, ctx_ref), moves.start(branch_hbm, branch_ref)]
    km = km_ref[...]
    moves.wait(*lead)
    pair = []
    for h in range(HEADS):
        comb = comb_ref[h // 2][:, hs(h % 2)]
        pf = fw_ref[hs(h), :].astype(F32)
        g = nn(comb, gct_ref[hs(h), :])
        gs = (pf * (g - jnp.sum(pf * g, axis=0, keepdims=True))).astype(BF16)
        gq_ref[hs(h), :] = tn(km[:, hs(h)], gs).astype(BF16)
        pair.append(nt(gs, qt_ref[hs(h), :]))
        if h % 2:
            gkm_ref[:, (h - 1) * HDIM : (h + 1) * HDIM] = jnp.concatenate(pair, 1)
            pair = []
    moves.start(gq_ref, gq_hbm)
    moves.wait(values)
    odd = me_ref[1] % 2 == 1
    widen(vwide, vt_ref, vb_ref, va_ref, odd)
    widen(gwide, gct_ref, gb_ref, ga_ref, odd)
    step = 256
    tokens = vt_ref.shape[1]
    flip = (
        lax.broadcasted_iota(jnp.int32, (step, step), 0)
        + lax.broadcasted_iota(jnp.int32, (step, step), 1)
        == step - 1
    ).astype(BF16)
    rows = []
    for h in range(HEADS):
        y = nt(stacked(gwide, h, step, EDGE), band(taps_ref[h : h + 1, :], step))
        for b in range(tokens // step):
            gvc_ref[hs(h), b * step : (b + 1) * step] = y[b * HDIM : (b + 1) * HDIM, :]
        turned = nn(stacked(gct_ref, h, step, 0), flip).astype(BF16)
        d = tn(turned, stacked(vwide, h, step, EDGE))
        d = pltpu.roll(d, 0, 1, stride=1, stride_axis=0)
        rows.append(jnp.sum(d, axis=0, keepdims=True))
    moves.start(gvc_ref, gvc_hbm)
    rows = jnp.concatenate(rows + [jnp.zeros((4, step + 2 * EDGE), F32)], 0)
    first = step - 1 + EDGE - REACH
    taps = pltpu.roll(rows, step + 2 * EDGE - first, 1)[:HEADS, :128]
    width = ctx_ref.shape[0]
    taps = jnp.concatenate([taps, jnp.zeros((HEADS, width - 128), F32)], 1)
    little = jnp.concatenate(
        [sums_ref[0:4, :], taps, jnp.zeros((128 - 4 - HEADS, width), F32)], 0
    )
    y_ref[:, width:] = little.T.astype(BF16)
    moves.wait(*rest)
    y_ref[:, :width] = nn(ctx_ref[...], branch_ref[...]).astype(BF16)
    size = width // count
    for k in range(count):
        outs[k][...] = y_ref[pl.ds(pl.multiple_of((me_ref[0] ^ k) * size, 16), size), :]
    moves.wait()


def gap(count, me, gct, fw, qt, vt, ctxt, branch, comb, km, vb, va, gb, ga, taps, sums, after=()):
    width, tokens = vt.shape
    flat = pltpu.VMEM((width, tokens), BF16)
    wide = pltpu.VMEM((width, tokens + 2 * EDGE), BF16)
    *pieces, gq, gvc, gkm = call(
        functools.partial(gap_kernel, count),
        (me, gct, fw, qt, vt, ctxt, branch, comb, km, vb, va, gb, ga, taps, sums),
        [sspec()] + [aspec()] * 6 + [vspec()] * 8,
        [shape((width // count, width + 128), BF16)] * count
        + [shape(gct.shape, BF16), shape(gct.shape, F32), shape(km.shape, F32)],
        [vspec()] * count + [aspec()] * 2 + [vspec()],
        "gap",
        cost(1e9, 1e6),
        scratch=[flat] * 5
        + [
            pltpu.VMEM((tokens, width), BF16),
            flat,
            pltpu.VMEM((width, tokens), F32),
            wide,
            wide,
            pltpu.VMEM((width, width + 128), BF16),
            pltpu.SemaphoreType.DMA((8,)),
        ],
        after=after,
    )
    return pieces, gq, gvc, gkm


def rear_kernel(count, size, me_ref, eb_hbm, vt_hbm, kt_hbm, gvc_hbm, xt_hbm, gq_hbm, z_ref, gc_ref,
                mixn_ref, st_ref, own_ref, qm_ref, km_ref, gkmp_ref, xmt_ref, a_ref, zs, ps, ms, ns, *refs):
    outs = refs[:count]
    (gk_hbm, gv_hbm, land_ref, gqm_ref, gkm_ref, eb_ref, vt_ref, kt_ref, gvc_ref, xt_ref, gq_ref, gk_ref, gv_ref,
     y_ref, sems) = refs[count:]
    moves = Moves(sems)
    early = [
        moves.start(a, b)
        for a, b in ((vt_hbm, vt_ref), (eb_hbm, eb_ref), (kt_hbm, kt_ref), (gvc_hbm, gvc_ref))
    ]
    late = [moves.start(xt_hbm, xt_ref), moves.start(gq_hbm, gq_ref)]
    qm, km = qm_ref[...], km_ref[...]
    lane = lanes((LANDMARKS, 128))
    slots = range(-(-HEADS // size))
    heads = [me_ref[1] + size * j for j in slots]
    safe = [jnp.minimum(h, HEADS - 1) for h in heads]
    gz = [nt3(half(gc_ref[h // 2], h), half(mixn_ref[h // 2], h)) for h in safe]
    ga = [jnp.zeros((LANDMARKS, LANDMARKS), F32) for _ in slots]
    stats = st_ref[...]
    scale = jnp.exp(own_ref[...] - stats)
    moves.wait(*early)
    for p in range(HEADS // 2):
        if p < PINV_ITERS:
            i = PINV_ITERS - 1 - p
            for j in slots:
                gz[j], ga[j] = inverse_step(
                    zs[i, j], ps[i, j], ms[i, j], ns[i, j], a_ref[j], gz[j], ga[j]
                )
        pair = []
        for h in (2 * p, 2 * p + 1):
            gmix = tn3(z_ref[h], gc_ref[p][:, hs(h % 2)]).astype(BF16)
            dot = jnp.sum(gmix.astype(F32) * mixn_ref[p][:, hs(h % 2)], axis=1, keepdims=True)
            factor = scale[:, h : h + 1] / stats[:, 16 + h : 17 + h]
            pb = eb_ref[hs(h), :].astype(F32) * factor
            gs = (pb * (nn(gmix, vt_ref[hs(h), :]) - dot)).astype(BF16)
            gk_ref[hs(h), :] = tn(qm[:, hs(h)], gs).astype(BF16)
            gv_ref[hs(h), :] = (tn(gmix, pb.astype(BF16)) + gvc_ref[hs(h), :]).astype(BF16)
            pair.append(nt(gs, kt_ref[hs(h), :]))
        both = slice(p * 128, p * 128 + 128)
        gqm_ref[:, both] = jnp.concatenate(pair, 1)
        gkm_ref[:, both] = gkmp_ref[:, both]
    moves.start(gk_ref, gk_hbm)
    moves.start(gv_ref, gv_hbm)
    moves.wait(*late)
    width = xt_ref.shape[0]
    rows = width // count

    def weight(i, y):
        y_ref[i] = y.astype(BF16)
        for k in range(count):
            moves.start(y_ref.at[i, pl.ds(k * rows, rows)], outs[k].at[i])

    weight(2, nt(xt_ref[...], gv_ref[...]))
    for j in slots:
        h = safe[j]
        high, low = split(score_grad(a_ref[j], gz[j], ga[j]))
        at = pl.ds(pl.multiple_of(h // 2 * 128, 128), 128)
        qmh = half(qm_ref[:, at].astype(F32), h).astype(BF16)
        kmh = half(km_ref[:, at].astype(F32), h).astype(BF16)
        gq = nn(jnp.concatenate([high, low], 1), jnp.concatenate([kmh] * 2, 0))
        gk = tn(jnp.concatenate([high, low], 0), jnp.concatenate([qmh] * 2, 0))
        mine = ((lane >= HDIM) == (h % 2 == 1)) & (heads[j] < HEADS)
        gqm_ref[:, at] = gqm_ref[:, at] + jnp.where(mine, jnp.concatenate([gq, gq], 1), 0.0)
        gkm_ref[:, at] = gkm_ref[:, at] + jnp.where(mine, jnp.concatenate([gk, gk], 1), 0.0)
    land_ref[...] = jnp.concatenate([gqm_ref[...], gkm_ref[...]], 1).astype(BF16)
    weight(0, nt(xt_ref[...], gq_ref[...]) + nn(xmt_ref[...], gqm_ref[...].astype(BF16)))
    weight(1, nt(xt_ref[...], gk_ref[...]) + nn(xmt_ref[...], gkm_ref[...].astype(BF16)))
    moves.wait()


def rear(count, size, me, eb, vt, kt, gvc, xt, gq, z, gc, mixn, stats, own, qm, km, gkm, xmt, a, saved,
         after=()):
    width, tokens = vt.shape
    rows = width // count
    flat = pltpu.VMEM((width, tokens), BF16)
    mark = pltpu.VMEM(qm.shape, F32)
    *pieces, gk, gv, land = call(
        functools.partial(rear_kernel, count, size),
        (me, eb, vt, kt, gvc, xt, gq, z, gc, mixn, stats, own, qm, km, gkm, xmt, a, *saved),
        [sspec()] + [aspec()] * 6 + [vspec()] * 14,
        [shape((3, rows, width), BF16)] * count + [shape(vt.shape, BF16)] * 2
        + [shape((LANDMARKS, 2 * width), BF16)],
        [aspec()] * (count + 2) + [vspec()],
        "rear",
        cost(2e9, 2e6),
        scratch=[mark] * 2
        + [flat] * 3
        + [pltpu.VMEM((width, tokens), F32)]
        + [flat] * 4
        + [
            pltpu.VMEM((3, width, width), BF16),
            pltpu.SemaphoreType.DMA((8 + 3 * count,)),
        ],
        after=after,
    )
    return [piece.reshape(3 * rows, width) for piece in pieces], gk, gv, land


def last_kernel(count, me_ref, gq_ref, gk_ref, gv_ref, first_ref, *refs):
    pieces = refs[:count]
    out_ref, w_ref, sems = refs[count:]
    me = me_ref[0]
    width = gq_ref.shape[0]

    @pl.when(pl.program_id(0) == 0)
    def _():
        placed(pieces, w_ref, sems, me, True)
        placed(pieces, w_ref, sems, me, False)

    wq, wk, wv = (w_ref[:, i * width : (i + 1) * width] for i in range(3))
    g = SCALE * (nn(wq, gq_ref[...]) + nn(wk, gk_ref[...])) + nn(wv, gv_ref[...])
    out_ref[...] = first_ref[...] + g.T


def last(me, gq, gk, gv, first, pieces, after=()):
    width, tokens = gq.shape
    return call(
        functools.partial(last_kernel, len(pieces)),
        (me, gq, gk, gv, first, *pieces),
        [sspec(), tall(width), tall(width), tall(width), row(width)] + [aspec()] * len(pieces),
        shape((tokens, width), F32),
        row(width),
        "last",
        cost(4e8, 1e6),
        grid=(tokens // STEP,),
        scratch=[
            pltpu.VMEM((width, 3 * width), BF16),
            pltpu.SemaphoreType.DMA((len(pieces),)),
        ],
        after=after,
    )


def share_kernel(segment, count, me_ref, own_ref, most_ref, *refs):
    pieces = refs[:count]
    out_ref, w_ref, sems = refs[count:]
    own = own_ref[...]
    width = own.shape[1] // 2
    pieces = [piece.at[:, pl.ds(0, 2 * width)] for piece in pieces]
    placed(pieces, w_ref, sems, me_ref[0], True)
    placed(pieces, w_ref, sems, me_ref[0], False)
    marks = (SCALE / segment) * (
        nt(own[:, :width].astype(BF16), w_ref[:, :width])
        + nt(own[:, width:].astype(BF16), w_ref[:, width : 2 * width])
    )
    for m in range(own.shape[0]):
        rows = slice(m * segment, (m + 1) * segment)
        out_ref[rows, :] = (most_ref[rows, :] + marks[m : m + 1, :]).astype(BF16)


def share(me, own, most, pieces):
    tokens, width = most.shape
    return call(
        functools.partial(share_kernel, tokens // own.shape[0], len(pieces)),
        (me, own, most, *pieces),
        [sspec(), vspec(), vspec()] + [aspec()] * len(pieces),
        shape(most.shape, BF16),
        vspec(),
        "share",
        cost(4e8, 1e6),
        scratch=[
            pltpu.VMEM((width, 2 * width), BF16),
            pltpu.SemaphoreType.DMA((len(pieces),)),
        ],
    )


def bits(axis):
    size = lax.axis_size(axis)
    assert size & (size - 1) == 0
    return [1 << i for i in range(size.bit_length() - 1)]


def swap(array, axis, bit):
    return lax.ppermute(array, axis, [(i, i ^ bit) for i in range(lax.axis_size(axis))])


def neighbours(array):
    size = lax.axis_size("seq")
    odd = [(i, i + 1) for i in range(1, size - 1, 2)]
    return swap(array, "seq", 1), lax.ppermute(array, "seq", odd + [(j, i) for i, j in odd])


def spread(pieces, axis, steps):
    for bit in steps:
        pieces = {**pieces, **{k | bit: swap(piece, axis, bit) for k, piece in pieces.items()}}
    return pieces


def far(array, axis):
    return spread({0: array}, axis, bits(axis)[1:])


def near(pieces, axis):
    pieces = spread(pieces, axis, bits(axis)[:1])
    return [pieces[k] for k in range(lax.axis_size(axis))]


def gathered(array, axis):
    return near(far(array, axis), axis)


def tie(*values):
    return lax.optimization_barrier(values)


def rows_out(array, groups=None):
    size = len(groups[0]) if groups else lax.axis_size("seq")
    blocks = array.reshape(size, -1, array.shape[1])
    return lax.all_to_all(blocks, "seq", 0, 0, axis_index_groups=groups)


def rows_in(blocks):
    return jnp.sum(blocks.astype(F32), axis=0)


def copies(array, axis, groups=None):
    size = len(groups[0]) if groups else lax.axis_size(axis)
    blocks = jnp.broadcast_to(array[None], (size, *array.shape))
    return lax.all_to_all(blocks, axis, 0, 0, axis_index_groups=groups)


class Total:
    def __init__(self, pieces, order):
        self.pieces = dict(enumerate(pieces))
        self.order = list(order)
        self.back = [step for step in reversed(order) if step[0] != "swap"]
        self.got = None

    def send(self, *values):
        if not self.order and not self.back:
            return values
        back = not self.order
        kind, what = self.back[0] if back else self.order[0]
        axis = "seq"
        if kind == "swap":
            axis = "fsdp"
            sent = {k: p for k, p in self.pieces.items() if k & what}
            self.pieces = {k: p for k, p in self.pieces.items() if not k & what}
        elif kind == "half" and not back:
            piece = self.pieces[0]
            upper = ((lax.axis_index("seq") & what) != 0).astype(jnp.int32)
            half = piece.shape[0] // 2
            self.pieces = {0: lax.dynamic_slice_in_dim(piece, upper * half, half, 0)}
            sent = {0: lax.dynamic_slice_in_dim(piece, (1 - upper) * half, half, 0)}
        elif kind == "rows" and back:
            size = len(what[0]) if what else lax.axis_size("seq")
            sent = {0: jnp.broadcast_to(self.pieces[0][None], (size, *self.pieces[0].shape))}
        elif kind == "rows":
            size = len(what[0]) if what else lax.axis_size("seq")
            sent = {0: self.pieces[0].reshape(size, -1, self.pieces[0].shape[1])}
        else:
            sent = dict(self.pieces)
        if values:
            sent, values = tie(sent, values)
        if kind == "rows":
            self.got = {
                k: lax.all_to_all(p, "seq", 0, 0, axis_index_groups=what) for k, p in sent.items()
            }
        else:
            self.got = {k: swap(p, axis, what) for k, p in sent.items()}
        return values

    def take(self):
        if self.order:
            kind, what = self.order.pop(0)
            if kind == "rows":
                self.pieces = {0: rows_in(self.got[0]).astype(BF16)}
            else:
                extra = what if kind == "swap" else 0
                self.pieces = {
                    k: (p.astype(F32) + self.got[k | extra].astype(F32)).astype(BF16)
                    for k, p in self.pieces.items()
                }
        else:
            kind, what = self.back.pop(0)
            mine, other = self.pieces[0], self.got[0]
            if kind == "rows":
                self.pieces = {0: other.reshape(-1, other.shape[2])}
            else:
                upper = (lax.axis_index("seq") & what) != 0
                self.pieces = {
                    0: jnp.where(
                        upper, jnp.concatenate([other, mine], 0), jnp.concatenate([mine, other], 0)
                    )
                }
        self.got = None

    def step(self, *values):
        self.got, values = tie(self.got, values)
        self.take()
        return self.send(*values)

    def finish(self):
        while self.got is not None:
            self.step()
        return self.pieces[0]


def orders():
    size = lax.axis_size("seq")
    over = [("swap", bit) for bit in bits("fsdp")]
    parts = size // 4
    groups = [[low + parts * high for high in range(4)] for low in range(parts)]
    near = [("half", bit) for bit in bits("seq") if bit < parts]
    tree = over + [("half", bit) for bit in bits("seq")]
    return over, over + near + [("rows", groups)], over + [("rows", None)], tree


def shards(
    inputs,
    cotangent,
    query_weight,
    key_weight,
    value_weight,
    output_weight,
    up_weight,
    down_weight,
    norm_gain,
    norm_shift,
    final_gain,
    final_shift,
    conv_kernel,
):
    x = inputs[0]
    ct = cotangent[0]
    tokens, width = x.shape
    marks = LANDMARKS // lax.axis_size("seq")
    segment = tokens // marks
    count = lax.axis_size("fsdp")
    rows = width // count
    here = lax.axis_index("fsdp")
    place = lax.axis_index("seq")
    size = lax.axis_size("seq")
    me = jnp.stack([here, place]).astype(jnp.int32)
    over, nested, flat, tree = orders()

    packed, xm = pack(x, (query_weight, key_weight, value_weight), size, marks)
    first_weights = far(packed, "fsdp")
    space = 256 + 2 * EDGE
    taps = jnp.pad(conv_kernel.T, ((0, 4), (EDGE - REACH, space - KERNEL - EDGE + REACH)))
    spat = jnp.pad(conv_kernel[::-1].T, ((0, 4), (EDGE - REACH, space - KERNEL - EDGE + REACH)))
    xm, taps, spat, me = tie(xm, taps, spat, me)
    xm = lax.all_to_all(xm, "seq", 0, 0).reshape(LANDMARKS, width)
    gains = jnp.stack([norm_gain, norm_shift, final_gain, final_shift] * 2)
    gains = gathered(gains, "fsdp")
    first_weights, gains, xm, output_weight = tie(first_weights, gains, xm, output_weight)
    first_weights, up_weight, output_weight, down_weight = tie(
        first_weights, up_weight, output_weight, down_weight
    )
    wqkv = near(first_weights, "fsdp")
    side = (place & 1).astype(jnp.int32)
    up_far = spread({0: lax.dynamic_slice_in_dim(up_weight, side * (rows // 2), rows // 2, 0)}, "fsdp", bits("fsdp")[1:])
    up_far = [up_far[k] for k in range(2, count, 2)]
    wo = far(output_weight, "fsdp")
    down = far(down_weight, "fsdp")
    source = lax.broadcasted_iota(jnp.int32, (8, width), 1) // rows ^ here
    gains = sum(
        jnp.where(source == k, jnp.concatenate([piece.astype(F32)] * count, 1), 0.0)
        for k, piece in enumerate(gains)
    )

    (xt, xmt, qt, kt, vt, fw, eb, own, msg, qm, km, v_edge) = front(me, x, xm, wqkv, size)
    v_edges = neighbours(v_edge)
    msg, up_far, v_edges = tie(msg, up_far, v_edges)
    msgs = lax.all_to_all(msg, "seq", 0, 0)
    up_other = [swap(piece, "seq", 1) for piece in up_far]
    z, a, *saved = inverse(me, qm, km, size)
    v_edges, z = tie(v_edges, z)
    convt = conv(me, vt, v_edges, taps)
    down, wo, convt, up_far, up_other = tie(down, wo, convt, up_far, up_other)
    up = [up_weight, swap(up_weight, "fsdp", 1)]
    for mine, other in zip(up_far, up_other):
        up += [mine, other, swap(mine, "fsdp", 1), swap(other, "fsdp", 1)]
    wo = near(wo, "fsdp")
    down = near(down, "fsdp")

    (ctxt, hidt, act, out, redt, ge, first, branch, gct, g_edge, sums, comb, mixn, stats, gc) = mid(
        me, z, msgs, fw, convt, x, ct, gains, wo, up, down
    )
    hops = bits("seq")

    def exchange(bit):
        return swap(gc.astype(BF16), "seq", bit)

    got = exchange(hops[0])
    g_edges = neighbours(g_edge)
    d_up = grad_up(count, hidt, ge)
    t_up = Total(d_up, tree)
    t_up.send()
    got, d_up, g_edges = tie(got, d_up, g_edges)
    gc = gc + got.astype(F32)
    got = exchange(hops[1])
    (act,) = t_up.step(act)
    d_down = grad_down(count, me, redt, act, after=d_up)
    t_down = Total(d_down, over)
    t_down.send()
    got, d_down = tie(got, d_down)
    gc = gc + got.astype(F32)
    got = exchange(hops[2])
    gct, d_down = t_down.step(gct, d_down)
    d_o, gq, gvc, gkm = gap(
        count, me, gct, fw, qt, vt, ctxt, branch, comb, km, *v_edges, *g_edges, spat, sums, after=d_down
    )
    t_o = Total(d_o, over)
    t_o.send()
    got, gvc = tie(got, gvc)
    gc = gc + got.astype(F32)
    for bit in hops[3:]:
        gc = gc + exchange(bit).astype(F32)
    (gc,) = t_up.step(gc)
    (gc,) = t_o.step(gc)
    d_qkv, gk, gv, land = rear(
        count, size, me, eb, vt, kt, gvc, xt, gq, z, gc, mixn, stats, own, qm, km, gkm, xmt, a, saved, after=d_o
    )
    t_qkv = Total(d_qkv, tree)
    t_qkv.send()
    landed = rows_out(land)
    while t_o.got is not None:
        (gk,) = t_o.step(gk)
    g_o = t_o.pieces[0]
    while t_down.got is not None:
        (gk,) = t_down.step(gk)
    part = t_down.pieces[0].shape[1]
    g_down = t_down.pieces[0].reshape(-1, width)
    sizes = [g_down.shape[0], rows, rows * 128 // width]
    both = jnp.concatenate([g_down, g_o[:, :width], g_o[:, width:].reshape(-1, width)], 0)
    t_both = Total([both], tree[len(over) :])
    (gk,) = t_both.send(gk)
    (gk,) = t_up.step(gk)
    for _ in over[:-1]:
        (gk,) = t_qkv.step(gk)
    most = last(me, gq, gk, gv, first, wqkv)
    for t in (t_up, t_both):
        (most,) = t.step(most)
    landed, most = tie(landed, most)
    grad_x = share(me, rows_in(landed), most, wqkv)
    g_up = g_both = None
    while any(t.got is not None for t in (t_qkv, t_up, t_both)):
        for t in (t_qkv, t_up, t_both):
            if t.got is not None:
                (grad_x,) = t.step(grad_x)
        if g_up is None and t_up.got is None:
            g_up, grad_x = tie(t_up.pieces[0].astype(F32), grad_x)
        if g_both is None and t_both.got is None:
            both = t_both.pieces[0].astype(F32)
            little = both[sizes[0] + sizes[1] :].reshape(rows, 128)
            tap = jnp.where(here == 0, little[:KERNEL, 4 : 4 + HEADS], 0.0)
            g_both = (
                both[: sizes[0]].reshape(width, part).T,
                both[sizes[0] : sizes[0] + sizes[1]],
                [little[:, i] for i in range(4)],
                tap,
            )
            g_both, grad_x = tie(g_both, grad_x)
            g_down, g_o, g_gains, tap = g_both
            for _, bit in over:
                tap = tap + swap(tap, "fsdp", bit)
    qkv = t_qkv.pieces[0].astype(F32)

    return (
        out[None],
        grad_x[None],
        SCALE * qkv[:rows],
        SCALE * qkv[rows : 2 * rows],
        qkv[2 * rows :],
        g_o,
        g_up,
        g_down,
        g_gains[0],
        g_gains[1],
        g_gains[2],
        g_gains[3],
        tap,
    )


def solution(mesh):
    tokens = P("fsdp", "seq", None)
    matrix = P("fsdp", None)
    row = P("fsdp")
    in_specs = (tokens,) * 2 + (matrix,) * 6 + (row,) * 4 + (P(),)
    out_specs = (tokens,) * 2 + (matrix,) * 6 + (row,) * 4 + (P(),)
    return jax.shard_map(shards, mesh=mesh, in_specs=in_specs, out_specs=out_specs, check_vma=False)
```

```python
import functools

import jax
import jax.numpy as jnp
from jax import lax
from jax.experimental import pallas as pl
from jax.experimental.pallas import tpu as pltpu
from jax.sharding import PartitionSpec as P

HEADS = 12
HDIM = 64
LANDMARKS = 64
KERNEL = 65
PINV_ITERS = 6
REACH = KERNEL // 2
EDGE = 128
SCALE = HDIM ** (-0.25)
F32 = jnp.float32
BF16 = jnp.bfloat16
VM = 56 * 1024 * 1024


def nn(a, b):
    return jnp.dot(a, b, preferred_element_type=F32)


def nt(a, b):
    return lax.dot_general(a, b, (((1,), (1,)), ((), ())), preferred_element_type=F32)


def tn(a, b):
    return lax.dot_general(a, b, (((0,), (0,)), ((), ())), preferred_element_type=F32)


def split(a):
    high = a.astype(BF16)
    return high, (a - high.astype(F32)).astype(BF16)


def nn3(a, b):
    ah, al = split(a)
    bh, bl = split(b)
    return nn(jnp.concatenate([ah, ah, al], 1), jnp.concatenate([bh, bl, bh], 0))


def nt3(a, b):
    ah, al = split(a)
    bh, bl = split(b)
    return nt(jnp.concatenate([ah, ah, al], 1), jnp.concatenate([bh, bl, bh], 1))


def tn3(a, b):
    ah, al = split(a)
    bh, bl = split(b)
    return tn(jnp.concatenate([ah, ah, al], 0), jnp.concatenate([bh, bl, bh], 0))


def lanes(shape):
    return lax.broadcasted_iota(jnp.int32, shape, len(shape) - 1)


def hs(h):
    return slice(h * HDIM, (h + 1) * HDIM)


def vspec():
    return pl.BlockSpec(memory_space=pltpu.VMEM)


def sspec():
    return pl.BlockSpec(memory_space=pltpu.SMEM)


def aspec():
    return pl.BlockSpec(memory_space=pl.ANY)


def shape(dims, kind):
    return jax.ShapeDtypeStruct(tuple(dims), kind)


def params():
    return pltpu.CompilerParams(vmem_limit_bytes=VM)


def cost(flops, traffic, trans=0):
    return pl.CostEstimate(flops=1, bytes_accessed=1, transcendentals=0)


def call(kernel, args, in_specs, out_shape, out_specs, name, work, grid=(), scratch=(), after=()):
    count, extra = len(args), len(after)

    def body(*refs):
        kernel(*refs[:count], *refs[count + extra :])

    return pl.pallas_call(
        body,
        grid=grid,
        out_shape=out_shape,
        in_specs=list(in_specs) + [aspec()] * extra,
        out_specs=out_specs,
        scratch_shapes=list(scratch),
        compiler_params=params(),
        cost_estimate=work,
        name=name,
    )(*args, *after)


def placed(pieces, whole, sems, me, start):
    rows = pieces[0].shape[0]
    for k, piece in enumerate(pieces):
        at = pl.multiple_of((me ^ k) * rows, 16)
        copy = pltpu.make_async_copy(piece, whole.at[pl.ds(at, rows)], sems.at[k])
        if start:
            copy.start()
        else:
            copy.wait()


def placed_halves(pieces, whole, sems, me, side, start):
    rows = pieces[0].shape[0]
    for i, piece in enumerate(pieces):
        if i < 2:
            at = (me ^ i) * rows
        else:
            at = (me ^ (i // 2 + 1)) * rows + (side ^ (i % 2)) * (rows // 2)
        to = whole.at[pl.ds(pl.multiple_of(at, 16), piece.shape[0])]
        copy = pltpu.make_async_copy(piece, to, sems.at[i])
        if start:
            copy.start()
        else:
            copy.wait()


def xor_rows(out_ref, value, me, count):
    rows = value.shape[0] // count
    for r in range(count):
        at = pl.multiple_of((me ^ r) * rows, 16)
        out_ref[pl.ds(at, rows), :] = value[r * rows : (r + 1) * rows]


def pack_kernel(x_ref, *refs):
    weights, (all_ref, xm_ref, sems) = refs[:-3], refs[-3:]
    copies = []
    for i, w in enumerate(weights):
        to = all_ref.at[:, pl.ds(i * w.shape[1], w.shape[1])]
        copies.append(pltpu.make_async_copy(w, to, sems.at[i]))
        copies[-1].start()
    size, marks, width = xm_ref.shape
    tokens = x_ref.shape[0]
    segment = tokens // marks
    means = [
        jnp.mean(x_ref[m * segment : (m + 1) * segment, :].astype(F32), axis=0, keepdims=True)
        for m in range(marks)
    ]
    means = jnp.concatenate(means, 0)
    for i in range(size):
        xm_ref[i] = means
    for copy in copies:
        copy.wait()


def pack(x, weights, size, marks):
    rows, width = weights[0].shape
    return call(
        pack_kernel,
        (x, *weights),
        [vspec()] * 4,
        [shape((rows, 3 * width), BF16), shape((size, marks, width), F32)],
        [vspec()] * 2,
        "pack",
        cost(1e6, 1e5),
        scratch=[pltpu.SemaphoreType.DMA((3,))],
    )


def front_kernel(count, me_ref, x_ref, xm_ref, *refs):
    pieces = refs[:count]
    outs = refs[count : count + 6]
    xmt_ref, st_ref, msg_ref, qm_ref, km_ref, edge_ref = refs[count + 6 : count + 12]
    flats = refs[count + 12 : count + 18]
    xt_ref, qt_ref, kt_ref, vt_ref, fw_ref, eb_ref = flats
    w_ref, sems, out_sems, head_sems = refs[count + 18 :]
    me = me_ref[0]

    def out(i):
        return pltpu.make_async_copy(flats[i], outs[i], out_sems.at[i])

    def pair_out(i, pair):
        at = pl.ds(pair * 128, 128)
        return pltpu.make_async_copy(flats[i].at[at], outs[i].at[at], head_sems.at[i - 4, pair])

    placed(pieces, w_ref, sems, me, True)
    tokens, width = x_ref.shape
    step = 256
    for b in range(tokens // step):
        rows = slice(b * step, (b + 1) * step)
        xor_rows(xt_ref.at[:, rows], x_ref[rows, :].T, me, count)
    out(0).start()
    high, low = split(xm_ref[...])
    wide = jnp.concatenate([xm_ref[...], jnp.zeros_like(xm_ref)], 0)
    xor_rows(xmt_ref, wide.T.astype(BF16)[:, :LANDMARKS], me, count)
    placed(pieces, w_ref, sems, me, False)
    both = w_ref[:, : 2 * width]
    marks = SCALE * (nn(high, both) + nn(low, both))
    qm = marks[:, :width].astype(BF16)
    km = marks[:, width:].astype(BF16)
    qm_ref[...] = qm
    km_ref[...] = km
    for i, (to, scale) in enumerate(((qt_ref, SCALE), (kt_ref, SCALE), (vt_ref, None))):
        for b in range(tokens // step):
            rows = slice(b * step, (b + 1) * step)
            y = nn(x_ref[rows, :], w_ref[:, i * width : (i + 1) * width])
            if scale is not None:
                y = y * scale
            y = y.astype(BF16)
            if i == 2 and b == 0:
                edge_ref[:REACH] = y[:REACH]
            if i == 2 and b == tokens // step - 1:
                edge_ref[REACH:] = y[step - REACH :]
            to[:, rows] = y.T
        out(1 + i).start()
    lane = lanes((LANDMARKS, 128))
    stats = jnp.zeros((LANDMARKS, 128), F32)
    pair = []
    for h in range(HEADS):
        s = nn(km[:, hs(h)], qt_ref[hs(h), :])
        s = jnp.exp(s - jnp.max(s, axis=0, keepdims=True))
        fw_ref[hs(h), :] = (s * (1.0 / jnp.sum(s, axis=0, keepdims=True))).astype(BF16)
        s = nn(qm[:, hs(h)], kt_ref[hs(h), :])
        top = jnp.max(s, axis=1, keepdims=True).astype(BF16).astype(F32)
        e = jnp.exp(s - top).astype(BF16)
        eb_ref[hs(h), :] = e
        total = jnp.sum(e.astype(F32), axis=1, keepdims=True)
        stats = jnp.where(lane == h, top, stats)
        stats = jnp.where(lane == 16 + h, total, stats)
        pair.append(nt(e, vt_ref[hs(h), :]))
        if h % 2:
            both = jnp.concatenate(pair, 1).astype(BF16)
            for d in range(msg_ref.shape[0]):
                msg_ref[d, h // 2] = both
            pair = []
            pair_out(4, h // 2).start()
            pair_out(5, h // 2).start()
    st_ref[...] = stats
    for d in range(msg_ref.shape[0]):
        msg_ref[d, HEADS // 2] = stat_message(stats)
    for i in range(4):
        out(i).wait()
    for h in range(HEADS // 2):
        pair_out(4, h).wait()
        pair_out(5, h).wait()


def stat_message(stats):
    lane = lanes(stats.shape)
    high = stats.astype(BF16).astype(F32)
    low = pltpu.roll(stats - high, 16, 1)
    return jnp.where((lane >= 32) & (lane < 48), low, high).astype(BF16)


def front(me, x, xm, pieces, size):
    tokens, width = x.shape
    pairs = HEADS // 2
    flat = shape((width, tokens), BF16)
    xt, qt, kt, vt, fw, eb, xmt, st, msg, qm, km, edge = call(
        functools.partial(front_kernel, len(pieces)),
        (me, x, xm, *pieces),
        [sspec(), vspec(), vspec()] + [aspec()] * len(pieces),
        [flat] * 6
        + [
            shape((width, LANDMARKS), BF16),
            shape((LANDMARKS, 128), F32),
            shape((size, pairs + 1, LANDMARKS, 128), BF16),
            shape((LANDMARKS, width), BF16),
            shape((LANDMARKS, width), BF16),
            shape((2 * REACH, width), BF16),
        ],
        [aspec()] * 6 + [vspec()] * 6,
        "front",
        cost(4.5e8, 1.6e6),
        scratch=[pltpu.VMEM((width, tokens), BF16) for _ in range(6)]
        + [
            pltpu.VMEM((width, 3 * width), BF16),
            pltpu.SemaphoreType.DMA((len(pieces),)),
            pltpu.SemaphoreType.DMA((4,)),
            pltpu.SemaphoreType.DMA((2, pairs)),
        ],
    )
    return xt, xmt, qt, kt, vt, fw, eb, st, msg, qm, km, edge


def merged(msg_ref, mixn_ref, st_ref):
    lane = lanes((LANDMARKS, 128))
    size = msg_ref.shape[0]
    stats = []
    for d in range(size):
        got = msg_ref[d, HEADS // 2].astype(F32)
        stats.append(got + jnp.where((lane >= 16) & (lane < 32), pltpu.roll(got, 112, 1), 0.0))
    largest = functools.reduce(jnp.maximum, stats)
    weights = [jnp.exp(jnp.minimum(st - largest, 0.0)) for st in stats]
    total = sum(st * pltpu.roll(w, 16, 1) for st, w in zip(stats, weights))
    st_ref[...] = jnp.where(lane < 16, largest, total)
    for i in range(HEADS // 2):

        def both(a, at):
            return jnp.where(lane < HDIM, a[:, at : at + 1], a[:, at + 1 : at + 2])

        y = sum(msg_ref[d, i].astype(F32) * both(weights[d], 2 * i) for d in range(size))
        mixn_ref[i] = y / both(total, 16 + 2 * i)


def eye(scale):
    n = LANDMARKS
    return jnp.where(
        lax.broadcasted_iota(jnp.int32, (n, n), 0) == lax.broadcasted_iota(jnp.int32, (n, n), 1),
        jnp.float32(scale),
        0.0,
    )


def landmark_softmax(qm, km, h):
    s = nt(qm[:, hs(h)], km[:, hs(h)])
    s = jnp.exp(s - jnp.max(s, axis=1, keepdims=True))
    return s / jnp.sum(s, axis=1, keepdims=True)


def first_inverse(a):
    columns = jnp.max(jnp.sum(a, axis=0, keepdims=True), axis=1, keepdims=True)
    rows = jnp.max(jnp.sum(a, axis=1, keepdims=True), axis=0, keepdims=True)
    return a.T * (1.0 / (columns * rows))


def inverse_kernel(size, me_ref, qm_ref, km_ref, z_ref, a_out, zs, ps, ms, ns, a_ref, p_ref, m_ref, n_ref):
    qm, km = qm_ref[...], km_ref[...]
    every = range(HEADS)
    slots = range(-(-HEADS // size))
    mine = [jnp.minimum(me_ref[1] + size * j, HEADS - 1) for j in slots]
    for h in every:
        a = landmark_softmax(qm, km, h)
        a_ref[h] = a
        z_ref[h] = first_inverse(a)
    for j in slots:
        a_out[j] = a_ref[mine[j]]

    def step(i, carry):
        p = [nn3(a_ref[h], z_ref[h]) for h in every]
        m = [eye(15.0) - nn3(x, eye(7.0) - x) for x in p]
        n = [eye(13.0) - nn3(x, y) for x, y in zip(p, m)]
        for h in every:
            p_ref[h] = p[h]
            m_ref[h] = m[h]
            n_ref[h] = n[h]
        for j in slots:
            ps[i, j] = p_ref[mine[j]]
            ms[i, j] = m_ref[mine[j]]
            ns[i, j] = n_ref[mine[j]]
            zs[i, j] = z_ref[mine[j]]
        for h in every:
            z_ref[h] = 0.25 * nn3(z_ref[h], n[h])
        return carry

    lax.fori_loop(0, PINV_ITERS, step, 0)


def inverse(me, qm, km, size):
    square = (HEADS, LANDMARKS, LANDMARKS)
    few = (-(-HEADS // size), LANDMARKS, LANDMARKS)
    return call(
        functools.partial(inverse_kernel, size),
        (me, qm, km),
        [sspec()] + [vspec()] * 2,
        [shape(square, F32), shape(few, F32)] + [shape((PINV_ITERS,) + few, F32)] * 4,
        [vspec()] * 6,
        "inverse",
        cost(1e8, 1e6),
        scratch=[pltpu.VMEM(square, F32)] * 4,
    )


def half(pair, h):
    return jnp.where(h % 2 == 0, pair[:, :HDIM], pair[:, HDIM:])


def inverse_step(z, p, m, n, a, gz, ga):
    g = 0.25 * gz
    g3 = -tn3(z, g)
    g2 = -tn3(p, g3)
    gp = nt3(g3, m) + nt3(g2, eye(7.0) - p) - tn3(p, g2)
    return nt3(g, n) + tn3(a, gp), ga + nt3(gp, z)


def score_grad(a, gfirst, ga):
    csum = jnp.sum(a, axis=0, keepdims=True)
    rsum = jnp.sum(a, axis=1, keepdims=True)
    cmax = jnp.max(csum, axis=1, keepdims=True)
    rmax = jnp.max(rsum, axis=0, keepdims=True)
    scale = 1.0 / (cmax * rmax)
    gs = jnp.sum(jnp.sum(gfirst * a.T, axis=1, keepdims=True), axis=0, keepdims=True)
    ctop = (csum == cmax).astype(F32)
    rtop = (rsum == rmax).astype(F32)
    gcol = -gs * scale / cmax * ctop / jnp.sum(ctop, axis=1, keepdims=True)
    grow = -gs * scale / rmax * rtop / jnp.sum(rtop, axis=0, keepdims=True)
    g = ga + gfirst.T * scale + gcol + grow
    return a * (g - jnp.sum(g * a, axis=1, keepdims=True))


def widen(out_ref, flat_ref, pair_ref, next_ref, odd):
    width, tokens = flat_ref.shape
    zero = jnp.zeros((EDGE - REACH, width), BF16)
    pair, other = pair_ref[...].astype(F32), next_ref[...].astype(F32)
    before = jnp.where(odd, pair[REACH:], other[REACH:]).astype(BF16)
    after = jnp.where(odd, other[:REACH], pair[:REACH]).astype(BF16)
    out_ref[:, :EDGE] = jnp.concatenate([zero, before], 0).T
    out_ref[:, EDGE : EDGE + tokens] = flat_ref[...]
    out_ref[:, EDGE + tokens :] = jnp.concatenate([after, zero], 0).T


def band(row, step):
    wide = jnp.broadcast_to(row, (step, step + 2 * EDGE))
    return pltpu.roll(wide, 0, 1, stride=1, stride_axis=0).astype(BF16)


def stacked(ref, h, step, margin):
    blocks = (ref.shape[1] - 2 * margin) // step if margin else ref.shape[1] // step
    return jnp.concatenate(
        [ref[hs(h), b * step : (b + 1) * step + 2 * margin] for b in range(blocks)], 0
    )


def pair_rows(tokens):
    return pl.BlockSpec((128, tokens), lambda i: (i, 0))


def pair_lanes(rows):
    return pl.BlockSpec((rows, 128), lambda i: (0, i))


def pair_block(*dims):
    return pl.BlockSpec((1, *dims), lambda i: (i, 0, 0))


def conv_kernel_body(me_ref, vt_ref, pair_ref, next_ref, taps_ref, out_ref, wide_ref):
    widen(wide_ref, vt_ref, pair_ref, next_ref, me_ref[1] % 2 == 1)
    step = 256
    for h in range(HEADS):
        y = nt(stacked(wide_ref, h, step, EDGE), band(taps_ref[h : h + 1, :], step))
        for b in range(vt_ref.shape[1] // step):
            out_ref[hs(h), b * step : (b + 1) * step] = y[b * HDIM : (b + 1) * HDIM, :]


def conv(me, vt, edges, taps):
    width, tokens = vt.shape
    return call(
        conv_kernel_body,
        (me, vt, *edges, taps),
        [sspec()] + [vspec()] * 4,
        shape(vt.shape, F32),
        vspec(),
        "conv",
        cost(2e9, 6e6),
        scratch=[pltpu.VMEM((width, tokens + 2 * EDGE), BF16)],
    )


def gelu_pair(x):
    phi = 0.5 * (1.0 + lax.erf(x * (0.5**0.5)))
    return x * phi, phi + x * ((0.5 / jnp.pi) ** 0.5 * jnp.exp(-0.5 * x * x))


def norm_stats(r):
    center = r - jnp.mean(r, axis=-1, keepdims=True)
    rstd = lax.rsqrt(jnp.mean(center * center, axis=-1, keepdims=True) + 1e-05)
    return center * rstd, rstd


def norm_back(gy, xhat, rstd):
    return rstd * (
        gy - jnp.mean(gy, axis=-1, keepdims=True) - xhat * jnp.mean(gy * xhat, axis=-1, keepdims=True)
    )


STEP = 256


def whole(a):
    return pl.BlockSpec(a.shape, lambda i, n=a.ndim: (0,) * n)


def fixed(*dims):
    return pl.BlockSpec(dims, lambda i, n=len(dims): (0,) * n)


def tall(rows):
    return pl.BlockSpec((rows, STEP), lambda i: (0, i))


def row(width):
    return pl.BlockSpec((STEP, width), lambda i: (i, 0))


def mid_kernel(count, me_ref, z_ref, msg_ref, fw_ref, conv_ref, x_ref, ct_ref, gains_ref, *refs):
    halves = 2 * count - 2
    wo, down, up = refs[:count], refs[count : 2 * count], refs[2 * count : 2 * count + halves]
    (ctx_ref, hidt_ref, act_ref, out_ref, redt_ref, ge_ref, first_ref, branch_ref, gct_ref, edge_ref,
     sums_ref, comb_ref, mixn_ref, st_ref, gc_ref, wo_ref, up_ref, down_ref, slope_ref,
     sems, up_sems) = refs[2 * count + halves :]
    me, side = me_ref[0], me_ref[1] % 2
    at = pl.program_id(0)
    begin = at == 0
    part = up_ref.shape[1] // count

    @pl.when(begin)
    def _():
        placed(wo, wo_ref, sems.at[0], me, True)
        placed_halves(up, up_ref, up_sems, me, side, True)
        placed(down, down_ref, sems.at[1], me, True)
        merged(msg_ref, mixn_ref, st_ref)
        for i in range(HEADS // 2):
            mixed = mixn_ref[i]
            comb_ref[i] = jnp.concatenate(
                [nn3(z_ref[2 * i], mixed[:, :HDIM]), nn3(z_ref[2 * i + 1], mixed[:, HDIM:])], 1
            ).astype(BF16)
        sums_ref[...] = jnp.zeros_like(sums_ref)
        gc_ref[...] = jnp.zeros_like(gc_ref)
        placed(wo, wo_ref, sems.at[0], me, False)

    for h in range(HEADS):
        att = tn(comb_ref[h // 2][:, hs(h % 2)], fw_ref[hs(h), :])
        ctx_ref[hs(h), :] = (att + conv_ref[hs(h), :]).astype(BF16)
    branch = nn(ctx_ref[...].T, wo_ref[...])
    xhat1, rstd1 = norm_stats(x_ref[...].astype(F32) + branch)
    hidden = xhat1 * gains_ref[0:1, :] + gains_ref[1:2, :]
    hid = hidden.astype(BF16)
    xor_rows(hidt_ref, hid.T, me, count)

    @pl.when(begin)
    def _():
        placed_halves(up, up_ref, up_sems, me, side, False)

    for c in range(count):
        cols = slice(c * part, (c + 1) * part)
        act, slope = gelu_pair(nn(hid, up_ref[:, cols]))
        act_ref[:, cols] = act.astype(BF16)
        slope_ref[:, cols] = slope.astype(BF16)

    @pl.when(begin)
    def _():
        placed(down, down_ref, sems.at[1], me, False)

    xhat, rstd = norm_stats(hidden + nn(act_ref[...], down_ref[...]))
    out_ref[...] = (xhat * gains_ref[2:3, :] + gains_ref[3:4, :]).astype(BF16)
    ct = ct_ref[...].astype(F32)
    sums_ref[2:3, :] = sums_ref[2:3, :] + jnp.sum(ct * xhat, axis=0, keepdims=True)
    sums_ref[3:4, :] = sums_ref[3:4, :] + jnp.sum(ct, axis=0, keepdims=True)
    second = norm_back(ct * gains_ref[2:3, :], xhat, rstd)
    red = second.astype(BF16)
    redt_ref[...] = red.T
    for k in range(count):
        cols = slice(k * part, (k + 1) * part)
        ge = nt(red, down_ref[cols, :]) * slope_ref[:, cols].astype(F32)
        ge_ref[:, cols] = ge.astype(BF16)
    g = second + nt(ge_ref[...], up_ref[...])
    sums_ref[0:1, :] = sums_ref[0:1, :] + jnp.sum(g * xhat1, axis=0, keepdims=True)
    sums_ref[1:2, :] = sums_ref[1:2, :] + jnp.sum(g, axis=0, keepdims=True)
    first = norm_back(g * gains_ref[0:1, :], xhat1, rstd1)
    first_ref[...] = first
    back = first.astype(BF16)
    branch_ref[...] = back
    gctx = nt(back, wo_ref[...]).astype(BF16)

    @pl.when(begin)
    def _():
        edge_ref[:REACH] = gctx[:REACH]

    @pl.when(at == pl.num_programs(0) - 1)
    def _():
        edge_ref[REACH:] = gctx[gctx.shape[0] - REACH :]

    gct_ref[...] = gctx.T
    for i in range(HEADS // 2):
        gc_ref[i] = gc_ref[i] + jnp.concatenate(
            [nt(fw_ref[hs(h), :], gct_ref[hs(h), :]) for h in (2 * i, 2 * i + 1)], 1
        )


def mid(me, z, msgs, fw, convt, x, ct, gains, wo, up, down, after=()):
    tokens, width = x.shape
    ff = up[0].shape[1]
    pairs = HEADS // 2
    pieces = (*wo, *down, *up)
    flat, wide = shape((width, tokens), BF16), shape((tokens, ff), BF16)
    return call(
        functools.partial(mid_kernel, len(wo)),
        (me, z, msgs, fw, convt, x, ct, gains, *pieces),
        [sspec(), whole(z), whole(msgs), tall(width), tall(width), row(width), row(width), whole(gains)]
        + [aspec()] * len(pieces),
        [
            flat,
            flat,
            wide,
            shape((tokens, width), BF16),
            flat,
            wide,
            shape((tokens, width), F32),
            shape((tokens, width), BF16),
            flat,
            shape((2 * REACH, width), BF16),
            shape((8, width), F32),
            shape((pairs, LANDMARKS, 128), BF16),
            shape((pairs, LANDMARKS, 128), F32),
            shape((LANDMARKS, 128), F32),
            shape((pairs, LANDMARKS, 128), F32),
        ],
        [tall(width), tall(width), row(ff), row(width), tall(width), row(ff), row(width), row(width),
         tall(width), fixed(2 * REACH, width), fixed(8, width),
         fixed(pairs, LANDMARKS, 128), fixed(pairs, LANDMARKS, 128), fixed(LANDMARKS, 128),
         fixed(pairs, LANDMARKS, 128)],
        "mid",
        cost(2e9, 3e6),
        grid=(tokens // STEP,),
        scratch=[
            pltpu.VMEM((width, width), BF16),
            pltpu.VMEM((width, ff), BF16),
            pltpu.VMEM((ff, width), BF16),
            pltpu.VMEM((STEP, ff), BF16),
            pltpu.SemaphoreType.DMA((2, len(wo))),
            pltpu.SemaphoreType.DMA((len(up),)),
        ],
        after=after,
    )


def grad_down_kernel(count, me_ref, red_ref, act_ref, *outs):
    part = act_ref.shape[1] // count
    for k in range(count):
        at = pl.ds(pl.multiple_of((me_ref[0] ^ k) * part, 128), part)
        outs[k][...] = nn(red_ref[...], act_ref[:, at]).astype(BF16)


def grad_down(count, me, redt, act, after=()):
    width = redt.shape[0]
    return call(
        functools.partial(grad_down_kernel, count),
        (me, redt, act),
        [sspec(), vspec(), vspec()],
        [shape((width, act.shape[1] // count), BF16)] * count,
        [vspec()] * count,
        "grad_down",
        cost(5e8, 1e6),
        after=after,
    )


def grad_up_kernel(count, hid_ref, ge_ref, *outs):
    y = nn(hid_ref[...], ge_ref[...]).astype(BF16)
    rows = y.shape[0] // count
    for k in range(count):
        outs[k][...] = y[k * rows : (k + 1) * rows]


def grad_up(count, hidt, ge, after=()):
    width, tokens = hidt.shape
    ff = ge.shape[1]
    step = 768
    return call(
        functools.partial(grad_up_kernel, count),
        (hidt, ge),
        [whole(hidt), pl.BlockSpec((tokens, step), lambda i: (0, i))],
        [shape((width // count, ff), BF16)] * count,
        [pl.BlockSpec((width // count, step), lambda i: (0, i))] * count,
        "grad_up",
        cost(5e8, 1e6),
        grid=(ff // step,),
        after=after,
    )


class Moves:
    def __init__(self, sems):
        self.sems, self.used, self.open = sems, 0, []

    def start(self, src, dst):
        copy = pltpu.make_async_copy(src, dst, self.sems.at[self.used])
        self.used += 1
        copy.start()
        self.open.append(copy)
        return copy

    def wait(self, *copies):
        for copy in copies or list(self.open):
            copy.wait()
            self.open.remove(copy)


def gap_kernel(count, me_ref, gct_hbm, fw_hbm, qt_hbm, vt_hbm, ctx_hbm, branch_hbm, comb_ref, km_ref,
               vb_ref, va_ref, gb_ref, ga_ref, taps_ref, sums_ref, *refs):
    outs = refs[:count]
    (gq_hbm, gvc_hbm, gkm_ref, gct_ref, fw_ref, qt_ref, vt_ref, ctx_ref, branch_ref, gq_ref, gvc_ref,
     vwide, gwide, y_ref, sems) = refs[count:]
    moves = Moves(sems)
    lead = [
        moves.start(a, b)
        for a, b in ((gct_hbm, gct_ref), (fw_hbm, fw_ref), (qt_hbm, qt_ref))
    ]
    values = moves.start(vt_hbm, vt_ref)
    rest = [moves.start(ctx_hbm, ctx_ref), moves.start(branch_hbm, branch_ref)]
    km = km_ref[...]
    moves.wait(*lead)
    pair = []
    for h in range(HEADS):
        comb = comb_ref[h // 2][:, hs(h % 2)]
        pf = fw_ref[hs(h), :].astype(F32)
        g = nn(comb, gct_ref[hs(h), :])
        gs = (pf * (g - jnp.sum(pf * g, axis=0, keepdims=True))).astype(BF16)
        gq_ref[hs(h), :] = tn(km[:, hs(h)], gs).astype(BF16)
        pair.append(nt(gs, qt_ref[hs(h), :]))
        if h % 2:
            gkm_ref[:, (h - 1) * HDIM : (h + 1) * HDIM] = jnp.concatenate(pair, 1)
            pair = []
    moves.start(gq_ref, gq_hbm)
    moves.wait(values)
    odd = me_ref[1] % 2 == 1
    widen(vwide, vt_ref, vb_ref, va_ref, odd)
    widen(gwide, gct_ref, gb_ref, ga_ref, odd)
    step = 256
    tokens = vt_ref.shape[1]
    flip = (
        lax.broadcasted_iota(jnp.int32, (step, step), 0)
        + lax.broadcasted_iota(jnp.int32, (step, step), 1)
        == step - 1
    ).astype(BF16)
    rows = []
    for h in range(HEADS):
        y = nt(stacked(gwide, h, step, EDGE), band(taps_ref[h : h + 1, :], step))
        for b in range(tokens // step):
            gvc_ref[hs(h), b * step : (b + 1) * step] = y[b * HDIM : (b + 1) * HDIM, :]
        turned = nn(stacked(gct_ref, h, step, 0), flip).astype(BF16)
        d = tn(turned, stacked(vwide, h, step, EDGE))
        d = pltpu.roll(d, 0, 1, stride=1, stride_axis=0)
        rows.append(jnp.sum(d, axis=0, keepdims=True))
    moves.start(gvc_ref, gvc_hbm)
    rows = jnp.concatenate(rows + [jnp.zeros((4, step + 2 * EDGE), F32)], 0)
    first = step - 1 + EDGE - REACH
    taps = pltpu.roll(rows, step + 2 * EDGE - first, 1)[:HEADS, :128]
    width = ctx_ref.shape[0]
    taps = jnp.concatenate([taps, jnp.zeros((HEADS, width - 128), F32)], 1)
    little = jnp.concatenate(
        [sums_ref[0:4, :], taps, jnp.zeros((128 - 4 - HEADS, width), F32)], 0
    )
    y_ref[:, width:] = little.T.astype(BF16)
    moves.wait(*rest)
    y_ref[:, :width] = nn(ctx_ref[...], branch_ref[...]).astype(BF16)
    size = width // count
    for k in range(count):
        outs[k][...] = y_ref[pl.ds(pl.multiple_of((me_ref[0] ^ k) * size, 16), size), :]
    moves.wait()


def gap(count, me, gct, fw, qt, vt, ctxt, branch, comb, km, vb, va, gb, ga, taps, sums, after=()):
    width, tokens = vt.shape
    flat = pltpu.VMEM((width, tokens), BF16)
    wide = pltpu.VMEM((width, tokens + 2 * EDGE), BF16)
    *pieces, gq, gvc, gkm = call(
        functools.partial(gap_kernel, count),
        (me, gct, fw, qt, vt, ctxt, branch, comb, km, vb, va, gb, ga, taps, sums),
        [sspec()] + [aspec()] * 6 + [vspec()] * 8,
        [shape((width // count, width + 128), BF16)] * count
        + [shape(gct.shape, BF16), shape(gct.shape, F32), shape(km.shape, F32)],
        [vspec()] * count + [aspec()] * 2 + [vspec()],
        "gap",
        cost(1e9, 1e6),
        scratch=[flat] * 5
        + [
            pltpu.VMEM((tokens, width), BF16),
            flat,
            pltpu.VMEM((width, tokens), F32),
            wide,
            wide,
            pltpu.VMEM((width, width + 128), BF16),
            pltpu.SemaphoreType.DMA((8,)),
        ],
        after=after,
    )
    return pieces, gq, gvc, gkm


def rear_kernel(count, size, me_ref, eb_hbm, vt_hbm, kt_hbm, gvc_hbm, xt_hbm, gq_hbm, z_ref, most_ref, last_ref,
                mixn_ref, st_ref, own_ref, qm_ref, km_ref, gkmp_ref, xmt_ref, a_ref, zs, ps, ms, ns, *refs):
    outs = refs[:count]
    (gk_hbm, gv_hbm, land_ref, gc_ref, gqm_ref, gkm_ref, eb_ref, vt_ref, kt_ref, gvc_ref, xt_ref, gq_ref, gk_ref, gv_ref,
     y_ref, sems) = refs[count:]
    moves = Moves(sems)
    early = [
        moves.start(a, b)
        for a, b in ((vt_hbm, vt_ref), (eb_hbm, eb_ref), (kt_hbm, kt_ref), (gvc_hbm, gvc_ref))
    ]
    late = [moves.start(xt_hbm, xt_ref), moves.start(gq_hbm, gq_ref)]
    qm, km = qm_ref[...], km_ref[...]
    lane = lanes((LANDMARKS, 128))
    gc_ref[...] = most_ref[...] + last_ref[...].astype(F32)
    slots = range(-(-HEADS // size))
    heads = [me_ref[1] + size * j for j in slots]
    safe = [jnp.minimum(h, HEADS - 1) for h in heads]
    gz = [nt3(half(gc_ref[h // 2], h), half(mixn_ref[h // 2], h)) for h in safe]
    ga = [jnp.zeros((LANDMARKS, LANDMARKS), F32) for _ in slots]
    stats = st_ref[...]
    scale = jnp.exp(own_ref[...] - stats)
    moves.wait(*early)
    for p in range(HEADS // 2):
        if p < PINV_ITERS:
            i = PINV_ITERS - 1 - p
            for j in slots:
                gz[j], ga[j] = inverse_step(
                    zs[i, j], ps[i, j], ms[i, j], ns[i, j], a_ref[j], gz[j], ga[j]
                )
        pair = []
        for h in (2 * p, 2 * p + 1):
            gmix = tn3(z_ref[h], gc_ref[p][:, hs(h % 2)]).astype(BF16)
            dot = jnp.sum(gmix.astype(F32) * mixn_ref[p][:, hs(h % 2)], axis=1, keepdims=True)
            factor = scale[:, h : h + 1] / stats[:, 16 + h : 17 + h]
            pb = eb_ref[hs(h), :].astype(F32) * factor
            gs = (pb * (nn(gmix, vt_ref[hs(h), :]) - dot)).astype(BF16)
            gk_ref[hs(h), :] = tn(qm[:, hs(h)], gs).astype(BF16)
            gv_ref[hs(h), :] = (tn(gmix, pb.astype(BF16)) + gvc_ref[hs(h), :]).astype(BF16)
            pair.append(nt(gs, kt_ref[hs(h), :]))
        both = slice(p * 128, p * 128 + 128)
        gqm_ref[:, both] = jnp.concatenate(pair, 1)
        gkm_ref[:, both] = gkmp_ref[:, both]
    moves.start(gk_ref, gk_hbm)
    moves.start(gv_ref, gv_hbm)
    moves.wait(*late)
    width = xt_ref.shape[0]
    rows = width // count

    def weight(i, y):
        y_ref[i] = y.astype(BF16)
        for k in range(count):
            moves.start(y_ref.at[i, pl.ds(k * rows, rows)], outs[k].at[i])

    weight(2, nt(xt_ref[...], gv_ref[...]))
    for j in slots:
        h = safe[j]
        high, low = split(score_grad(a_ref[j], gz[j], ga[j]))
        at = pl.ds(pl.multiple_of(h // 2 * 128, 128), 128)
        qmh = half(qm_ref[:, at].astype(F32), h).astype(BF16)
        kmh = half(km_ref[:, at].astype(F32), h).astype(BF16)
        gq = nn(jnp.concatenate([high, low], 1), jnp.concatenate([kmh] * 2, 0))
        gk = tn(jnp.concatenate([high, low], 0), jnp.concatenate([qmh] * 2, 0))
        mine = ((lane >= HDIM) == (h % 2 == 1)) & (heads[j] < HEADS)
        gqm_ref[:, at] = gqm_ref[:, at] + jnp.where(mine, jnp.concatenate([gq, gq], 1), 0.0)
        gkm_ref[:, at] = gkm_ref[:, at] + jnp.where(mine, jnp.concatenate([gk, gk], 1), 0.0)
    land_ref[...] = jnp.concatenate([gqm_ref[...], gkm_ref[...]], 1).astype(BF16)
    weight(0, nt(xt_ref[...], gq_ref[...]) + nn(xmt_ref[...], gqm_ref[...].astype(BF16)))
    weight(1, nt(xt_ref[...], gk_ref[...]) + nn(xmt_ref[...], gkm_ref[...].astype(BF16)))
    moves.wait()


def rear(count, size, me, eb, vt, kt, gvc, xt, gq, z, gc, got, mixn, stats, own, qm, km, gkm, xmt, a, saved,
         after=()):
    width, tokens = vt.shape
    rows = width // count
    flat = pltpu.VMEM((width, tokens), BF16)
    mark = pltpu.VMEM(qm.shape, F32)
    *pieces, gk, gv, land = call(
        functools.partial(rear_kernel, count, size),
        (me, eb, vt, kt, gvc, xt, gq, z, gc, got, mixn, stats, own, qm, km, gkm, xmt, a, *saved),
        [sspec()] + [aspec()] * 6 + [vspec()] * 15,
        [shape((3, rows, width), BF16)] * count + [shape(vt.shape, BF16)] * 2
        + [shape((LANDMARKS, 2 * width), BF16)],
        [aspec()] * (count + 2) + [vspec()],
        "rear",
        cost(2e9, 2e6),
        scratch=[pltpu.VMEM(gc.shape, F32)]
        + [mark] * 2
        + [flat] * 3
        + [pltpu.VMEM((width, tokens), F32)]
        + [flat] * 4
        + [
            pltpu.VMEM((3, width, width), BF16),
            pltpu.SemaphoreType.DMA((8 + 3 * count,)),
        ],
        after=after,
    )
    return [piece.reshape(3 * rows, width) for piece in pieces], gk, gv, land


def last_kernel(count, me_ref, gq_ref, gk_ref, gv_ref, first_ref, *refs):
    pieces = refs[:count]
    out_ref, w_ref, sems = refs[count:]
    me = me_ref[0]
    width = gq_ref.shape[0]

    @pl.when(pl.program_id(0) == 0)
    def _():
        placed(pieces, w_ref, sems, me, True)
        placed(pieces, w_ref, sems, me, False)

    wq, wk, wv = (w_ref[:, i * width : (i + 1) * width] for i in range(3))
    g = SCALE * (nn(wq, gq_ref[...]) + nn(wk, gk_ref[...])) + nn(wv, gv_ref[...])
    out_ref[...] = first_ref[...] + g.T


def last(me, gq, gk, gv, first, pieces, after=()):
    width, tokens = gq.shape
    return call(
        functools.partial(last_kernel, len(pieces)),
        (me, gq, gk, gv, first, *pieces),
        [sspec(), tall(width), tall(width), tall(width), row(width)] + [aspec()] * len(pieces),
        shape((tokens, width), F32),
        row(width),
        "last",
        cost(4e8, 1e6),
        grid=(tokens // STEP,),
        scratch=[
            pltpu.VMEM((width, 3 * width), BF16),
            pltpu.SemaphoreType.DMA((len(pieces),)),
        ],
        after=after,
    )


def share_kernel(segment, count, me_ref, own_ref, most_ref, *refs):
    pieces = refs[:count]
    out_ref, w_ref, sems = refs[count:]
    own = own_ref[...]
    width = own.shape[1] // 2
    pieces = [piece.at[:, pl.ds(0, 2 * width)] for piece in pieces]
    placed(pieces, w_ref, sems, me_ref[0], True)
    placed(pieces, w_ref, sems, me_ref[0], False)
    marks = (SCALE / segment) * (
        nt(own[:, :width].astype(BF16), w_ref[:, :width])
        + nt(own[:, width:].astype(BF16), w_ref[:, width : 2 * width])
    )
    for m in range(own.shape[0]):
        rows = slice(m * segment, (m + 1) * segment)
        out_ref[rows, :] = (most_ref[rows, :] + marks[m : m + 1, :]).astype(BF16)


def share(me, own, most, pieces):
    tokens, width = most.shape
    return call(
        functools.partial(share_kernel, tokens // own.shape[0], len(pieces)),
        (me, own, most, *pieces),
        [sspec(), vspec(), vspec()] + [aspec()] * len(pieces),
        shape(most.shape, BF16),
        vspec(),
        "share",
        cost(4e8, 1e6),
        scratch=[
            pltpu.VMEM((width, 2 * width), BF16),
            pltpu.SemaphoreType.DMA((len(pieces),)),
        ],
    )


def bits(axis):
    size = lax.axis_size(axis)
    assert size & (size - 1) == 0
    return [1 << i for i in range(size.bit_length() - 1)]


def swap(array, axis, bit):
    return lax.ppermute(array, axis, [(i, i ^ bit) for i in range(lax.axis_size(axis))])


def neighbours(array):
    size = lax.axis_size("seq")
    odd = [(i, i + 1) for i in range(1, size - 1, 2)]
    return swap(array, "seq", 1), lax.ppermute(array, "seq", odd + [(j, i) for i, j in odd])


def spread(pieces, axis, steps):
    for bit in steps:
        pieces = {**pieces, **{k | bit: swap(piece, axis, bit) for k, piece in pieces.items()}}
    return pieces


def far(array, axis):
    return spread({0: array}, axis, bits(axis)[1:])


def near(pieces, axis):
    pieces = spread(pieces, axis, bits(axis)[:1])
    return [pieces[k] for k in range(lax.axis_size(axis))]


def gathered(array, axis):
    return near(far(array, axis), axis)


def tie(*values):
    return lax.optimization_barrier(values)


def rows_out(array, groups=None):
    size = len(groups[0]) if groups else lax.axis_size("seq")
    blocks = array.reshape(size, -1, array.shape[1])
    return lax.all_to_all(blocks, "seq", 0, 0, axis_index_groups=groups)


def rows_in(blocks):
    return jnp.sum(blocks.astype(F32), axis=0)


def copies(array, axis, groups=None):
    size = len(groups[0]) if groups else lax.axis_size(axis)
    blocks = jnp.broadcast_to(array[None], (size, *array.shape))
    return lax.all_to_all(blocks, axis, 0, 0, axis_index_groups=groups)


class Total:
    def __init__(self, pieces, order):
        self.pieces = dict(enumerate(pieces))
        self.order = list(order)
        self.back = [step for step in reversed(order) if step[0] != "swap"]
        self.got = None

    def send(self, *values):
        if not self.order and not self.back:
            return values
        back = not self.order
        kind, what = self.back[0] if back else self.order[0]
        axis = "seq"
        if kind == "swap":
            axis = "fsdp"
            sent = {k: p for k, p in self.pieces.items() if k & what}
            self.pieces = {k: p for k, p in self.pieces.items() if not k & what}
        elif kind == "half" and not back:
            piece = self.pieces[0]
            upper = ((lax.axis_index("seq") & what) != 0).astype(jnp.int32)
            half = piece.shape[0] // 2
            self.pieces = {0: lax.dynamic_slice_in_dim(piece, upper * half, half, 0)}
            sent = {0: lax.dynamic_slice_in_dim(piece, (1 - upper) * half, half, 0)}
        elif kind == "rows" and back:
            size = len(what[0]) if what else lax.axis_size("seq")
            sent = {0: jnp.broadcast_to(self.pieces[0][None], (size, *self.pieces[0].shape))}
        elif kind == "rows":
            size = len(what[0]) if what else lax.axis_size("seq")
            sent = {0: self.pieces[0].reshape(size, -1, self.pieces[0].shape[1])}
        else:
            sent = dict(self.pieces)
        if values:
            sent, values = tie(sent, values)
        if kind == "rows":
            self.got = {
                k: lax.all_to_all(p, "seq", 0, 0, axis_index_groups=what) for k, p in sent.items()
            }
        else:
            self.got = {k: swap(p, axis, what) for k, p in sent.items()}
        return values

    def take(self):
        if self.order:
            kind, what = self.order.pop(0)
            if kind == "rows":
                self.pieces = {0: rows_in(self.got[0]).astype(BF16)}
            else:
                extra = what if kind == "swap" else 0
                self.pieces = {
                    k: (p.astype(F32) + self.got[k | extra].astype(F32)).astype(BF16)
                    for k, p in self.pieces.items()
                }
        else:
            kind, what = self.back.pop(0)
            mine, other = self.pieces[0], self.got[0]
            if kind == "rows":
                self.pieces = {0: other.reshape(-1, other.shape[2])}
            else:
                upper = (lax.axis_index("seq") & what) != 0
                self.pieces = {
                    0: jnp.where(
                        upper, jnp.concatenate([other, mine], 0), jnp.concatenate([mine, other], 0)
                    )
                }
        self.got = None

    def step(self, *values):
        self.got, values = tie(self.got, values)
        self.take()
        return self.send(*values)

    def finish(self):
        while self.got is not None:
            self.step()
        return self.pieces[0]


def orders():
    size = lax.axis_size("seq")
    over = [("swap", bit) for bit in bits("fsdp")]
    parts = size // 4
    groups = [[low + parts * high for high in range(4)] for low in range(parts)]
    near = [("half", bit) for bit in bits("seq") if bit < parts]
    tree = over + [("half", bit) for bit in bits("seq")]
    return over, over + near + [("rows", groups)], over + [("rows", None)], tree


def shards(
    inputs,
    cotangent,
    query_weight,
    key_weight,
    value_weight,
    output_weight,
    up_weight,
    down_weight,
    norm_gain,
    norm_shift,
    final_gain,
    final_shift,
    conv_kernel,
):
    x = inputs[0]
    ct = cotangent[0]
    tokens, width = x.shape
    marks = LANDMARKS // lax.axis_size("seq")
    segment = tokens // marks
    count = lax.axis_size("fsdp")
    rows = width // count
    here = lax.axis_index("fsdp")
    place = lax.axis_index("seq")
    size = lax.axis_size("seq")
    me = jnp.stack([here, place]).astype(jnp.int32)
    over, nested, flat, tree = orders()

    packed, xm = pack(x, (query_weight, key_weight, value_weight), size, marks)
    first_weights = far(packed, "fsdp")
    space = 256 + 2 * EDGE
    taps = jnp.pad(conv_kernel.T, ((0, 4), (EDGE - REACH, space - KERNEL - EDGE + REACH)))
    spat = jnp.pad(conv_kernel[::-1].T, ((0, 4), (EDGE - REACH, space - KERNEL - EDGE + REACH)))
    xm, taps, spat, me = tie(xm, taps, spat, me)
    xm = lax.all_to_all(xm, "seq", 0, 0).reshape(LANDMARKS, width)
    gains = jnp.stack([norm_gain, norm_shift, final_gain, final_shift] * 2)
    gains = gathered(gains, "fsdp")
    first_weights, gains, xm, output_weight = tie(first_weights, gains, xm, output_weight)
    first_weights, up_weight, output_weight, down_weight = tie(
        first_weights, up_weight, output_weight, down_weight
    )
    wqkv = near(first_weights, "fsdp")
    side = (place & 1).astype(jnp.int32)
    up_far = spread({0: lax.dynamic_slice_in_dim(up_weight, side * (rows // 2), rows // 2, 0)}, "fsdp", bits("fsdp")[1:])
    up_far = [up_far[k] for k in range(2, count, 2)]
    wo = far(output_weight, "fsdp")
    down = far(down_weight, "fsdp")
    source = lax.broadcasted_iota(jnp.int32, (8, width), 1) // rows ^ here
    gains = sum(
        jnp.where(source == k, jnp.concatenate([piece.astype(F32)] * count, 1), 0.0)
        for k, piece in enumerate(gains)
    )

    (xt, xmt, qt, kt, vt, fw, eb, own, msg, qm, km, v_edge) = front(me, x, xm, wqkv, size)
    v_edges = neighbours(v_edge)
    msg, up_far, v_edges = tie(msg, up_far, v_edges)
    msgs = lax.all_to_all(msg, "seq", 0, 0)
    up_other = [swap(piece, "seq", 1) for piece in up_far]
    z, a, *saved = inverse(me, qm, km, size)
    v_edges, z = tie(v_edges, z)
    convt = conv(me, vt, v_edges, taps)
    down, wo, convt, up_far, up_other = tie(down, wo, convt, up_far, up_other)
    up = [up_weight, swap(up_weight, "fsdp", 1)]
    for mine, other in zip(up_far, up_other):
        up += [mine, other, swap(mine, "fsdp", 1), swap(other, "fsdp", 1)]
    wo = near(wo, "fsdp")
    down = near(down, "fsdp")

    (ctxt, hidt, act, out, redt, ge, first, branch, gct, g_edge, sums, comb, mixn, stats, gc) = mid(
        me, z, msgs, fw, convt, x, ct, gains, wo, up, down
    )
    hops = bits("seq")

    def exchange(bit):
        return swap(gc.astype(BF16), "seq", bit)

    got = exchange(hops[0])
    g_edges = neighbours(g_edge)
    d_up = grad_up(count, hidt, ge)
    t_up = Total(d_up, tree)
    t_up.send()
    got, d_up, g_edges = tie(got, d_up, g_edges)
    gc = gc + got.astype(F32)
    got = exchange(hops[1])
    (act,) = t_up.step(act)
    d_down = grad_down(count, me, redt, act, after=d_up)
    t_down = Total(d_down, over)
    t_down.send()
    got, d_down = tie(got, d_down)
    gc = gc + got.astype(F32)
    got = exchange(hops[2])
    gct, d_down = t_down.step(gct, d_down)
    d_o, gq, gvc, gkm = gap(
        count, me, gct, fw, qt, vt, ctxt, branch, comb, km, *v_edges, *g_edges, spat, sums, after=d_down
    )
    t_o = Total(d_o, over)
    t_o.send()
    got, gvc = tie(got, gvc)
    for bit in hops[3:]:
        gc = gc + got.astype(F32)
        got = exchange(bit)
    (got,) = t_up.step(got)
    (got,) = t_o.step(got)
    d_qkv, gk, gv, land = rear(
        count, size, me, eb, vt, kt, gvc, xt, gq, z, gc, got, mixn, stats, own, qm, km, gkm, xmt, a, saved, after=d_o
    )
    t_qkv = Total(d_qkv, tree)
    t_qkv.send()
    landed = rows_out(land)
    while t_o.got is not None:
        (gk,) = t_o.step(gk)
    g_o = t_o.pieces[0]
    while t_down.got is not None:
        (gk,) = t_down.step(gk)
    part = t_down.pieces[0].shape[1]
    g_down = t_down.pieces[0].reshape(-1, width)
    sizes = [g_down.shape[0], rows, rows * 128 // width]
    both = jnp.concatenate([g_down, g_o[:, :width], g_o[:, width:].reshape(-1, width)], 0)
    t_both = Total([both], tree[len(over) :])
    (gk,) = t_both.send(gk)
    (gk,) = t_up.step(gk)
    for _ in over[:-1]:
        (gk,) = t_qkv.step(gk)
    most = last(me, gq, gk, gv, first, wqkv)
    for t in (t_up, t_both):
        (most,) = t.step(most)
    landed, most = tie(landed, most)
    grad_x = share(me, rows_in(landed), most, wqkv)
    g_up = g_both = None
    while any(t.got is not None for t in (t_qkv, t_up, t_both)):
        for t in (t_qkv, t_up, t_both):
            if t.got is not None:
                (grad_x,) = t.step(grad_x)
        if g_up is None and t_up.got is None:
            g_up, grad_x = tie(t_up.pieces[0].astype(F32), grad_x)
        if g_both is None and t_both.got is None:
            both = t_both.pieces[0].astype(F32)
            little = both[sizes[0] + sizes[1] :].reshape(rows, 128)
            tap = jnp.where(here == 0, little[:KERNEL, 4 : 4 + HEADS], 0.0)
            g_both = (
                both[: sizes[0]].reshape(width, part).T,
                both[sizes[0] : sizes[0] + sizes[1]],
                [little[:, i] for i in range(4)],
                tap,
            )
            g_both, grad_x = tie(g_both, grad_x)
            g_down, g_o, g_gains, tap = g_both
            for _, bit in over:
                tap = tap + swap(tap, "fsdp", bit)
    qkv = t_qkv.pieces[0].astype(F32)

    return (
        out[None],
        grad_x[None],
        SCALE * qkv[:rows],
        SCALE * qkv[rows : 2 * rows],
        qkv[2 * rows :],
        g_o,
        g_up,
        g_down,
        g_gains[0],
        g_gains[1],
        g_gains[2],
        g_gains[3],
        tap,
    )


def solution(mesh):
    tokens = P("fsdp", "seq", None)
    matrix = P("fsdp", None)
    row = P("fsdp")
    in_specs = (tokens,) * 2 + (matrix,) * 6 + (row,) * 4 + (P(),)
    out_specs = (tokens,) * 2 + (matrix,) * 6 + (row,) * 4 + (P(),)
    return jax.shard_map(shards, mesh=mesh, in_specs=in_specs, out_specs=out_specs, check_vma=False)
```
